32 devices in a mesh: seq: 4 (over y, x), blk: 8 (over z, core).
Axes of the slice: x: 2, y: 2, z: 4, core: 2. Of those that a mesh axis runs over, the one named last changes fastest.
Arguments:
- tokens: bfloat16 [8, 1024, 768], P('seq', 'blk'), may hold values from -6 to 6
- grad_out: bfloat16 [8, 1024, 768], P('seq', 'blk'), may hold values from -6 to 6
- masked: int32 [8, 1024], P('seq', 'blk'), may hold values from 0 to 1, as said below
- token_order: int32 [8, 12, 1024], P('seq', None, 'blk'), may hold values from 0 to 127, as said below
- cluster_match: int32 [8, 12, 8], P('seq', None, 'blk'), may hold values from 0 to 7, each once within a row
- w_query: bfloat16 [768, 768], P(('seq', 'blk')), may hold values from -0.3125 to 0.3125
- w_key: bfloat16 [768, 768], P(('seq', 'blk')), may hold values from -0.3125 to 0.3125
- w_value: bfloat16 [768, 768], P(('seq', 'blk')), may hold values from -0.21875 to 0.21875
- w_out: bfloat16 [768, 768], P(('seq', 'blk')), may hold values from -0.875 to 0.875
- w_up: bfloat16 [768, 3072], P(('seq', 'blk')), may hold values from -0.21875 to 0.21875
- w_down: bfloat16 [3072, 768], P(('seq', 'blk')), may hold values from -0.109375 to 0.109375
- b_query: bfloat16 [768], P(('seq', 'blk')), may hold values from -1.75 to 1.75
- b_value: bfloat16 [768], P(('seq', 'blk')), may hold values from -1.75 to 1.75
- b_out: bfloat16 [768], P(('seq', 'blk')), may hold values from -1.75 to 1.75
- b_up: bfloat16 [3072], P(('seq', 'blk')), may hold values from -1.75 to 1.75
- b_down: bfloat16 [768], P(('seq', 'blk')), may hold values from -1.75 to 1.75
- gain_attn: bfloat16 [768], P(('seq', 'blk')), may hold values from 0.5 to 1.5
- shift_attn: bfloat16 [768], P(('seq', 'blk')), may hold values from -1.75 to 1.75
- gain_ffn: bfloat16 [768], P(('seq', 'blk')), may hold values from 0.5 to 1.5
- shift_ffn: bfloat16 [768], P(('seq', 'blk')), may hold values from -1.75 to 1.75
Outputs:
- output: bfloat16 [8, 1024, 768], P('seq', 'blk')
- d_tokens: float32 [8, 1024, 768], P('seq', 'blk')
- d_w_query: float32 [768, 768], P(('seq', 'blk'))
- d_w_key: float32 [768, 768], P(('seq', 'blk'))
- d_w_value: float32 [768, 768], P(('seq', 'blk'))
- d_w_out: float32 [768, 768], P(('seq', 'blk'))
- d_w_up: float32 [768, 3072], P(('seq', 'blk'))
- d_w_down: float32 [3072, 768], P(('seq', 'blk'))
- d_b_query: float32 [768], P(('seq', 'blk'))
- d_b_value: float32 [768], P(('seq', 'blk'))
- d_b_out: float32 [768], P(('seq', 'blk'))
- d_b_up: float32 [3072], P(('seq', 'blk'))
- d_b_down: float32 [768], P(('seq', 'blk'))
- d_gain_attn: float32 [768], P(('seq', 'blk'))
- d_shift_attn: float32 [768], P(('seq', 'blk'))
- d_gain_ffn: float32 [768], P(('seq', 'blk'))
- d_shift_ffn: float32 [768], P(('seq', 'blk'))
The draws below stay inside these ranges and needn't reach their ends.
Inputs may be any that keep to these rules, and one draw needn't show every extreme that they name: `token_order`: within each aligned block of 128 positions, a head's entries are each of 0 to 127 once. `cluster_match`: for each sequence and head, every key cluster is named once. `masked`: the share of ones varies from sequence to sequence (between 1/32 and 1/2).
All inputs are finite; a program needn't handle non-finite values.
Results may differ from the reference program's by a relative error of at most 0.015.
Values may be sent and summed in bfloat16 or wider, within the bound.
A program may use at most 192 MiB of HBM per device.

```python
import math
import jax
import jax.numpy as jnp
from jax import lax

D = 768
HEADS = 12
HD = 64
FF = 3072
CL = 128
TS = 128
SEQS = 8
SEQLEN = 1024
NCL = 8


def draw_token_order(key, part):
    blocks = SEQLEN // TS
    keys_all = jax.random.split(key, SEQS * HEADS * blocks)

    def one_block(block_key):
        return jax.random.permutation(block_key, TS)
    orders = jax.vmap(one_block)(keys_all)
    return orders.reshape(SEQS, HEADS, SEQLEN).astype(jnp.int32)


def draw_masked(key, part):
    level_key = jax.random.fold_in(key, 11)
    pick_key = jax.random.fold_in(key, 23)
    levels = jax.random.randint(level_key, (SEQS, 1), 0, 5)
    limits = jnp.left_shift(jnp.ones((SEQS, 1), jnp.int32), levels.astype(jnp.int32))
    picks = jax.random.randint(pick_key, (SEQS, SEQLEN), 0, 32)
    return (picks < limits).astype(jnp.int32)


def block_levels(rng, dims, cuts, least, largest):
    def one(position, shards_of):
        steps = jax.random.uniform(jax.random.fold_in(jax.random.fold_in(rng, 6), position), (shards_of,), jnp.float32, least / len(cuts), largest / len(cuts))
        return jnp.repeat(jnp.exp(steps), dims[position] // shards_of).reshape((-1,) + (1,) * (len(dims) - position - 1))

    factor_of = one(*cuts[0])
    for cut in cuts[1:]:
        factor_of = factor_of * one(*cut)
    return factor_of


def noise(key, shape, spread, most, pieces=(), kind=jnp.bfloat16):
    values = spread * jax.random.normal(key, shape, jnp.float32)
    if pieces:
        values = values * block_levels(key, shape, pieces, -0.22, 0.18)
    return jnp.clip(values, -most, most).astype(kind)


def setup_inputs(seed: int = 0) -> dict:
    key_of = jax.random.split(jax.random.key(seed), 21)
    tokens = noise(key_of[0], (SEQS, SEQLEN, D), 1.0, 6.0, ((0, 4), (1, 8)))
    grad_out = noise(key_of[1], (SEQS, SEQLEN, D), 1.0, 6.0, ((0, 4), (1, 8)))
    masked = draw_masked(jax.random.fold_in(key_of[20], 71), 0)
    token_order = draw_token_order(jax.random.fold_in(key_of[20], 71), 0)
    cluster_match = jax.vmap(lambda own: jax.random.permutation(own, NCL))(jax.random.split(key_of[4], SEQS * HEADS)).reshape((SEQS, HEADS, NCL)).astype(jnp.int32)
    w_query = noise(key_of[5], (D, D), (D // 2) ** -0.5, 0.3125, ((0, 32),))
    w_key = noise(key_of[6], (D, D), (D // 2) ** -0.5, 0.3125, ((0, 32),))
    w_value = noise(key_of[7], (D, D), D ** -0.5, 0.21875, ((0, 32),))
    w_out = noise(key_of[8], (D, D), (D // 16) ** -0.5, 0.875, ((0, 32),))
    w_up = noise(key_of[9], (D, FF), D ** -0.5, 0.21875, ((0, 32),))
    w_down = noise(key_of[10], (FF, D), FF ** -0.5, 0.109375, ((0, 32),))
    b_query = noise(key_of[11], (D,), 0.3, 1.75, ((0, 32),))
    b_value = noise(key_of[12], (D,), 0.3, 1.75, ((0, 32),))
    b_out = noise(key_of[13], (D,), 0.3, 1.75, ((0, 32),))
    b_up = noise(key_of[14], (FF,), 0.3, 1.75, ((0, 32),))
    b_down = noise(key_of[15], (D,), 0.3, 1.75, ((0, 32),))
    gain_attn = jnp.clip(1.0 + 0.1 * jax.random.normal(key_of[16], (D,), jnp.float32), 0.5, 1.5).astype(jnp.bfloat16)
    shift_attn = noise(key_of[17], (D,), 0.3, 1.75, ((0, 32),))
    gain_ffn = jnp.clip(1.0 + 0.1 * jax.random.normal(key_of[18], (D,), jnp.float32), 0.5, 1.5).astype(jnp.bfloat16)
    shift_ffn = noise(key_of[19], (D,), 0.3, 1.75, ((0, 32),))
    return {"tokens": tokens, "grad_out": grad_out, "masked": masked, "token_order": token_order, "cluster_match": cluster_match, "w_query": w_query, "w_key": w_key, "w_value": w_value, "w_out": w_out, "w_up": w_up, "w_down": w_down, "b_query": b_query, "b_value": b_value, "b_out": b_out, "b_up": b_up, "b_down": b_down, "gain_attn": gain_attn, "shift_attn": shift_attn, "gain_ffn": gain_ffn, "shift_ffn": shift_ffn}


EPS = 1e-05

@jax.custom_vjp
def low(v):
    return lax.optimization_barrier(v.astype(jnp.bfloat16)).astype(jnp.float32)

@jax.custom_vjp
def low_back(v):
    return v

def low_keep(v):
    return (low(v), None)

def low_pass(kept, grad):
    return (grad,)

def back_keep(v):
    return (v, None)

def back_low(kept, grad):
    return (low(grad),)
low.defvjp(low_keep, low_pass)
low_back.defvjp(back_keep, back_low)

def product(left, right):
    return jnp.dot(left, right, precision=lax.Precision.HIGHEST)

def norm_rows(hidden, gain_row, shift_row):
    row_mean = lax.optimization_barrier(jnp.mean(hidden, axis=-1, keepdims=True))
    centered = hidden - row_mean
    variance = lax.optimization_barrier(jnp.mean(centered * centered, axis=-1, keepdims=True))
    return centered * lax.rsqrt(variance + EPS) * gain_row + shift_row

def place_back(mixed_rows, positions):
    return jnp.zeros_like(mixed_rows).at[positions].set(mixed_rows)

def layer(tokens_seq, params, positions, matched):
    w_query, w_key, w_value, w_out, w_up, w_down, b_query, b_value, b_out, b_up, b_down, gain_attn, shift_attn, gain_ffn, shift_ffn = params
    length = tokens_seq.shape[0]
    score_scale = 1.0 / math.sqrt(HD)
    queries = low(low_back(product(tokens_seq, w_query) + b_query))
    key_rows = low(low_back(product(tokens_seq, w_key)))
    value_rows = low(low_back(product(tokens_seq, w_value) + b_value))

    def clustered(flat_rows):
        heads_first = flat_rows.reshape(length, HEADS, HD).transpose(1, 0, 2)
        picked = jnp.take_along_axis(heads_first, positions[:, :, None], axis=1)
        return picked.reshape(HEADS, NCL, CL, HD)
    query_perm = clustered(queries)
    key_perm = clustered(key_rows)
    value_perm = clustered(value_rows)
    key_sel = jnp.take_along_axis(key_perm, matched[:, :, None, None], axis=1)
    value_sel = jnp.take_along_axis(value_perm, matched[:, :, None, None], axis=1)
    scores = low_back(jnp.einsum('hcqd,hckd->hcqk', query_perm, key_sel, precision=lax.Precision.HIGHEST) * score_scale)
    attn_probs = low(jax.nn.softmax(scores, axis=-1))
    mixed_rows = jnp.einsum('hcqk,hckd->hcqd', attn_probs, value_sel, precision=lax.Precision.HIGHEST).reshape(HEADS, length, HD)
    placed = jax.vmap(place_back)(mixed_rows, positions)
    attended = low(low_back(placed.transpose(1, 0, 2).reshape(length, D)))
    branch = low_back(product(attended, w_out) + b_out)
    normed = norm_rows(tokens_seq + branch, gain_attn, shift_attn)
    inner_sum = low_back(product(low(normed), w_up) + b_up)
    active = low(jax.nn.gelu(inner_sum, approximate=False))
    outer_sum = low_back(product(active, w_down) + b_down)
    return norm_rows(normed + outer_sum, gain_ffn, shift_ffn)

def add_grads(running, addend):
    return running + addend

def reference(tokens, grad_out, masked, token_order, cluster_match, w_query, w_key, w_value, w_out, w_up, w_down, b_query, b_value, b_out, b_up, b_down, gain_attn, shift_attn, gain_ffn, shift_ffn):
    params = tuple((weight.astype(jnp.float32) for weight in (w_query, w_key, w_value, w_out, w_up, w_down, b_query, b_value, b_out, b_up, b_down, gain_attn, shift_attn, gain_ffn, shift_ffn)))
    block_start = jnp.arange(SEQLEN, dtype=jnp.int32) // TS * TS

    def one_sequence(totals, inputs):
        tokens_seq, grad_seq, mask_seq, order_seq, match_seq = inputs
        positions = (order_seq + block_start[None, :]).astype(jnp.int32)

        def forward(row_block, weights):
            return layer(row_block, weights, positions, match_seq)
        result, pullback = jax.vjp(forward, tokens_seq.astype(jnp.float32), params)
        upstream = grad_seq.astype(jnp.float32) * mask_seq.astype(jnp.float32)[:, None]
        d_rows, d_weights = pullback(upstream)
        totals = jax.tree.map(add_grads, totals, d_weights)
        return (totals, (result.astype(jnp.bfloat16), d_rows))
    zero_grads = tuple((jnp.zeros_like(weight) for weight in params))
    totals, (outputs, d_tokens) = lax.scan(one_sequence, zero_grads, (tokens, grad_out, masked, token_order, cluster_match))
    return (outputs, d_tokens, totals[0], totals[1], totals[2], totals[3], totals[4], totals[5], totals[6], totals[7], totals[8], totals[9], totals[10], totals[11], totals[12], totals[13], totals[14])
```

```python
import functools
import math

import jax
import jax.numpy as jnp
from jax import lax
from jax.experimental import pallas as pl
from jax.experimental.pallas import tpu as pltpu
from jax.sharding import PartitionSpec as P

HEADS = 12
CL = 128
EPS = 1e-05
MESH = pl.DeviceIdType.MESH
SEQ, BLK = BOTH = ("seq", "blk")
F32 = jnp.float32
BF16 = jnp.bfloat16


def norm_rows(hidden, gain_row, shift_row):
    row_mean = jnp.mean(hidden, axis=-1, keepdims=True)
    centered = hidden - row_mean
    variance = jnp.mean(centered * centered, axis=-1, keepdims=True)
    return centered * lax.rsqrt(variance + EPS) * gain_row + shift_row


def gelu_exact(inner_sum):
    return jax.nn.gelu(inner_sum, approximate=False)


def to_heads(flat_rows, groups, local_len):
    return flat_rows.reshape(groups, local_len, HEADS, -1).transpose(0, 2, 1, 3)


def from_heads(head_rows):
    groups, head_count, local_len, head_dim = head_rows.shape
    return head_rows.transpose(0, 2, 1, 3).reshape(groups * local_len, head_count * head_dim)


def reorder(head_rows, positions):
    return jnp.take_along_axis(head_rows, positions[..., None], axis=2)


def general(
    tokens,
    grad_out,
    masked,
    token_order,
    cluster_match,
    w_query,
    w_key,
    w_value,
    w_out,
    w_up,
    w_down,
    b_query,
    b_value,
    b_out,
    b_up,
    b_down,
    gain_attn,
    shift_attn,
    gain_ffn,
    shift_ffn,
):
    groups, local_len, width = tokens.shape
    row_count = groups * local_len
    head_dim = width // HEADS
    clusters = local_len // CL
    score_scale = 1.0 / math.sqrt(head_dim)
    gathered = (
        lax.all_gather(w_query, BOTH, axis=0, tiled=True),
        lax.all_gather(w_key, BOTH, axis=0, tiled=True),
        lax.all_gather(w_value, BOTH, axis=0, tiled=True),
        lax.all_gather(w_out, BOTH, axis=0, tiled=True),
        lax.all_gather(w_up, BOTH, axis=0, tiled=True),
        lax.all_gather(w_down, BOTH, axis=0, tiled=True),
        lax.all_gather(b_query, BOTH, axis=0, tiled=True),
        lax.all_gather(b_value, BOTH, axis=0, tiled=True),
        lax.all_gather(b_out, BOTH, axis=0, tiled=True),
        lax.all_gather(b_up, BOTH, axis=0, tiled=True),
        lax.all_gather(b_down, BOTH, axis=0, tiled=True),
        lax.all_gather(gain_attn, BOTH, axis=0, tiled=True),
        lax.all_gather(shift_attn, BOTH, axis=0, tiled=True),
        lax.all_gather(gain_ffn, BOTH, axis=0, tiled=True),
        lax.all_gather(shift_ffn, BOTH, axis=0, tiled=True),
    )
    (
        full_query,
        full_key,
        full_value,
        full_out,
        full_up,
        full_down,
        bias_query,
        bias_value,
        bias_out,
        bias_up,
        bias_down,
        norm_gain1,
        norm_shift1,
        norm_gain2,
        norm_shift2,
    ) = gathered
    flat_tokens = tokens.reshape(row_count, width)
    inverse = jnp.argsort(token_order, axis=-1)
    cluster_shape = (groups, HEADS, clusters, CL, head_dim)
    query_low = (
        jnp.dot(flat_tokens, full_query, preferred_element_type=jnp.float32)
        + bias_query.astype(jnp.float32)
    ).astype(jnp.bfloat16)
    key_low = jnp.dot(flat_tokens, full_key, preferred_element_type=jnp.float32).astype(
        jnp.bfloat16
    )
    value_low = (
        jnp.dot(flat_tokens, full_value, preferred_element_type=jnp.float32)
        + bias_value.astype(jnp.float32)
    ).astype(jnp.bfloat16)
    query_perm = reorder(to_heads(query_low, groups, local_len), token_order).reshape(cluster_shape)
    key_perm = reorder(to_heads(key_low, groups, local_len), token_order).reshape(cluster_shape)
    value_perm = reorder(to_heads(value_low, groups, local_len), token_order).reshape(cluster_shape)
    empty_sel = jnp.zeros(cluster_shape, jnp.bfloat16)
    key_piece = lax.all_gather(key_perm, BLK, axis=2, tiled=True)
    value_piece = lax.all_gather(value_perm, BLK, axis=2, tiled=True)
    piece_len = key_piece.shape[2]
    offset = cluster_match
    select = (offset[..., None] == jnp.arange(piece_len, dtype=jnp.int32)).astype(jnp.bfloat16)
    inside = ((offset >= 0) & (offset < piece_len))[..., None, None]
    new_keys = jnp.einsum(
        "ghcj,ghjkd->ghckd", select, key_piece, preferred_element_type=jnp.float32
    ).astype(jnp.bfloat16)
    new_values = jnp.einsum(
        "ghcj,ghjkd->ghckd", select, value_piece, preferred_element_type=jnp.float32
    ).astype(jnp.bfloat16)
    key_sel = jnp.where(inside, new_keys, empty_sel)
    value_sel = jnp.where(inside, new_values, empty_sel)
    scores = (
        jnp.einsum("ghcqd,ghckd->ghcqk", query_perm, key_sel, preferred_element_type=jnp.float32)
        * score_scale
    )
    row_max = jnp.max(scores, axis=-1, keepdims=True)
    log_total = row_max + jnp.log(jnp.sum(jnp.exp(scores - row_max), axis=-1, keepdims=True))
    attn_probs = jnp.exp(scores - log_total)
    probs_low = attn_probs.astype(jnp.bfloat16)
    mixed_perm = jnp.einsum(
        "ghcqk,ghckd->ghcqd", probs_low, value_sel, preferred_element_type=jnp.float32
    ).reshape(groups, HEADS, local_len, head_dim)
    attended = from_heads(reorder(mixed_perm, inverse)).astype(jnp.bfloat16)
    branch = jnp.dot(attended, full_out, preferred_element_type=jnp.float32) + bias_out.astype(
        jnp.float32
    )
    resid = flat_tokens.astype(jnp.float32) + branch
    normed, pull_first = jax.vjp(
        norm_rows, resid, norm_gain1.astype(jnp.float32), norm_shift1.astype(jnp.float32)
    )
    normed_low = normed.astype(jnp.bfloat16)
    inner_sum = jnp.dot(normed_low, full_up, preferred_element_type=jnp.float32) + bias_up.astype(
        jnp.float32
    )
    active, pull_gelu = jax.vjp(gelu_exact, inner_sum)
    active_low = active.astype(jnp.bfloat16)
    outer_sum = jnp.dot(
        active_low, full_down, preferred_element_type=jnp.float32
    ) + bias_down.astype(jnp.float32)
    final_rows, pull_second = jax.vjp(
        norm_rows,
        normed + outer_sum,
        norm_gain2.astype(jnp.float32),
        norm_shift2.astype(jnp.float32),
    )
    result = final_rows.astype(jnp.bfloat16).reshape(groups, local_len, width)
    back_weights = (
        lax.all_gather(w_query, BOTH, axis=0, tiled=True),
        lax.all_gather(w_key, BOTH, axis=0, tiled=True),
        lax.all_gather(w_value, BOTH, axis=0, tiled=True),
        lax.all_gather(w_out, BOTH, axis=0, tiled=True),
        lax.all_gather(w_up, BOTH, axis=0, tiled=True),
        lax.all_gather(w_down, BOTH, axis=0, tiled=True),
        lax.all_gather(b_query, BOTH, axis=0, tiled=True),
        lax.all_gather(b_value, BOTH, axis=0, tiled=True),
        lax.all_gather(b_out, BOTH, axis=0, tiled=True),
        lax.all_gather(b_up, BOTH, axis=0, tiled=True),
        lax.all_gather(b_down, BOTH, axis=0, tiled=True),
        lax.all_gather(gain_attn, BOTH, axis=0, tiled=True),
        lax.all_gather(shift_attn, BOTH, axis=0, tiled=True),
        lax.all_gather(gain_ffn, BOTH, axis=0, tiled=True),
        lax.all_gather(shift_ffn, BOTH, axis=0, tiled=True),
    )
    back_query, back_key, back_value, back_out, back_up, back_down = back_weights[:6]
    upstream = grad_out.reshape(row_count, width).astype(jnp.float32) * masked.reshape(
        row_count, 1
    ).astype(jnp.float32)
    d_sum2, d_gain2, d_shift2 = pull_second(upstream)
    d_outer = d_sum2.astype(jnp.bfloat16)
    g_down = jnp.einsum("rf,rd->fd", active_low, d_outer, preferred_element_type=jnp.float32)
    g_bdown = jnp.sum(d_outer.astype(jnp.float32), axis=0)
    d_active = jnp.einsum("rd,fd->rf", d_outer, back_down, preferred_element_type=jnp.float32)
    d_inner = pull_gelu(d_active)[0].astype(jnp.bfloat16)
    g_up = jnp.einsum("rd,rf->df", normed_low, d_inner, preferred_element_type=jnp.float32)
    g_bup = jnp.sum(d_inner.astype(jnp.float32), axis=0)
    d_normed = d_sum2 + jnp.einsum(
        "rf,df->rd", d_inner, back_up, preferred_element_type=jnp.float32
    )
    d_resid, d_gain1, d_shift1 = pull_first(d_normed)
    d_branch = d_resid.astype(jnp.bfloat16)
    g_out = jnp.einsum("ri,rd->id", attended, d_branch, preferred_element_type=jnp.float32)
    g_bout = jnp.sum(d_branch.astype(jnp.float32), axis=0)
    d_attended = jnp.einsum(
        "rd,id->ri", d_branch, back_out, preferred_element_type=jnp.float32
    ).astype(jnp.bfloat16)
    d_mixed = reorder(to_heads(d_attended, groups, local_len), token_order).reshape(cluster_shape)
    scores_again = (
        jnp.einsum("ghcqd,ghckd->ghcqk", query_perm, key_sel, preferred_element_type=jnp.float32)
        * score_scale
    )
    probs_again = jnp.exp(scores_again - log_total)
    probs_again_low = probs_again.astype(jnp.bfloat16)
    d_probs = jnp.einsum(
        "ghcqd,ghckd->ghcqk", d_mixed, value_sel, preferred_element_type=jnp.float32
    )
    d_scores = (
        probs_again * (d_probs - jnp.sum(probs_again * d_probs, axis=-1, keepdims=True))
    ).astype(jnp.bfloat16)
    d_query_perm = (
        jnp.einsum("ghcqk,ghckd->ghcqd", d_scores, key_sel, preferred_element_type=jnp.float32)
        * score_scale
    )
    d_key_sel = (
        jnp.einsum("ghcqk,ghcqd->ghckd", d_scores, query_perm, preferred_element_type=jnp.float32)
        * score_scale
    )
    d_value_sel = jnp.einsum(
        "ghcqk,ghcqd->ghckd", probs_again_low, d_mixed, preferred_element_type=jnp.float32
    )
    sent = jnp.concatenate([d_key_sel, d_value_sel], axis=-1)
    my_start = lax.axis_index(BLK) * clusters
    piece_grads = lax.all_gather(sent.astype(jnp.bfloat16), BLK, axis=2, tiled=True).astype(
        jnp.float32
    )
    piece_match = lax.all_gather(
        cluster_match.astype(jnp.float32).astype(jnp.bfloat16), BLK, axis=2, tiled=True
    ).astype(jnp.float32)
    offset = piece_match.astype(jnp.int32) - my_start
    select = (offset[..., None] == jnp.arange(clusters, dtype=jnp.int32)).astype(jnp.float32)
    owned = jnp.zeros(sent.shape, jnp.float32) + jnp.einsum(
        "ghjc,ghjke->ghcke", select, piece_grads, precision=lax.Precision.HIGHEST
    )
    back_kv = reorder(owned.reshape(groups, HEADS, local_len, 2 * head_dim), inverse)
    d_key = from_heads(back_kv[..., :head_dim]).astype(jnp.bfloat16)
    d_value = from_heads(back_kv[..., head_dim:]).astype(jnp.bfloat16)
    d_query = from_heads(
        reorder(d_query_perm.reshape(groups, HEADS, local_len, head_dim), inverse)
    ).astype(jnp.bfloat16)
    g_query = jnp.einsum("ri,rd->id", flat_tokens, d_query, preferred_element_type=jnp.float32)
    g_key = jnp.einsum("ri,rd->id", flat_tokens, d_key, preferred_element_type=jnp.float32)
    g_value = jnp.einsum("ri,rd->id", flat_tokens, d_value, preferred_element_type=jnp.float32)
    g_bquery = jnp.sum(d_query.astype(jnp.float32), axis=0)
    g_bvalue = jnp.sum(d_value.astype(jnp.float32), axis=0)
    d_tokens_flat = (
        d_resid
        + jnp.einsum("rd,id->ri", d_query, back_query, preferred_element_type=jnp.float32)
        + jnp.einsum("rd,id->ri", d_key, back_key, preferred_element_type=jnp.float32)
        + jnp.einsum("rd,id->ri", d_value, back_value, preferred_element_type=jnp.float32)
    )
    summed = (
        lax.psum_scatter(g_query, BOTH, scatter_dimension=0, tiled=True),
        lax.psum_scatter(g_key, BOTH, scatter_dimension=0, tiled=True),
        lax.psum_scatter(g_value, BOTH, scatter_dimension=0, tiled=True),
        lax.psum_scatter(g_out, BOTH, scatter_dimension=0, tiled=True),
        lax.psum_scatter(g_up, BOTH, scatter_dimension=0, tiled=True),
        lax.psum_scatter(g_down, BOTH, scatter_dimension=0, tiled=True),
        lax.psum_scatter(g_bquery, BOTH, scatter_dimension=0, tiled=True),
        lax.psum_scatter(g_bvalue, BOTH, scatter_dimension=0, tiled=True),
        lax.psum_scatter(g_bout, BOTH, scatter_dimension=0, tiled=True),
        lax.psum_scatter(g_bup, BOTH, scatter_dimension=0, tiled=True),
        lax.psum_scatter(g_bdown, BOTH, scatter_dimension=0, tiled=True),
        lax.psum_scatter(d_gain1, BOTH, scatter_dimension=0, tiled=True),
        lax.psum_scatter(d_shift1, BOTH, scatter_dimension=0, tiled=True),
        lax.psum_scatter(d_gain2, BOTH, scatter_dimension=0, tiled=True),
        lax.psum_scatter(d_shift2, BOTH, scatter_dimension=0, tiled=True),
    )
    return (result, d_tokens_flat.reshape(groups, local_len, width)) + tuple(summed)


class Place:
    def __init__(self):
        s, b = lax.axis_index("seq"), lax.axis_index("blk")
        self.s, self.b = s, b
        z, c = b // 2, b % 2
        self.z, self.c = z, c
        self.zlo, self.zhi = z % 2, z // 2
        self.sx = s + 1 - 2 * (s % 2)
        self.sy = s + 2 - 4 * (s // 2)
        self.sd = self.sy + 1 - 2 * (s % 2)
        self.zn = z + 1 - 2 * self.zlo
        self.zf = z + 2 - 4 * self.zhi
        self.znf = self.zf + 1 - 2 * self.zlo
        self.bc = b + 1 - 2 * c
        self.bn, self.bf, self.bnf = self.zn * 2 + c, self.zf * 2 + c, self.znf * 2 + c
        self.core = (s, self.bc)
        self.n = (s, self.bn)
        self.f = (s, self.bf)
        self.nf = (s, self.bnf)
        self.x = (self.sx, b)
        self.y = (self.sy, b)


class Wire:
    def __init__(self, send, recv, local):
        self.send, self.recv, self.local = send, recv, local
        self.n_send = self.n_local = self.n_recv = 0
        self.sent, self.locals, self.slots = [], [], {}

    def slot(self, key):
        if key not in self.slots:
            self.slots[key] = self.n_recv
            self.n_recv += 1
        return self.slots[key]

    def put(self, src, dst, to, key):
        cp = pltpu.make_async_remote_copy(
            src, dst, self.send.at[self.n_send], self.recv.at[self.slot(key)],
            device_id=to, device_id_type=MESH,
        )
        self.n_send += 1
        cp.start()
        self.sent.append(cp)

    def got(self, dst, key):
        pltpu.make_async_copy(dst, dst, self.recv.at[self.slot(key)]).wait()

    def move(self, src, dst):
        cp = pltpu.make_async_copy(src, dst, self.local.at[self.n_local])
        self.n_local += 1
        cp.start()
        return cp

    def finish(self):
        for cp in self.sent:
            cp.wait_send()


def greet(peers):
    bar = pltpu.get_barrier_semaphore()
    for to in peers:
        pl.semaphore_signal(bar, inc=1, device_id=to, device_id_type=MESH)
    pl.semaphore_wait(bar, len(peers))


def head_columns(wqkv, t, c0):
    parts = [wqkv[t, :, :, :, :, pl.ds(c0, 128)], wqkv[t, :, :, :, :, 256:384]]
    return jnp.concatenate([v.astype(F32).reshape(768, 128).astype(BF16) for v in parts], axis=1)


def gather_kernel(
    tok, mt, vec, wq, wk, wv, wo_s, wu_s, wd_s,
    wo, wu, wd, wqkv, xg, qkv, att, match, vecs,
    stage, bias, att_buf, m_smem, send, recv, local,
):
    p = Place()
    w = Wire(send, recv, local)
    s, b, z, c = p.s, p.b, p.z, p.c
    zp, g = p.zlo, p.zhi
    greet([p.core, p.n, p.f, p.nf, p.x, p.y, (s, p.zn * 2 + 1 - c), (s, p.zf * 2 + 1 - c), (s, p.znf * 2 + 1 - c)])

    wo5, wu5, wd5, wq6 = wo, wu, wd, wqkv
    slot = s * 8 + b

    w.put(tok.at[g], xg.at[b], p.n, "xn")
    w.put(tok.at[1 - g], xg.at[b], p.f, "xf")
    for t, ref in enumerate((wq, wk, wv)):
        for h in range(2):
            stage[h, t] = ref[:, h * 384 : (h + 1) * 384]
    w.put(stage.at[1 - zp], wq6.at[:, s, z, c], p.n, "qn")
    w.put(stage.at[zp], wq6.at[:, s, z, c], p.f, "qf")
    w.put(stage.at[1 - zp], wq6.at[:, s, z, c], p.nf, "qnf")
    w.put(mt, match.at[b], p.core, "m0")
    w.put(vec, vecs.at[slot], p.core, "v0")
    w.put(tok.at[g], xg.at[b], p.core, "xc0")
    mine = [
        w.move(mt, match.at[b]),
        w.move(vec, vecs.at[slot]),
        w.move(stage.at[zp], wq6.at[:, s, z, c]),
        w.move(tok.at[g], xg.at[b]),
        w.move(wo_s, wo5.at[s, z, c]),
        w.move(wu_s, wu5.at[s, z, c]),
        w.move(wd_s, wd5.at[s, z, c]),
    ]

    chunks = [
        (wo5, wo_s, 0, 24, 0, 768),
        (wu5, wu_s, 0, 24, 0, 1536),
        (wu5, wu_s, 0, 24, 1536, 1536),
        (wd5, wd_s, 0, 48, 0, 768),
        (wd5, wd_s, 48, 48, 0, 768),
    ]

    def own(k):
        v, src, r0, nr, c0, nc = chunks[k]
        return src.at[pl.ds(r0, nr), pl.ds(c0, nc)]

    def one(k, zz):
        v, src, r0, nr, c0, nc = chunks[k]
        return v.at[s, zz, c, pl.ds(r0, nr), pl.ds(c0, nc)]

    def col(k, ss, cc, half=None):
        if k < 0:
            v = wq6.at[:, ss, :, cc]
            if half == 0:
                return wq6.at[:, ss, :, cc, :, pl.ds(0, 256)]
            if half == 1:
                return wq6.at[:, ss, :, cc, :, pl.ds(256, 128)]
            return v
        v, src, r0, nr, c0, nc = chunks[k]
        if half is not None:
            nc = nc // 2
            c0 = c0 + half * nc
        return v.at[ss, :, cc, pl.ds(r0, nr), pl.ds(c0, nc)]

    def z_start(k):
        w.put(own(k), one(k, z), p.n, ("n", k))
        w.put(own(k), one(k, z), p.f, ("f", k))

    def z_forward(k):
        w.got(one(k, p.zf), ("f", k))
        w.put(one(k, p.zf), one(k, p.zf), p.n, ("nf", k))

    def plane(k):
        if k < 0:
            w.got(wq6.at[:, s, p.zn, c], "qn")
            w.got(wq6.at[:, s, p.zf, c], "qf")
            w.got(wq6.at[:, s, p.znf, c], "qnf")
        else:
            w.got(one(k, p.zn), ("n", k))
            w.got(one(k, p.znf), ("nf", k))
        w.put(col(k, s, c, 0), col(k, s, c, 0), p.x, ("xA", k))
        w.put(col(k, s, c, 1), col(k, s, c, 1), p.y, ("yB", k))
        w.put(col(k, s, c, 1), col(k, s, c, 1), p.x, ("xB", k))
        w.put(col(k, s, c, 0), col(k, s, c, 0), p.y, ("yA", k))
        w.put(col(k, s, c), col(k, s, c), p.core, ("c0", k))

    def diagonal(k):
        w.got(col(k, p.sx, c, 0), ("xA", k))
        w.put(col(k, p.sx, c, 0), col(k, p.sx, c, 0), p.y, ("ydA", k))
        w.got(col(k, p.sy, c, 1), ("yB", k))
        w.put(col(k, p.sy, c, 1), col(k, p.sy, c, 1), p.x, ("xdB", k))

    def across(k):
        w.got(col(k, p.sx, c, 1), ("xB", k))
        w.put(col(k, p.sx, c), col(k, p.sx, c), p.core, ("c1", k))
        w.got(col(k, p.sy, c, 0), ("yA", k))
        w.put(col(k, p.sy, c), col(k, p.sy, c), p.core, ("c2", k))

    def last(k):
        w.got(col(k, p.sd, c, 0), ("ydA", k))
        w.got(col(k, p.sd, c, 1), ("xdB", k))
        w.put(col(k, p.sd, c), col(k, p.sd, c), p.core, ("c3", k))

    def complete(k):
        w.got(col(k, s, 1 - c), ("c0", k))
        w.got(col(k, p.sx, 1 - c), ("c1", k))
        w.got(col(k, p.sy, 1 - c), ("c2", k))
        w.got(col(k, p.sd, 1 - c), ("c3", k))

    for cp in mine:
        cp.wait()
    z_start(0)
    z_start(1)

    w.got(match.at[p.bc], "m0")
    w.put(match.at[pl.ds(2 * z, 2)], match.at[pl.ds(2 * z, 2)], p.n, "m1")
    w.got(vecs.at[s * 8 + p.bc], "v0")
    w.put(vecs.at[pl.ds(s * 8 + 2 * z, 2)], vecs.at[pl.ds(s * 8 + 2 * z, 2)], p.n, "v1")
    plane(-1)
    w.got(xg.at[p.bn], "xn")
    w.put(xg.at[p.bn], xg.at[p.bn], p.core, "xc1")
    w.got(xg.at[p.bf], "xf")
    w.put(xg.at[p.bf], xg.at[p.bf], p.n, "xnf")
    w.put(xg.at[p.bf], xg.at[p.bf], p.core, "xc2")
    w.got(match.at[pl.ds(2 * p.zn, 2)], "m1")
    w.put(match.at[pl.ds(4 * g, 4)], match.at[pl.ds(4 * g, 4)], p.f, "m2")
    w.got(vecs.at[pl.ds(s * 8 + 2 * p.zn, 2)], "v1")
    w.put(vecs.at[pl.ds(s * 8 + 4 * g, 4)], vecs.at[pl.ds(s * 8 + 4 * g, 4)], p.f, "v2")
    diagonal(-1)
    z_forward(0)
    z_start(2)
    plane(0)
    across(-1)
    w.got(vecs.at[pl.ds(s * 8 + 4 - 4 * g, 4)], "v2")
    w.put(vecs.at[pl.ds(s * 8, 8)], vecs.at[pl.ds(s * 8, 8)], p.x, "v3")
    w.got(match.at[pl.ds(4 - 4 * g, 4)], "m2")
    z_forward(1)
    z_start(3)
    diagonal(0)
    plane(1)
    w.got(xg.at[p.bnf], "xnf")
    w.put(xg.at[p.bnf], xg.at[p.bnf], p.core, "xc3")
    last(-1)
    w.got(vecs.at[pl.ds(p.sx * 8, 8)], "v3")
    w.put(vecs.at[pl.ds((s // 2) * 16, 16)], vecs.at[pl.ds((s // 2) * 16, 16)], p.y, "v4")
    z_forward(2)
    z_start(4)
    across(0)
    diagonal(1)
    plane(2)
    get_match = w.move(match, m_smem)
    w.got(vecs.at[pl.ds((1 - s // 2) * 16, 16)], "v4")

    lane = lax.broadcasted_iota(jnp.int32, (32, 768), 1)
    owner = (lane * 2731) >> 16
    mine_lane = owner == lax.broadcasted_iota(jnp.int32, (32, 768), 0)
    lane2 = lax.broadcasted_iota(jnp.int32, (128, 768), 1)
    spread = (lane2 - 24 * ((lane2 * 2731) >> 16) == lax.broadcasted_iota(jnp.int32, (128, 768), 0)).astype(F32).astype(BF16)
    for row in range(2):
        part = jnp.dot(vecs[:, row, :], spread, preferred_element_type=F32)
        bias[row] = jnp.sum(jnp.where(mine_lane, part, 0.0), axis=0, keepdims=True)

    complete(-1)
    for blk, key in ((p.bc, "xc0"), (p.zn * 2 + 1 - c, "xc1"), (p.zf * 2 + 1 - c, "xc2"), (p.znf * 2 + 1 - c, "xc3")):
        w.got(xg.at[blk], key)

    c0 = pl.multiple_of(128 * c, 128)
    b0 = pl.multiple_of(384 * zp + 128 * c, 128)
    b1 = pl.multiple_of(384 * zp + 256, 128)
    steps = [
        lambda: (z_forward(3), last(0), across(1)),
        lambda: (diagonal(2), plane(3)),
        lambda: (z_forward(4), last(1)),
    ]
    for t in range(3):
        wt = head_columns(wqkv, t, c0)
        for m in range(2):
            x = xg[4 * m : 4 * m + 4].reshape(512, 768)
            r = jnp.dot(x, wt, preferred_element_type=F32)
            if t != 1:
                row = 0 if t == 0 else 1
                r = r + jnp.concatenate([bias[row, :, pl.ds(b0, 128)], bias[row, :, pl.ds(b1, 128)]], axis=1)
            r = r.astype(BF16)
            for i in range(4):
                for tl in range(2):
                    qkv[t, tl, 4 * m + i] = r[128 * i : 128 * (i + 1), 128 * tl : 128 * (tl + 1)]
        steps[t]()

    get_match.wait()
    left = lax.broadcasted_iota(jnp.int32, (128, 128), 1) < 64
    zero = jnp.zeros((128, 128), BF16)

    def attend(tl, blk, i):
        q = qkv[0, tl, blk]
        head0 = 6 * zp + (2 * c if tl == 0 else 4)
        outs = []
        for e in range(2):
            m = m_smem[blk, 0, g * HEADS + head0 + e]
            k, v = qkv[1, tl, m], qkv[2, tl, m]
            qm = jnp.where(left if e == 0 else jnp.logical_not(left), q, zero)
            sc = lax.dot_general(qm, k, (((1,), (1,)), ((), ())), preferred_element_type=F32) * 0.125
            ex = jnp.exp(sc - jnp.max(sc, axis=-1, keepdims=True))
            pr = (ex * (1.0 / jnp.sum(ex, axis=-1, keepdims=True))).astype(BF16)
            outs.append(jnp.dot(pr, v, preferred_element_type=F32))
        att_buf[i] = jnp.where(left, outs[0], outs[1]).astype(BF16)

    def send(tl, zz, cc, i):
        col0 = pl.multiple_of(384 * zp + (128 * c if tl == 0 else 256), 128)
        dst = att.at[g, :, pl.ds(col0, 128)]
        if i in (0, 8):
            return w.move(att_buf.at[i], dst)
        tile = 6 * g + 3 * zp + (c if tl == 0 else 2)
        cp = pltpu.make_async_remote_copy(
            att_buf.at[i], dst, w.send.at[w.n_send], recv_att.at[tile],
            device_id=(s, zz * 2 + cc), device_id_type=MESH,
        )
        w.n_send += 1
        cp.start()
        w.sent.append(cp)
        return None

    n0 = w.n_recv_base = 96
    recv_att = w.recv.at[pl.ds(n0, 12)]
    zs = [p.zf, p.znf, p.zn, z]
    items = []
    for zz in zs:
        items += [(0, zz, c), (0, zz, 1 - c), (1, zz, c)]
    inter = {
        2: lambda: (diagonal(3), plane(4)),
        5: lambda: (across(2),),
        8: lambda: (last(2), diagonal(4)),
        10: lambda: (across(3),),
    }
    keep = []
    index = {}
    for j, (tl, zz, cc) in enumerate(items):
        home = zz is z and cc is c
        i = (0 if tl == 0 else 8) if home else [1, 2, 3, 4, 5, 6, 7, 9, 10, 11][len(index)]
        if not home:
            index[i] = 1
        attend(tl, zz * 2 + cc, i)
        cp = send(tl, zz, cc, i)
        if cp is not None:
            keep.append(cp)
        if j in inter:
            inter[j]()

    last(3)
    across(4)
    last(4)
    for cp in keep:
        cp.wait()
    for k in range(5):
        complete(k)
    def got_tile(gg, tile):
        dst = att.at[gg, :, pl.ds(pl.multiple_of(128 * tile, 128), 128)]
        pltpu.make_async_copy(dst, dst, recv_att.at[6 * gg + tile]).wait()

    for tile in range(6):
        got_tile(1 - g, tile)
    for tile in range(3):
        got_tile(g, 3 - 3 * zp + tile)
    got_tile(g, 3 * zp + 1 - c)
    w.finish()


def gather_call(tok, mt, vec, wq, wk, wv, wo, wu, wd):
    V = pl.BlockSpec(memory_space=pltpu.VMEM)
    A = pl.BlockSpec(memory_space=pl.ANY)
    S = jax.ShapeDtypeStruct
    return pl.pallas_call(
        gather_kernel,
        out_shape=(
            S((4, 4, 2, 24, 768), BF16), S((4, 4, 2, 24, 3072), BF16), S((4, 4, 2, 96, 768), BF16),
            S((3, 4, 4, 2, 24, 384), BF16),
            S((8, 128, 768), BF16), S((3, 2, 8, 128, 128), BF16), S((2, 128, 768), BF16),
            S((8, 8, 128), jnp.int32), S((32, 16, 128), BF16),
        ),
        in_specs=[V] * 6 + [A] * 3,
        out_specs=(A, A, A, V, V, V, V, V, V),
        scratch_shapes=[
            pltpu.VMEM((2, 3, 24, 384), BF16),
            pltpu.VMEM((2, 1, 768), F32),
            pltpu.VMEM((12, 128, 128), BF16),
            pltpu.SMEM((8, 8, 128), jnp.int32),
            pltpu.SemaphoreType.DMA((128,)),
            pltpu.SemaphoreType.DMA((112,)),
            pltpu.SemaphoreType.DMA((16,)),
        ],
        compiler_params=pltpu.CompilerParams(collective_id=0, has_side_effects=True, vmem_limit_bytes=48 << 20),
        name="gather",
    )(tok, mt, vec, wq, wk, wv, wo, wu, wd)


def pack_inputs(cluster_match, vectors, b_up):
    mt = jnp.pad(cluster_match.reshape(1, 24), ((0, 7), (0, 104)))
    rows = [jnp.pad(v.reshape(1, 24), ((0, 0), (0, 104))) for v in vectors]
    rows.append(jnp.pad(b_up.reshape(1, 96), ((0, 0), (0, 32))))
    rows.append(jnp.zeros((16 - len(rows), 128), BF16))
    return mt, jnp.concatenate(rows, axis=0)


def scatter_kernel(
    gd, gu, go, gvec, datt, dh1, xg, qkv, wqkv, match,
    od, ou, oo, oqkv, dtok, ovec,
    dap, ds_buf, p_buf, dqkv, gq, rq, accq, row, vacc, dtk, rtk, rtn, rtf, m_smem,
    rv0, rv1, rv2, rv3, rv4,
    rqdx, rqdy, rqx, rqy, rqz,
    *rest,
):
    n_chunks = 5
    bufs = [rest[6 * k : 6 * k + 6] for k in range(n_chunks)]
    send, recv, local = rest[6 * n_chunks :]
    p = Place()
    w = Wire(send, recv, local)
    s, b, z, c = p.s, p.b, p.z, p.c
    zp, g = p.zlo, p.zhi
    left = lax.broadcasted_iota(jnp.int32, (128, 128), 1) < 64
    zero = jnp.zeros((128, 128), BF16)

    for i in range(4):
        other = 2 * i + 1 - c
        dap[1, other] = zero
        dqkv[0, 1, other] = zero
        for e in range(2):
            ds_buf[1, e, other] = zero
            p_buf[1, e, other] = zero
    row[...] = jnp.zeros_like(row)
    get_match = w.move(match, m_smem)

    greet([p.core, p.n, p.f, p.nf, p.x, p.y, (s, p.zn * 2 + 1 - c), (s, p.zf * 2 + 1 - c), (s, p.znf * 2 + 1 - c)])

    gd5, gu5, go5, gq6 = gd, gu, go, gq
    chunks = [
        (gd5, od, 0, 48, 0, 768),
        (gd5, od, 48, 48, 0, 768),
        (gu5, ou, 0, 24, 0, 1536),
        (gu5, ou, 0, 24, 1536, 1536),
        (go5, oo, 0, 24, 0, 768),
    ]

    for zz in (p.zf, p.znf, p.zn, z):
        gg, zq = zz // 2, zz % 2
        for tl, cc in ((0, 1 - c), (0, c), (1, c)):
            col = pl.multiple_of(384 * zq + (256 if tl else 128 * cc), 128)
            src = datt.at[gg, :, pl.ds(col, 128)]
            if zz is z and cc is c:
                w.move(src, dap.at[tl, b])
            else:
                cp = pltpu.make_async_remote_copy(
                    src, dap.at[tl, b], w.send.at[w.n_send], recv.at[96 + 8 * tl + b],
                    device_id=(s, zz * 2 + cc), device_id_type=MESH,
                )
                w.n_send += 1
                cp.start()
                w.sent.append(cp)

    def region(k, ss, cc, half=None):
        v, out, r0, nr, c0, nc = chunks[k]
        if half is not None:
            nc = nc // 2
            c0 = c0 + half * nc
        return v.at[ss, :, cc, pl.ds(r0, nr), pl.ds(c0, nc)]

    def cols(k, half):
        nc = chunks[k][5] // 2
        return pl.ds(half * nc, nc)

    def pair_start(k):
        v, out, r0, nr, c0, nc = chunks[k]
        w.put(v.at[:, :, 1 - c, pl.ds(r0, nr), pl.ds(c0, nc)], bufs[k][0], p.core, ("c", k))

    def pair_add(k):
        v, out, r0, nr, c0, nc = chunks[k]
        rc, rdx, rdy, rx, ry, rz = bufs[k]
        w.got(rc, ("c", k))

        def add(ss):
            def one(i, carry):
                rc[ss, i] = rc[ss, i] + v[ss, i, c, r0 : r0 + nr, c0 : c0 + nc]
                return carry
            lax.fori_loop(0, 4, one, 0)

        add(p.sd)
        w.put(rc.at[p.sd, :, :, cols(k, 0)], rdx, p.x, ("dx", k))
        w.put(rc.at[p.sd, :, :, cols(k, 1)], rdy, p.y, ("dy", k))
        add(p.sx)
        w.put(rc.at[p.sx, :, :, cols(k, 0)], rx.at[:, :, cols(k, 0)], p.x, ("xA", k))
        add(p.sy)
        w.put(rc.at[p.sy, :, :, cols(k, 1)], ry.at[:, :, cols(k, 1)], p.y, ("yB", k))
        add(s)

    def diagonal(k):
        rc, rdx, rdy, rx, ry, rz = bufs[k]
        w.got(rdx, ("dx", k))
        rc[p.sy, :, :, cols(k, 0)] = rc[p.sy, :, :, cols(k, 0)] + rdx[...]
        w.put(rc.at[p.sy, :, :, cols(k, 0)], ry.at[:, :, cols(k, 0)], p.y, ("yA", k))
        w.got(rdy, ("dy", k))
        rc[p.sx, :, :, cols(k, 1)] = rc[p.sx, :, :, cols(k, 1)] + rdy[...]
        w.put(rc.at[p.sx, :, :, cols(k, 1)], rx.at[:, :, cols(k, 1)], p.x, ("xB", k))

    def plane(k):
        rc, rdx, rdy, rx, ry, rz = bufs[k]
        w.got(rx.at[:, :, cols(k, 0)], ("xA", k))
        w.got(rx.at[:, :, cols(k, 1)], ("xB", k))
        w.got(ry.at[:, :, cols(k, 1)], ("yB", k))
        w.got(ry.at[:, :, cols(k, 0)], ("yA", k))

        def one(i, carry):
            rc[s, i] = (rc[s, i].astype(F32) + rx[i].astype(F32) + ry[i].astype(F32)).astype(BF16)
            return carry

        lax.fori_loop(0, 4, one, 0)
        w.put(rc.at[s, p.znf], rz.at[0], p.n, ("z0", k))
        w.put(rc.at[s, p.zn], rz.at[1], p.n, ("z1", k))

    def far(k):
        rc, rdx, rdy, rx, ry, rz = bufs[k]
        w.got(rz.at[0], ("z0", k))
        rc[s, p.zf] = rc[s, p.zf] + rz[0]
        w.put(rc.at[s, p.zf], rz.at[2], p.f, ("z2", k))

    def final(k):
        v, out, r0, nr, c0, nc = chunks[k]
        rc, rdx, rdy, rx, ry, rz = bufs[k]
        w.got(rz.at[1], ("z1", k))
        w.got(rz.at[2], ("z2", k))
        out[r0 : r0 + nr, c0 : c0 + nc] = rc[s, z].astype(F32) + rz[1].astype(F32) + rz[2].astype(F32)

    for k in range(n_chunks):
        pair_start(k)
    pair_add(0)
    pair_add(1)
    diagonal(0)

    for tl in range(2):
        for zz in (p.zf, p.znf, p.zn, z):
            for cc in (1 - c, c):
                if tl == 1 and cc is not c:
                    continue
                if zz is z and cc is c:
                    continue
                blk = zz * 2 + cc
                pltpu.make_async_copy(dap.at[tl, blk], dap.at[tl, blk], recv.at[96 + 8 * tl + blk]).wait()
    get_match.wait()
    for i in (1, 2):
        pltpu.make_async_copy(dap.at[0, 0], dap.at[0, 0], local.at[i]).wait()
    pair_add(2)

    def weights(tl, e, q, k):
        qm = jnp.where(left if e == 0 else jnp.logical_not(left), q, zero)
        sc = lax.dot_general(qm, k, (((1,), (1,)), ((), ())), preferred_element_type=F32) * 0.125
        ex = jnp.exp(sc - jnp.max(sc, axis=-1, keepdims=True))
        return ex * (1.0 / jnp.sum(ex, axis=-1, keepdims=True))

    def head(tl, e):
        return g * HEADS + 6 * zp + (2 * c if tl == 0 else 4) + e

    def queries(tl, blk):
        q, da = qkv[0, tl, blk], dap[tl, blk]
        outs = []
        for e in range(2):
            m = m_smem[blk, 0, head(tl, e)]
            k, v = qkv[1, tl, m], qkv[2, tl, m]
            pr = weights(tl, e, q, k)
            dam = jnp.where(left if e == 0 else jnp.logical_not(left), da, zero)
            dp = lax.dot_general(dam, v, (((1,), (1,)), ((), ())), preferred_element_type=F32)
            ds = (pr * (dp - jnp.sum(pr * dp, axis=-1, keepdims=True))).astype(BF16)
            ds_buf[tl, e, blk] = ds
            p_buf[tl, e, blk] = pr.astype(BF16)
            outs.append(jnp.dot(ds, k, preferred_element_type=F32) * 0.125)
        dqkv[0, tl, blk] = jnp.where(left, outs[0], outs[1]).astype(BF16)

    def keys(tl, n):
        dk, dv = [], []
        for e in range(2):
            cq = 0
            for i in range(8):
                cq = jnp.where(m_smem[i, 0, head(tl, e)] == n, i, cq)
            ds, pr = ds_buf[tl, e, cq], p_buf[tl, e, cq]
            q, da = qkv[0, tl, cq], dap[tl, cq]
            dk.append(lax.dot_general(ds, q, (((0,), (0,)), ((), ())), preferred_element_type=F32) * 0.125)
            dv.append(lax.dot_general(pr, da, (((0,), (0,)), ((), ())), preferred_element_type=F32))
        dqkv[1, tl, n] = jnp.where(left, dk[0], dk[1]).astype(BF16)
        dqkv[2, tl, n] = jnp.where(left, dv[0], dv[1]).astype(BF16)

    def loop(n, body):
        def run(i, carry):
            body(i)
            return carry
        lax.fori_loop(0, n, run, 0)

    loop(8, lambda i: queries(0, i))
    diagonal(1)
    pair_add(3)
    loop(4, lambda i: queries(1, 2 * i + c))
    plane(0)
    diagonal(2)
    loop(8, lambda i: keys(0, i))
    pair_add(4)
    plane(1)
    far(0)
    loop(8, lambda i: keys(1, i))
    diagonal(3)
    far(1)

    c0 = pl.multiple_of(128 * c, 128)
    b0 = pl.multiple_of(384 * zp + 128 * c, 128)
    b1 = pl.multiple_of(384 * zp + 256, 128)

    def flat(t, m):
        return jnp.concatenate(
            [dqkv[t, tl, 4 * m : 4 * m + 4].reshape(512, 128) for tl in range(2)], axis=1
        )

    for m in range(2):
        total = None
        for t in range(3):
            wt = head_columns(wqkv, t, c0)
            r = lax.dot_general(flat(t, m), wt, (((1,), (1,)), ((), ())), preferred_element_type=F32)
            total = r if total is None else total + r
        dtk[4 * m : 4 * m + 4] = total.astype(BF16).reshape(4, 128, 768)
    dtk4 = dtk.reshape(4, 2, 128, 768)
    w.put(dtk4.at[:, 1 - c], rtk, p.core, "t0")

    for t in range(3):
        acc = None
        for m in range(2):
            x = xg[4 * m : 4 * m + 4].reshape(512, 768)
            r = lax.dot_general(x, flat(t, m), (((0,), (0,)), ((), ())), preferred_element_type=F32)
            acc = r if acc is None else acc + r
        gq[t] = acc.reshape(4, 4, 2, 24, 256).astype(BF16)
    w.put(gq6.at[:, :, :, 1 - c], rq, p.core, "q0")

    diagonal(4)
    plane(2)
    w.got(rtk, "t0")
    loop(4, lambda i: rtk.__setitem__(i, rtk[i] + dtk[2 * i + c]))
    w.put(rtk.at[p.znf], rtn.at[0], p.n, "t1")
    w.put(rtk.at[p.zn], rtn.at[1], p.n, "t2")

    w.got(rq, "q0")
    o0 = pl.multiple_of(128 * (1 - c), 128)

    def pair_q(i):
        for t in range(3):
            for zz in range(4):
                accq[t, i, zz, :, pl.ds(c0, 128)] = gq6[t, i, zz, c, :, 0:128]
                accq[t, i, zz, :, pl.ds(o0, 128)] = rq[t, i, zz, :, 0:128]
                accq[t, i, zz, :, 256:384] = gq6[t, i, zz, c, :, 128:256] + rq[t, i, zz, :, 128:256]

    loop(4, pair_q)
    A, B = pl.ds(0, 256), pl.ds(256, 128)
    w.put(accq.at[:, p.sd, :, :, A], rqdx, p.x, "qdx")
    w.put(accq.at[:, p.sd, :, :, B], rqdy, p.y, "qdy")

    for r, t in ((0, 0), (1, 2)):
        f = [jnp.sum(dqkv[t, tl].reshape(1024, 128).astype(F32), axis=0, keepdims=True) for tl in range(2)]
        row[r, :, pl.ds(b0, 128)] = f[0]
        row[r, :, pl.ds(b1, 128)] = f[1]
    lane = lax.broadcasted_iota(jnp.int32, (32, 768), 1)
    mine_lane = ((lane * 2731) >> 16) == lax.broadcasted_iota(jnp.int32, (32, 768), 0)
    lane2 = lax.broadcasted_iota(jnp.int32, (128, 768), 1)
    spread = (lane2 - 24 * ((lane2 * 2731) >> 16) == lax.broadcasted_iota(jnp.int32, (128, 768), 0)).astype(F32)
    vacc[...] = gvec[...]
    for r in range(2):
        part = jnp.where(mine_lane, row[r], 0.0)
        vacc[:, r, :] = lax.dot_general(
            part, spread, (((1,), (1,)), ((), ())), preferred_element_type=F32, precision=lax.Precision.HIGHEST
        )
    ya = s // 2
    w.put(vacc.at[pl.ds(16 * (1 - ya), 16)], rv0, p.y, "v0")

    far(2)
    final(0)
    w.got(rqdx, "qdx")
    accq[:, p.sy, :, :, 0:256] = accq[:, p.sy, :, :, 0:256] + rqdx[...]
    w.put(accq.at[:, p.sy], rqy, p.y, "qy")
    w.got(rqdy, "qdy")
    accq[:, p.sx, :, :, 256:384] = accq[:, p.sx, :, :, 256:384] + rqdy[...]
    w.put(accq.at[:, p.sx], rqx, p.x, "qx")

    w.got(rtn.at[0], "t1")
    rtk[p.zf] = rtk[p.zf] + rtn[0]
    w.put(rtk.at[p.zf], rtf, p.f, "t3")

    w.got(rv0, "v0")
    vacc[pl.ds(16 * ya, 16)] = vacc[pl.ds(16 * ya, 16)] + rv0[...]
    w.put(vacc.at[pl.ds(8 * p.sx, 8)], rv1, p.x, "v1")
    plane(3)
    final(1)
    far(3)
    plane(4)
    w.got(rv1, "v1")
    vacc[pl.ds(8 * s, 8)] = vacc[pl.ds(8 * s, 8)] + rv1[...]
    w.put(vacc.at[pl.ds(8 * s + 4 * (1 - g), 4)], rv2, p.f, "v2")

    w.got(rqx, "qx")
    w.got(rqy, "qy")
    for t in range(3):
        accq[t, s] = (accq[t, s].astype(F32) + rqx[t].astype(F32) + rqy[t].astype(F32)).astype(BF16)
    w.put(accq.at[:, s, p.znf], rqz.at[0], p.f, "qz0")
    w.put(accq.at[:, s, p.zf], rqz.at[1], p.f, "qz1")
    far(4)
    w.got(rv2, "v2")
    vacc[pl.ds(8 * s + 4 * g, 4)] = vacc[pl.ds(8 * s + 4 * g, 4)] + rv2[...]
    w.put(vacc.at[pl.ds(8 * s + 2 * p.zn, 2)], rv3, p.n, "v3")
    w.got(rqz.at[0], "qz0")
    accq[:, s, p.zn] = accq[:, s, p.zn] + rqz[0]
    w.put(accq.at[:, s, p.zn], rqz.at[2], p.n, "qz2")
    final(2)
    w.got(rv3, "v3")
    vacc[pl.ds(8 * s + 2 * z, 2)] = vacc[pl.ds(8 * s + 2 * z, 2)] + rv3[...]
    w.put(vacc.at[8 * s + p.bc], rv4, p.core, "v4")
    final(3)
    w.got(rtn.at[1], "t2")
    w.got(rtf, "t3")
    dtok[g] = dh1[g] + rtk[z].astype(F32) + rtn[1].astype(F32)
    dtok[1 - g] = dh1[1 - g] + rtf[...].astype(F32)
    final(4)
    w.got(rv4, "v4")
    ovec[...] = vacc[8 * s + b] + rv4[...]
    w.got(rqz.at[1], "qz1")
    w.got(rqz.at[2], "qz2")
    q0 = pl.multiple_of(384 * zp, 128)
    q1 = pl.multiple_of(384 * (1 - zp), 128)
    for t in range(3):
        oqkv[t, :, pl.ds(q0, 384)] = accq[t, s, z].astype(F32) + rqz[1, t].astype(F32)
        oqkv[t, :, pl.ds(q1, 384)] = rqz[2, t].astype(F32)
    w.finish()


def scatter_call(gd, gu, go, gvec, datt, dh1, xg, qkv, wqkv, match):
    V = pl.BlockSpec(memory_space=pltpu.VMEM)
    S = jax.ShapeDtypeStruct
    VM = pltpu.VMEM
    per_chunk = []
    for nr, nc in ((48, 768), (48, 768), (24, 1536), (24, 1536), (24, 768)):
        per_chunk += [
            VM((4, 4, nr, nc), BF16), VM((4, nr, nc // 2), BF16), VM((4, nr, nc // 2), BF16),
            VM((4, nr, nc), BF16), VM((4, nr, nc), BF16), VM((3, nr, nc), BF16),
        ]
    return pl.pallas_call(
        scatter_kernel,
        out_shape=(
            S((96, 768), F32), S((24, 3072), F32), S((24, 768), F32), S((3, 24, 768), F32),
            S((2, 128, 768), F32), S((16, 128), F32),
        ),
        in_specs=[V] * 10,
        out_specs=(V,) * 6,
        scratch_shapes=[
            VM((2, 8, 128, 128), BF16), VM((2, 2, 8, 128, 128), BF16), VM((2, 2, 8, 128, 128), BF16),
            VM((3, 2, 8, 128, 128), BF16), VM((3, 4, 4, 2, 24, 256), BF16), VM((3, 4, 4, 24, 256), BF16),
            VM((3, 4, 4, 24, 384), BF16), VM((2, 1, 768), F32), VM((32, 16, 128), F32),
            VM((8, 128, 768), BF16), VM((4, 128, 768), BF16), VM((2, 128, 768), BF16), VM((128, 768), BF16),
            pltpu.SMEM((8, 8, 128), jnp.int32),
            VM((16, 16, 128), F32), VM((8, 16, 128), F32), VM((4, 16, 128), F32), VM((2, 16, 128), F32), VM((16, 128), F32),
            VM((3, 4, 24, 256), BF16), VM((3, 4, 24, 128), BF16), VM((3, 4, 24, 384), BF16), VM((3, 4, 24, 384), BF16),
            VM((3, 3, 24, 384), BF16),
            *per_chunk,
            pltpu.SemaphoreType.DMA((112,)),
            pltpu.SemaphoreType.DMA((112,)),
            pltpu.SemaphoreType.DMA((4,)),
        ],
        compiler_params=pltpu.CompilerParams(collective_id=1, has_side_effects=True, vmem_limit_bytes=58 << 20),
        name="scatter",
    )(gd, gu, go, gvec, datt, dh1, xg, qkv, wqkv, match)


def middle(tokens, grad_out, masked, att, full_out, full_up, full_down, vecs):
    groups, local_len, width = tokens.shape
    row_count = groups * local_len

    def vector(k):
        return vecs[:, k, :24].reshape(768).astype(F32)

    bias_out, bias_down, gain1, shift1, gain2, shift2 = (vector(k) for k in range(2, 8))
    bias_up = vecs[:, 8, :96].reshape(3072).astype(F32)
    flat_tokens = tokens.reshape(row_count, width)
    attended = att.reshape(row_count, width)
    branch = jnp.dot(attended, full_out, preferred_element_type=F32) + bias_out
    normed, pull_first = jax.vjp(norm_rows, flat_tokens.astype(F32) + branch, gain1, shift1)
    normed_low = normed.astype(BF16)
    inner_sum = jnp.dot(normed_low, full_up, preferred_element_type=F32) + bias_up
    active, pull_gelu = jax.vjp(gelu_exact, inner_sum)
    active_low = active.astype(BF16)
    outer_sum = jnp.dot(active_low, full_down, preferred_element_type=F32) + bias_down
    final_rows, pull_second = jax.vjp(norm_rows, normed + outer_sum, gain2, shift2)
    upstream = grad_out.reshape(row_count, width).astype(F32) * masked.reshape(row_count, 1).astype(F32)
    d_sum2, d_gain2, d_shift2 = pull_second(upstream)
    d_outer = d_sum2.astype(BF16)
    g_down = jnp.einsum("rf,rd->fd", active_low, d_outer, preferred_element_type=F32).astype(BF16)
    g_bdown = jnp.sum(d_outer.astype(F32), axis=0)
    d_active = jnp.einsum("rd,fd->rf", d_outer, full_down, preferred_element_type=F32)
    d_inner = pull_gelu(d_active)[0].astype(BF16)
    g_up = jnp.einsum("rd,rf->df", normed_low, d_inner, preferred_element_type=F32).astype(BF16)
    g_bup = jnp.sum(d_inner.astype(F32), axis=0)
    d_normed = d_sum2 + jnp.einsum("rf,df->rd", d_inner, full_up, preferred_element_type=F32)
    d_resid, d_gain1, d_shift1 = pull_first(d_normed)
    d_branch = d_resid.astype(BF16)
    g_out = jnp.einsum("ri,rd->id", attended, d_branch, preferred_element_type=F32).astype(BF16)
    g_bout = jnp.sum(d_branch.astype(F32), axis=0)
    d_attended = jnp.einsum("rd,id->ri", d_branch, full_out, preferred_element_type=F32).astype(BF16)
    none = jnp.zeros_like(g_bout)
    rows = jnp.stack([none, none, g_bout, g_bdown, d_gain1, d_shift1, d_gain2, d_shift2])
    rows = jnp.pad(rows.reshape(8, 32, 24).transpose(1, 0, 2), ((0, 0), (0, 0), (0, 104)))
    tail = jnp.pad(g_bup.reshape(32, 1, 96), ((0, 0), (0, 7), (0, 32)))
    gvec = jnp.concatenate([rows, tail], axis=1)
    result = final_rows.astype(BF16).reshape(groups, local_len, width)
    return (
        result, g_down, g_up, g_out, gvec,
        d_attended.reshape(groups, local_len, width), d_resid.reshape(groups, local_len, width),
    )


def column(
    tokens, grad_out, masked, token_order, cluster_match,
    w_query, w_key, w_value, w_out, w_up, w_down,
    b_query, b_value, b_out, b_up, b_down,
    gain_attn, shift_attn, gain_ffn, shift_ffn,
):
    vectors = (b_query, b_value, b_out, b_down, gain_attn, shift_attn, gain_ffn, shift_ffn)
    mt, vec = pack_inputs(cluster_match, vectors, b_up)
    full_out, full_up, full_down, wqkv, xg, qkv, att, match, vecs = gather_call(
        tokens, mt, vec, w_query, w_key, w_value, w_out, w_up, w_down
    )
    result, g_down, g_up, g_out, gvec, d_att, d_resid = middle(
        tokens, grad_out, masked, att, full_out.reshape(768, 768), full_up.reshape(768, 3072),
        full_down.reshape(3072, 768), vecs,
    )
    o_down, o_up, o_out, o_qkv, d_tokens, o_vec = scatter_call(
        g_down.reshape(4, 4, 2, 96, 768), g_up.reshape(4, 4, 2, 24, 3072), g_out.reshape(4, 4, 2, 24, 768),
        gvec, d_att, d_resid, xg, qkv, wqkv, match
    )
    small = [o_vec[k, :24] for k in range(8)]
    return (
        result, d_tokens, o_qkv[0], o_qkv[1], o_qkv[2], o_out, o_up, o_down,
        small[0], small[1], small[2], o_vec[8, :96], small[3],
        small[4], small[5], small[6], small[7],
    )


def solution(mesh):
    fits = mesh.shape[SEQ] == 4 and mesh.shape[BLK] == 8
    return jax.shard_map(
        column if fits else general,
        mesh=mesh,
        in_specs=(
            P(SEQ, BLK, None),
            P(SEQ, BLK, None),
            P(SEQ, BLK),
            P(SEQ, None, BLK),
            P(SEQ, None, BLK),
            P(BOTH, None),
            P(BOTH, None),
            P(BOTH, None),
            P(BOTH, None),
            P(BOTH, None),
            P(BOTH, None),
            P(BOTH),
            P(BOTH),
            P(BOTH),
            P(BOTH),
            P(BOTH),
            P(BOTH),
            P(BOTH),
            P(BOTH),
            P(BOTH),
        ),
        out_specs=(
            P(SEQ, BLK, None),
            P(SEQ, BLK, None),
            P(BOTH, None),
            P(BOTH, None),
            P(BOTH, None),
            P(BOTH, None),
            P(BOTH, None),
            P(BOTH, None),
            P(BOTH),
            P(BOTH),
            P(BOTH),
            P(BOTH),
            P(BOTH),
            P(BOTH),
            P(BOTH),
            P(BOTH),
            P(BOTH),
        ),
        check_vma=False,
    )
```

```python
import functools
import math

import jax
import jax.numpy as jnp
from jax import lax
from jax.experimental import pallas as pl
from jax.experimental.pallas import tpu as pltpu
from jax.sharding import PartitionSpec as P

HEADS = 12
CL = 128
EPS = 1e-05
MESH = pl.DeviceIdType.MESH
SEQ, BLK = BOTH = ("seq", "blk")
F32 = jnp.float32
BF16 = jnp.bfloat16


def norm_rows(hidden, gain_row, shift_row):
    row_mean = jnp.mean(hidden, axis=-1, keepdims=True)
    centered = hidden - row_mean
    variance = jnp.mean(centered * centered, axis=-1, keepdims=True)
    return centered * lax.rsqrt(variance + EPS) * gain_row + shift_row


def gelu_exact(inner_sum):
    return jax.nn.gelu(inner_sum, approximate=False)


def to_heads(flat_rows, groups, local_len):
    return flat_rows.reshape(groups, local_len, HEADS, -1).transpose(0, 2, 1, 3)


def from_heads(head_rows):
    groups, head_count, local_len, head_dim = head_rows.shape
    return head_rows.transpose(0, 2, 1, 3).reshape(groups * local_len, head_count * head_dim)


def reorder(head_rows, positions):
    return jnp.take_along_axis(head_rows, positions[..., None], axis=2)


def general(
    tokens,
    grad_out,
    masked,
    token_order,
    cluster_match,
    w_query,
    w_key,
    w_value,
    w_out,
    w_up,
    w_down,
    b_query,
    b_value,
    b_out,
    b_up,
    b_down,
    gain_attn,
    shift_attn,
    gain_ffn,
    shift_ffn,
):
    groups, local_len, width = tokens.shape
    row_count = groups * local_len
    head_dim = width // HEADS
    clusters = local_len // CL
    score_scale = 1.0 / math.sqrt(head_dim)
    gathered = (
        lax.all_gather(w_query, BOTH, axis=0, tiled=True),
        lax.all_gather(w_key, BOTH, axis=0, tiled=True),
        lax.all_gather(w_value, BOTH, axis=0, tiled=True),
        lax.all_gather(w_out, BOTH, axis=0, tiled=True),
        lax.all_gather(w_up, BOTH, axis=0, tiled=True),
        lax.all_gather(w_down, BOTH, axis=0, tiled=True),
        lax.all_gather(b_query, BOTH, axis=0, tiled=True),
        lax.all_gather(b_value, BOTH, axis=0, tiled=True),
        lax.all_gather(b_out, BOTH, axis=0, tiled=True),
        lax.all_gather(b_up, BOTH, axis=0, tiled=True),
        lax.all_gather(b_down, BOTH, axis=0, tiled=True),
        lax.all_gather(gain_attn, BOTH, axis=0, tiled=True),
        lax.all_gather(shift_attn, BOTH, axis=0, tiled=True),
        lax.all_gather(gain_ffn, BOTH, axis=0, tiled=True),
        lax.all_gather(shift_ffn, BOTH, axis=0, tiled=True),
    )
    (
        full_query,
        full_key,
        full_value,
        full_out,
        full_up,
        full_down,
        bias_query,
        bias_value,
        bias_out,
        bias_up,
        bias_down,
        norm_gain1,
        norm_shift1,
        norm_gain2,
        norm_shift2,
    ) = gathered
    flat_tokens = tokens.reshape(row_count, width)
    inverse = jnp.argsort(token_order, axis=-1)
    cluster_shape = (groups, HEADS, clusters, CL, head_dim)
    query_low = (
        jnp.dot(flat_tokens, full_query, preferred_element_type=jnp.float32)
        + bias_query.astype(jnp.float32)
    ).astype(jnp.bfloat16)
    key_low = jnp.dot(flat_tokens, full_key, preferred_element_type=jnp.float32).astype(
        jnp.bfloat16
    )
    value_low = (
        jnp.dot(flat_tokens, full_value, preferred_element_type=jnp.float32)
        + bias_value.astype(jnp.float32)
    ).astype(jnp.bfloat16)
    query_perm = reorder(to_heads(query_low, groups, local_len), token_order).reshape(cluster_shape)
    key_perm = reorder(to_heads(key_low, groups, local_len), token_order).reshape(cluster_shape)
    value_perm = reorder(to_heads(value_low, groups, local_len), token_order).reshape(cluster_shape)
    empty_sel = jnp.zeros(cluster_shape, jnp.bfloat16)
    key_piece = lax.all_gather(key_perm, BLK, axis=2, tiled=True)
    value_piece = lax.all_gather(value_perm, BLK, axis=2, tiled=True)
    piece_len = key_piece.shape[2]
    offset = cluster_match
    select = (offset[..., None] == jnp.arange(piece_len, dtype=jnp.int32)).astype(jnp.bfloat16)
    inside = ((offset >= 0) & (offset < piece_len))[..., None, None]
    new_keys = jnp.einsum(
        "ghcj,ghjkd->ghckd", select, key_piece, preferred_element_type=jnp.float32
    ).astype(jnp.bfloat16)
    new_values = jnp.einsum(
        "ghcj,ghjkd->ghckd", select, value_piece, preferred_element_type=jnp.float32
    ).astype(jnp.bfloat16)
    key_sel = jnp.where(inside, new_keys, empty_sel)
    value_sel = jnp.where(inside, new_values, empty_sel)
    scores = (
        jnp.einsum("ghcqd,ghckd->ghcqk", query_perm, key_sel, preferred_element_type=jnp.float32)
        * score_scale
    )
    row_max = jnp.max(scores, axis=-1, keepdims=True)
    log_total = row_max + jnp.log(jnp.sum(jnp.exp(scores - row_max), axis=-1, keepdims=True))
    attn_probs = jnp.exp(scores - log_total)
    probs_low = attn_probs.astype(jnp.bfloat16)
    mixed_perm = jnp.einsum(
        "ghcqk,ghckd->ghcqd", probs_low, value_sel, preferred_element_type=jnp.float32
    ).reshape(groups, HEADS, local_len, head_dim)
    attended = from_heads(reorder(mixed_perm, inverse)).astype(jnp.bfloat16)
    branch = jnp.dot(attended, full_out, preferred_element_type=jnp.float32) + bias_out.astype(
        jnp.float32
    )
    resid = flat_tokens.astype(jnp.float32) + branch
    normed, pull_first = jax.vjp(
        norm_rows, resid, norm_gain1.astype(jnp.float32), norm_shift1.astype(jnp.float32)
    )
    normed_low = normed.astype(jnp.bfloat16)
    inner_sum = jnp.dot(normed_low, full_up, preferred_element_type=jnp.float32) + bias_up.astype(
        jnp.float32
    )
    active, pull_gelu = jax.vjp(gelu_exact, inner_sum)
    active_low = active.astype(jnp.bfloat16)
    outer_sum = jnp.dot(
        active_low, full_down, preferred_element_type=jnp.float32
    ) + bias_down.astype(jnp.float32)
    final_rows, pull_second = jax.vjp(
        norm_rows,
        normed + outer_sum,
        norm_gain2.astype(jnp.float32),
        norm_shift2.astype(jnp.float32),
    )
    result = final_rows.astype(jnp.bfloat16).reshape(groups, local_len, width)
    back_weights = (
        lax.all_gather(w_query, BOTH, axis=0, tiled=True),
        lax.all_gather(w_key, BOTH, axis=0, tiled=True),
        lax.all_gather(w_value, BOTH, axis=0, tiled=True),
        lax.all_gather(w_out, BOTH, axis=0, tiled=True),
        lax.all_gather(w_up, BOTH, axis=0, tiled=True),
        lax.all_gather(w_down, BOTH, axis=0, tiled=True),
        lax.all_gather(b_query, BOTH, axis=0, tiled=True),
        lax.all_gather(b_value, BOTH, axis=0, tiled=True),
        lax.all_gather(b_out, BOTH, axis=0, tiled=True),
        lax.all_gather(b_up, BOTH, axis=0, tiled=True),
        lax.all_gather(b_down, BOTH, axis=0, tiled=True),
        lax.all_gather(gain_attn, BOTH, axis=0, tiled=True),
        lax.all_gather(shift_attn, BOTH, axis=0, tiled=True),
        lax.all_gather(gain_ffn, BOTH, axis=0, tiled=True),
        lax.all_gather(shift_ffn, BOTH, axis=0, tiled=True),
    )
    back_query, back_key, back_value, back_out, back_up, back_down = back_weights[:6]
    upstream = grad_out.reshape(row_count, width).astype(jnp.float32) * masked.reshape(
        row_count, 1
    ).astype(jnp.float32)
    d_sum2, d_gain2, d_shift2 = pull_second(upstream)
    d_outer = d_sum2.astype(jnp.bfloat16)
    g_down = jnp.einsum("rf,rd->fd", active_low, d_outer, preferred_element_type=jnp.float32)
    g_bdown = jnp.sum(d_outer.astype(jnp.float32), axis=0)
    d_active = jnp.einsum("rd,fd->rf", d_outer, back_down, preferred_element_type=jnp.float32)
    d_inner = pull_gelu(d_active)[0].astype(jnp.bfloat16)
    g_up = jnp.einsum("rd,rf->df", normed_low, d_inner, preferred_element_type=jnp.float32)
    g_bup = jnp.sum(d_inner.astype(jnp.float32), axis=0)
    d_normed = d_sum2 + jnp.einsum(
        "rf,df->rd", d_inner, back_up, preferred_element_type=jnp.float32
    )
    d_resid, d_gain1, d_shift1 = pull_first(d_normed)
    d_branch = d_resid.astype(jnp.bfloat16)
    g_out = jnp.einsum("ri,rd->id", attended, d_branch, preferred_element_type=jnp.float32)
    g_bout = jnp.sum(d_branch.astype(jnp.float32), axis=0)
    d_attended = jnp.einsum(
        "rd,id->ri", d_branch, back_out, preferred_element_type=jnp.float32
    ).astype(jnp.bfloat16)
    d_mixed = reorder(to_heads(d_attended, groups, local_len), token_order).reshape(cluster_shape)
    scores_again = (
        jnp.einsum("ghcqd,ghckd->ghcqk", query_perm, key_sel, preferred_element_type=jnp.float32)
        * score_scale
    )
    probs_again = jnp.exp(scores_again - log_total)
    probs_again_low = probs_again.astype(jnp.bfloat16)
    d_probs = jnp.einsum(
        "ghcqd,ghckd->ghcqk", d_mixed, value_sel, preferred_element_type=jnp.float32
    )
    d_scores = (
        probs_again * (d_probs - jnp.sum(probs_again * d_probs, axis=-1, keepdims=True))
    ).astype(jnp.bfloat16)
    d_query_perm = (
        jnp.einsum("ghcqk,ghckd->ghcqd", d_scores, key_sel, preferred_element_type=jnp.float32)
        * score_scale
    )
    d_key_sel = (
        jnp.einsum("ghcqk,ghcqd->ghckd", d_scores, query_perm, preferred_element_type=jnp.float32)
        * score_scale
    )
    d_value_sel = jnp.einsum(
        "ghcqk,ghcqd->ghckd", probs_again_low, d_mixed, preferred_element_type=jnp.float32
    )
    sent = jnp.concatenate([d_key_sel, d_value_sel], axis=-1)
    my_start = lax.axis_index(BLK) * clusters
    piece_grads = lax.all_gather(sent.astype(jnp.bfloat16), BLK, axis=2, tiled=True).astype(
        jnp.float32
    )
    piece_match = lax.all_gather(
        cluster_match.astype(jnp.float32).astype(jnp.bfloat16), BLK, axis=2, tiled=True
    ).astype(jnp.float32)
    offset = piece_match.astype(jnp.int32) - my_start
    select = (offset[..., None] == jnp.arange(clusters, dtype=jnp.int32)).astype(jnp.float32)
    owned = jnp.zeros(sent.shape, jnp.float32) + jnp.einsum(
        "ghjc,ghjke->ghcke", select, piece_grads, precision=lax.Precision.HIGHEST
    )
    back_kv = reorder(owned.reshape(groups, HEADS, local_len, 2 * head_dim), inverse)
    d_key = from_heads(back_kv[..., :head_dim]).astype(jnp.bfloat16)
    d_value = from_heads(back_kv[..., head_dim:]).astype(jnp.bfloat16)
    d_query = from_heads(
        reorder(d_query_perm.reshape(groups, HEADS, local_len, head_dim), inverse)
    ).astype(jnp.bfloat16)
    g_query = jnp.einsum("ri,rd->id", flat_tokens, d_query, preferred_element_type=jnp.float32)
    g_key = jnp.einsum("ri,rd->id", flat_tokens, d_key, preferred_element_type=jnp.float32)
    g_value = jnp.einsum("ri,rd->id", flat_tokens, d_value, preferred_element_type=jnp.float32)
    g_bquery = jnp.sum(d_query.astype(jnp.float32), axis=0)
    g_bvalue = jnp.sum(d_value.astype(jnp.float32), axis=0)
    d_tokens_flat = (
        d_resid
        + jnp.einsum("rd,id->ri", d_query, back_query, preferred_element_type=jnp.float32)
        + jnp.einsum("rd,id->ri", d_key, back_key, preferred_element_type=jnp.float32)
        + jnp.einsum("rd,id->ri", d_value, back_value, preferred_element_type=jnp.float32)
    )
    summed = (
        lax.psum_scatter(g_query, BOTH, scatter_dimension=0, tiled=True),
        lax.psum_scatter(g_key, BOTH, scatter_dimension=0, tiled=True),
        lax.psum_scatter(g_value, BOTH, scatter_dimension=0, tiled=True),
        lax.psum_scatter(g_out, BOTH, scatter_dimension=0, tiled=True),
        lax.psum_scatter(g_up, BOTH, scatter_dimension=0, tiled=True),
        lax.psum_scatter(g_down, BOTH, scatter_dimension=0, tiled=True),
        lax.psum_scatter(g_bquery, BOTH, scatter_dimension=0, tiled=True),
        lax.psum_scatter(g_bvalue, BOTH, scatter_dimension=0, tiled=True),
        lax.psum_scatter(g_bout, BOTH, scatter_dimension=0, tiled=True),
        lax.psum_scatter(g_bup, BOTH, scatter_dimension=0, tiled=True),
        lax.psum_scatter(g_bdown, BOTH, scatter_dimension=0, tiled=True),
        lax.psum_scatter(d_gain1, BOTH, scatter_dimension=0, tiled=True),
        lax.psum_scatter(d_shift1, BOTH, scatter_dimension=0, tiled=True),
        lax.psum_scatter(d_gain2, BOTH, scatter_dimension=0, tiled=True),
        lax.psum_scatter(d_shift2, BOTH, scatter_dimension=0, tiled=True),
    )
    return (result, d_tokens_flat.reshape(groups, local_len, width)) + tuple(summed)


OWN, NEAR, FAR, NEARFAR = range(4)
NT = (((1,), (1,)), ((), ()))
TN = (((0,), (0,)), ((), ()))


class Place:
    def __init__(self):
        s, b = lax.axis_index(SEQ), lax.axis_index(BLK)
        self.s, self.b = s, b
        z, c = b // 2, b % 2
        self.z, self.c = z, c
        self.zlo, self.zhi = z % 2, z // 2
        self.sx = s + 1 - 2 * (s % 2)
        self.sy = s + 2 - 4 * (s // 2)
        self.sd = self.sy + 1 - 2 * (s % 2)
        self.zn = z + 1 - 2 * self.zlo
        self.zf = z + 2 - 4 * self.zhi
        self.znf = self.zf + 1 - 2 * self.zlo
        self.bc = b + 1 - 2 * c
        self.bn, self.bf, self.bnf = self.zn * 2 + c, self.zf * 2 + c, self.znf * 2 + c
        self.core = (s, self.bc)
        self.n = (s, self.bn)
        self.f = (s, self.bf)
        self.nf = (s, self.bnf)
        self.x = (self.sx, b)
        self.y = (self.sy, b)


class Wire:
    def __init__(self, send, recv, local):
        self.send, self.recv, self.local = send, recv, local
        self.n_send = self.n_local = self.n_recv = 0
        self.sent, self.slots = [], {}

    def slot(self, key):
        if key not in self.slots:
            self.slots[key] = self.n_recv
            self.n_recv += 1
        return self.slots[key]

    def block(self, n):
        first = self.n_recv
        self.n_recv += n
        return first

    def put(self, src, dst, to, key, at=None):
        at = self.slot(key) if at is None else at
        cp = pltpu.make_async_remote_copy(
            src, dst, self.send.at[self.n_send], self.recv.at[at], device_id=to, device_id_type=MESH
        )
        self.n_send += 1
        cp.start()
        self.sent.append(cp)

    def got(self, dst, key, at=None):
        at = self.slot(key) if at is None else at
        pltpu.make_async_copy(dst, dst, self.recv.at[at]).wait()

    def move(self, src, dst):
        cp = pltpu.make_async_copy(src, dst, self.local.at[self.n_local])
        self.n_local += 1
        cp.start()
        return cp

    def finish(self):
        for cp in self.sent:
            cp.wait_send()


def greet(peers):
    bar = pltpu.get_barrier_semaphore()
    for to in peers:
        pl.semaphore_signal(bar, inc=1, device_id=to, device_id_type=MESH)
    pl.semaphore_wait(bar, len(peers))


def loop(n, body):
    def run(i, carry):
        body(i)
        return carry

    lax.fori_loop(0, n, run, 0)


def joined(v):
    return v.astype(F32).reshape(768, v.shape[-1]).astype(BF16)


def mean(v):
    return jnp.mean(v, axis=-1, keepdims=True)


def total(v):
    return jnp.sum(v, axis=0, keepdims=True)


def layer_kernel(
    tok_h, go_h, mask, cm, wq, wk, wv, wo_s, wu_s, wd_s,
    *others,
):
    vectors, (result, od, ou, oo, oqkv, dtok, ovec, sc, *sems) = others[:9], others[9:]
    p = Place()
    w = Wire(*sems)
    s, b, z, c = p.s, p.b, p.z, p.c
    zp, g = p.zlo, p.zhi
    zs = (z, p.zn, p.zf, p.znf)
    wou, wd, wqkv, xg, qkv, att, vecs = (sc[k] for k in ("wou", "wd", "wqkv", "xg", "qkv", "att", "vecs"))
    match, m_smem, stage, stage_ou, rows, bup = (sc[k] for k in ("match", "ms", "stage", "sou", "rows", "bup"))

    early = [w.move(ref.at[:, pl.ds(384 * h, 384)], stage.at[h, t]) for t, ref in enumerate((wq, wk, wv)) for h in range(2)]
    ou_in = [w.move(wo_s, stage_ou.at[:, pl.ds(0, 768)]), w.move(wu_s, stage_ou.at[:, pl.ds(768, 3072)])]
    tok, grad = sc["tok"], sc["grad"]
    tok_in, grad_in = w.move(tok_h, tok), w.move(go_h, grad)
    dap, ds_buf, p_buf, dqkv, vacc = (sc[k] for k in ("dap", "ds", "p", "dqkv", "vacc"))
    left = lax.broadcasted_iota(jnp.int32, (128, 128), 1) < 64
    zero = jnp.zeros((128, 128), BF16)
    for i in range(4):
        other = 2 * i + 1 - c
        dap[1, other] = zero
        dqkv[0, 1, other] = zero
        for e in range(2):
            ds_buf[1, e, other] = zero
            p_buf[1, e, other] = zero
    vec_own, match_own = sc["vo"], sc["mo"]
    vec_own[...] = jnp.zeros_like(vec_own)
    for k, ref in enumerate(vectors):
        vec_own[0:1, 24 * k : 24 * k + ref.shape[0]] = ref[...].reshape(1, ref.shape[0])
    match_own[:, 0:12] = jnp.broadcast_to(cm[...], (2, 12, 128))
    slot = s * 8 + b
    for cp in early:
        cp.wait()
    greet([p.core, p.n, p.f, p.nf, p.x, p.y, (s, p.zn * 2 + 1 - c), (s, p.zf * 2 + 1 - c), (s, p.znf * 2 + 1 - c)])

    def at_rows(n, ss, zz, cc):
        return pl.ds(pl.multiple_of(n * (ss * 8 + zz * 2 + cc), 8), n)

    def reg(k, ss, u, cc, half=None):
        zz = zs[u]
        if k == 0:
            cols = (pl.ds(0, 384), pl.ds(0, 256), pl.ds(256, 128))[0 if half is None else 1 + half]
            return wqkv.at[:, ss * 8 + zz * 2 + cc, :, cols]
        if k == 1:
            cols = pl.ds(0, 3840) if half is None else pl.ds(1920 * half, 1920)
            return wou.at[ss * 8 + zz * 2 + cc, :, cols]
        cols = pl.ds(0, 768) if half is None else pl.ds(384 * half, 384)
        return wd.at[at_rows(96, ss, zz, cc), cols]

    own_src = {1: stage_ou, 2: wd_s}

    def to_plane(k, u, src=None):
        r = reg(k, s, u, c)
        src = r if src is None else src
        w.put(src, r, p.x, (0, k, u))
        w.put(src, r, p.y, (1, k, u))

    def to_core(k, ss, u, name):
        r = reg(k, ss, u, c)
        w.put(r, r, p.core, (name, k, u))

    def z_start(k):
        r = reg(k, s, OWN, c)
        w.put(own_src[k], r, p.n, (2, k))
        w.put(own_src[k], r, p.f, (3, k))

    def near(k):
        w.got(reg(k, s, NEAR, c), (2, k))
        to_plane(k, NEAR)
        to_core(k, s, NEAR, 5)

    def far(k):
        r = reg(k, s, FAR, c)
        w.got(r, (3, k))
        w.put(r, r, p.n, (4, k))
        to_plane(k, FAR)
        to_core(k, s, FAR, 5)

    def nearfar(k):
        w.got(reg(k, s, NEARFAR, c), (4, k))
        to_plane(k, NEARFAR)
        to_core(k, s, NEARFAR, 5)

    def turn(k, u):
        w.got(reg(k, p.sx, u, c), (0, k, u))
        r = reg(k, p.sx, u, c, 0)
        w.put(r, r, p.y, (6, k, u))
        to_core(k, p.sx, u, 8)
        w.got(reg(k, p.sy, u, c), (1, k, u))
        r = reg(k, p.sy, u, c, 1)
        w.put(r, r, p.x, (7, k, u))
        to_core(k, p.sy, u, 9)

    def corner(k, u):
        w.got(reg(k, p.sd, u, c, 0), (6, k, u))
        w.got(reg(k, p.sd, u, c, 1), (7, k, u))
        to_core(k, p.sd, u, 10)

    def complete(k):
        for u in range(4):
            for name, ss in ((5, s), (8, p.sx), (9, p.sy), (10, p.sd)):
                w.got(reg(k, ss, u, 1 - c), (name, k, u))

    own = reg(0, s, OWN, c)
    w.put(stage.at[1 - zp], own, p.n, (2, 0))
    w.put(stage.at[zp], own, p.f, (3, 0))
    w.put(stage.at[1 - zp], own, p.nf, (4, 0))
    w.put(tok_h.at[g], xg.at[b], p.n, 20)
    w.put(tok_h.at[1 - g], xg.at[b], p.f, 21)
    w.put(stage.at[zp], own, p.x, (0, 0, OWN))
    w.put(stage.at[zp], own, p.y, (1, 0, OWN))
    w.put(match_own, match.at[b], p.core, 30)
    w.put(vec_own, vecs.at[slot], p.core, 40)
    w.put(tok_h.at[g], xg.at[b], p.core, 23)
    for cp in ou_in:
        cp.wait()
    to_plane(1, OWN, stage_ou)
    mine = [
        w.move(stage.at[zp], own), w.move(match_own, match.at[b]), w.move(vec_own, vecs.at[slot]),
        w.move(tok_h.at[g], xg.at[b]), w.move(wd_s, reg(2, s, OWN, c)), w.move(stage_ou, reg(1, s, OWN, c)),
    ]
    for cp in mine:
        cp.wait()
    to_core(0, s, OWN, 5)

    def vec_to(lo, n, to, key):
        r = vecs.at[pl.ds(lo, n)]
        w.put(r, r, to, key)

    def match_to(lo, n, to, key):
        r = match.at[pl.ds(lo, n)]
        w.put(r, r, to, key)

    w.got(match.at[p.bc], 30)
    match_to(2 * z, 2, p.n, 31)
    w.got(vecs.at[s * 8 + p.bc], 40)
    vec_to(s * 8 + 2 * z, 2, p.n, 41)
    for u, name in ((NEAR, 2), (FAR, 3), (NEARFAR, 4)):
        w.got(reg(0, s, u, c), (name, 0))
        to_plane(0, u)
        to_core(0, s, u, 5)
    z_start(1)
    to_core(1, s, OWN, 5)
    to_core(2, s, OWN, 5)
    turn(0, OWN)
    w.got(xg.at[p.bn], 20)
    w.put(xg.at[p.bn], xg.at[p.bn], p.core, 24)
    w.got(xg.at[p.bf], 21)
    w.put(xg.at[p.bf], xg.at[p.bf], p.n, 22)
    w.put(xg.at[p.bf], xg.at[p.bf], p.core, 25)
    w.got(match.at[pl.ds(2 * p.zn, 2)], 31)
    match_to(4 * g, 4, p.f, 32)
    w.got(vecs.at[pl.ds(s * 8 + 2 * p.zn, 2)], 41)
    vec_to(s * 8 + 4 * g, 4, p.f, 42)
    turn(0, NEAR)
    turn(0, FAR)
    turn(0, NEARFAR)
    to_plane(2, OWN, wd_s)
    z_start(2)
    turn(1, OWN)
    w.got(vecs.at[pl.ds(s * 8 + 4 - 4 * g, 4)], 42)
    vec_to(s * 8, 8, p.x, 43)
    w.got(match.at[pl.ds(4 - 4 * g, 4)], 32)
    get_match = w.move(match, m_smem)
    near(1)
    far(1)
    w.got(xg.at[p.bnf], 22)
    w.put(xg.at[p.bnf], xg.at[p.bnf], p.core, 26)
    for u in range(4):
        corner(0, u)
    w.got(vecs.at[pl.ds(p.sx * 8, 8)], 43)
    vec_to((s // 2) * 16, 16, p.y, 44)
    complete(0)
    for blk, key in ((p.bc, 23), (p.zn * 2 + 1 - c, 24), (p.zf * 2 + 1 - c, 25), (p.znf * 2 + 1 - c, 26)):
        w.got(xg.at[blk], key)
    w.got(vecs.at[pl.ds((1 - s // 2) * 16, 16)], 44)

    lane = lax.broadcasted_iota(jnp.int32, (32, 768), 1)
    mine_lane = ((lane * 2731) >> 16) == lax.broadcasted_iota(jnp.int32, (32, 768), 0)
    lane2 = lax.broadcasted_iota(jnp.int32, (384, 768), 1)
    place = lane2 - 24 * ((lane2 * 2731) >> 16) - lax.broadcasted_iota(jnp.int32, (384, 768), 0)
    flat_vec = vecs[:, 0, :]

    def vector_row(k):
        part = jnp.dot(flat_vec, (place == -24 * k).astype(F32).astype(BF16), preferred_element_type=F32)
        rows[k] = jnp.sum(jnp.where(mine_lane, part, 0.0), axis=0, keepdims=True)

    def up_row(i):
        l3 = lax.broadcasted_iota(jnp.int32, (384, 768), 1) + 768 * i
        d3 = (l3 * 43691) >> 22
        hit = l3 - 96 * d3 - lax.broadcasted_iota(jnp.int32, (384, 768), 0) == -192
        part = jnp.dot(flat_vec, hit.astype(F32).astype(BF16), preferred_element_type=F32)
        owner = ((lax.broadcasted_iota(jnp.int32, (32, 768), 1) + 768 * i) * 43691) >> 22
        here = owner == lax.broadcasted_iota(jnp.int32, (32, 768), 0)
        bup[:, 768 * i : 768 * (i + 1)] = jnp.sum(jnp.where(here, part, 0.0), axis=0, keepdims=True)

    vector_row(0)
    vector_row(1)

    c0 = pl.multiple_of(128 * c, 128)
    b0 = pl.multiple_of(384 * zp + 128 * c, 128)
    b1 = pl.multiple_of(384 * zp + 256, 128)

    def head_columns(t):
        return jnp.concatenate([joined(wqkv[t, :, :, pl.ds(c0, 128)]), joined(wqkv[t, :, :, 256:384])], axis=1)

    for t in range(3):
        wt = head_columns(t)
        for m in range(2):
            r = jnp.dot(xg[4 * m : 4 * m + 4].reshape(512, 768), wt, preferred_element_type=F32)
            if t != 1:
                row = 0 if t == 0 else 1
                r = r + jnp.concatenate([rows[row, :, pl.ds(b0, 128)], rows[row, :, pl.ds(b1, 128)]], axis=1)
            r = r.astype(BF16)
            for i in range(4):
                for tl in range(2):
                    qkv[t, tl, 4 * m + i] = r[128 * i : 128 * (i + 1), 128 * tl : 128 * (tl + 1)]

    get_match.wait()
    att_buf = sc["ab"]

    def mask_head(e, v):
        return jnp.where(left if e == 0 else jnp.logical_not(left), v, zero)

    def weights(e, q, k):
        score = lax.dot_general(mask_head(e, q), k, NT, preferred_element_type=F32) * 0.125
        ex = jnp.exp(score - jnp.max(score, axis=-1, keepdims=True))
        return ex * (1.0 / jnp.sum(ex, axis=-1, keepdims=True))

    def head(tl, e):
        return 6 * zp + (2 * c if tl == 0 else 4) + e

    def attend(tl, blk, i):
        q = qkv[0, tl, blk]
        outs = []
        for e in range(2):
            m = m_smem[blk, g, head(tl, e), 0]
            pr = weights(e, q, qkv[1, tl, m]).astype(BF16)
            outs.append(jnp.dot(pr, qkv[2, tl, m], preferred_element_type=F32))
        att_buf[i] = jnp.where(left, outs[0], outs[1]).astype(BF16)

    tiles = w.block(12)

    def send_tile(tl, zz, cc, i):
        dst = att.at[g, :, pl.ds(pl.multiple_of(384 * zp + (128 * c if tl == 0 else 256), 128), 128)]
        if i in (0, 8):
            keep.append(w.move(att_buf.at[i], dst))
        else:
            w.put(att_buf.at[i], dst, (s, zz * 2 + cc), None, tiles + 6 * g + 3 * zp + (c if tl == 0 else 2))

    items = []
    for zz in (p.zf, p.znf, p.zn, z):
        items += [(0, zz, c), (0, zz, 1 - c), (1, zz, c)]
    between = {
        0: lambda: nearfar(1), 2: lambda: turn(1, NEAR), 4: lambda: turn(2, OWN),
        6: lambda: corner(1, OWN), 8: lambda: near(2), 10: lambda: turn(1, FAR),
    }
    keep = []
    free = [1, 2, 3, 4, 5, 6, 7, 9, 10, 11]
    for j, (tl, zz, cc) in enumerate(items):
        home = zz is z and cc is c
        i = (0 if tl == 0 else 8) if home else free.pop(0)
        attend(tl, zz * 2 + cc, i)
        send_tile(tl, zz, cc, i)
        if j in between:
            between[j]()
    far(2)
    corner(1, NEAR)
    turn(1, NEARFAR)
    turn(2, NEAR)
    for k in range(2, 8):
        vector_row(k)
    for i in range(4):
        up_row(i)
    corner(1, FAR)
    nearfar(2)
    corner(2, OWN)
    corner(1, NEARFAR)
    turn(2, FAR)
    complete(1)

    def got_tile(gg, tile):
        w.got(att.at[gg, :, pl.ds(pl.multiple_of(128 * tile, 128), 128)], None, tiles + 6 * gg + tile)

    for tile in range(6):
        got_tile(1 - g, tile)
    for tile in range(3):
        got_tile(g, 3 - 3 * zp + tile)
    got_tile(g, 3 * zp + 1 - c)
    for cp in keep + [tok_in, grad_in]:
        cp.wait()

    n1, nlow, act, slope, dh2, dinner = (sc[k] for k in ("n1", "nlow", "act", "slope", "dh2", "din"))

    def whole(ref):
        return ref[...].reshape(256, 768)

    h = whole(tok).astype(F32) + jnp.dot(whole(att), joined(wou[:, :, 0:768]), preferred_element_type=F32) + rows[2]
    h = h - mean(h)
    r1 = lax.rsqrt(mean(h * h) + EPS)
    n1[...] = h * r1
    nlow[...] = (n1[...] * rows[4] + rows[5]).astype(BF16)

    def up(j):
        cols = slice(512 * j, 512 * (j + 1))
        u = jnp.dot(nlow[...], joined(wou[:, :, 768 + 512 * j : 768 + 512 * (j + 1)]), preferred_element_type=F32) + bup[:, cols]
        cdf = 0.5 + 0.5 * lax.erf(u * 0.7071067811865476)
        act[:, cols] = (u * cdf).astype(BF16)
        slope[:, cols] = cdf + u * (jnp.exp(-0.5 * u * u) * 0.3989422804014327)

    up(0)
    corner(2, NEAR)
    up(1)
    up(2)
    turn(2, NEARFAR)
    up(3)
    corner(2, FAR)
    up(4)
    up(5)
    corner(2, NEARFAR)
    complete(2)

    h = jnp.dot(act[...], wd[...], preferred_element_type=F32) + rows[3] + (n1[...] * rows[4] + rows[5])
    h = h - mean(h)
    r2 = lax.rsqrt(mean(h * h) + EPS)
    n2 = h * r2
    result[...] = (n2 * rows[6] + rows[7]).astype(BF16).reshape(2, 128, 768)
    eye = lax.broadcasted_iota(jnp.int32, (128, 128), 0) == lax.broadcasted_iota(jnp.int32, (128, 128), 1)
    keepers = [
        jnp.sum(jnp.where(eye, mask[i : i + 1].astype(F32), 0.0), axis=-1, keepdims=True) for i in range(2)
    ]
    gr = whole(grad).astype(F32) * jnp.concatenate(keepers, axis=0)
    sums = sc["sums"]
    sums[6] = total(gr * n2)
    sums[7] = total(gr)
    e = gr * rows[6]
    d = r2 * (e - mean(e) - n2 * mean(e * n2))
    dh2[...] = d
    dz = sc["dz"]
    dz[...] = d.astype(BF16)
    sums[3] = total(dz[...].astype(F32))

    gd, gu, go, gq = (sc[k] for k in ("gd", "gu", "go", "gq"))

    def down_gradient(i):
        r = lax.dot_general(act[:, 384 * i : 384 * (i + 1)], dz[...], TN, preferred_element_type=F32)
        gd[i // 2, 2 * (i % 2) : 2 * (i % 2) + 2] = r.astype(BF16).reshape(2, 2, 96, 768)

    chunks = [
        (gd, od, 0, 48, 0, 768),
        (gd, od, 48, 48, 0, 768),
        (gu, ou, 0, 24, 0, 1536),
        (gu, ou, 0, 24, 1536, 1536),
        (go, oo, 0, 24, 0, 768),
    ]
    bufs = sc["bufs"]

    def cols(k, half):
        nc = chunks[k][5] // 2
        return pl.ds(half * nc, nc)

    def pair_start(k):
        v, out, q0, nr, k0, nc = chunks[k]
        w.put(v.at[:, :, 1 - c, pl.ds(q0, nr), pl.ds(k0, nc)], bufs[k][0], p.core, (50, k))

    def pair_add(k):
        v, out, q0, nr, k0, nc = chunks[k]
        rc, rdx, rdy, rx, ry, rz = bufs[k]
        w.got(rc, (50, k))

        def add(ss):
            def one(i):
                rc[ss, i] = rc[ss, i] + v[ss, i, c, q0 : q0 + nr, k0 : k0 + nc]

            loop(4, one)

        add(p.sd)
        w.put(rc.at[p.sd, :, :, cols(k, 0)], rdx, p.x, (51, k))
        w.put(rc.at[p.sd, :, :, cols(k, 1)], rdy, p.y, (52, k))
        add(p.sx)
        w.put(rc.at[p.sx, :, :, cols(k, 0)], rx.at[:, :, cols(k, 0)], p.x, (53, k))
        add(p.sy)
        w.put(rc.at[p.sy, :, :, cols(k, 1)], ry.at[:, :, cols(k, 1)], p.y, (54, k))
        add(s)

    def diagonal(k):
        rc, rdx, rdy, rx, ry, rz = bufs[k]
        w.got(rdx, (51, k))
        rc[p.sy, :, :, cols(k, 0)] = rc[p.sy, :, :, cols(k, 0)] + rdx[...]
        w.put(rc.at[p.sy, :, :, cols(k, 0)], ry.at[:, :, cols(k, 0)], p.y, (55, k))
        w.got(rdy, (52, k))
        rc[p.sx, :, :, cols(k, 1)] = rc[p.sx, :, :, cols(k, 1)] + rdy[...]
        w.put(rc.at[p.sx, :, :, cols(k, 1)], rx.at[:, :, cols(k, 1)], p.x, (56, k))

    def plane(k):
        rc, rdx, rdy, rx, ry, rz = bufs[k]
        w.got(rx.at[:, :, cols(k, 0)], (53, k))
        w.got(rx.at[:, :, cols(k, 1)], (56, k))
        w.got(ry.at[:, :, cols(k, 1)], (54, k))
        w.got(ry.at[:, :, cols(k, 0)], (55, k))

        def one(i):
            rc[s, i] = (rc[s, i].astype(F32) + rx[i].astype(F32) + ry[i].astype(F32)).astype(BF16)

        loop(4, one)
        w.put(rc.at[s, p.znf], rz.at[0], p.n, (57, k))
        w.put(rc.at[s, p.zn], rz.at[1], p.n, (58, k))

    def last(k):
        rc, rdx, rdy, rx, ry, rz = bufs[k]
        w.got(rz.at[0], (57, k))
        rc[s, p.zf] = rc[s, p.zf] + rz[0]
        w.put(rc.at[s, p.zf], rz.at[2], p.f, (59, k))

    def final(k):
        v, out, q0, nr, k0, nc = chunks[k]
        rc, rdx, rdy, rx, ry, rz = bufs[k]
        w.got(rz.at[1], (58, k))
        w.got(rz.at[2], (59, k))
        out[q0 : q0 + nr, k0 : k0 + nc] = rc[s, z].astype(F32) + rz[1].astype(F32) + rz[2].astype(F32)

    for i in range(8):
        down_gradient(i)
    pair_start(0)
    pair_start(1)

    def inner_gradient(j):
        cc = slice(512 * j, 512 * (j + 1))
        r = lax.dot_general(dz[...], wd[512 * j : 512 * (j + 1), :], NT, preferred_element_type=F32)
        r = (r * slope[:, cc]).astype(BF16)
        dinner[:, cc] = r
        sc["sup"][:, cc] = total(r.astype(F32))

    for j in range(3):
        inner_gradient(j)
    pair_add(0)
    for j in range(3, 6):
        inner_gradient(j)
    pair_add(1)
    diagonal(0)
    d = dh2[...]
    for j in range(6):
        wt = joined(wou[:, :, 768 + 512 * j : 768 + 512 * (j + 1)])
        d = d + lax.dot_general(dinner[:, 512 * j : 512 * (j + 1)], wt, NT, preferred_element_type=F32)
    sums[4] = total(d * n1[...])
    sums[5] = total(d)
    e = d * rows[4]
    d = r1 * (e - mean(e) - n1[...] * mean(e * n1[...]))
    dh1 = dh2
    dh1[...] = d
    dbr = sc["dbr"]
    dbr[...] = d.astype(BF16)
    sums[2] = total(dbr[...].astype(F32))
    datt = sc["datt"]
    r = lax.dot_general(dbr[...], joined(wou[:, :, 0:768]), NT, preferred_element_type=F32)
    datt[...] = r.astype(BF16).reshape(2, 128, 768)

    back = w.block(16)
    here = []
    for zz in (p.zf, p.znf, p.zn, z):
        gg, zq = zz // 2, zz % 2
        for tl, cc in ((0, 1 - c), (0, c), (1, c)):
            src = datt.at[gg, :, pl.ds(pl.multiple_of(384 * zq + (256 if tl else 128 * cc), 128), 128)]
            if zz is z and cc is c:
                here.append(w.move(src, dap.at[tl, b]))
            else:
                w.put(src, dap.at[tl, b], (s, zz * 2 + cc), None, back + 8 * tl + b)

    def up_gradient(j):
        r = lax.dot_general(nlow[...], dinner[:, 512 * j : 512 * (j + 1)], TN, preferred_element_type=F32)
        gu[:, :, :, :, 512 * j : 512 * (j + 1)] = r.reshape(4, 4, 2, 24, 512).astype(BF16)

    for j in range(3):
        up_gradient(j)
    pair_start(2)
    diagonal(1)
    for j in range(3, 6):
        up_gradient(j)
    pair_start(3)
    pair_add(2)
    r = lax.dot_general(whole(att), dbr[...], TN, preferred_element_type=F32)
    go[...] = r.reshape(4, 4, 2, 24, 768).astype(BF16)
    pair_start(4)
    plane(0)

    for tl in range(2):
        for zz in (p.zf, p.znf, p.zn, z):
            for cc in (1 - c, c):
                if (tl == 1 and cc is not c) or (zz is z and cc is c):
                    continue
                w.got(dap.at[tl, zz * 2 + cc], None, back + 8 * tl + zz * 2 + cc)
    for cp in here:
        cp.wait()

    def queries(tl, blk):
        q, da = qkv[0, tl, blk], dap[tl, blk]
        outs = []
        for e in range(2):
            m = m_smem[blk, g, head(tl, e), 0]
            k, v = qkv[1, tl, m], qkv[2, tl, m]
            pr = weights(e, q, k)
            dp = lax.dot_general(mask_head(e, da), v, NT, preferred_element_type=F32)
            ds = (pr * (dp - jnp.sum(pr * dp, axis=-1, keepdims=True))).astype(BF16)
            ds_buf[tl, e, blk] = ds
            p_buf[tl, e, blk] = pr.astype(BF16)
            outs.append(jnp.dot(ds, k, preferred_element_type=F32) * 0.125)
        dqkv[0, tl, blk] = jnp.where(left, outs[0], outs[1]).astype(BF16)

    def keys(tl, n):
        dk, dv = [], []
        for e in range(2):
            cq = 0
            for i in range(8):
                cq = jnp.where(m_smem[i, g, head(tl, e), 0] == n, i, cq)
            ds, pr = ds_buf[tl, e, cq], p_buf[tl, e, cq]
            dk.append(lax.dot_general(ds, qkv[0, tl, cq], TN, preferred_element_type=F32) * 0.125)
            dv.append(lax.dot_general(pr, dap[tl, cq], TN, preferred_element_type=F32))
        dqkv[1, tl, n] = jnp.where(left, dk[0], dk[1]).astype(BF16)
        dqkv[2, tl, n] = jnp.where(left, dv[0], dv[1]).astype(BF16)

    loop(8, lambda i: queries(0, i))
    diagonal(2)
    pair_add(3)
    plane(1)
    loop(4, lambda i: queries(1, 2 * i + c))
    last(0)
    loop(8, lambda i: keys(0, i))
    pair_add(4)
    diagonal(3)
    loop(8, lambda i: keys(1, i))
    last(1)
    plane(2)

    dtk, rtk, rtn, rtf = (sc[k] for k in ("dtk", "rtk", "rtn", "rtf"))

    def flat(t, m):
        return jnp.concatenate([dqkv[t, tl, 4 * m : 4 * m + 4].reshape(512, 128) for tl in range(2)], axis=1)

    for m in range(2):
        r = 0.0
        for t in range(3):
            r = r + lax.dot_general(flat(t, m), head_columns(t), NT, preferred_element_type=F32)
        dtk[2 * m : 2 * m + 2] = r.astype(BF16).reshape(2, 2, 128, 768)
    w.put(dtk.at[:, 1 - c], rtk, p.core, 60)

    rq, accq, rqdx, rqdy, rqx, rqy, rqz = (sc[k] for k in ("rq", "accq", "rqdx", "rqdy", "rqx", "rqy", "rqz"))
    for t in range(3):
        r = 0.0
        for m in range(2):
            x = xg[4 * m : 4 * m + 4].reshape(512, 768)
            r = r + lax.dot_general(x, flat(t, m), TN, preferred_element_type=F32)
        gq[t] = r.reshape(4, 4, 2, 24, 256).astype(BF16)
    w.put(gq.at[:, :, :, 1 - c], rq, p.core, 61)

    diagonal(4)
    w.got(rtk, 60)
    loop(4, lambda i: rtk.__setitem__(i, rtk[i] + dtk[i, c]))
    w.put(rtk.at[p.znf], rtn.at[0], p.n, 62)
    w.put(rtk.at[p.zn], rtn.at[1], p.n, 63)

    w.got(rq, 61)
    o0 = pl.multiple_of(128 * (1 - c), 128)

    def pair_q(i):
        for t in range(3):
            for zz in range(4):
                accq[t, i, zz, :, pl.ds(c0, 128)] = gq[t, i, zz, c, :, 0:128]
                accq[t, i, zz, :, pl.ds(o0, 128)] = rq[t, i, zz, :, 0:128]
                accq[t, i, zz, :, 256:384] = gq[t, i, zz, c, :, 128:256] + rq[t, i, zz, :, 128:256]

    loop(4, pair_q)
    w.put(accq.at[:, p.sd, :, :, pl.ds(0, 256)], rqdx, p.x, 64)
    w.put(accq.at[:, p.sd, :, :, pl.ds(256, 128)], rqdy, p.y, 65)
    plane(3)
    last(2)
    final(0)

    sums[0] = jnp.zeros((1, 768), F32)
    sums[1] = jnp.zeros((1, 768), F32)
    for r, t in ((0, 0), (1, 2)):
        f = [total(dqkv[t, tl].reshape(1024, 128).astype(F32)) for tl in range(2)]
        sums[r, :, pl.ds(b0, 128)] = f[0]
        sums[r, :, pl.ds(b1, 128)] = f[1]
    vl = lax.broadcasted_iota(jnp.int32, (128, 768), 1)
    spot = (vl - 24 * ((vl * 2731) >> 16) == lax.broadcasted_iota(jnp.int32, (128, 768), 0)).astype(F32)

    def fold(part, hit):
        return lax.dot_general(part, hit, NT, preferred_element_type=F32, precision=lax.Precision.HIGHEST)

    for r in range(8):
        vacc[:, r, :] = fold(jnp.where(mine_lane, sums[r], 0.0), spot)
    up_sum = 0.0
    for i in range(4):
        l3 = lax.broadcasted_iota(jnp.int32, (128, 768), 1) + 768 * i
        hit = (l3 - 96 * ((l3 * 43691) >> 22) == lax.broadcasted_iota(jnp.int32, (128, 768), 0)).astype(F32)
        owner = ((lax.broadcasted_iota(jnp.int32, (32, 768), 1) + 768 * i) * 43691) >> 22
        at = owner == lax.broadcasted_iota(jnp.int32, (32, 768), 0)
        up_sum = up_sum + fold(jnp.where(at, sc["sup"][:, 768 * i : 768 * (i + 1)], 0.0), hit)
    vacc[:, 8, :] = up_sum
    rv0, rv1, rv2, rv3, rv4 = sc["rv"]
    ya = s // 2
    w.put(vacc.at[pl.ds(16 * (1 - ya), 16)], rv0, p.y, 70)

    w.got(rqdx, 64)
    accq[:, p.sy, :, :, 0:256] = accq[:, p.sy, :, :, 0:256] + rqdx[...]
    w.put(accq.at[:, p.sy], rqy, p.y, 66)
    w.got(rqdy, 65)
    accq[:, p.sx, :, :, 256:384] = accq[:, p.sx, :, :, 256:384] + rqdy[...]
    w.put(accq.at[:, p.sx], rqx, p.x, 67)

    w.got(rtn.at[0], 62)
    rtk[p.zf] = rtk[p.zf] + rtn[0]
    w.put(rtk.at[p.zf], rtf, p.f, 68)
    final(1)
    last(3)
    plane(4)
    w.got(rv0, 70)
    vacc[pl.ds(16 * ya, 16)] = vacc[pl.ds(16 * ya, 16)] + rv0[...]
    w.put(vacc.at[pl.ds(8 * p.sx, 8)], rv1, p.x, 71)
    final(2)
    last(4)
    w.got(rv1, 71)
    vacc[pl.ds(8 * s, 8)] = vacc[pl.ds(8 * s, 8)] + rv1[...]
    w.put(vacc.at[pl.ds(8 * s + 4 * (1 - g), 4)], rv2, p.f, 72)

    w.got(rqx, 67)
    w.got(rqy, 66)
    for t in range(3):
        accq[t, s] = (accq[t, s].astype(F32) + rqx[t].astype(F32) + rqy[t].astype(F32)).astype(BF16)
    w.put(accq.at[:, s, p.znf], rqz.at[0], p.f, 80)
    w.put(accq.at[:, s, p.zf], rqz.at[1], p.f, 81)
    w.got(rv2, 72)
    vacc[pl.ds(8 * s + 4 * g, 4)] = vacc[pl.ds(8 * s + 4 * g, 4)] + rv2[...]
    w.put(vacc.at[pl.ds(8 * s + 2 * p.zn, 2)], rv3, p.n, 73)
    w.got(rqz.at[0], 80)
    accq[:, s, p.zn] = accq[:, s, p.zn] + rqz[0]
    w.put(accq.at[:, s, p.zn], rqz.at[2], p.n, 82)
    final(3)
    w.got(rv3, 73)
    vacc[pl.ds(8 * s + 2 * z, 2)] = vacc[pl.ds(8 * s + 2 * z, 2)] + rv3[...]
    w.put(vacc.at[8 * s + p.bc], rv4, p.core, 74)
    w.got(rtn.at[1], 63)
    w.got(rtf, 68)
    d = dh1[...].reshape(2, 128, 768)
    dtok[...] = d
    dtok[g] = dtok[g] + rtk[z].astype(F32) + rtn[1].astype(F32)
    dtok[1 - g] = dtok[1 - g] + rtf[...].astype(F32)
    final(4)
    w.got(rv4, 74)
    ovec[...] = vacc[8 * s + b] + rv4[...]
    w.got(rqz.at[1], 81)
    w.got(rqz.at[2], 82)
    q0 = pl.multiple_of(384 * zp, 128)
    q1 = pl.multiple_of(384 * (1 - zp), 128)
    for t in range(3):
        oqkv[t, :, pl.ds(q0, 384)] = accq[t, s, z].astype(F32) + rqz[1, t].astype(F32)
        oqkv[t, :, pl.ds(q1, 384)] = rqz[2, t].astype(F32)
    w.finish()


def scratch():
    VM = pltpu.VMEM
    per_chunk = []
    for nr, nc in ((48, 768), (48, 768), (24, 1536), (24, 1536), (24, 768)):
        per_chunk.append((
            VM((4, 4, nr, nc), BF16), VM((4, nr, nc // 2), BF16), VM((4, nr, nc // 2), BF16),
            VM((4, nr, nc), BF16), VM((4, nr, nc), BF16), VM((3, nr, nc), BF16),
        ))
    return dict(
        wou=VM((32, 24, 3840), BF16), wd=VM((3072, 768), BF16), wqkv=VM((3, 32, 24, 384), BF16),
        xg=VM((8, 128, 768), BF16), qkv=VM((3, 2, 8, 128, 128), BF16), att=VM((2, 128, 768), BF16),
        vecs=VM((32, 8, 384), BF16), match=VM((8, 2, 16, 128), jnp.int32), ms=pltpu.SMEM((8, 2, 16, 128), jnp.int32),
        stage=VM((2, 3, 24, 384), BF16), sou=VM((24, 3840), BF16), rows=VM((8, 1, 768), F32), bup=VM((1, 3072), F32),
        tok=VM((2, 128, 768), BF16), grad=VM((2, 128, 768), BF16), vo=VM((8, 384), BF16), mo=VM((2, 16, 128), jnp.int32),
        ab=VM((12, 128, 128), BF16), dap=VM((2, 8, 128, 128), BF16), ds=VM((2, 2, 8, 128, 128), BF16),
        p=VM((2, 2, 8, 128, 128), BF16), dqkv=VM((3, 2, 8, 128, 128), BF16), vacc=VM((32, 16, 128), F32),
        n1=VM((256, 768), F32), nlow=VM((256, 768), BF16), act=VM((256, 3072), BF16), slope=VM((256, 3072), F32),
        dh2=VM((256, 768), F32), din=VM((256, 3072), BF16), sums=VM((8, 1, 768), F32), sup=VM((1, 3072), F32),
        dz=VM((256, 768), BF16), dbr=VM((256, 768), BF16), datt=VM((2, 128, 768), BF16),
        gd=VM((4, 4, 2, 96, 768), BF16), gu=VM((4, 4, 2, 24, 3072), BF16), go=VM((4, 4, 2, 24, 768), BF16),
        gq=VM((3, 4, 4, 2, 24, 256), BF16), rq=VM((3, 4, 4, 24, 256), BF16), accq=VM((3, 4, 4, 24, 384), BF16),
        dtk=VM((4, 2, 128, 768), BF16), rtk=VM((4, 128, 768), BF16), rtn=VM((2, 128, 768), BF16), rtf=VM((128, 768), BF16),
        rv=tuple(VM((n, 16, 128) if n > 1 else (16, 128), F32) for n in (16, 8, 4, 2, 1)),
        rqdx=VM((3, 4, 24, 256), BF16), rqdy=VM((3, 4, 24, 128), BF16), rqx=VM((3, 4, 24, 384), BF16),
        rqy=VM((3, 4, 24, 384), BF16), rqz=VM((3, 3, 24, 384), BF16), bufs=tuple(per_chunk),
    )


def hand_out(result, od, ou, oo, oqkv, dtok, ovec, *rest):
    outs, sem = rest[:17], rest[17]
    pairs = [(result, outs[0]), (dtok, outs[1]), (oqkv.at[0], outs[2]), (oqkv.at[1], outs[3]), (oqkv.at[2], outs[4])]
    pairs += [(oo, outs[5]), (ou, outs[6]), (od, outs[7])]
    copies = [pltpu.make_async_copy(a, o, sem.at[i]) for i, (a, o) in enumerate(pairs)]
    for cp in copies:
        cp.start()
    for row, out in zip((0, 1, 2, 8, 3, 4, 5, 6, 7), outs[8:], strict=True):
        out[...] = ovec[row, 0 : out.shape[0]]
    for cp in copies:
        cp.wait()


def column(
    tokens, grad_out, masked, token_order, cluster_match,
    w_query, w_key, w_value, w_out, w_up, w_down,
    b_query, b_value, b_out, b_up, b_down,
    gain_attn, shift_attn, gain_ffn, shift_ffn,
):
    V = pl.BlockSpec(memory_space=pltpu.VMEM)
    A = pl.BlockSpec(memory_space=pl.ANY)
    S = jax.ShapeDtypeStruct
    vectors = (b_query, b_value, b_out, b_down, gain_attn, shift_attn, gain_ffn, shift_ffn, b_up)
    got = pl.pallas_call(
        layer_kernel,
        out_shape=(
            S((2, 128, 768), BF16), S((96, 768), F32), S((24, 3072), F32), S((24, 768), F32), S((3, 24, 768), F32),
            S((2, 128, 768), F32), S((16, 128), F32),
        ),
        in_specs=[A, A, V, V] + [A] * 6 + [V] * 9,
        out_specs=(V,) * 7,
        scratch_shapes=[scratch(), *(pltpu.SemaphoreType.DMA((n,)) for n in (207, 215, 21))],
        compiler_params=pltpu.CompilerParams(collective_id=0, has_side_effects=True, vmem_limit_bytes=62 << 20),
        name="layer",
    )(tokens, grad_out, masked, cluster_match, w_query, w_key, w_value, w_out, w_up, w_down, *vectors)
    square = S((24, 768), F32)
    outs = (S((2, 128, 768), BF16), S((2, 128, 768), F32)) + (square,) * 4 + (S((24, 3072), F32), S((96, 768), F32))
    outs += tuple(S((n,), F32) for n in (24, 24, 24, 96, 24, 24, 24, 24, 24))
    return pl.pallas_call(
        hand_out,
        out_shape=outs,
        in_specs=[V] * 7,
        out_specs=(A,) * 8 + (V,) * 9,
        scratch_shapes=[pltpu.SemaphoreType.DMA((8,))],
        name="results",
    )(*got)


def solution(mesh):
    fits = mesh.shape[SEQ] == 4 and mesh.shape[BLK] == 8
    return jax.shard_map(
        column if fits else general,
        mesh=mesh,
        in_specs=(
            P(SEQ, BLK, None),
            P(SEQ, BLK, None),
            P(SEQ, BLK),
            P(SEQ, None, BLK),
            P(SEQ, None, BLK),
            P(BOTH, None),
            P(BOTH, None),
            P(BOTH, None),
            P(BOTH, None),
            P(BOTH, None),
            P(BOTH, None),
            P(BOTH),
            P(BOTH),
            P(BOTH),
            P(BOTH),
            P(BOTH),
            P(BOTH),
            P(BOTH),
            P(BOTH),
            P(BOTH),
        ),
        out_specs=(
            P(SEQ, BLK, None),
            P(SEQ, BLK, None),
            P(BOTH, None),
            P(BOTH, None),
            P(BOTH, None),
            P(BOTH, None),
            P(BOTH, None),
            P(BOTH, None),
            P(BOTH),
            P(BOTH),
            P(BOTH),
            P(BOTH),
            P(BOTH),
            P(BOTH),
            P(BOTH),
            P(BOTH),
            P(BOTH),
        ),
        check_vma=False,
    )
```

```python
import functools
import math

import jax
import jax.numpy as jnp
from jax import lax
from jax.experimental import pallas as pl
from jax.experimental.pallas import tpu as pltpu
from jax.sharding import PartitionSpec as P

HEADS = 12
CL = 128
EPS = 1e-05
MESH = pl.DeviceIdType.MESH
SEQ, BLK = BOTH = ("seq", "blk")
F32 = jnp.float32
BF16 = jnp.bfloat16


def norm_rows(hidden, gain_row, shift_row):
    row_mean = jnp.mean(hidden, axis=-1, keepdims=True)
    centered = hidden - row_mean
    variance = jnp.mean(centered * centered, axis=-1, keepdims=True)
    return centered * lax.rsqrt(variance + EPS) * gain_row + shift_row


def gelu_exact(inner_sum):
    return jax.nn.gelu(inner_sum, approximate=False)


def to_heads(flat_rows, groups, local_len):
    return flat_rows.reshape(groups, local_len, HEADS, -1).transpose(0, 2, 1, 3)


def from_heads(head_rows):
    groups, head_count, local_len, head_dim = head_rows.shape
    return head_rows.transpose(0, 2, 1, 3).reshape(groups * local_len, head_count * head_dim)


def reorder(head_rows, positions):
    return jnp.take_along_axis(head_rows, positions[..., None], axis=2)


def general(
    tokens,
    grad_out,
    masked,
    token_order,
    cluster_match,
    w_query,
    w_key,
    w_value,
    w_out,
    w_up,
    w_down,
    b_query,
    b_value,
    b_out,
    b_up,
    b_down,
    gain_attn,
    shift_attn,
    gain_ffn,
    shift_ffn,
):
    groups, local_len, width = tokens.shape
    row_count = groups * local_len
    head_dim = width // HEADS
    clusters = local_len // CL
    score_scale = 1.0 / math.sqrt(head_dim)
    gathered = (
        lax.all_gather(w_query, BOTH, axis=0, tiled=True),
        lax.all_gather(w_key, BOTH, axis=0, tiled=True),
        lax.all_gather(w_value, BOTH, axis=0, tiled=True),
        lax.all_gather(w_out, BOTH, axis=0, tiled=True),
        lax.all_gather(w_up, BOTH, axis=0, tiled=True),
        lax.all_gather(w_down, BOTH, axis=0, tiled=True),
        lax.all_gather(b_query, BOTH, axis=0, tiled=True),
        lax.all_gather(b_value, BOTH, axis=0, tiled=True),
        lax.all_gather(b_out, BOTH, axis=0, tiled=True),
        lax.all_gather(b_up, BOTH, axis=0, tiled=True),
        lax.all_gather(b_down, BOTH, axis=0, tiled=True),
        lax.all_gather(gain_attn, BOTH, axis=0, tiled=True),
        lax.all_gather(shift_attn, BOTH, axis=0, tiled=True),
        lax.all_gather(gain_ffn, BOTH, axis=0, tiled=True),
        lax.all_gather(shift_ffn, BOTH, axis=0, tiled=True),
    )
    (
        full_query,
        full_key,
        full_value,
        full_out,
        full_up,
        full_down,
        bias_query,
        bias_value,
        bias_out,
        bias_up,
        bias_down,
        norm_gain1,
        norm_shift1,
        norm_gain2,
        norm_shift2,
    ) = gathered
    flat_tokens = tokens.reshape(row_count, width)
    inverse = jnp.argsort(token_order, axis=-1)
    cluster_shape = (groups, HEADS, clusters, CL, head_dim)
    query_low = (
        jnp.dot(flat_tokens, full_query, preferred_element_type=jnp.float32)
        + bias_query.astype(jnp.float32)
    ).astype(jnp.bfloat16)
    key_low = jnp.dot(flat_tokens, full_key, preferred_element_type=jnp.float32).astype(
        jnp.bfloat16
    )
    value_low = (
        jnp.dot(flat_tokens, full_value, preferred_element_type=jnp.float32)
        + bias_value.astype(jnp.float32)
    ).astype(jnp.bfloat16)
    query_perm = reorder(to_heads(query_low, groups, local_len), token_order).reshape(cluster_shape)
    key_perm = reorder(to_heads(key_low, groups, local_len), token_order).reshape(cluster_shape)
    value_perm = reorder(to_heads(value_low, groups, local_len), token_order).reshape(cluster_shape)
    empty_sel = jnp.zeros(cluster_shape, jnp.bfloat16)
    key_piece = lax.all_gather(key_perm, BLK, axis=2, tiled=True)
    value_piece = lax.all_gather(value_perm, BLK, axis=2, tiled=True)
    piece_len = key_piece.shape[2]
    offset = cluster_match
    select = (offset[..., None] == jnp.arange(piece_len, dtype=jnp.int32)).astype(jnp.bfloat16)
    inside = ((offset >= 0) & (offset < piece_len))[..., None, None]
    new_keys = jnp.einsum(
        "ghcj,ghjkd->ghckd", select, key_piece, preferred_element_type=jnp.float32
    ).astype(jnp.bfloat16)
    new_values = jnp.einsum(
        "ghcj,ghjkd->ghckd", select, value_piece, preferred_element_type=jnp.float32
    ).astype(jnp.bfloat16)
    key_sel = jnp.where(inside, new_keys, empty_sel)
    value_sel = jnp.where(inside, new_values, empty_sel)
    scores = (
        jnp.einsum("ghcqd,ghckd->ghcqk", query_perm, key_sel, preferred_element_type=jnp.float32)
        * score_scale
    )
    row_max = jnp.max(scores, axis=-1, keepdims=True)
    log_total = row_max + jnp.log(jnp.sum(jnp.exp(scores - row_max), axis=-1, keepdims=True))
    attn_probs = jnp.exp(scores - log_total)
    probs_low = attn_probs.astype(jnp.bfloat16)
    mixed_perm = jnp.einsum(
        "ghcqk,ghckd->ghcqd", probs_low, value_sel, preferred_element_type=jnp.float32
    ).reshape(groups, HEADS, local_len, head_dim)
    attended = from_heads(reorder(mixed_perm, inverse)).astype(jnp.bfloat16)
    branch = jnp.dot(attended, full_out, preferred_element_type=jnp.float32) + bias_out.astype(
        jnp.float32
    )
    resid = flat_tokens.astype(jnp.float32) + branch
    normed, pull_first = jax.vjp(
        norm_rows, resid, norm_gain1.astype(jnp.float32), norm_shift1.astype(jnp.float32)
    )
    normed_low = normed.astype(jnp.bfloat16)
    inner_sum = jnp.dot(normed_low, full_up, preferred_element_type=jnp.float32) + bias_up.astype(
        jnp.float32
    )
    active, pull_gelu = jax.vjp(gelu_exact, inner_sum)
    active_low = active.astype(jnp.bfloat16)
    outer_sum = jnp.dot(
        active_low, full_down, preferred_element_type=jnp.float32
    ) + bias_down.astype(jnp.float32)
    final_rows, pull_second = jax.vjp(
        norm_rows,
        normed + outer_sum,
        norm_gain2.astype(jnp.float32),
        norm_shift2.astype(jnp.float32),
    )
    result = final_rows.astype(jnp.bfloat16).reshape(groups, local_len, width)
    back_weights = (
        lax.all_gather(w_query, BOTH, axis=0, tiled=True),
        lax.all_gather(w_key, BOTH, axis=0, tiled=True),
        lax.all_gather(w_value, BOTH, axis=0, tiled=True),
        lax.all_gather(w_out, BOTH, axis=0, tiled=True),
        lax.all_gather(w_up, BOTH, axis=0, tiled=True),
        lax.all_gather(w_down, BOTH, axis=0, tiled=True),
        lax.all_gather(b_query, BOTH, axis=0, tiled=True),
        lax.all_gather(b_value, BOTH, axis=0, tiled=True),
        lax.all_gather(b_out, BOTH, axis=0, tiled=True),
        lax.all_gather(b_up, BOTH, axis=0, tiled=True),
        lax.all_gather(b_down, BOTH, axis=0, tiled=True),
        lax.all_gather(gain_attn, BOTH, axis=0, tiled=True),
        lax.all_gather(shift_attn, BOTH, axis=0, tiled=True),
        lax.all_gather(gain_ffn, BOTH, axis=0, tiled=True),
        lax.all_gather(shift_ffn, BOTH, axis=0, tiled=True),
    )
    back_query, back_key, back_value, back_out, back_up, back_down = back_weights[:6]
    upstream = grad_out.reshape(row_count, width).astype(jnp.float32) * masked.reshape(
        row_count, 1
    ).astype(jnp.float32)
    d_sum2, d_gain2, d_shift2 = pull_second(upstream)
    d_outer = d_sum2.astype(jnp.bfloat16)
    g_down = jnp.einsum("rf,rd->fd", active_low, d_outer, preferred_element_type=jnp.float32)
    g_bdown = jnp.sum(d_outer.astype(jnp.float32), axis=0)
    d_active = jnp.einsum("rd,fd->rf", d_outer, back_down, preferred_element_type=jnp.float32)
    d_inner = pull_gelu(d_active)[0].astype(jnp.bfloat16)
    g_up = jnp.einsum("rd,rf->df", normed_low, d_inner, preferred_element_type=jnp.float32)
    g_bup = jnp.sum(d_inner.astype(jnp.float32), axis=0)
    d_normed = d_sum2 + jnp.einsum(
        "rf,df->rd", d_inner, back_up, preferred_element_type=jnp.float32
    )
    d_resid, d_gain1, d_shift1 = pull_first(d_normed)
    d_branch = d_resid.astype(jnp.bfloat16)
    g_out = jnp.einsum("ri,rd->id", attended, d_branch, preferred_element_type=jnp.float32)
    g_bout = jnp.sum(d_branch.astype(jnp.float32), axis=0)
    d_attended = jnp.einsum(
        "rd,id->ri", d_branch, back_out, preferred_element_type=jnp.float32
    ).astype(jnp.bfloat16)
    d_mixed = reorder(to_heads(d_attended, groups, local_len), token_order).reshape(cluster_shape)
    scores_again = (
        jnp.einsum("ghcqd,ghckd->ghcqk", query_perm, key_sel, preferred_element_type=jnp.float32)
        * score_scale
    )
    probs_again = jnp.exp(scores_again - log_total)
    probs_again_low = probs_again.astype(jnp.bfloat16)
    d_probs = jnp.einsum(
        "ghcqd,ghckd->ghcqk", d_mixed, value_sel, preferred_element_type=jnp.float32
    )
    d_scores = (
        probs_again * (d_probs - jnp.sum(probs_again * d_probs, axis=-1, keepdims=True))
    ).astype(jnp.bfloat16)
    d_query_perm = (
        jnp.einsum("ghcqk,ghckd->ghcqd", d_scores, key_sel, preferred_element_type=jnp.float32)
        * score_scale
    )
    d_key_sel = (
        jnp.einsum("ghcqk,ghcqd->ghckd", d_scores, query_perm, preferred_element_type=jnp.float32)
        * score_scale
    )
    d_value_sel = jnp.einsum(
        "ghcqk,ghcqd->ghckd", probs_again_low, d_mixed, preferred_element_type=jnp.float32
    )
    sent = jnp.concatenate([d_key_sel, d_value_sel], axis=-1)
    my_start = lax.axis_index(BLK) * clusters
    piece_grads = lax.all_gather(sent.astype(jnp.bfloat16), BLK, axis=2, tiled=True).astype(
        jnp.float32
    )
    piece_match = lax.all_gather(
        cluster_match.astype(jnp.float32).astype(jnp.bfloat16), BLK, axis=2, tiled=True
    ).astype(jnp.float32)
    offset = piece_match.astype(jnp.int32) - my_start
    select = (offset[..., None] == jnp.arange(clusters, dtype=jnp.int32)).astype(jnp.float32)
    owned = jnp.zeros(sent.shape, jnp.float32) + jnp.einsum(
        "ghjc,ghjke->ghcke", select, piece_grads, precision=lax.Precision.HIGHEST
    )
    back_kv = reorder(owned.reshape(groups, HEADS, local_len, 2 * head_dim), inverse)
    d_key = from_heads(back_kv[..., :head_dim]).astype(jnp.bfloat16)
    d_value = from_heads(back_kv[..., head_dim:]).astype(jnp.bfloat16)
    d_query = from_heads(
        reorder(d_query_perm.reshape(groups, HEADS, local_len, head_dim), inverse)
    ).astype(jnp.bfloat16)
    g_query = jnp.einsum("ri,rd->id", flat_tokens, d_query, preferred_element_type=jnp.float32)
    g_key = jnp.einsum("ri,rd->id", flat_tokens, d_key, preferred_element_type=jnp.float32)
    g_value = jnp.einsum("ri,rd->id", flat_tokens, d_value, preferred_element_type=jnp.float32)
    g_bquery = jnp.sum(d_query.astype(jnp.float32), axis=0)
    g_bvalue = jnp.sum(d_value.astype(jnp.float32), axis=0)
    d_tokens_flat = (
        d_resid
        + jnp.einsum("rd,id->ri", d_query, back_query, preferred_element_type=jnp.float32)
        + jnp.einsum("rd,id->ri", d_key, back_key, preferred_element_type=jnp.float32)
        + jnp.einsum("rd,id->ri", d_value, back_value, preferred_element_type=jnp.float32)
    )
    summed = (
        lax.psum_scatter(g_query, BOTH, scatter_dimension=0, tiled=True),
        lax.psum_scatter(g_key, BOTH, scatter_dimension=0, tiled=True),
        lax.psum_scatter(g_value, BOTH, scatter_dimension=0, tiled=True),
        lax.psum_scatter(g_out, BOTH, scatter_dimension=0, tiled=True),
        lax.psum_scatter(g_up, BOTH, scatter_dimension=0, tiled=True),
        lax.psum_scatter(g_down, BOTH, scatter_dimension=0, tiled=True),
        lax.psum_scatter(g_bquery, BOTH, scatter_dimension=0, tiled=True),
        lax.psum_scatter(g_bvalue, BOTH, scatter_dimension=0, tiled=True),
        lax.psum_scatter(g_bout, BOTH, scatter_dimension=0, tiled=True),
        lax.psum_scatter(g_bup, BOTH, scatter_dimension=0, tiled=True),
        lax.psum_scatter(g_bdown, BOTH, scatter_dimension=0, tiled=True),
        lax.psum_scatter(d_gain1, BOTH, scatter_dimension=0, tiled=True),
        lax.psum_scatter(d_shift1, BOTH, scatter_dimension=0, tiled=True),
        lax.psum_scatter(d_gain2, BOTH, scatter_dimension=0, tiled=True),
        lax.psum_scatter(d_shift2, BOTH, scatter_dimension=0, tiled=True),
    )
    return (result, d_tokens_flat.reshape(groups, local_len, width)) + tuple(summed)


OWN, NEAR, FAR, NEARFAR = range(4)
NT = (((1,), (1,)), ((), ()))
TN = (((0,), (0,)), ((), ()))


class Place:
    def __init__(self):
        s, b = lax.axis_index(SEQ), lax.axis_index(BLK)
        self.s, self.b = s, b
        z, c = b // 2, b % 2
        self.z, self.c = z, c
        self.zlo, self.zhi = z % 2, z // 2
        self.sx = s + 1 - 2 * (s % 2)
        self.sy = s + 2 - 4 * (s // 2)
        self.sd = self.sy + 1 - 2 * (s % 2)
        self.zn = z + 1 - 2 * self.zlo
        self.zf = z + 2 - 4 * self.zhi
        self.znf = self.zf + 1 - 2 * self.zlo
        self.bc = b + 1 - 2 * c
        self.bn, self.bf, self.bnf = self.zn * 2 + c, self.zf * 2 + c, self.znf * 2 + c
        self.core = (s, self.bc)
        self.n = (s, self.bn)
        self.f = (s, self.bf)
        self.nf = (s, self.bnf)
        self.x = (self.sx, b)
        self.y = (self.sy, b)


class Wire:
    def __init__(self, send, recv, local):
        self.send, self.recv, self.local = send, recv, local
        self.n_send = self.n_local = self.n_recv = 0
        self.sent, self.slots, self.lots = [], {}, {}

    def slot(self, key):
        if key not in self.slots:
            self.slots[key] = self.n_recv
            self.n_recv += 1
        return self.slots[key]

    def put(self, src, dst, to, key, lot=None):
        at = self.slot(key)
        if lot is None or lot not in self.lots:
            index = self.n_send
            self.n_send += 1
            if lot is not None:
                self.lots[lot] = index
        else:
            index = self.lots[lot]
        cp = pltpu.make_async_remote_copy(
            src, dst, self.send.at[index], self.recv.at[at], device_id=to, device_id_type=MESH
        )
        cp.start()
        if lot is None:
            self.sent.append(cp)

    def got(self, dst, key):
        at = self.slot(key)
        pltpu.make_async_copy(dst, dst, self.recv.at[at]).wait()

    def move(self, src, dst):
        cp = pltpu.make_async_copy(src, dst, self.local.at[self.n_local])
        self.n_local += 1
        cp.start()
        return cp

    def finish(self, sizes):
        for lot, ref in sizes.items():
            pltpu.make_async_copy(ref, ref, self.send.at[self.lots[lot]]).wait()
        for cp in self.sent:
            cp.wait_send()


def greet(peers):
    bar = pltpu.get_barrier_semaphore()
    for to in peers:
        pl.semaphore_signal(bar, inc=1, device_id=to, device_id_type=MESH)
    pl.semaphore_wait(bar, len(peers))


def loop(n, body):
    def run(i, carry):
        body(i)
        return carry

    lax.fori_loop(0, n, run, 0)


def joined(v):
    return v.astype(F32).reshape(768, v.shape[-1]).astype(BF16)


def mean(v):
    return jnp.mean(v, axis=-1, keepdims=True)


def total(v):
    return jnp.sum(v, axis=0, keepdims=True)


def layer_kernel(
    tok_h, go_h, mask, cm, wq, wk, wv, wo_s, wu_s, wd_s,
    *others,
):
    vectors, (result, od, ou, oo, oqkv, dtok, ovec, sc, *sems) = others[:9], others[9:]
    p = Place()
    w = Wire(*sems)
    s, b, z, c = p.s, p.b, p.z, p.c
    zp, g = p.zlo, p.zhi
    zs = (z, p.zn, p.zf, p.znf)
    wou, wd, wqkv, xg, qkv, att = (sc[k] for k in ("wou", "wd", "wqkv", "xg", "qkv", "att"))
    match, m_smem, stage, stage_ou, rows, bup = (sc[k] for k in ("match", "ms", "stage", "sou", "rows", "bup"))

    raw = sc["raw"]
    early = [w.move(ref, raw.at[t]) for t, ref in enumerate((wq, wk, wv))]
    ou_in = [w.move(wo_s, stage_ou.at[:, pl.ds(0, 768)]), w.move(wu_s, stage_ou.at[:, pl.ds(768, 3072)])]
    tok, grad = sc["tok"], sc["grad"]
    tok_in, grad_in = w.move(tok_h, tok), w.move(go_h, grad)
    dap, ds_buf, p_buf, dqkv = (sc[k] for k in ("dap", "ds", "p", "dqkv"))
    left = lax.broadcasted_iota(jnp.int32, (128, 128), 1) < 64
    zero = jnp.zeros((128, 128), BF16)
    for i in range(4):
        other = 2 * i + 1 - c
        dap[1, other] = zero
        dqkv[0, 1, other] = zero
        for e in range(2):
            ds_buf[1, e, other] = zero
            p_buf[1, e, other] = zero
    vec_own, match_own = sc["vo"], sc["mo"]
    vec_own[...] = jnp.zeros_like(vec_own)
    for k, ref in enumerate(vectors):
        vec_own[0:1, 24 * k : 24 * k + ref.shape[0]] = ref[...].astype(F32).reshape(1, ref.shape[0])
    number = 12 * lax.broadcasted_iota(jnp.int32, (2, 12, 128), 0) + lax.broadcasted_iota(jnp.int32, (2, 12, 128), 1)
    spot = number == lax.broadcasted_iota(jnp.int32, (2, 12, 128), 2)
    line = jnp.where(spot, jnp.broadcast_to(cm[...], (2, 12, 128)), 0)
    match_own[...] = jnp.broadcast_to(jnp.sum(jnp.sum(line, axis=1), axis=0, keepdims=True), (8, 128))
    slot = s * 8 + b
    for cp in early:
        cp.wait()
    for h in range(2):
        parts = [raw[t, :, 384 * h : 384 * (h + 1)].astype(F32) for t in range(3)]
        stage[h] = jnp.concatenate(parts + [vec_own[...]], axis=0).astype(BF16)
    greet([p.core, p.n, p.f, p.nf, p.x, p.y, (s, p.zn * 2 + 1 - c), (s, p.zf * 2 + 1 - c), (s, p.znf * 2 + 1 - c)])

    def at_rows(n, ss, zz, cc):
        return pl.ds(pl.multiple_of(n * (ss * 8 + zz * 2 + cc), 8), n)

    def reg(k, ss, u, cc, half=None):
        zz = zs[u]
        if k == 0:
            cols = (pl.ds(0, 384), pl.ds(0, 256), pl.ds(256, 128))[0 if half is None else 1 + half]
            return wqkv.at[ss * 8 + zz * 2 + cc, :, cols]
        if k == 1:
            cols = pl.ds(0, 3840) if half is None else pl.ds(1920 * half, 1920)
            return wou.at[ss * 8 + zz * 2 + cc, :, cols]
        cols = pl.ds(0, 768) if half is None else pl.ds(384 * half, 384)
        return wd.at[at_rows(96, ss, zz, cc), cols]

    own_src = {1: stage_ou, 2: wd_s}

    def to_plane(k, u, src=None):
        r = reg(k, s, u, c)
        src = r if src is None else src
        w.put(src, r, p.x, (0, k, u), lot=k)
        w.put(src, r, p.y, (1, k, u), lot=k)

    def to_core(k, ss, u):
        r = reg(k, ss, u, c)
        w.put(r, r, p.core, (5, k), lot=k)

    def z_start(k):
        r = reg(k, s, OWN, c)
        w.put(own_src[k], r, p.n, (2, k), lot=k)
        w.put(own_src[k], r, p.f, (3, k), lot=k)

    def near(k):
        w.got(reg(k, s, NEAR, c), (2, k))
        to_plane(k, NEAR)
        to_core(k, s, NEAR)

    def far(k):
        r = reg(k, s, FAR, c)
        w.got(r, (3, k))
        w.put(r, r, p.n, (4, k), lot=k)
        to_plane(k, FAR)
        to_core(k, s, FAR)

    def nearfar(k):
        w.got(reg(k, s, NEARFAR, c), (4, k))
        to_plane(k, NEARFAR)
        to_core(k, s, NEARFAR)

    def turn(k, u):
        w.got(reg(k, p.sx, u, c), (0, k, u))
        r = reg(k, p.sx, u, c, 0)
        w.put(r, r, p.y, (6, k, u), lot=k)
        to_core(k, p.sx, u)
        w.got(reg(k, p.sy, u, c), (1, k, u))
        r = reg(k, p.sy, u, c, 1)
        w.put(r, r, p.x, (6, k, u), lot=k)
        to_core(k, p.sy, u)

    def corner(k, u):
        w.got(reg(k, p.sd, u, c), (6, k, u))
        to_core(k, p.sd, u)

    def complete(k):
        w.got((wqkv.at[pl.ds(0, 16)], wou.at[pl.ds(0, 16)], wd.at[pl.ds(0, 1536)])[k], (5, k))

    own = reg(0, s, OWN, c)
    for cp in ou_in:
        cp.wait()
    w.put(stage_ou, reg(1, s, OWN, c), p.n, (2, 1), lot=1)
    w.put(stage_ou, reg(1, s, OWN, c), p.f, (3, 1), lot=1)
    to_plane(1, OWN, stage_ou)
    w.put(stage.at[1 - zp], own, p.n, (2, 0), lot=0)
    w.put(stage.at[zp], own, p.f, (3, 0), lot=0)
    w.put(stage.at[1 - zp], own, p.nf, (4, 0), lot=0)
    w.put(stage.at[zp], own, p.x, (0, 0, OWN), lot=0)
    w.put(stage.at[zp], own, p.y, (1, 0, OWN), lot=0)
    w.put(tok_h.at[1 - g], xg.at[b], p.f, 21)
    w.put(tok_h.at[g], xg.at[b], p.n, 20)
    to_plane(2, OWN, wd_s)
    for zz in zs:
        for cc in (c, 1 - c):
            if not (zz is z and cc is c):
                w.put(match_own, match.at[b], (s, zz * 2 + cc), 92, lot=92)
    w.put(tok_h.at[g], xg.at[b], p.core, 23)
    mine = [
        w.move(stage_ou, reg(1, s, OWN, c)), w.move(stage.at[zp], own), w.move(match_own, match.at[b]),
        w.move(tok_h.at[g], xg.at[b]), w.move(wd_s, reg(2, s, OWN, c)),
    ]
    for cp in mine:
        cp.wait()
    for k in range(3):
        to_core(k, s, OWN)
    near(1)
    turn(1, OWN)
    far(1)
    for u, name in ((NEAR, 2), (FAR, 3), (NEARFAR, 4)):
        w.got(reg(0, s, u, c), (name, 0))
        to_plane(0, u)
        to_core(0, s, u)
    w.got(xg.at[p.bf], 21)
    w.put(xg.at[p.bf], xg.at[p.bf], p.n, 22)
    w.put(xg.at[p.bf], xg.at[p.bf], p.core, 23)
    nearfar(1)
    z_start(2)
    turn(0, OWN)
    w.got(xg.at[p.bn], 20)
    w.put(xg.at[p.bn], xg.at[p.bn], p.core, 23)
    turn(2, OWN)
    turn(1, NEAR)
    corner(1, OWN)
    for u in (NEAR, FAR, NEARFAR):
        turn(0, u)
    turn(1, FAR)
    for u in range(4):
        corner(0, u)
    w.got(match.at[pl.ds(0, 7)], 92)
    get_match = w.move(match, m_smem)
    w.got(xg.at[p.bnf], 22)
    w.put(xg.at[p.bnf], xg.at[p.bnf], p.core, 23)
    corner(1, NEAR)
    turn(1, NEARFAR)
    near(2)
    complete(0)
    w.got(xg.at[pl.ds(0, 4)], 23)

    lane = lax.broadcasted_iota(jnp.int32, (32, 768), 1)
    mine_lane = ((lane * 2731) >> 16) == lax.broadcasted_iota(jnp.int32, (32, 768), 0)
    lane2 = lax.broadcasted_iota(jnp.int32, (384, 768), 1)
    place = lane2 - 24 * ((lane2 * 2731) >> 16) - lax.broadcasted_iota(jnp.int32, (384, 768), 0)
    flat_vec = wqkv[:, 64:80, :].astype(F32)[:, 8, :].astype(BF16)

    def vector_row(k):
        part = jnp.dot(flat_vec, (place == -24 * k).astype(F32).astype(BF16), preferred_element_type=F32)
        rows[k] = jnp.sum(jnp.where(mine_lane, part, 0.0), axis=0, keepdims=True)

    def up_row(i):
        l3 = lax.broadcasted_iota(jnp.int32, (384, 768), 1) + 768 * i
        d3 = (l3 * 43691) >> 22
        hit = l3 - 96 * d3 - lax.broadcasted_iota(jnp.int32, (384, 768), 0) == -192
        part = jnp.dot(flat_vec, hit.astype(F32).astype(BF16), preferred_element_type=F32)
        owner = ((lax.broadcasted_iota(jnp.int32, (32, 768), 1) + 768 * i) * 43691) >> 22
        here = owner == lax.broadcasted_iota(jnp.int32, (32, 768), 0)
        bup[:, 768 * i : 768 * (i + 1)] = jnp.sum(jnp.where(here, part, 0.0), axis=0, keepdims=True)

    vector_row(0)
    vector_row(1)

    c0 = pl.multiple_of(128 * c, 128)
    b0 = pl.multiple_of(384 * zp + 128 * c, 128)
    b1 = pl.multiple_of(384 * zp + 256, 128)

    columns = sc["cols"]
    for i, v in enumerate((wqkv[:, :, pl.ds(c0, 128)].astype(F32), wqkv[:, :, 256:384].astype(F32))):
        for t in range(3):
            first = 256 * t + 128 * i
            columns[:, first : first + 128] = v[:, 24 * t : 24 * t + 24].reshape(768, 128).astype(BF16)
    for m in range(4):
        r = jnp.dot(xg[2 * m : 2 * m + 2].reshape(256, 768), columns[...], preferred_element_type=F32)
        for t in range(3):
            for tl in range(2):
                part = r[:, 256 * t + 128 * tl : 256 * t + 128 * (tl + 1)]
                if t != 1:
                    part = part + rows[t // 2, :, pl.ds(b1 if tl else b0, 128)]
                qkv[t, tl, 2 * m : 2 * m + 2] = part.astype(BF16).reshape(2, 128, 128)

    get_match.wait()
    att_buf = sc["ab"]

    def mask_head(e, v):
        return jnp.where(left if e == 0 else jnp.logical_not(left), v, zero)

    def weights(e, q, k):
        score = lax.dot_general(mask_head(e, q), k, NT, preferred_element_type=F32) * 0.125
        ex = jnp.exp(score - jnp.max(score, axis=-1, keepdims=True))
        return ex * (1.0 / jnp.sum(ex, axis=-1, keepdims=True))

    def head(tl, e):
        return 6 * zp + (2 * c if tl == 0 else 4) + e

    def attend(tl, blk, i):
        q = qkv[0, tl, blk]
        outs = []
        for e in range(2):
            m = m_smem[blk, 0, HEADS * g + head(tl, e)]
            pr = weights(e, q, qkv[1, tl, m]).astype(BF16)
            outs.append(jnp.dot(pr, qkv[2, tl, m], preferred_element_type=F32))
        att_buf[i] = jnp.where(left, outs[0], outs[1]).astype(BF16)


    def send_tile(tl, zz, cc, i):
        dst = att.at[g, :, pl.ds(pl.multiple_of(384 * zp + (128 * c if tl == 0 else 256), 128), 128)]
        if i in (0, 8):
            keep.append(w.move(att_buf.at[i], dst))
        else:
            w.put(att_buf.at[i], dst, (s, zz * 2 + cc), 90, lot=90)

    between = (
        lambda: (corner(2, OWN), corner(1, FAR)), lambda: (far(2), corner(1, NEARFAR)),
        lambda: turn(2, NEAR), lambda: nearfar(2),
    )
    keep = []
    for j, zz in enumerate((p.zf, p.znf, p.zn, z)):
        trio = [(0, c, 0 if zz is z else 1 + 2 * j), (0, 1 - c, 2 + 2 * j if j < 3 else 7), (1, c, 8 if zz is z else 9 + j)]
        for tl, cc, i in trio:
            attend(tl, zz * 2 + cc, i)
        for tl, cc, i in trio:
            send_tile(tl, zz, cc, i)
        between[j]()
    for k in range(2, 8):
        vector_row(k)
    for i in range(4):
        up_row(i)
    turn(2, FAR)
    complete(1)

    w.got(att_buf.at[pl.ds(0, 10)], 90)
    for cp in keep + [tok_in, grad_in]:
        cp.wait()

    n1, nlow, act, slope, dh2 = (sc[k] for k in ("n1", "nlow", "act", "slope", "dh2"))
    dinner = act

    def whole(ref):
        return ref[...].reshape(256, 768)

    h = whole(tok).astype(F32) + jnp.dot(whole(att), joined(wou[:, :, 0:768]), preferred_element_type=F32) + rows[2]
    h = h - mean(h)
    r1 = lax.rsqrt(mean(h * h) + EPS)
    n1[...] = h * r1
    nlow[...] = (n1[...] * rows[4] + rows[5]).astype(BF16)

    def up(j):
        cols = slice(512 * j, 512 * (j + 1))
        u = jnp.dot(nlow[...], joined(wou[:, :, 768 + 512 * j : 768 + 512 * (j + 1)]), preferred_element_type=F32) + bup[:, cols]
        cdf = 0.5 + 0.5 * lax.erf(u * 0.7071067811865476)
        act[:, cols] = (u * cdf).astype(BF16)
        slope[:, cols] = cdf + u * (jnp.exp(-0.5 * u * u) * 0.3989422804014327)

    up(0)
    corner(2, NEAR)
    up(1)
    up(2)
    turn(2, NEARFAR)
    up(3)
    corner(2, FAR)
    up(4)
    up(5)
    corner(2, NEARFAR)
    complete(2)

    h = jnp.dot(act[...], wd[...], preferred_element_type=F32) + rows[3] + (n1[...] * rows[4] + rows[5])
    h = h - mean(h)
    r2 = lax.rsqrt(mean(h * h) + EPS)
    n2 = h * r2
    result[...] = (n2 * rows[6] + rows[7]).astype(BF16).reshape(2, 128, 768)
    eye = lax.broadcasted_iota(jnp.int32, (128, 128), 0) == lax.broadcasted_iota(jnp.int32, (128, 128), 1)
    keepers = [
        jnp.sum(jnp.where(eye, mask[i : i + 1].astype(F32), 0.0), axis=-1, keepdims=True) for i in range(2)
    ]
    gr = whole(grad).astype(F32) * jnp.concatenate(keepers, axis=0)
    sums = sc["sums"]
    sums[6] = total(gr * n2)
    sums[7] = total(gr)
    e = gr * rows[6]
    d = r2 * (e - mean(e) - n2 * mean(e * n2))
    dh2[...] = d
    dz = sc["dz"]
    dz[...] = d.astype(BF16)
    sums[3] = total(dz[...].astype(F32))

    gd, gu, go, gq, gvec = (sc[k] for k in ("gd", "gu", "go", "gq", "gvec"))

    def down_gradient(i):
        r = lax.dot_general(act[:, 384 * i : 384 * (i + 1)], dz[...], TN, preferred_element_type=F32)
        gd[i // 2, 2 * (i % 2) : 2 * (i % 2) + 2] = r.astype(BF16).reshape(2, 2, 96, 768)

    chunks = [
        (gd, od, 0, 48, 0, 768),
        (gd, od, 48, 48, 0, 768),
        (gu, ou, 0, 24, 0, 1536),
        (gu, ou, 0, 24, 1536, 1536),
        (go, oo, 0, 24, 0, 768),
        (gvec.reshape(4, 4, 2, 8, 256), ovec, 0, 8, 0, 256),
    ]
    bufs = sc["bufs"]

    def cols(k, half):
        nc = chunks[k][5] // 2
        return pl.ds(half * nc, nc)

    def pair_start(k):
        v, out, q0, nr, k0, nc = chunks[k]
        w.put(v.at[:, :, 1 - c, pl.ds(q0, nr), pl.ds(k0, nc)], bufs[k][0], p.core, (50, k), lot=50 + k)

    def pair_add(k):
        v, out, q0, nr, k0, nc = chunks[k]
        rc, rdx, rdy, rx, ry, rz = bufs[k]
        w.got(rc, (50, k))

        def add(ss):
            def one(i):
                rc[ss, i] = rc[ss, i] + v[ss, i, c, q0 : q0 + nr, k0 : k0 + nc]

            loop(4, one)

        add(p.sd)
        w.put(rc.at[p.sd, :, :, cols(k, 0)], rdx, p.x, (51, k), lot=50 + k)
        w.put(rc.at[p.sd, :, :, cols(k, 1)], rdy, p.y, (52, k), lot=50 + k)
        add(p.sx)
        w.put(rc.at[p.sx, :, :, cols(k, 0)], rx.at[:, :, cols(k, 0)], p.x, (53, k), lot=50 + k)
        add(p.sy)
        w.put(rc.at[p.sy, :, :, cols(k, 1)], ry.at[:, :, cols(k, 1)], p.y, (54, k), lot=50 + k)
        add(s)

    def diagonal(k):
        rc, rdx, rdy, rx, ry, rz = bufs[k]
        w.got(rdx, (51, k))
        rc[p.sy, :, :, cols(k, 0)] = rc[p.sy, :, :, cols(k, 0)] + rdx[...]
        w.put(rc.at[p.sy, :, :, cols(k, 0)], ry.at[:, :, cols(k, 0)], p.y, (54, k), lot=50 + k)
        w.got(rdy, (52, k))
        rc[p.sx, :, :, cols(k, 1)] = rc[p.sx, :, :, cols(k, 1)] + rdy[...]
        w.put(rc.at[p.sx, :, :, cols(k, 1)], rx.at[:, :, cols(k, 1)], p.x, (53, k), lot=50 + k)

    def plane(k):
        rc, rdx, rdy, rx, ry, rz = bufs[k]
        w.got(rx, (53, k))
        w.got(ry, (54, k))

        def one(i):
            rc[s, i] = (rc[s, i].astype(F32) + rx[i].astype(F32) + ry[i].astype(F32)).astype(rc.dtype)

        loop(4, one)
        w.put(rc.at[s, p.znf], rz.at[0], p.n, (57, k), lot=50 + k)
        w.put(rc.at[s, p.zn], rz.at[1], p.n, (58, k), lot=50 + k)

    def last(k):
        rc, rdx, rdy, rx, ry, rz = bufs[k]
        w.got(rz.at[0], (57, k))
        rc[s, p.zf] = rc[s, p.zf] + rz[0]
        w.put(rc.at[s, p.zf], rz.at[2], p.f, (58, k), lot=50 + k)

    def final(k):
        v, out, q0, nr, k0, nc = chunks[k]
        rc, rdx, rdy, rx, ry, rz = bufs[k]
        w.got(rz.at[pl.ds(1, 2)], (58, k))
        out[q0 : q0 + nr, k0 : k0 + nc] = rc[s, z].astype(F32) + rz[1].astype(F32) + rz[2].astype(F32)

    for i in range(8):
        down_gradient(i)
    pair_start(0)
    pair_start(1)

    def inner_gradient(j):
        cc = slice(512 * j, 512 * (j + 1))
        r = lax.dot_general(dz[...], wd[512 * j : 512 * (j + 1), :], NT, preferred_element_type=F32)
        r = (r * slope[:, cc]).astype(BF16)
        dinner[:, cc] = r
        sc["sup"][:, cc] = total(r.astype(F32))

    for j in range(3):
        inner_gradient(j)
    pair_add(0)
    for j in range(3, 6):
        inner_gradient(j)
    pair_add(1)
    d = dh2[...]
    for j in range(6):
        wt = joined(wou[:, :, 768 + 512 * j : 768 + 512 * (j + 1)])
        d = d + lax.dot_general(dinner[:, 512 * j : 512 * (j + 1)], wt, NT, preferred_element_type=F32)
    sums[4] = total(d * n1[...])
    sums[5] = total(d)
    e = d * rows[4]
    d = r1 * (e - mean(e) - n1[...] * mean(e * n1[...]))
    dh1 = dh2
    dh1[...] = d
    dbr = sc["dbr"]
    dbr[...] = d.astype(BF16)
    sums[2] = total(dbr[...].astype(F32))
    datt = sc["datt"]
    r = lax.dot_general(dbr[...], joined(wou[:, :, 0:768]), NT, preferred_element_type=F32)
    datt[...] = r.astype(BF16).reshape(2, 128, 768)

    here = []
    for zz in (p.zf, p.znf, p.zn, z):
        gg, zq = zz // 2, zz % 2
        for tl, cc in ((0, 1 - c), (0, c), (1, c)):
            src = datt.at[gg, :, pl.ds(pl.multiple_of(384 * zq + (256 if tl else 128 * cc), 128), 128)]
            if zz is z and cc is c:
                here.append(w.move(src, dap.at[tl, b]))
            else:
                w.put(src, dap.at[tl, b], (s, zz * 2 + cc), 91, lot=91)

    def up_gradient(j):
        r = lax.dot_general(nlow[...], dinner[:, 512 * j : 512 * (j + 1)], TN, preferred_element_type=F32)
        gu[:, :, :, :, 512 * j : 512 * (j + 1)] = r.reshape(4, 4, 2, 24, 512).astype(BF16)

    diagonal(0)
    for j in range(3):
        up_gradient(j)
    pair_start(2)
    for j in range(3, 6):
        up_gradient(j)
    pair_start(3)
    diagonal(1)
    pair_add(2)
    r = lax.dot_general(whole(att), dbr[...], TN, preferred_element_type=F32)
    go[...] = r.reshape(4, 4, 2, 24, 768).astype(BF16)
    pair_start(4)
    pair_add(3)

    vl = lax.broadcasted_iota(jnp.int32, (128, 768), 1)
    spot = (vl - 24 * ((vl * 2731) >> 16) == lax.broadcasted_iota(jnp.int32, (128, 768), 0)).astype(F32).astype(BF16)

    def fold(part, hit):
        high = part.astype(BF16)
        low = (part - high.astype(F32)).astype(BF16)
        return lax.dot_general(high, hit, NT, preferred_element_type=F32) + lax.dot_general(
            low, hit, NT, preferred_element_type=F32
        )

    def fold_rows(lo, n):
        part = jnp.concatenate([jnp.where(mine_lane, sums[k], 0.0) for k in range(lo, lo + n)], axis=0)
        r = fold(part, spot)
        for k in range(n):
            gvec[:, lo + k, 0:128] = r[32 * k : 32 * (k + 1)]

    gvec[:, :, 128:256] = jnp.zeros((32, 8, 128), F32)
    fold_rows(2, 6)
    r = 0.0
    for i in range(4):
        l3 = lax.broadcasted_iota(jnp.int32, (128, 768), 1) + 768 * i
        hit = (l3 - 96 * ((l3 * 43691) >> 22) == lax.broadcasted_iota(jnp.int32, (128, 768), 0)).astype(F32).astype(BF16)
        owner = ((lax.broadcasted_iota(jnp.int32, (32, 768), 1) + 768 * i) * 43691) >> 22
        at = owner == lax.broadcasted_iota(jnp.int32, (32, 768), 0)
        r = r + fold(jnp.where(at, sc["sup"][:, 768 * i : 768 * (i + 1)], 0.0), hit)
    gvec[:, 0, 128:256] = r
    pair_add(4)

    w.got(att_buf.at[pl.ds(0, 10)], 91)
    for cp in here:
        cp.wait()

    def queries(tl, blk):
        q, da = qkv[0, tl, blk], dap[tl, blk]
        outs = []
        for e in range(2):
            m = m_smem[blk, 0, HEADS * g + head(tl, e)]
            k, v = qkv[1, tl, m], qkv[2, tl, m]
            pr = weights(e, q, k)
            dp = lax.dot_general(mask_head(e, da), v, NT, preferred_element_type=F32)
            ds = (pr * (dp - jnp.sum(pr * dp, axis=-1, keepdims=True))).astype(BF16)
            ds_buf[tl, e, blk] = ds
            p_buf[tl, e, blk] = pr.astype(BF16)
            outs.append(jnp.dot(ds, k, preferred_element_type=F32) * 0.125)
        dqkv[0, tl, blk] = jnp.where(left, outs[0], outs[1]).astype(BF16)

    def keys(tl, n):
        dk, dv = [], []
        for e in range(2):
            cq = 0
            for i in range(8):
                cq = jnp.where(m_smem[i, 0, HEADS * g + head(tl, e)] == n, i, cq)
            ds, pr = ds_buf[tl, e, cq], p_buf[tl, e, cq]
            dk.append(lax.dot_general(ds, qkv[0, tl, cq], TN, preferred_element_type=F32) * 0.125)
            dv.append(lax.dot_general(pr, dap[tl, cq], TN, preferred_element_type=F32))
        dqkv[1, tl, n] = jnp.where(left, dk[0], dk[1]).astype(BF16)
        dqkv[2, tl, n] = jnp.where(left, dv[0], dv[1]).astype(BF16)

    def both(f, i):
        f(2 * i)
        f(2 * i + 1)

    plane(0)
    loop(4, lambda i: both(lambda n: queries(0, n), i))
    diagonal(2)
    plane(1)
    loop(2, lambda i: both(lambda n: queries(1, 2 * n + c), i))
    last(0)
    loop(4, lambda i: both(lambda n: keys(0, n), i))
    diagonal(3)
    last(1)
    loop(4, lambda i: both(lambda n: keys(1, n), i))

    dtk, rtk, rtn, rtf = (sc[k] for k in ("dtk", "rtk", "rtn", "rtf"))

    def flat(m):
        return jnp.concatenate(
            [dqkv[t, tl, 4 * m : 4 * m + 4].reshape(512, 128) for t in range(3) for tl in range(2)], axis=1
        )

    for m in range(2):
        r = lax.dot_general(flat(m), columns[...], NT, preferred_element_type=F32)
        dtk[2 * m : 2 * m + 2] = r.astype(BF16).reshape(2, 2, 128, 768)
    w.put(dtk.at[:, 1 - c], rtk, p.core, 60)

    rq, accq, rqdx, rqdy, rqx, rqy, rqz = (sc[k] for k in ("rq", "accq", "rqdx", "rqdy", "rqx", "rqy", "rqz"))
    r = 0.0
    for m in range(2):
        x = xg[4 * m : 4 * m + 4].reshape(512, 768)
        r = r + lax.dot_general(x, flat(m), TN, preferred_element_type=F32)
    for t in range(3):
        gq[t] = r[:, 256 * t : 256 * (t + 1)].reshape(4, 4, 2, 24, 256).astype(BF16)
    w.put(gq.at[:, :, :, 1 - c], rq, p.core, 61)

    w.got(rtk, 60)
    loop(4, lambda i: rtk.__setitem__(i, rtk[i] + dtk[i, c]))
    w.put(rtk.at[p.znf], rtn.at[0], p.n, 62)
    w.put(rtk.at[p.zn], rtn.at[1], p.n, 63)

    sums[0] = jnp.zeros((1, 768), F32)
    sums[1] = jnp.zeros((1, 768), F32)
    for r, t in ((0, 0), (1, 2)):
        f = [total(dqkv[t, tl].reshape(1024, 128).astype(F32)) for tl in range(2)]
        sums[r, :, pl.ds(b0, 128)] = f[0]
        sums[r, :, pl.ds(b1, 128)] = f[1]
    fold_rows(0, 2)
    pair_start(5)

    w.got(rq, 61)
    o0 = pl.multiple_of(128 * (1 - c), 128)

    def pair_q(i):
        for t in range(3):
            for zz in range(4):
                accq[t, i, zz, :, pl.ds(c0, 128)] = gq[t, i, zz, c, :, 0:128]
                accq[t, i, zz, :, pl.ds(o0, 128)] = rq[t, i, zz, :, 0:128]
                accq[t, i, zz, :, 256:384] = gq[t, i, zz, c, :, 128:256] + rq[t, i, zz, :, 128:256]

    pair_q(p.sd)
    w.put(accq.at[:, p.sd, :, :, pl.ds(0, 256)], rqdx, p.x, 64)
    w.put(accq.at[:, p.sd, :, :, pl.ds(256, 128)], rqdy, p.y, 65)
    diagonal(4)
    pair_q(p.sx)
    pair_q(p.sy)
    pair_q(s)
    pair_add(5)
    plane(2)
    w.got(rtn.at[0], 62)
    rtk[p.zf] = rtk[p.zf] + rtn[0]
    w.put(rtk.at[p.zf], rtf, p.f, 68)
    w.got(rqdx, 64)
    accq[:, p.sy, :, :, 0:256] = accq[:, p.sy, :, :, 0:256] + rqdx[...]
    w.put(accq.at[:, p.sy], rqy, p.y, 66)
    w.got(rqdy, 65)
    accq[:, p.sx, :, :, 256:384] = accq[:, p.sx, :, :, 256:384] + rqdy[...]
    w.put(accq.at[:, p.sx], rqx, p.x, 67)
    diagonal(5)
    plane(3)
    last(2)
    plane(4)
    last(3)
    final(0)
    final(1)
    last(4)
    w.got(rqx, 67)
    w.got(rqy, 66)
    for t in range(3):
        accq[t, s] = (accq[t, s].astype(F32) + rqx[t].astype(F32) + rqy[t].astype(F32)).astype(BF16)
    w.put(accq.at[:, s, p.znf], rqz.at[0], p.f, 80)
    w.put(accq.at[:, s, p.zf], rqz.at[1], p.f, 81)
    plane(5)
    final(2)
    w.got(rqz.at[0], 80)
    accq[:, s, p.zn] = accq[:, s, p.zn] + rqz[0]
    w.put(accq.at[:, s, p.zn], rqz.at[2], p.n, 82)
    last(5)
    final(3)
    final(4)
    w.got(rtn.at[1], 63)
    w.got(rtf, 68)
    d = dh1[...].reshape(2, 128, 768)
    dtok[...] = d
    dtok[g] = dtok[g] + rtk[z].astype(F32) + rtn[1].astype(F32)
    dtok[1 - g] = dtok[1 - g] + rtf[...].astype(F32)
    w.got(rqz.at[1], 81)
    q0 = pl.multiple_of(384 * zp, 128)
    q1 = pl.multiple_of(384 * (1 - zp), 128)
    for t in range(3):
        oqkv[t, :, pl.ds(q0, 384)] = accq[t, s, z].astype(F32) + rqz[1, t].astype(F32)
    w.got(rqz.at[2], 82)
    for t in range(3):
        oqkv[t, :, pl.ds(q1, 384)] = rqz[2, t].astype(F32)
    final(5)
    w.finish({
        0: wqkv.at[pl.ds(0, 31)], 1: wou.at[pl.ds(0, 31)], 2: wd.at[pl.ds(0, 2976)],
        50: wd.at[pl.ds(0, 1488)], 51: wd.at[pl.ds(0, 1488)],
        52: wou.at[pl.ds(0, 31), :, pl.ds(0, 1536)], 53: wou.at[pl.ds(0, 31), :, pl.ds(0, 1536)],
        54: wou.at[pl.ds(0, 31), :, pl.ds(0, 768)], 55: gvec.at[pl.ds(0, 31)],
        90: att_buf.at[pl.ds(0, 10)], 91: att_buf.at[pl.ds(0, 10)], 92: match.at[pl.ds(0, 7)],
    })


def scratch():
    VM = pltpu.VMEM
    per_chunk = []
    for nr, nc in ((48, 768), (48, 768), (24, 1536), (24, 1536), (24, 768), (8, 256)):
        kind = F32 if nr == 8 else BF16
        shapes = ((4, 4, nr, nc), (4, nr, nc // 2), (4, nr, nc // 2), (4, nr, nc), (4, nr, nc), (3, nr, nc))
        per_chunk.append(tuple(VM(shape, kind) for shape in shapes))
    return dict(
        wou=VM((32, 24, 3840), BF16), wd=VM((3072, 768), BF16), wqkv=VM((32, 80, 384), BF16), raw=VM((3, 24, 768), BF16),
        cols=VM((768, 768), BF16), gvec=VM((32, 8, 256), F32),
        xg=VM((8, 128, 768), BF16), qkv=VM((3, 2, 8, 128, 128), BF16), att=VM((2, 128, 768), BF16),
        match=VM((8, 8, 128), jnp.int32), ms=pltpu.SMEM((8, 8, 128), jnp.int32),
        stage=VM((2, 80, 384), BF16), sou=VM((24, 3840), BF16), rows=VM((8, 1, 768), F32), bup=VM((1, 3072), F32),
        tok=VM((2, 128, 768), BF16), grad=VM((2, 128, 768), BF16), vo=VM((8, 384), F32), mo=VM((8, 128), jnp.int32),
        ab=VM((12, 128, 128), BF16), dap=VM((2, 8, 128, 128), BF16), ds=VM((2, 2, 8, 128, 128), BF16),
        p=VM((2, 2, 8, 128, 128), BF16), dqkv=VM((3, 2, 8, 128, 128), BF16),
        n1=VM((256, 768), F32), nlow=VM((256, 768), BF16), act=VM((256, 3072), BF16), slope=VM((256, 3072), F32),
        dh2=VM((256, 768), F32), sums=VM((8, 1, 768), F32), sup=VM((1, 3072), F32),
        dz=VM((256, 768), BF16), dbr=VM((256, 768), BF16), datt=VM((2, 128, 768), BF16),
        gd=VM((4, 4, 2, 96, 768), BF16), gu=VM((4, 4, 2, 24, 3072), BF16), go=VM((4, 4, 2, 24, 768), BF16),
        gq=VM((3, 4, 4, 2, 24, 256), BF16), rq=VM((3, 4, 4, 24, 256), BF16), accq=VM((3, 4, 4, 24, 384), BF16),
        dtk=VM((4, 2, 128, 768), BF16), rtk=VM((4, 128, 768), BF16), rtn=VM((2, 128, 768), BF16), rtf=VM((128, 768), BF16),
        rqdx=VM((3, 4, 24, 256), BF16), rqdy=VM((3, 4, 24, 128), BF16), rqx=VM((3, 4, 24, 384), BF16),
        rqy=VM((3, 4, 24, 384), BF16), rqz=VM((3, 3, 24, 384), BF16), bufs=tuple(per_chunk),
    )


def hand_out(result, od, ou, oo, oqkv, dtok, ovec, *rest):
    outs, sem = rest[:17], rest[17]
    pairs = [(result, outs[0]), (dtok, outs[1]), (oqkv.at[0], outs[2]), (oqkv.at[1], outs[3]), (oqkv.at[2], outs[4])]
    pairs += [(oo, outs[5]), (ou, outs[6]), (od, outs[7])]
    copies = [pltpu.make_async_copy(a, o, sem.at[i]) for i, (a, o) in enumerate(pairs)]
    for cp in copies:
        cp.start()
    for row, out in zip((0, 1, 2, None, 3, 4, 5, 6, 7), outs[8:], strict=True):
        out[...] = ovec[0, 128:224] if row is None else ovec[row, 0:24]
    for cp in copies:
        cp.wait()


def column(
    tokens, grad_out, masked, token_order, cluster_match,
    w_query, w_key, w_value, w_out, w_up, w_down,
    b_query, b_value, b_out, b_up, b_down,
    gain_attn, shift_attn, gain_ffn, shift_ffn,
):
    V = pl.BlockSpec(memory_space=pltpu.VMEM)
    A = pl.BlockSpec(memory_space=pl.ANY)
    S = jax.ShapeDtypeStruct
    vectors = (b_query, b_value, b_out, b_down, gain_attn, shift_attn, gain_ffn, shift_ffn, b_up)
    got = pl.pallas_call(
        layer_kernel,
        out_shape=(
            S((2, 128, 768), BF16), S((96, 768), F32), S((24, 3072), F32), S((24, 768), F32), S((3, 24, 768), F32),
            S((2, 128, 768), F32), S((8, 256), F32),
        ),
        in_specs=[A, A, V, V] + [A] * 6 + [V] * 9,
        out_specs=(V,) * 7,
        scratch_shapes=[scratch(), *(pltpu.SemaphoreType.DMA((n,)) for n in (31, 112, 17))],
        compiler_params=pltpu.CompilerParams(collective_id=0, has_side_effects=True, vmem_limit_bytes=62 << 20),
        name="layer",
    )(tokens, grad_out, masked, cluster_match, w_query, w_key, w_value, w_out, w_up, w_down, *vectors)
    square = S((24, 768), F32)
    outs = (S((2, 128, 768), BF16), S((2, 128, 768), F32)) + (square,) * 4 + (S((24, 3072), F32), S((96, 768), F32))
    outs += tuple(S((n,), F32) for n in (24, 24, 24, 96, 24, 24, 24, 24, 24))
    return pl.pallas_call(
        hand_out,
        out_shape=outs,
        in_specs=[V] * 7,
        out_specs=(A,) * 8 + (V,) * 9,
        scratch_shapes=[pltpu.SemaphoreType.DMA((8,))],
        name="results",
    )(*got)


def solution(mesh):
    fits = mesh.shape[SEQ] == 4 and mesh.shape[BLK] == 8
    return jax.shard_map(
        column if fits else general,
        mesh=mesh,
        in_specs=(
            P(SEQ, BLK, None),
            P(SEQ, BLK, None),
            P(SEQ, BLK),
            P(SEQ, None, BLK),
            P(SEQ, None, BLK),
            P(BOTH, None),
            P(BOTH, None),
            P(BOTH, None),
            P(BOTH, None),
            P(BOTH, None),
            P(BOTH, None),
            P(BOTH),
            P(BOTH),
            P(BOTH),
            P(BOTH),
            P(BOTH),
            P(BOTH),
            P(BOTH),
            P(BOTH),
            P(BOTH),
        ),
        out_specs=(
            P(SEQ, BLK, None),
            P(SEQ, BLK, None),
            P(BOTH, None),
            P(BOTH, None),
            P(BOTH, None),
            P(BOTH, None),
            P(BOTH, None),
            P(BOTH, None),
            P(BOTH),
            P(BOTH),
            P(BOTH),
            P(BOTH),
            P(BOTH),
            P(BOTH),
            P(BOTH),
            P(BOTH),
            P(BOTH),
        ),
        check_vma=False,
    )
```

```python
import functools
import math

import jax
import jax.numpy as jnp
from jax import lax
from jax.experimental import pallas as pl
from jax.experimental.pallas import tpu as pltpu
from jax.sharding import PartitionSpec as P

HEADS = 12
CL = 128
EPS = 1e-05
MESH = pl.DeviceIdType.MESH
SEQ, BLK = BOTH = ("seq", "blk")
F32 = jnp.float32
BF16 = jnp.bfloat16


def norm_rows(hidden, gain_row, shift_row):
    row_mean = jnp.mean(hidden, axis=-1, keepdims=True)
    centered = hidden - row_mean
    variance = jnp.mean(centered * centered, axis=-1, keepdims=True)
    return centered * lax.rsqrt(variance + EPS) * gain_row + shift_row


def gelu_exact(inner_sum):
    return jax.nn.gelu(inner_sum, approximate=False)


def to_heads(flat_rows, groups, local_len):
    return flat_rows.reshape(groups, local_len, HEADS, -1).transpose(0, 2, 1, 3)


def from_heads(head_rows):
    groups, head_count, local_len, head_dim = head_rows.shape
    return head_rows.transpose(0, 2, 1, 3).reshape(groups * local_len, head_count * head_dim)


def reorder(head_rows, positions):
    return jnp.take_along_axis(head_rows, positions[..., None], axis=2)


def general(
    tokens,
    grad_out,
    masked,
    token_order,
    cluster_match,
    w_query,
    w_key,
    w_value,
    w_out,
    w_up,
    w_down,
    b_query,
    b_value,
    b_out,
    b_up,
    b_down,
    gain_attn,
    shift_attn,
    gain_ffn,
    shift_ffn,
):
    groups, local_len, width = tokens.shape
    row_count = groups * local_len
    head_dim = width // HEADS
    clusters = local_len // CL
    score_scale = 1.0 / math.sqrt(head_dim)
    gathered = (
        lax.all_gather(w_query, BOTH, axis=0, tiled=True),
        lax.all_gather(w_key, BOTH, axis=0, tiled=True),
        lax.all_gather(w_value, BOTH, axis=0, tiled=True),
        lax.all_gather(w_out, BOTH, axis=0, tiled=True),
        lax.all_gather(w_up, BOTH, axis=0, tiled=True),
        lax.all_gather(w_down, BOTH, axis=0, tiled=True),
        lax.all_gather(b_query, BOTH, axis=0, tiled=True),
        lax.all_gather(b_value, BOTH, axis=0, tiled=True),
        lax.all_gather(b_out, BOTH, axis=0, tiled=True),
        lax.all_gather(b_up, BOTH, axis=0, tiled=True),
        lax.all_gather(b_down, BOTH, axis=0, tiled=True),
        lax.all_gather(gain_attn, BOTH, axis=0, tiled=True),
        lax.all_gather(shift_attn, BOTH, axis=0, tiled=True),
        lax.all_gather(gain_ffn, BOTH, axis=0, tiled=True),
        lax.all_gather(shift_ffn, BOTH, axis=0, tiled=True),
    )
    (
        full_query,
        full_key,
        full_value,
        full_out,
        full_up,
        full_down,
        bias_query,
        bias_value,
        bias_out,
        bias_up,
        bias_down,
        norm_gain1,
        norm_shift1,
        norm_gain2,
        norm_shift2,
    ) = gathered
    flat_tokens = tokens.reshape(row_count, width)
    inverse = jnp.argsort(token_order, axis=-1)
    cluster_shape = (groups, HEADS, clusters, CL, head_dim)
    query_low = (
        jnp.dot(flat_tokens, full_query, preferred_element_type=jnp.float32)
        + bias_query.astype(jnp.float32)
    ).astype(jnp.bfloat16)
    key_low = jnp.dot(flat_tokens, full_key, preferred_element_type=jnp.float32).astype(
        jnp.bfloat16
    )
    value_low = (
        jnp.dot(flat_tokens, full_value, preferred_element_type=jnp.float32)
        + bias_value.astype(jnp.float32)
    ).astype(jnp.bfloat16)
    query_perm = reorder(to_heads(query_low, groups, local_len), token_order).reshape(cluster_shape)
    key_perm = reorder(to_heads(key_low, groups, local_len), token_order).reshape(cluster_shape)
    value_perm = reorder(to_heads(value_low, groups, local_len), token_order).reshape(cluster_shape)
    empty_sel = jnp.zeros(cluster_shape, jnp.bfloat16)
    key_piece = lax.all_gather(key_perm, BLK, axis=2, tiled=True)
    value_piece = lax.all_gather(value_perm, BLK, axis=2, tiled=True)
    piece_len = key_piece.shape[2]
    offset = cluster_match
    select = (offset[..., None] == jnp.arange(piece_len, dtype=jnp.int32)).astype(jnp.bfloat16)
    inside = ((offset >= 0) & (offset < piece_len))[..., None, None]
    new_keys = jnp.einsum(
        "ghcj,ghjkd->ghckd", select, key_piece, preferred_element_type=jnp.float32
    ).astype(jnp.bfloat16)
    new_values = jnp.einsum(
        "ghcj,ghjkd->ghckd", select, value_piece, preferred_element_type=jnp.float32
    ).astype(jnp.bfloat16)
    key_sel = jnp.where(inside, new_keys, empty_sel)
    value_sel = jnp.where(inside, new_values, empty_sel)
    scores = (
        jnp.einsum("ghcqd,ghckd->ghcqk", query_perm, key_sel, preferred_element_type=jnp.float32)
        * score_scale
    )
    row_max = jnp.max(scores, axis=-1, keepdims=True)
    log_total = row_max + jnp.log(jnp.sum(jnp.exp(scores - row_max), axis=-1, keepdims=True))
    attn_probs = jnp.exp(scores - log_total)
    probs_low = attn_probs.astype(jnp.bfloat16)
    mixed_perm = jnp.einsum(
        "ghcqk,ghckd->ghcqd", probs_low, value_sel, preferred_element_type=jnp.float32
    ).reshape(groups, HEADS, local_len, head_dim)
    attended = from_heads(reorder(mixed_perm, inverse)).astype(jnp.bfloat16)
    branch = jnp.dot(attended, full_out, preferred_element_type=jnp.float32) + bias_out.astype(
        jnp.float32
    )
    resid = flat_tokens.astype(jnp.float32) + branch
    normed, pull_first = jax.vjp(
        norm_rows, resid, norm_gain1.astype(jnp.float32), norm_shift1.astype(jnp.float32)
    )
    normed_low = normed.astype(jnp.bfloat16)
    inner_sum = jnp.dot(normed_low, full_up, preferred_element_type=jnp.float32) + bias_up.astype(
        jnp.float32
    )
    active, pull_gelu = jax.vjp(gelu_exact, inner_sum)
    active_low = active.astype(jnp.bfloat16)
    outer_sum = jnp.dot(
        active_low, full_down, preferred_element_type=jnp.float32
    ) + bias_down.astype(jnp.float32)
    final_rows, pull_second = jax.vjp(
        norm_rows,
        normed + outer_sum,
        norm_gain2.astype(jnp.float32),
        norm_shift2.astype(jnp.float32),
    )
    result = final_rows.astype(jnp.bfloat16).reshape(groups, local_len, width)
    back_weights = (
        lax.all_gather(w_query, BOTH, axis=0, tiled=True),
        lax.all_gather(w_key, BOTH, axis=0, tiled=True),
        lax.all_gather(w_value, BOTH, axis=0, tiled=True),
        lax.all_gather(w_out, BOTH, axis=0, tiled=True),
        lax.all_gather(w_up, BOTH, axis=0, tiled=True),
        lax.all_gather(w_down, BOTH, axis=0, tiled=True),
        lax.all_gather(b_query, BOTH, axis=0, tiled=True),
        lax.all_gather(b_value, BOTH, axis=0, tiled=True),
        lax.all_gather(b_out, BOTH, axis=0, tiled=True),
        lax.all_gather(b_up, BOTH, axis=0, tiled=True),
        lax.all_gather(b_down, BOTH, axis=0, tiled=True),
        lax.all_gather(gain_attn, BOTH, axis=0, tiled=True),
        lax.all_gather(shift_attn, BOTH, axis=0, tiled=True),
        lax.all_gather(gain_ffn, BOTH, axis=0, tiled=True),
        lax.all_gather(shift_ffn, BOTH, axis=0, tiled=True),
    )
    back_query, back_key, back_value, back_out, back_up, back_down = back_weights[:6]
    upstream = grad_out.reshape(row_count, width).astype(jnp.float32) * masked.reshape(
        row_count, 1
    ).astype(jnp.float32)
    d_sum2, d_gain2, d_shift2 = pull_second(upstream)
    d_outer = d_sum2.astype(jnp.bfloat16)
    g_down = jnp.einsum("rf,rd->fd", active_low, d_outer, preferred_element_type=jnp.float32)
    g_bdown = jnp.sum(d_outer.astype(jnp.float32), axis=0)
    d_active = jnp.einsum("rd,fd->rf", d_outer, back_down, preferred_element_type=jnp.float32)
    d_inner = pull_gelu(d_active)[0].astype(jnp.bfloat16)
    g_up = jnp.einsum("rd,rf->df", normed_low, d_inner, preferred_element_type=jnp.float32)
    g_bup = jnp.sum(d_inner.astype(jnp.float32), axis=0)
    d_normed = d_sum2 + jnp.einsum(
        "rf,df->rd", d_inner, back_up, preferred_element_type=jnp.float32
    )
    d_resid, d_gain1, d_shift1 = pull_first(d_normed)
    d_branch = d_resid.astype(jnp.bfloat16)
    g_out = jnp.einsum("ri,rd->id", attended, d_branch, preferred_element_type=jnp.float32)
    g_bout = jnp.sum(d_branch.astype(jnp.float32), axis=0)
    d_attended = jnp.einsum(
        "rd,id->ri", d_branch, back_out, preferred_element_type=jnp.float32
    ).astype(jnp.bfloat16)
    d_mixed = reorder(to_heads(d_attended, groups, local_len), token_order).reshape(cluster_shape)
    scores_again = (
        jnp.einsum("ghcqd,ghckd->ghcqk", query_perm, key_sel, preferred_element_type=jnp.float32)
        * score_scale
    )
    probs_again = jnp.exp(scores_again - log_total)
    probs_again_low = probs_again.astype(jnp.bfloat16)
    d_probs = jnp.einsum(
        "ghcqd,ghckd->ghcqk", d_mixed, value_sel, preferred_element_type=jnp.float32
    )
    d_scores = (
        probs_again * (d_probs - jnp.sum(probs_again * d_probs, axis=-1, keepdims=True))
    ).astype(jnp.bfloat16)
    d_query_perm = (
        jnp.einsum("ghcqk,ghckd->ghcqd", d_scores, key_sel, preferred_element_type=jnp.float32)
        * score_scale
    )
    d_key_sel = (
        jnp.einsum("ghcqk,ghcqd->ghckd", d_scores, query_perm, preferred_element_type=jnp.float32)
        * score_scale
    )
    d_value_sel = jnp.einsum(
        "ghcqk,ghcqd->ghckd", probs_again_low, d_mixed, preferred_element_type=jnp.float32
    )
    sent = jnp.concatenate([d_key_sel, d_value_sel], axis=-1)
    my_start = lax.axis_index(BLK) * clusters
    piece_grads = lax.all_gather(sent.astype(jnp.bfloat16), BLK, axis=2, tiled=True).astype(
        jnp.float32
    )
    piece_match = lax.all_gather(
        cluster_match.astype(jnp.float32).astype(jnp.bfloat16), BLK, axis=2, tiled=True
    ).astype(jnp.float32)
    offset = piece_match.astype(jnp.int32) - my_start
    select = (offset[..., None] == jnp.arange(clusters, dtype=jnp.int32)).astype(jnp.float32)
    owned = jnp.zeros(sent.shape, jnp.float32) + jnp.einsum(
        "ghjc,ghjke->ghcke", select, piece_grads, precision=lax.Precision.HIGHEST
    )
    back_kv = reorder(owned.reshape(groups, HEADS, local_len, 2 * head_dim), inverse)
    d_key = from_heads(back_kv[..., :head_dim]).astype(jnp.bfloat16)
    d_value = from_heads(back_kv[..., head_dim:]).astype(jnp.bfloat16)
    d_query = from_heads(
        reorder(d_query_perm.reshape(groups, HEADS, local_len, head_dim), inverse)
    ).astype(jnp.bfloat16)
    g_query = jnp.einsum("ri,rd->id", flat_tokens, d_query, preferred_element_type=jnp.float32)
    g_key = jnp.einsum("ri,rd->id", flat_tokens, d_key, preferred_element_type=jnp.float32)
    g_value = jnp.einsum("ri,rd->id", flat_tokens, d_value, preferred_element_type=jnp.float32)
    g_bquery = jnp.sum(d_query.astype(jnp.float32), axis=0)
    g_bvalue = jnp.sum(d_value.astype(jnp.float32), axis=0)
    d_tokens_flat = (
        d_resid
        + jnp.einsum("rd,id->ri", d_query, back_query, preferred_element_type=jnp.float32)
        + jnp.einsum("rd,id->ri", d_key, back_key, preferred_element_type=jnp.float32)
        + jnp.einsum("rd,id->ri", d_value, back_value, preferred_element_type=jnp.float32)
    )
    summed = (
        lax.psum_scatter(g_query, BOTH, scatter_dimension=0, tiled=True),
        lax.psum_scatter(g_key, BOTH, scatter_dimension=0, tiled=True),
        lax.psum_scatter(g_value, BOTH, scatter_dimension=0, tiled=True),
        lax.psum_scatter(g_out, BOTH, scatter_dimension=0, tiled=True),
        lax.psum_scatter(g_up, BOTH, scatter_dimension=0, tiled=True),
        lax.psum_scatter(g_down, BOTH, scatter_dimension=0, tiled=True),
        lax.psum_scatter(g_bquery, BOTH, scatter_dimension=0, tiled=True),
        lax.psum_scatter(g_bvalue, BOTH, scatter_dimension=0, tiled=True),
        lax.psum_scatter(g_bout, BOTH, scatter_dimension=0, tiled=True),
        lax.psum_scatter(g_bup, BOTH, scatter_dimension=0, tiled=True),
        lax.psum_scatter(g_bdown, BOTH, scatter_dimension=0, tiled=True),
        lax.psum_scatter(d_gain1, BOTH, scatter_dimension=0, tiled=True),
        lax.psum_scatter(d_shift1, BOTH, scatter_dimension=0, tiled=True),
        lax.psum_scatter(d_gain2, BOTH, scatter_dimension=0, tiled=True),
        lax.psum_scatter(d_shift2, BOTH, scatter_dimension=0, tiled=True),
    )
    return (result, d_tokens_flat.reshape(groups, local_len, width)) + tuple(summed)


OWN, NEAR, FAR, NEARFAR = range(4)
NT = (((1,), (1,)), ((), ()))
TN = (((0,), (0,)), ((), ()))


class Place:
    def __init__(self):
        s, b = lax.axis_index(SEQ), lax.axis_index(BLK)
        self.s, self.b = s, b
        z, c = b // 2, b % 2
        self.z, self.c = z, c
        self.zlo, self.zhi = z % 2, z // 2
        self.sx = s + 1 - 2 * (s % 2)
        self.sy = s + 2 - 4 * (s // 2)
        self.sd = self.sy + 1 - 2 * (s % 2)
        self.zn = z + 1 - 2 * self.zlo
        self.zf = z + 2 - 4 * self.zhi
        self.znf = self.zf + 1 - 2 * self.zlo
        self.bc = b + 1 - 2 * c
        self.bn, self.bf, self.bnf = self.zn * 2 + c, self.zf * 2 + c, self.znf * 2 + c
        self.core = (s, self.bc)
        self.n = (s, self.bn)
        self.f = (s, self.bf)
        self.nf = (s, self.bnf)
        self.x = (self.sx, b)
        self.y = (self.sy, b)


class Wire:
    def __init__(self, send, recv, local):
        self.send, self.recv, self.local = send, recv, local
        self.n_send = self.n_local = self.n_recv = 0
        self.sent, self.slots, self.lots = [], {}, {}

    def slot(self, key):
        if key not in self.slots:
            self.slots[key] = self.n_recv
            self.n_recv += 1
        return self.slots[key]

    def put(self, src, dst, to, key, lot=None):
        at = self.slot(key)
        if lot is None or lot not in self.lots:
            index = self.n_send
            self.n_send += 1
            if lot is not None:
                self.lots[lot] = index
        else:
            index = self.lots[lot]
        cp = pltpu.make_async_remote_copy(
            src, dst, self.send.at[index], self.recv.at[at], device_id=to, device_id_type=MESH
        )
        cp.start()
        if lot is None:
            self.sent.append(cp)

    def got(self, dst, key):
        at = self.slot(key)
        pltpu.make_async_copy(dst, dst, self.recv.at[at]).wait()

    def move(self, src, dst):
        cp = pltpu.make_async_copy(src, dst, self.local.at[self.n_local])
        self.n_local += 1
        cp.start()
        return cp

    def finish(self, sizes):
        for lot, ref in sizes.items():
            pltpu.make_async_copy(ref, ref, self.send.at[self.lots[lot]]).wait()
        for cp in self.sent:
            cp.wait_send()


def greet(peers):
    bar = pltpu.get_barrier_semaphore()
    for to in peers:
        pl.semaphore_signal(bar, inc=1, device_id=to, device_id_type=MESH)
    pl.semaphore_wait(bar, len(peers))


def loop(n, body):
    def run(i, carry):
        body(i)
        return carry

    lax.fori_loop(0, n, run, 0)


def joined(v):
    return v.astype(F32).reshape(768, v.shape[-1]).astype(BF16)


def mean(v):
    return jnp.mean(v, axis=-1, keepdims=True)


def total(v):
    return jnp.sum(v, axis=0, keepdims=True)


def layer_kernel(
    tok_h, go_h, mask, cm, wq, wk, wv, wo_s, wu_s, wd_s,
    *others,
):
    vectors, (result, od, ou, oo, oqkv, dtok, ovec, sc, *sems) = others[:9], others[9:]
    p = Place()
    w = Wire(*sems)
    s, b, z, c = p.s, p.b, p.z, p.c
    zp, g = p.zlo, p.zhi
    zs = (z, p.zn, p.zf, p.znf)
    wou, wd, wqkv, xg, qkv, att = (sc[k] for k in ("wou", "wd", "wqkv", "xg", "qkv", "att"))
    match, m_smem, stage, rows, bup = (sc[k] for k in ("match", "ms", "stage", "rows", "bup"))

    raw = sc["raw"]
    early = [w.move(ref, raw.at[t]) for t, ref in enumerate((wq, wk, wv))]
    tok, grad = sc["tok"], sc["grad"]
    slot = s * 8 + b
    mine = [
        w.move(wo_s, wou.at[slot, :, pl.ds(0, 768)]), w.move(wu_s, wou.at[slot, :, pl.ds(768, 3072)]),
        w.move(wd_s, wd.at[pl.ds(pl.multiple_of(96 * slot, 96), 96)]), w.move(tok_h.at[g], xg.at[b]),
    ]
    tok_in, grad_in = w.move(tok_h, tok), w.move(go_h, grad)
    greet([p.core, p.n, p.f, p.nf, p.x, p.y, (s, p.zn * 2 + 1 - c), (s, p.zf * 2 + 1 - c), (s, p.znf * 2 + 1 - c)])

    def at_rows(n, ss, zz, cc):
        return pl.ds(pl.multiple_of(n * (ss * 8 + zz * 2 + cc), 8), n)

    def reg(k, ss, u, cc, half=None):
        zz = zs[u]
        if k == 0:
            cols = (pl.ds(0, 384), pl.ds(0, 256), pl.ds(256, 128))[0 if half is None else 1 + half]
            return wqkv.at[ss * 8 + zz * 2 + cc, :, cols]
        if k == 1:
            cols = pl.ds(0, 3840) if half is None else pl.ds(1920 * half, 1920)
            return wou.at[ss * 8 + zz * 2 + cc, :, cols]
        cols = pl.ds(0, 768) if half is None else pl.ds(384 * half, 384)
        return wd.at[at_rows(96, ss, zz, cc), cols]

    def to_plane(k, u, src=None):
        r = reg(k, s, u, c)
        src = r if src is None else src
        w.put(src, r, p.x, (0, k, u), lot=k)
        w.put(src, r, p.y, (1, k, u), lot=k)

    def to_core(k, ss, u):
        r = reg(k, ss, u, c)
        w.put(r, r, p.core, (5, k), lot=k)

    def z_start(k):
        r = reg(k, s, OWN, c)
        w.put(r, r, p.n, (2, k), lot=k)
        w.put(r, r, p.f, (3, k), lot=k)

    def near(k):
        w.got(reg(k, s, NEAR, c), (2, k))
        to_plane(k, NEAR)
        to_core(k, s, NEAR)

    def far(k):
        r = reg(k, s, FAR, c)
        w.got(r, (3, k))
        w.put(r, r, p.n, (4, k), lot=k)
        to_plane(k, FAR)
        to_core(k, s, FAR)

    def nearfar(k):
        w.got(reg(k, s, NEARFAR, c), (4, k))
        to_plane(k, NEARFAR)
        to_core(k, s, NEARFAR)

    def turn(k, u):
        w.got(reg(k, p.sx, u, c), (0, k, u))
        r = reg(k, p.sx, u, c, 0)
        w.put(r, r, p.y, (6, k, u), lot=k)
        to_core(k, p.sx, u)
        w.got(reg(k, p.sy, u, c), (1, k, u))
        r = reg(k, p.sy, u, c, 1)
        w.put(r, r, p.x, (6, k, u), lot=k)
        to_core(k, p.sy, u)

    def corner(k, u):
        w.got(reg(k, p.sd, u, c), (6, k, u))
        to_core(k, p.sd, u)

    def complete(k):
        w.got((wqkv.at[pl.ds(0, 16)], wou.at[pl.ds(0, 16)], wd.at[pl.ds(0, 1536)])[k], (5, k))

    own = reg(0, s, OWN, c)

    def own_out_up(to, key):
        w.put(wu_s, wou.at[slot, :, pl.ds(768, 3072)], to, key, lot=1)
        w.put(wo_s, wou.at[slot, :, pl.ds(0, 768)], to, key, lot=1)

    own_out_up(p.n, (2, 1))
    own_out_up(p.x, (0, 1, OWN))
    own_out_up(p.y, (1, 1, OWN))
    own_out_up(p.f, (3, 1))
    for cp in early:
        cp.wait()
    vec_own, match_own = sc["vo"], sc["mo"]
    vec_own[...] = jnp.zeros_like(vec_own)
    for k, ref in enumerate(vectors):
        vec_own[0:1, 24 * k : 24 * k + ref.shape[0]] = ref[...].astype(F32).reshape(1, ref.shape[0])
    for h in range(2):
        parts = [raw[t, :, 384 * h : 384 * (h + 1)].astype(F32) for t in range(3)]
        stage[h] = jnp.concatenate(parts + [vec_own[...]], axis=0).astype(BF16)
    w.put(stage.at[1 - zp], own, p.n, (2, 0), lot=0)
    w.put(stage.at[zp], own, p.f, (3, 0), lot=0)
    w.put(stage.at[1 - zp], own, p.nf, (4, 0), lot=0)
    w.put(stage.at[zp], own, p.x, (0, 0, OWN), lot=0)
    w.put(stage.at[zp], own, p.y, (1, 0, OWN), lot=0)
    w.put(tok_h.at[1 - g], xg.at[b], p.f, 21)
    w.put(tok_h.at[g], xg.at[b], p.n, 20)
    to_plane(2, OWN, wd_s)
    match_own[...] = jnp.zeros_like(match_own)
    match_own[0:2, 0:12] = cm[...]
    for zz in zs:
        for cc in (c, 1 - c):
            if not (zz is z and cc is c):
                w.put(match_own, match.at[b], (s, zz * 2 + cc), 92, lot=92)
    w.put(tok_h.at[g], xg.at[b], p.core, 23)
    mine += [w.move(stage.at[zp], own), w.move(match_own, match.at[b])]
    dap, ds_buf, p_buf, dqkv = (sc[k] for k in ("dap", "ds", "p", "dqkv"))
    left = lax.broadcasted_iota(jnp.int32, (128, 128), 1) < 64
    zero = jnp.zeros((128, 128), BF16)
    for i in range(4):
        other = 2 * i + 1 - c
        dap[1, other] = zero
        dqkv[0, 1, other] = zero
        for e in range(2):
            ds_buf[1, e, other] = zero
            p_buf[1, e, other] = zero
    for cp in mine:
        cp.wait()
    for k in range(3):
        to_core(k, s, OWN)
    near(1)
    turn(1, OWN)
    far(1)
    z_start(2)
    for u, name in ((NEAR, 2), (FAR, 3), (NEARFAR, 4)):
        w.got(reg(0, s, u, c), (name, 0))
        to_plane(0, u)
        to_core(0, s, u)
    w.got(xg.at[p.bf], 21)
    w.put(xg.at[p.bf], xg.at[p.bf], p.n, 22)
    w.put(xg.at[p.bf], xg.at[p.bf], p.core, 23)
    nearfar(1)
    turn(0, OWN)
    w.got(xg.at[p.bn], 20)
    w.put(xg.at[p.bn], xg.at[p.bn], p.core, 23)
    turn(2, OWN)
    turn(1, NEAR)
    corner(1, OWN)
    for u in (NEAR, FAR, NEARFAR):
        turn(0, u)
    turn(1, FAR)
    for u in range(4):
        corner(0, u)
    w.got(match.at[pl.ds(0, 7)], 92)
    get_match = w.move(match, m_smem)
    w.got(xg.at[p.bnf], 22)
    w.put(xg.at[p.bnf], xg.at[p.bnf], p.core, 23)
    near(2)
    far(2)
    corner(1, NEAR)
    turn(1, NEARFAR)
    complete(0)
    w.got(xg.at[pl.ds(0, 4)], 23)

    lane = lax.broadcasted_iota(jnp.int32, (32, 768), 1)
    mine_lane = ((lane * 2731) >> 16) == lax.broadcasted_iota(jnp.int32, (32, 768), 0)
    lane2 = lax.broadcasted_iota(jnp.int32, (384, 768), 1)
    place = lane2 - 24 * ((lane2 * 2731) >> 16) - lax.broadcasted_iota(jnp.int32, (384, 768), 0)
    flat_vec = wqkv[:, 64:80, :].astype(F32)[:, 8, :].astype(BF16)

    def vector_row(k):
        part = jnp.dot(flat_vec, (place == -24 * k).astype(F32).astype(BF16), preferred_element_type=F32)
        rows[k] = jnp.sum(jnp.where(mine_lane, part, 0.0), axis=0, keepdims=True)

    def up_row(i):
        l3 = lax.broadcasted_iota(jnp.int32, (384, 768), 1) + 768 * i
        d3 = (l3 * 43691) >> 22
        hit = l3 - 96 * d3 - lax.broadcasted_iota(jnp.int32, (384, 768), 0) == -192
        part = jnp.dot(flat_vec, hit.astype(F32).astype(BF16), preferred_element_type=F32)
        owner = ((lax.broadcasted_iota(jnp.int32, (32, 768), 1) + 768 * i) * 43691) >> 22
        here = owner == lax.broadcasted_iota(jnp.int32, (32, 768), 0)
        bup[:, 768 * i : 768 * (i + 1)] = jnp.sum(jnp.where(here, part, 0.0), axis=0, keepdims=True)

    vector_row(0)
    vector_row(1)

    c0 = pl.multiple_of(128 * c, 128)
    b0 = pl.multiple_of(384 * zp + 128 * c, 128)
    b1 = pl.multiple_of(384 * zp + 256, 128)

    columns = sc["cols"]
    for i, v in enumerate((wqkv[:, :, pl.ds(c0, 128)].astype(F32), wqkv[:, :, 256:384].astype(F32))):
        for t in range(3):
            first = 256 * t + 128 * i
            columns[:, first : first + 128] = v[:, 24 * t : 24 * t + 24].reshape(768, 128).astype(BF16)
    for m in range(4):
        r = jnp.dot(xg[2 * m : 2 * m + 2].reshape(256, 768), columns[...], preferred_element_type=F32)
        for t in range(3):
            for tl in range(2):
                part = r[:, 256 * t + 128 * tl : 256 * t + 128 * (tl + 1)]
                if t != 1:
                    part = part + rows[t // 2, :, pl.ds(b1 if tl else b0, 128)]
                qkv[t, tl, 2 * m : 2 * m + 2] = part.astype(BF16).reshape(2, 128, 128)

    get_match.wait()
    att_buf = sc["ab"]

    def mask_head(e, v):
        return jnp.where(left if e == 0 else jnp.logical_not(left), v, zero)

    def weights(e, q, k):
        score = lax.dot_general(mask_head(e, q), k, NT, preferred_element_type=F32) * 0.125
        ex = jnp.exp(score - jnp.max(score, axis=-1, keepdims=True))
        return ex * (1.0 / jnp.sum(ex, axis=-1, keepdims=True))

    def head(tl, e):
        return 6 * zp + (2 * c if tl == 0 else 4) + e

    def attend(tl, blk, i):
        q = qkv[0, tl, blk]
        outs = []
        for e in range(2):
            m = m_smem[blk, g, head(tl, e)]
            pr = weights(e, q, qkv[1, tl, m]).astype(BF16)
            outs.append(jnp.dot(pr, qkv[2, tl, m], preferred_element_type=F32))
        att_buf[i] = jnp.where(left, outs[0], outs[1]).astype(BF16)


    def send_tile(tl, zz, cc, i):
        dst = att.at[g, :, pl.ds(pl.multiple_of(384 * zp + (128 * c if tl == 0 else 256), 128), 128)]
        if i in (0, 8):
            keep.append(w.move(att_buf.at[i], dst))
        else:
            w.put(att_buf.at[i], dst, (s, zz * 2 + cc), 90, lot=90)

    between = (
        lambda: (nearfar(2), corner(2, OWN)), lambda: (turn(2, NEAR), corner(1, FAR)),
        lambda: (corner(1, NEARFAR), turn(2, FAR)), lambda: corner(2, NEAR),
    )
    keep = []
    for j, zz in enumerate((p.zf, p.znf, p.zn, z)):
        trio = [(0, c, 0 if zz is z else 1 + 2 * j), (0, 1 - c, 2 + 2 * j if j < 3 else 7), (1, c, 8 if zz is z else 9 + j)]
        for tl, cc, i in trio:
            attend(tl, zz * 2 + cc, i)
        for tl, cc, i in trio:
            send_tile(tl, zz, cc, i)
        between[j]()
    for k in range(2, 8):
        vector_row(k)
    for i in range(4):
        up_row(i)
    complete(1)

    w.got(att_buf.at[pl.ds(0, 10)], 90)
    for cp in keep + [tok_in, grad_in]:
        cp.wait()

    n1, nlow, act, slope, dh2 = (sc[k] for k in ("n1", "nlow", "act", "slope", "dh2"))
    dtk = sc["dtk"]
    dinner = dtk.reshape(4, 256, 768)

    def whole(ref):
        return ref[...].reshape(256, 768)

    h = whole(tok).astype(F32) + jnp.dot(whole(att), joined(wou[:, :, 0:768]), preferred_element_type=F32) + rows[2]
    h = h - mean(h)
    r1 = lax.rsqrt(mean(h * h) + EPS)
    n1[...] = h * r1
    nlow[...] = (n1[...] * rows[4] + rows[5]).astype(BF16)

    def up(j):
        cols = slice(512 * j, 512 * (j + 1))
        u = jnp.dot(nlow[...], joined(wou[:, :, 768 + 512 * j : 768 + 512 * (j + 1)]), preferred_element_type=F32) + bup[:, cols]
        cdf = 0.5 + 0.5 * lax.erf(u * 0.7071067811865476)
        act[:, cols] = (u * cdf).astype(BF16)
        slope[:, cols] = cdf + u * (jnp.exp(-0.5 * u * u) * 0.3989422804014327)

    up(0)
    up(1)
    up(2)
    turn(2, NEARFAR)
    up(3)
    corner(2, FAR)
    up(4)
    up(5)
    corner(2, NEARFAR)
    complete(2)

    h = jnp.dot(act[...], wd[...], preferred_element_type=F32) + rows[3] + (n1[...] * rows[4] + rows[5])
    h = h - mean(h)
    r2 = lax.rsqrt(mean(h * h) + EPS)
    n2 = h * r2
    result[...] = (n2 * rows[6] + rows[7]).astype(BF16).reshape(2, 128, 768)
    eye = lax.broadcasted_iota(jnp.int32, (128, 128), 0) == lax.broadcasted_iota(jnp.int32, (128, 128), 1)
    keepers = [
        jnp.sum(jnp.where(eye, mask[i : i + 1].astype(F32), 0.0), axis=-1, keepdims=True) for i in range(2)
    ]
    gr = whole(grad).astype(F32) * jnp.concatenate(keepers, axis=0)
    sums = sc["sums"]
    sums[6] = total(gr * n2)
    sums[7] = total(gr)
    e = gr * rows[6]
    d = r2 * (e - mean(e) - n2 * mean(e * n2))
    dh2[...] = d
    dz = sc["dz"]
    dz[...] = d.astype(BF16)
    sums[3] = total(dz[...].astype(F32))

    gd, gu, go, gq, gvec = (sc[k] for k in ("gd", "gu", "go", "gq", "gvec"))

    def down_gradient(ss):
        for i in range(2):
            columns = pl.ds(pl.multiple_of(768 * ss + 384 * i, 128), 384)
            r = lax.dot_general(act[:, columns], dz[...], TN, preferred_element_type=F32)
            gd[ss, 2 * i : 2 * i + 2] = r.astype(BF16).reshape(2, 2, 96, 768)

    chunks = [
        (gd, od, 0, 48, 0, 768),
        (gd, od, 48, 48, 0, 768),
        (gu, ou, 0, 24, 0, 1536),
        (gu, ou, 0, 24, 1536, 1536),
        (go, oo, 0, 24, 0, 768),
        (gvec.reshape(4, 4, 2, 8, 256), ovec, 0, 8, 0, 256),
    ]
    bufs = sc["bufs"]

    def cols(k, half):
        nc = chunks[k][5] // 2
        return pl.ds(half * nc, nc)

    def pair_start(k, which):
        v, out, q0, nr, k0, nc = chunks[k]
        for ss in which:
            src = v.at[ss, :, 1 - c, pl.ds(q0, nr), pl.ds(k0, nc)]
            w.put(src, bufs[k][0].at[ss], p.core, (50 if ss is p.sd else 49, k), lot=50 + k)

    far_column, rest = (p.sd,), (p.sx, p.sy, s)

    def add(k, ss):
        v, out, q0, nr, k0, nc = chunks[k]
        rc = bufs[k][0]

        def one(i):
            rc[ss, i] = rc[ss, i] + v[ss, i, c, q0 : q0 + nr, k0 : k0 + nc]

        loop(4, one)

    def pair_far(k):
        rc, rdx, rdy, rx, ry, rz = bufs[k]
        w.got(rc.at[p.sd], (50, k))
        add(k, p.sd)
        w.put(rc.at[p.sd, :, :, cols(k, 0)], rdx, p.x, (51, k), lot=50 + k)
        w.put(rc.at[p.sd, :, :, cols(k, 1)], rdy, p.y, (52, k), lot=50 + k)

    def pair_rest(k):
        rc, rdx, rdy, rx, ry, rz = bufs[k]
        w.got(rc.at[pl.ds(0, 3)], (49, k))
        add(k, p.sx)
        w.put(rc.at[p.sx, :, :, cols(k, 0)], rx.at[:, :, cols(k, 0)], p.x, (53, k), lot=50 + k)
        add(k, p.sy)
        w.put(rc.at[p.sy, :, :, cols(k, 1)], ry.at[:, :, cols(k, 1)], p.y, (54, k), lot=50 + k)
        add(k, s)

    def diagonal(k):
        rc, rdx, rdy, rx, ry, rz = bufs[k]
        w.got(rdx, (51, k))
        rc[p.sy, :, :, cols(k, 0)] = rc[p.sy, :, :, cols(k, 0)] + rdx[...]
        w.put(rc.at[p.sy, :, :, cols(k, 0)], ry.at[:, :, cols(k, 0)], p.y, (54, k), lot=50 + k)
        w.got(rdy, (52, k))
        rc[p.sx, :, :, cols(k, 1)] = rc[p.sx, :, :, cols(k, 1)] + rdy[...]
        w.put(rc.at[p.sx, :, :, cols(k, 1)], rx.at[:, :, cols(k, 1)], p.x, (53, k), lot=50 + k)

    def plane(k):
        rc, rdx, rdy, rx, ry, rz = bufs[k]
        w.got(rx, (53, k))
        w.got(ry, (54, k))

        def one(i):
            rc[s, i] = (rc[s, i].astype(F32) + rx[i].astype(F32) + ry[i].astype(F32)).astype(rc.dtype)

        loop(4, one)
        w.put(rc.at[s, p.znf], rz.at[0], p.n, (57, k), lot=50 + k)

    def plane_end(k):
        rc, rdx, rdy, rx, ry, rz = bufs[k]
        w.put(rc.at[s, p.zn], rz.at[1], p.n, (58, k), lot=50 + k)

    def last(k):
        rc, rdx, rdy, rx, ry, rz = bufs[k]
        w.got(rz.at[0], (57, k))
        rc[s, p.zf] = rc[s, p.zf] + rz[0]
        w.put(rc.at[s, p.zf], rz.at[2], p.f, (58, k), lot=50 + k)

    def final(k):
        v, out, q0, nr, k0, nc = chunks[k]
        rc, rdx, rdy, rx, ry, rz = bufs[k]
        w.got(rz.at[pl.ds(1, 2)], (58, k))
        out[q0 : q0 + nr, k0 : k0 + nc] = rc[s, z].astype(F32) + rz[1].astype(F32) + rz[2].astype(F32)

    down_gradient(p.sd)
    for k in range(2):
        pair_start(k, far_column)

    def inner_gradient(j):
        cc = slice(768 * j, 768 * (j + 1))
        r = lax.dot_general(dz[...], wd[cc, :], NT, preferred_element_type=F32)
        r = (r * slope[:, cc]).astype(BF16)
        dinner[j] = r
        sc["sup"][:, cc] = total(r.astype(F32))

    for j in range(4):
        inner_gradient(j)
    pair_far(0)
    pair_far(1)
    d = dh2[...]
    for j in range(4):
        wt = joined(wou[:, :, 768 + 768 * j : 768 + 768 * (j + 1)])
        d = d + lax.dot_general(dinner[j], wt, NT, preferred_element_type=F32)
    sums[4] = total(d * n1[...])
    sums[5] = total(d)
    e = d * rows[4]
    d = r1 * (e - mean(e) - n1[...] * mean(e * n1[...]))
    dh1 = dh2
    dh1[...] = d
    dbr = sc["dbr"]
    dbr[...] = d.astype(BF16)
    sums[2] = total(dbr[...].astype(F32))
    datt = sc["datt"]
    r = lax.dot_general(dbr[...], joined(wou[:, :, 0:768]), NT, preferred_element_type=F32)
    datt[...] = r.astype(BF16).reshape(2, 128, 768)

    here = []
    for zz in (p.zf, p.znf, p.zn, z):
        gg, zq = zz // 2, zz % 2
        for tl, cc in ((0, 1 - c), (0, c), (1, c)):
            src = datt.at[gg, :, pl.ds(pl.multiple_of(384 * zq + (256 if tl else 128 * cc), 128), 128)]
            if zz is z and cc is c:
                here.append(w.move(src, dap.at[tl, b]))
            else:
                w.put(src, dap.at[tl, b], (s, zz * 2 + cc), 91, lot=91)

    def up_gradient(j):
        r = lax.dot_general(nlow[...], dinner[j], TN, preferred_element_type=F32)
        gu[:, :, :, :, 768 * j : 768 * (j + 1)] = r.reshape(4, 4, 2, 24, 768).astype(BF16)

    for ss in rest:
        down_gradient(ss)
    for k in range(2):
        pair_start(k, rest)
    r = lax.dot_general(whole(att), dbr[...], TN, preferred_element_type=F32)
    go[...] = r.reshape(4, 4, 2, 24, 768).astype(BF16)
    pair_start(4, far_column)
    pair_start(4, rest)
    pair_rest(0)
    diagonal(0)
    pair_rest(1)
    diagonal(1)
    up_gradient(0)
    up_gradient(1)
    pair_start(2, far_column)
    pair_start(2, rest)
    up_gradient(2)
    up_gradient(3)
    pair_start(3, far_column)
    pair_start(3, rest)
    pair_far(2)
    pair_rest(2)

    vl = lax.broadcasted_iota(jnp.int32, (128, 768), 1)
    spot = (vl - 24 * ((vl * 2731) >> 16) == lax.broadcasted_iota(jnp.int32, (128, 768), 0)).astype(F32).astype(BF16)

    def fold(part, hit):
        high = part.astype(BF16)
        low = (part - high.astype(F32)).astype(BF16)
        return lax.dot_general(high, hit, NT, preferred_element_type=F32) + lax.dot_general(
            low, hit, NT, preferred_element_type=F32
        )

    def fold_rows(lo, n):
        part = jnp.concatenate([jnp.where(mine_lane, sums[k], 0.0) for k in range(lo, lo + n)], axis=0)
        r = fold(part, spot)
        for k in range(n):
            gvec[:, lo + k, 0:128] = r[32 * k : 32 * (k + 1)]

    gvec[:, :, 128:256] = jnp.zeros((32, 8, 128), F32)
    fold_rows(2, 6)
    r = 0.0
    for i in range(4):
        l3 = lax.broadcasted_iota(jnp.int32, (128, 768), 1) + 768 * i
        hit = (l3 - 96 * ((l3 * 43691) >> 22) == lax.broadcasted_iota(jnp.int32, (128, 768), 0)).astype(F32).astype(BF16)
        owner = ((lax.broadcasted_iota(jnp.int32, (32, 768), 1) + 768 * i) * 43691) >> 22
        at = owner == lax.broadcasted_iota(jnp.int32, (32, 768), 0)
        r = r + fold(jnp.where(at, sc["sup"][:, 768 * i : 768 * (i + 1)], 0.0), hit)
    gvec[:, 0, 128:256] = r

    w.got(att_buf.at[pl.ds(0, 10)], 91)
    for cp in here:
        cp.wait()

    def queries(tl, blk):
        q, da = qkv[0, tl, blk], dap[tl, blk]
        outs = []
        for e in range(2):
            m = m_smem[blk, g, head(tl, e)]
            k, v = qkv[1, tl, m], qkv[2, tl, m]
            pr = weights(e, q, k)
            dp = lax.dot_general(mask_head(e, da), v, NT, preferred_element_type=F32)
            ds = (pr * (dp - jnp.sum(pr * dp, axis=-1, keepdims=True))).astype(BF16)
            ds_buf[tl, e, blk] = ds
            p_buf[tl, e, blk] = pr.astype(BF16)
            outs.append(jnp.dot(ds, k, preferred_element_type=F32) * 0.125)
        dqkv[0, tl, blk] = jnp.where(left, outs[0], outs[1]).astype(BF16)

    def keys(tl, n):
        dk, dv = [], []
        for e in range(2):
            cq = 0
            for i in range(8):
                cq = jnp.where(m_smem[i, g, head(tl, e)] == n, i, cq)
            ds, pr = ds_buf[tl, e, cq], p_buf[tl, e, cq]
            dk.append(lax.dot_general(ds, qkv[0, tl, cq], TN, preferred_element_type=F32) * 0.125)
            dv.append(lax.dot_general(pr, dap[tl, cq], TN, preferred_element_type=F32))
        dqkv[1, tl, n] = jnp.where(left, dk[0], dk[1]).astype(BF16)
        dqkv[2, tl, n] = jnp.where(left, dv[0], dv[1]).astype(BF16)

    def both(f, i):
        f(2 * i)
        f(2 * i + 1)

    loop(2, lambda i: both(lambda n: queries(0, n), i))
    plane(0)
    plane_end(0)
    loop(2, lambda i: both(lambda n: queries(0, n), i + 2))
    plane(1)
    plane_end(1)
    loop(2, lambda i: both(lambda n: queries(1, 2 * n + c), i))
    pair_far(4)
    pair_rest(4)
    last(0)
    pair_far(3)
    pair_rest(3)
    loop(4, lambda i: both(lambda n: keys(0, n), i))
    diagonal(2)
    loop(4, lambda i: both(lambda n: keys(1, n), i))

    rtk, rtn, rtf = (sc[k] for k in ("rtk", "rtn", "rtf"))

    def flat(m):
        return jnp.concatenate(
            [dqkv[t, tl, 4 * m : 4 * m + 4].reshape(512, 128) for t in range(3) for tl in range(2)], axis=1
        )

    for m in range(2):
        r = lax.dot_general(flat(m), columns[...], NT, preferred_element_type=F32)
        dtk[2 * m : 2 * m + 2] = r.astype(BF16).reshape(2, 2, 128, 768)
    w.put(dtk.at[:, 1 - c], rtk, p.core, 60)

    rq, accq, rqdx, rqdy, rqx, rqy, rqz = (sc[k] for k in ("rq", "accq", "rqdx", "rqdy", "rqx", "rqy", "rqz"))
    r = 0.0
    for m in range(2):
        x = xg[4 * m : 4 * m + 4].reshape(512, 768)
        r = r + lax.dot_general(x, flat(m), TN, preferred_element_type=F32)
    for t in range(3):
        gq[t] = r[:, 256 * t : 256 * (t + 1)].reshape(4, 4, 2, 24, 256).astype(BF16)
    w.put(gq.at[:, :, :, 1 - c], rq, p.core, 61)
    last(1)
    w.got(rtk, 60)
    loop(4, lambda i: rtk.__setitem__(i, rtk[i] + dtk[i, c]))
    w.put(rtk.at[p.znf], rtn.at[0], p.n, 62)
    w.put(rtk.at[p.zn], rtn.at[1], p.n, 63)

    sums[0] = jnp.zeros((1, 768), F32)
    sums[1] = jnp.zeros((1, 768), F32)
    for r, t in ((0, 0), (1, 2)):
        f = [total(dqkv[t, tl].reshape(1024, 128).astype(F32)) for tl in range(2)]
        sums[r, :, pl.ds(b0, 128)] = f[0]
        sums[r, :, pl.ds(b1, 128)] = f[1]
    fold_rows(0, 2)
    pair_start(5, far_column)
    pair_start(5, rest)

    w.got(rq, 61)
    o0 = pl.multiple_of(128 * (1 - c), 128)

    def pair_q(i):
        for t in range(3):
            for zz in range(4):
                accq[t, i, zz, :, pl.ds(c0, 128)] = gq[t, i, zz, c, :, 0:128]
                accq[t, i, zz, :, pl.ds(o0, 128)] = rq[t, i, zz, :, 0:128]
                accq[t, i, zz, :, 256:384] = gq[t, i, zz, c, :, 128:256] + rq[t, i, zz, :, 128:256]

    pair_q(p.sd)
    w.put(accq.at[:, p.sd, :, :, pl.ds(0, 256)], rqdx, p.x, 64)
    w.put(accq.at[:, p.sd, :, :, pl.ds(256, 128)], rqdy, p.y, 65)
    diagonal(4)
    pair_far(5)
    pair_q(p.sx)
    pair_q(p.sy)
    pair_q(s)
    pair_rest(5)
    w.got(rtn.at[0], 62)
    rtk[p.zf] = rtk[p.zf] + rtn[0]
    w.put(rtk.at[p.zf], rtf, p.f, 68)
    diagonal(3)
    plane(2)
    plane_end(2)
    w.got(rqdx, 64)
    accq[:, p.sy, :, :, 0:256] = accq[:, p.sy, :, :, 0:256] + rqdx[...]
    w.put(accq.at[:, p.sy], rqy, p.y, 66)
    w.got(rqdy, 65)
    accq[:, p.sx, :, :, 256:384] = accq[:, p.sx, :, :, 256:384] + rqdy[...]
    w.put(accq.at[:, p.sx], rqx, p.x, 67)
    diagonal(5)
    plane(4)
    plane_end(4)
    last(2)
    final(0)
    final(1)
    plane(3)
    last(4)
    w.got(rqx, 67)
    w.got(rqy, 66)
    for t in range(3):
        accq[t, s] = (accq[t, s].astype(F32) + rqx[t].astype(F32) + rqy[t].astype(F32)).astype(BF16)
    w.put(accq.at[:, s, p.znf], rqz.at[0], p.f, 80)
    plane(5)
    last(3)
    w.got(rqz.at[0], 80)
    accq[:, s, p.zn] = accq[:, s, p.zn] + rqz[0]
    w.put(accq.at[:, s, p.zn], rqz.at[2], p.n, 82)
    plane_end(3)
    w.put(accq.at[:, s, p.zf], rqz.at[1], p.f, 81)
    plane_end(5)
    last(5)
    final(2)
    final(4)
    final(3)
    w.got(rtn.at[1], 63)
    w.got(rtf, 68)
    d = dh1[...].reshape(2, 128, 768)
    dtok[...] = d
    dtok[g] = dtok[g] + rtk[z].astype(F32) + rtn[1].astype(F32)
    dtok[1 - g] = dtok[1 - g] + rtf[...].astype(F32)
    w.got(rqz.at[1], 81)
    q0 = pl.multiple_of(384 * zp, 128)
    q1 = pl.multiple_of(384 * (1 - zp), 128)
    for t in range(3):
        oqkv[t, :, pl.ds(q0, 384)] = accq[t, s, z].astype(F32) + rqz[1, t].astype(F32)
    w.got(rqz.at[2], 82)
    for t in range(3):
        oqkv[t, :, pl.ds(q1, 384)] = rqz[2, t].astype(F32)
    final(5)
    w.finish({
        0: wqkv.at[pl.ds(0, 31)], 1: wou.at[pl.ds(0, 31)], 2: wd.at[pl.ds(0, 2976)],
        50: wd.at[pl.ds(0, 1488)], 51: wd.at[pl.ds(0, 1488)],
        52: wou.at[pl.ds(0, 31), :, pl.ds(0, 1536)], 53: wou.at[pl.ds(0, 31), :, pl.ds(0, 1536)],
        54: wou.at[pl.ds(0, 31), :, pl.ds(0, 768)], 55: gvec.at[pl.ds(0, 31)],
        90: att_buf.at[pl.ds(0, 10)], 91: att_buf.at[pl.ds(0, 10)], 92: match.at[pl.ds(0, 7)],
    })


def scratch():
    VM = pltpu.VMEM
    per_chunk = []
    for nr, nc in ((48, 768), (48, 768), (24, 1536), (24, 1536), (24, 768), (8, 256)):
        kind = F32 if nr == 8 else BF16
        shapes = ((4, 4, nr, nc), (4, nr, nc // 2), (4, nr, nc // 2), (4, nr, nc), (4, nr, nc), (3, nr, nc))
        per_chunk.append(tuple(VM(shape, kind) for shape in shapes))
    return dict(
        wou=VM((32, 24, 3840), BF16), wd=VM((3072, 768), BF16), wqkv=VM((32, 80, 384), BF16), raw=VM((3, 24, 768), BF16),
        cols=VM((768, 768), BF16), gvec=VM((32, 8, 256), F32),
        xg=VM((8, 128, 768), BF16), qkv=VM((3, 2, 8, 128, 128), BF16), att=VM((2, 128, 768), BF16),
        match=VM((8, 8, 128), jnp.int32), ms=pltpu.SMEM((8, 8, 128), jnp.int32),
        stage=VM((2, 80, 384), BF16), rows=VM((8, 1, 768), F32), bup=VM((1, 3072), F32),
        tok=VM((2, 128, 768), BF16), grad=VM((2, 128, 768), BF16), vo=VM((8, 384), F32), mo=VM((8, 128), jnp.int32),
        ab=VM((12, 128, 128), BF16), dap=VM((2, 8, 128, 128), BF16), ds=VM((2, 2, 8, 128, 128), BF16),
        p=VM((2, 2, 8, 128, 128), BF16), dqkv=VM((3, 2, 8, 128, 128), BF16),
        n1=VM((256, 768), F32), nlow=VM((256, 768), BF16), act=VM((256, 3072), BF16), slope=VM((256, 3072), F32),
        dh2=VM((256, 768), F32), sums=VM((8, 1, 768), F32), sup=VM((1, 3072), F32),
        dz=VM((256, 768), BF16), dbr=VM((256, 768), BF16), datt=VM((2, 128, 768), BF16),
        gd=VM((4, 4, 2, 96, 768), BF16), gu=VM((4, 4, 2, 24, 3072), BF16), go=VM((4, 4, 2, 24, 768), BF16),
        gq=VM((3, 4, 4, 2, 24, 256), BF16), rq=VM((3, 4, 4, 24, 256), BF16), accq=VM((3, 4, 4, 24, 384), BF16),
        dtk=VM((4, 2, 128, 768), BF16), rtk=VM((4, 128, 768), BF16), rtn=VM((2, 128, 768), BF16), rtf=VM((128, 768), BF16),
        rqdx=VM((3, 4, 24, 256), BF16), rqdy=VM((3, 4, 24, 128), BF16), rqx=VM((3, 4, 24, 384), BF16),
        rqy=VM((3, 4, 24, 384), BF16), rqz=VM((3, 3, 24, 384), BF16), bufs=tuple(per_chunk),
    )


def hand_out(result, od, ou, oo, oqkv, dtok, ovec, *rest):
    outs, sem, lines = rest[:17], rest[17], rest[18:]
    pairs = [(dtok.at[i, pl.ds(64 * j, 64)], outs[1].at[i, pl.ds(64 * j, 64)]) for i in range(2) for j in range(2)]
    pairs += [(result.at[i], outs[0].at[i]) for i in range(2)]
    pairs += [(ou.at[:, pl.ds(1536 * i, 1536)], outs[6].at[:, pl.ds(1536 * i, 1536)]) for i in range(2)]
    pairs += [(od.at[pl.ds(48 * i, 48)], outs[7].at[pl.ds(48 * i, 48)]) for i in range(2)]
    pairs += [(oqkv.at[0], outs[2]), (oqkv.at[1], outs[3]), (oqkv.at[2], outs[4]), (oo, outs[5])]
    copies = [pltpu.make_async_copy(a, o, sem.at[i]) for i, (a, o) in enumerate(pairs)]
    for cp in copies:
        cp.start()
    for i, (row, line) in enumerate(zip((0, 1, 2, None, 3, 4, 5, 6, 7), lines, strict=True)):
        line[...] = ovec[0, 128:224] if row is None else ovec[row, 0:24]
        cp = pltpu.make_async_copy(line, outs[8 + i], sem.at[14 + i])
        cp.start()
        copies.append(cp)
    for cp in copies:
        cp.wait()


def column(
    tokens, grad_out, masked, token_order, cluster_match,
    w_query, w_key, w_value, w_out, w_up, w_down,
    b_query, b_value, b_out, b_up, b_down,
    gain_attn, shift_attn, gain_ffn, shift_ffn,
):
    V = pl.BlockSpec(memory_space=pltpu.VMEM)
    A = pl.BlockSpec(memory_space=pl.ANY)
    S = jax.ShapeDtypeStruct
    vectors = (b_query, b_value, b_out, b_down, gain_attn, shift_attn, gain_ffn, shift_ffn, b_up)
    got = pl.pallas_call(
        layer_kernel,
        out_shape=(
            S((2, 128, 768), BF16), S((96, 768), F32), S((24, 3072), F32), S((24, 768), F32), S((3, 24, 768), F32),
            S((2, 128, 768), F32), S((8, 256), F32),
        ),
        in_specs=[A, A, V, V] + [A] * 6 + [V] * 9,
        out_specs=(V,) * 7,
        scratch_shapes=[scratch(), *(pltpu.SemaphoreType.DMA((n,)) for n in (31, 115, 16))],
        compiler_params=pltpu.CompilerParams(collective_id=0, has_side_effects=True, vmem_limit_bytes=62 << 20),
        name="layer",
    )(tokens, grad_out, masked, cluster_match.reshape(2, 12), w_query, w_key, w_value, w_out, w_up, w_down, *vectors)
    square = S((24, 768), F32)
    outs = (S((2, 128, 768), BF16), S((2, 128, 768), F32)) + (square,) * 4 + (S((24, 3072), F32), S((96, 768), F32))
    outs += tuple(S((n,), F32) for n in (24, 24, 24, 96, 24, 24, 24, 24, 24))
    return pl.pallas_call(
        hand_out,
        out_shape=outs,
        in_specs=[V] * 7,
        out_specs=(A,) * 17,
        scratch_shapes=[pltpu.SemaphoreType.DMA((23,))] + [pltpu.VMEM((96 if i == 3 else 24,), F32) for i in range(9)],
        name="results",
    )(*got)


def solution(mesh):
    fits = mesh.shape[SEQ] == 4 and mesh.shape[BLK] == 8
    return jax.shard_map(
        column if fits else general,
        mesh=mesh,
        in_specs=(
            P(SEQ, BLK, None),
            P(SEQ, BLK, None),
            P(SEQ, BLK),
            P(SEQ, None, BLK),
            P(SEQ, None, BLK),
            P(BOTH, None),
            P(BOTH, None),
            P(BOTH, None),
            P(BOTH, None),
            P(BOTH, None),
            P(BOTH, None),
            P(BOTH),
            P(BOTH),
            P(BOTH),
            P(BOTH),
            P(BOTH),
            P(BOTH),
            P(BOTH),
            P(BOTH),
            P(BOTH),
        ),
        out_specs=(
            P(SEQ, BLK, None),
            P(SEQ, BLK, None),
            P(BOTH, None),
            P(BOTH, None),
            P(BOTH, None),
            P(BOTH, None),
            P(BOTH, None),
            P(BOTH, None),
            P(BOTH),
            P(BOTH),
            P(BOTH),
            P(BOTH),
            P(BOTH),
            P(BOTH),
            P(BOTH),
            P(BOTH),
            P(BOTH),
        ),
        check_vma=False,
    )
```

```python
import functools
import math

import jax
import jax.numpy as jnp
from jax import lax
from jax.experimental import pallas as pl
from jax.experimental.pallas import tpu as pltpu
from jax.sharding import PartitionSpec as P

HEADS = 12
CL = 128
EPS = 1e-05
MESH = pl.DeviceIdType.MESH
SEQ, BLK = BOTH = ("seq", "blk")
F32 = jnp.float32
BF16 = jnp.bfloat16


def norm_rows(hidden, gain_row, shift_row):
    row_mean = jnp.mean(hidden, axis=-1, keepdims=True)
    centered = hidden - row_mean
    variance = jnp.mean(centered * centered, axis=-1, keepdims=True)
    return centered * lax.rsqrt(variance + EPS) * gain_row + shift_row


def gelu_exact(inner_sum):
    return jax.nn.gelu(inner_sum, approximate=False)


def to_heads(flat_rows, groups, local_len):
    return flat_rows.reshape(groups, local_len, HEADS, -1).transpose(0, 2, 1, 3)


def from_heads(head_rows):
    groups, head_count, local_len, head_dim = head_rows.shape
    return head_rows.transpose(0, 2, 1, 3).reshape(groups * local_len, head_count * head_dim)


def reorder(head_rows, positions):
    return jnp.take_along_axis(head_rows, positions[..., None], axis=2)


def general(
    tokens,
    grad_out,
    masked,
    token_order,
    cluster_match,
    w_query,
    w_key,
    w_value,
    w_out,
    w_up,
    w_down,
    b_query,
    b_value,
    b_out,
    b_up,
    b_down,
    gain_attn,
    shift_attn,
    gain_ffn,
    shift_ffn,
):
    groups, local_len, width = tokens.shape
    row_count = groups * local_len
    head_dim = width // HEADS
    clusters = local_len // CL
    score_scale = 1.0 / math.sqrt(head_dim)
    gathered = (
        lax.all_gather(w_query, BOTH, axis=0, tiled=True),
        lax.all_gather(w_key, BOTH, axis=0, tiled=True),
        lax.all_gather(w_value, BOTH, axis=0, tiled=True),
        lax.all_gather(w_out, BOTH, axis=0, tiled=True),
        lax.all_gather(w_up, BOTH, axis=0, tiled=True),
        lax.all_gather(w_down, BOTH, axis=0, tiled=True),
        lax.all_gather(b_query, BOTH, axis=0, tiled=True),
        lax.all_gather(b_value, BOTH, axis=0, tiled=True),
        lax.all_gather(b_out, BOTH, axis=0, tiled=True),
        lax.all_gather(b_up, BOTH, axis=0, tiled=True),
        lax.all_gather(b_down, BOTH, axis=0, tiled=True),
        lax.all_gather(gain_attn, BOTH, axis=0, tiled=True),
        lax.all_gather(shift_attn, BOTH, axis=0, tiled=True),
        lax.all_gather(gain_ffn, BOTH, axis=0, tiled=True),
        lax.all_gather(shift_ffn, BOTH, axis=0, tiled=True),
    )
    (
        full_query,
        full_key,
        full_value,
        full_out,
        full_up,
        full_down,
        bias_query,
        bias_value,
        bias_out,
        bias_up,
        bias_down,
        norm_gain1,
        norm_shift1,
        norm_gain2,
        norm_shift2,
    ) = gathered
    flat_tokens = tokens.reshape(row_count, width)
    inverse = jnp.argsort(token_order, axis=-1)
    cluster_shape = (groups, HEADS, clusters, CL, head_dim)
    query_low = (
        jnp.dot(flat_tokens, full_query, preferred_element_type=jnp.float32)
        + bias_query.astype(jnp.float32)
    ).astype(jnp.bfloat16)
    key_low = jnp.dot(flat_tokens, full_key, preferred_element_type=jnp.float32).astype(
        jnp.bfloat16
    )
    value_low = (
        jnp.dot(flat_tokens, full_value, preferred_element_type=jnp.float32)
        + bias_value.astype(jnp.float32)
    ).astype(jnp.bfloat16)
    query_perm = reorder(to_heads(query_low, groups, local_len), token_order).reshape(cluster_shape)
    key_perm = reorder(to_heads(key_low, groups, local_len), token_order).reshape(cluster_shape)
    value_perm = reorder(to_heads(value_low, groups, local_len), token_order).reshape(cluster_shape)
    empty_sel = jnp.zeros(cluster_shape, jnp.bfloat16)
    key_piece = lax.all_gather(key_perm, BLK, axis=2, tiled=True)
    value_piece = lax.all_gather(value_perm, BLK, axis=2, tiled=True)
    piece_len = key_piece.shape[2]
    offset = cluster_match
    select = (offset[..., None] == jnp.arange(piece_len, dtype=jnp.int32)).astype(jnp.bfloat16)
    inside = ((offset >= 0) & (offset < piece_len))[..., None, None]
    new_keys = jnp.einsum(
        "ghcj,ghjkd->ghckd", select, key_piece, preferred_element_type=jnp.float32
    ).astype(jnp.bfloat16)
    new_values = jnp.einsum(
        "ghcj,ghjkd->ghckd", select, value_piece, preferred_element_type=jnp.float32
    ).astype(jnp.bfloat16)
    key_sel = jnp.where(inside, new_keys, empty_sel)
    value_sel = jnp.where(inside, new_values, empty_sel)
    scores = (
        jnp.einsum("ghcqd,ghckd->ghcqk", query_perm, key_sel, preferred_element_type=jnp.float32)
        * score_scale
    )
    row_max = jnp.max(scores, axis=-1, keepdims=True)
    log_total = row_max + jnp.log(jnp.sum(jnp.exp(scores - row_max), axis=-1, keepdims=True))
    attn_probs = jnp.exp(scores - log_total)
    probs_low = attn_probs.astype(jnp.bfloat16)
    mixed_perm = jnp.einsum(
        "ghcqk,ghckd->ghcqd", probs_low, value_sel, preferred_element_type=jnp.float32
    ).reshape(groups, HEADS, local_len, head_dim)
    attended = from_heads(reorder(mixed_perm, inverse)).astype(jnp.bfloat16)
    branch = jnp.dot(attended, full_out, preferred_element_type=jnp.float32) + bias_out.astype(
        jnp.float32
    )
    resid = flat_tokens.astype(jnp.float32) + branch
    normed, pull_first = jax.vjp(
        norm_rows, resid, norm_gain1.astype(jnp.float32), norm_shift1.astype(jnp.float32)
    )
    normed_low = normed.astype(jnp.bfloat16)
    inner_sum = jnp.dot(normed_low, full_up, preferred_element_type=jnp.float32) + bias_up.astype(
        jnp.float32
    )
    active, pull_gelu = jax.vjp(gelu_exact, inner_sum)
    active_low = active.astype(jnp.bfloat16)
    outer_sum = jnp.dot(
        active_low, full_down, preferred_element_type=jnp.float32
    ) + bias_down.astype(jnp.float32)
    final_rows, pull_second = jax.vjp(
        norm_rows,
        normed + outer_sum,
        norm_gain2.astype(jnp.float32),
        norm_shift2.astype(jnp.float32),
    )
    result = final_rows.astype(jnp.bfloat16).reshape(groups, local_len, width)
    back_weights = (
        lax.all_gather(w_query, BOTH, axis=0, tiled=True),
        lax.all_gather(w_key, BOTH, axis=0, tiled=True),
        lax.all_gather(w_value, BOTH, axis=0, tiled=True),
        lax.all_gather(w_out, BOTH, axis=0, tiled=True),
        lax.all_gather(w_up, BOTH, axis=0, tiled=True),
        lax.all_gather(w_down, BOTH, axis=0, tiled=True),
        lax.all_gather(b_query, BOTH, axis=0, tiled=True),
        lax.all_gather(b_value, BOTH, axis=0, tiled=True),
        lax.all_gather(b_out, BOTH, axis=0, tiled=True),
        lax.all_gather(b_up, BOTH, axis=0, tiled=True),
        lax.all_gather(b_down, BOTH, axis=0, tiled=True),
        lax.all_gather(gain_attn, BOTH, axis=0, tiled=True),
        lax.all_gather(shift_attn, BOTH, axis=0, tiled=True),
        lax.all_gather(gain_ffn, BOTH, axis=0, tiled=True),
        lax.all_gather(shift_ffn, BOTH, axis=0, tiled=True),
    )
    back_query, back_key, back_value, back_out, back_up, back_down = back_weights[:6]
    upstream = grad_out.reshape(row_count, width).astype(jnp.float32) * masked.reshape(
        row_count, 1
    ).astype(jnp.float32)
    d_sum2, d_gain2, d_shift2 = pull_second(upstream)
    d_outer = d_sum2.astype(jnp.bfloat16)
    g_down = jnp.einsum("rf,rd->fd", active_low, d_outer, preferred_element_type=jnp.float32)
    g_bdown = jnp.sum(d_outer.astype(jnp.float32), axis=0)
    d_active = jnp.einsum("rd,fd->rf", d_outer, back_down, preferred_element_type=jnp.float32)
    d_inner = pull_gelu(d_active)[0].astype(jnp.bfloat16)
    g_up = jnp.einsum("rd,rf->df", normed_low, d_inner, preferred_element_type=jnp.float32)
    g_bup = jnp.sum(d_inner.astype(jnp.float32), axis=0)
    d_normed = d_sum2 + jnp.einsum(
        "rf,df->rd", d_inner, back_up, preferred_element_type=jnp.float32
    )
    d_resid, d_gain1, d_shift1 = pull_first(d_normed)
    d_branch = d_resid.astype(jnp.bfloat16)
    g_out = jnp.einsum("ri,rd->id", attended, d_branch, preferred_element_type=jnp.float32)
    g_bout = jnp.sum(d_branch.astype(jnp.float32), axis=0)
    d_attended = jnp.einsum(
        "rd,id->ri", d_branch, back_out, preferred_element_type=jnp.float32
    ).astype(jnp.bfloat16)
    d_mixed = reorder(to_heads(d_attended, groups, local_len), token_order).reshape(cluster_shape)
    scores_again = (
        jnp.einsum("ghcqd,ghckd->ghcqk", query_perm, key_sel, preferred_element_type=jnp.float32)
        * score_scale
    )
    probs_again = jnp.exp(scores_again - log_total)
    probs_again_low = probs_again.astype(jnp.bfloat16)
    d_probs = jnp.einsum(
        "ghcqd,ghckd->ghcqk", d_mixed, value_sel, preferred_element_type=jnp.float32
    )
    d_scores = (
        probs_again * (d_probs - jnp.sum(probs_again * d_probs, axis=-1, keepdims=True))
    ).astype(jnp.bfloat16)
    d_query_perm = (
        jnp.einsum("ghcqk,ghckd->ghcqd", d_scores, key_sel, preferred_element_type=jnp.float32)
        * score_scale
    )
    d_key_sel = (
        jnp.einsum("ghcqk,ghcqd->ghckd", d_scores, query_perm, preferred_element_type=jnp.float32)
        * score_scale
    )
    d_value_sel = jnp.einsum(
        "ghcqk,ghcqd->ghckd", probs_again_low, d_mixed, preferred_element_type=jnp.float32
    )
    sent = jnp.concatenate([d_key_sel, d_value_sel], axis=-1)
    my_start = lax.axis_index(BLK) * clusters
    piece_grads = lax.all_gather(sent.astype(jnp.bfloat16), BLK, axis=2, tiled=True).astype(
        jnp.float32
    )
    piece_match = lax.all_gather(
        cluster_match.astype(jnp.float32).astype(jnp.bfloat16), BLK, axis=2, tiled=True
    ).astype(jnp.float32)
    offset = piece_match.astype(jnp.int32) - my_start
    select = (offset[..., None] == jnp.arange(clusters, dtype=jnp.int32)).astype(jnp.float32)
    owned = jnp.zeros(sent.shape, jnp.float32) + jnp.einsum(
        "ghjc,ghjke->ghcke", select, piece_grads, precision=lax.Precision.HIGHEST
    )
    back_kv = reorder(owned.reshape(groups, HEADS, local_len, 2 * head_dim), inverse)
    d_key = from_heads(back_kv[..., :head_dim]).astype(jnp.bfloat16)
    d_value = from_heads(back_kv[..., head_dim:]).astype(jnp.bfloat16)
    d_query = from_heads(
        reorder(d_query_perm.reshape(groups, HEADS, local_len, head_dim), inverse)
    ).astype(jnp.bfloat16)
    g_query = jnp.einsum("ri,rd->id", flat_tokens, d_query, preferred_element_type=jnp.float32)
    g_key = jnp.einsum("ri,rd->id", flat_tokens, d_key, preferred_element_type=jnp.float32)
    g_value = jnp.einsum("ri,rd->id", flat_tokens, d_value, preferred_element_type=jnp.float32)
    g_bquery = jnp.sum(d_query.astype(jnp.float32), axis=0)
    g_bvalue = jnp.sum(d_value.astype(jnp.float32), axis=0)
    d_tokens_flat = (
        d_resid
        + jnp.einsum("rd,id->ri", d_query, back_query, preferred_element_type=jnp.float32)
        + jnp.einsum("rd,id->ri", d_key, back_key, preferred_element_type=jnp.float32)
        + jnp.einsum("rd,id->ri", d_value, back_value, preferred_element_type=jnp.float32)
    )
    summed = (
        lax.psum_scatter(g_query, BOTH, scatter_dimension=0, tiled=True),
        lax.psum_scatter(g_key, BOTH, scatter_dimension=0, tiled=True),
        lax.psum_scatter(g_value, BOTH, scatter_dimension=0, tiled=True),
        lax.psum_scatter(g_out, BOTH, scatter_dimension=0, tiled=True),
        lax.psum_scatter(g_up, BOTH, scatter_dimension=0, tiled=True),
        lax.psum_scatter(g_down, BOTH, scatter_dimension=0, tiled=True),
        lax.psum_scatter(g_bquery, BOTH, scatter_dimension=0, tiled=True),
        lax.psum_scatter(g_bvalue, BOTH, scatter_dimension=0, tiled=True),
        lax.psum_scatter(g_bout, BOTH, scatter_dimension=0, tiled=True),
        lax.psum_scatter(g_bup, BOTH, scatter_dimension=0, tiled=True),
        lax.psum_scatter(g_bdown, BOTH, scatter_dimension=0, tiled=True),
        lax.psum_scatter(d_gain1, BOTH, scatter_dimension=0, tiled=True),
        lax.psum_scatter(d_shift1, BOTH, scatter_dimension=0, tiled=True),
        lax.psum_scatter(d_gain2, BOTH, scatter_dimension=0, tiled=True),
        lax.psum_scatter(d_shift2, BOTH, scatter_dimension=0, tiled=True),
    )
    return (result, d_tokens_flat.reshape(groups, local_len, width)) + tuple(summed)


OWN, NEAR, FAR, NEARFAR = range(4)
NT = (((1,), (1,)), ((), ()))
TN = (((0,), (0,)), ((), ()))


class Place:
    def __init__(self):
        s, b = lax.axis_index(SEQ), lax.axis_index(BLK)
        self.s, self.b = s, b
        z, c = b // 2, b % 2
        self.z, self.c = z, c
        self.zlo, self.zhi = z % 2, z // 2
        self.sx = s + 1 - 2 * (s % 2)
        self.sy = s + 2 - 4 * (s // 2)
        self.sd = self.sy + 1 - 2 * (s % 2)
        self.zn = z + 1 - 2 * self.zlo
        self.zf = z + 2 - 4 * self.zhi
        self.znf = self.zf + 1 - 2 * self.zlo
        self.bc = b + 1 - 2 * c
        self.bn, self.bf, self.bnf = self.zn * 2 + c, self.zf * 2 + c, self.znf * 2 + c
        self.core = (s, self.bc)
        self.n = (s, self.bn)
        self.f = (s, self.bf)
        self.nf = (s, self.bnf)
        self.x = (self.sx, b)
        self.y = (self.sy, b)


class Wire:
    def __init__(self, send, recv, local):
        self.send, self.recv, self.local = send, recv, local
        self.n_send = self.n_local = self.n_recv = 0
        self.sent, self.slots, self.lots = [], {}, {}

    def slot(self, key):
        if key not in self.slots:
            self.slots[key] = self.n_recv
            self.n_recv += 1
        return self.slots[key]

    def put(self, src, dst, to, key, lot=None):
        at = self.slot(key)
        if lot is None or lot not in self.lots:
            index = self.n_send
            self.n_send += 1
            if lot is not None:
                self.lots[lot] = index
        else:
            index = self.lots[lot]
        cp = pltpu.make_async_remote_copy(
            src, dst, self.send.at[index], self.recv.at[at], device_id=to, device_id_type=MESH
        )
        cp.start()
        if lot is None:
            self.sent.append(cp)

    def got(self, dst, key):
        at = self.slot(key)
        pltpu.make_async_copy(dst, dst, self.recv.at[at]).wait()

    def move(self, src, dst):
        cp = pltpu.make_async_copy(src, dst, self.local.at[self.n_local])
        self.n_local += 1
        cp.start()
        return cp

    def finish(self, sizes):
        for lot, ref in sizes.items():
            pltpu.make_async_copy(ref, ref, self.send.at[self.lots[lot]]).wait()
        for cp in self.sent:
            cp.wait_send()


def greet(peers):
    bar = pltpu.get_barrier_semaphore()
    for to in peers:
        pl.semaphore_signal(bar, inc=1, device_id=to, device_id_type=MESH)
    pl.semaphore_wait(bar, len(peers))


def loop(n, body):
    def run(i, carry):
        body(i)
        return carry

    lax.fori_loop(0, n, run, 0)


def joined(v):
    return v.astype(F32).reshape(768, v.shape[-1]).astype(BF16)


def mean(v):
    return jnp.mean(v, axis=-1, keepdims=True)


def total(v):
    return jnp.sum(v, axis=0, keepdims=True)


def layer_kernel(
    tok_h, go_h, mask, cm, wq, wk, wv, wo_s, wu_s, wd_s,
    *others,
):
    vectors, (result, od, ou, oo, oqkv, dtok, ovec, sc, *sems) = others[:9], others[9:]
    p = Place()
    w = Wire(*sems)
    s, b, z, c = p.s, p.b, p.z, p.c
    zp, g = p.zlo, p.zhi
    zs = (z, p.zn, p.zf, p.znf)
    wou, wd, wqkv, xg, qkv, att = (sc[k] for k in ("wou", "wd", "wqkv", "xg", "qkv", "att"))
    match, m_smem, stage, rows, bup = (sc[k] for k in ("match", "ms", "stage", "rows", "bup"))

    raw = sc["raw"]
    early = [w.move(ref, raw.at[t]) for t, ref in enumerate((wq, wk, wv))]
    tok, grad = sc["tok"], sc["grad"]
    slot = s * 8 + b
    mine = [
        w.move(wo_s, wou.at[slot, :, pl.ds(0, 768)]), w.move(wu_s, wou.at[slot, :, pl.ds(768, 3072)]),
        w.move(wd_s, wd.at[pl.ds(pl.multiple_of(96 * slot, 96), 96)]), w.move(tok_h.at[g], xg.at[b]),
    ]
    tok_in, grad_in = w.move(tok_h, tok), w.move(go_h, grad)
    greet([p.core, p.n, p.f, p.nf, p.x, p.y, (s, p.zn * 2 + 1 - c), (s, p.zf * 2 + 1 - c), (s, p.znf * 2 + 1 - c)])

    def at_rows(n, ss, zz, cc):
        return pl.ds(pl.multiple_of(n * (ss * 8 + zz * 2 + cc), 8), n)

    def reg(k, ss, u, cc, half=None):
        zz = zs[u]
        if k == 0:
            cols = (pl.ds(0, 384), pl.ds(0, 256), pl.ds(256, 128))[0 if half is None else 1 + half]
            return wqkv.at[ss * 8 + zz * 2 + cc, :, cols]
        if k == 1:
            cols = pl.ds(0, 3840) if half is None else pl.ds(1920 * half, 1920)
            return wou.at[ss * 8 + zz * 2 + cc, :, cols]
        cols = pl.ds(0, 768) if half is None else pl.ds(384 * half, 384)
        return wd.at[at_rows(96, ss, zz, cc), cols]

    def to_plane(k, u, src=None):
        r = reg(k, s, u, c)
        src = r if src is None else src
        w.put(src, r, p.x, (0, k, u), lot=k)
        w.put(src, r, p.y, (1, k, u), lot=k)

    def to_core(k, ss, u):
        r = reg(k, ss, u, c)
        w.put(r, r, p.core, (5, k), lot=k)

    def z_start(k):
        r = reg(k, s, OWN, c)
        w.put(r, r, p.n, (2, k), lot=k)
        w.put(r, r, p.f, (3, k), lot=k)

    def near(k):
        w.got(reg(k, s, NEAR, c), (2, k))
        to_plane(k, NEAR)
        to_core(k, s, NEAR)

    def far(k):
        r = reg(k, s, FAR, c)
        w.got(r, (3, k))
        w.put(r, r, p.n, (4, k), lot=k)
        to_plane(k, FAR)
        to_core(k, s, FAR)

    def nearfar(k):
        w.got(reg(k, s, NEARFAR, c), (4, k))
        to_plane(k, NEARFAR)
        to_core(k, s, NEARFAR)

    def turn(k, u):
        w.got(reg(k, p.sx, u, c), (0, k, u))
        r = reg(k, p.sx, u, c, 0)
        w.put(r, r, p.y, (6, k, u), lot=k)
        to_core(k, p.sx, u)
        w.got(reg(k, p.sy, u, c), (1, k, u))
        r = reg(k, p.sy, u, c, 1)
        w.put(r, r, p.x, (6, k, u), lot=k)
        to_core(k, p.sy, u)

    def corner(k, u):
        w.got(reg(k, p.sd, u, c), (6, k, u))
        to_core(k, p.sd, u)

    def complete(k):
        w.got((wqkv.at[pl.ds(0, 16)], wou.at[pl.ds(0, 16)], wd.at[pl.ds(0, 1536)])[k], (5, k))

    own = reg(0, s, OWN, c)

    def own_out_up(to, key):
        w.put(wu_s, wou.at[slot, :, pl.ds(768, 3072)], to, key, lot=1)
        w.put(wo_s, wou.at[slot, :, pl.ds(0, 768)], to, key, lot=1)

    own_out_up(p.n, (2, 1))
    own_out_up(p.x, (0, 1, OWN))
    own_out_up(p.y, (1, 1, OWN))
    own_out_up(p.f, (3, 1))
    for cp in early:
        cp.wait()
    vec_own, match_own = sc["vo"], sc["mo"]
    vec_own[...] = jnp.zeros_like(vec_own)
    for k, ref in enumerate(vectors):
        vec_own[0:1, 24 * k : 24 * k + ref.shape[0]] = ref[...].astype(F32).reshape(1, ref.shape[0])
    for h in range(2):
        parts = [raw[t, :, 384 * h : 384 * (h + 1)].astype(F32) for t in range(3)]
        stage[h] = jnp.concatenate(parts + [vec_own[...]], axis=0).astype(BF16)
    w.put(stage.at[1 - zp], own, p.n, (2, 0), lot=0)
    w.put(stage.at[zp], own, p.f, (3, 0), lot=0)
    w.put(stage.at[1 - zp], own, p.nf, (4, 0), lot=0)
    w.put(stage.at[zp], own, p.x, (0, 0, OWN), lot=0)
    w.put(stage.at[zp], own, p.y, (1, 0, OWN), lot=0)
    w.put(tok_h.at[1 - g], xg.at[b], p.f, 21)
    w.put(tok_h.at[g], xg.at[b], p.n, 20)
    to_plane(2, OWN, wd_s)
    match_own[...] = jnp.zeros_like(match_own)
    match_own[0:2, 0:12] = cm[...]
    for zz in zs:
        for cc in (c, 1 - c):
            if not (zz is z and cc is c):
                w.put(match_own, match.at[b], (s, zz * 2 + cc), 92, lot=92)
    w.put(tok_h.at[g], xg.at[b], p.core, 23)
    mine += [w.move(stage.at[zp], own), w.move(match_own, match.at[b])]
    dap, ds_buf, p_buf, dqkv = (sc[k] for k in ("dap", "ds", "p", "dqkv"))
    left = lax.broadcasted_iota(jnp.int32, (128, 128), 1) < 64
    zero = jnp.zeros((128, 128), BF16)
    for i in range(4):
        other = 2 * i + 1 - c
        dap[1, other] = zero
        dqkv[0, 1, other] = zero
        for e in range(2):
            ds_buf[1, e, other] = zero
            p_buf[1, e, other] = zero
    for cp in mine:
        cp.wait()
    for k in range(3):
        to_core(k, s, OWN)
    near(1)
    turn(1, OWN)
    far(1)
    z_start(2)
    for u, name in ((NEAR, 2), (FAR, 3), (NEARFAR, 4)):
        w.got(reg(0, s, u, c), (name, 0))
        to_plane(0, u)
        to_core(0, s, u)
    turn(0, OWN)
    turn(2, OWN)
    w.got(xg.at[p.bf], 21)
    w.put(xg.at[p.bf], xg.at[p.bf], p.n, 22)
    w.put(xg.at[p.bf], xg.at[p.bf], p.core, 23)
    w.got(xg.at[p.bn], 20)
    w.put(xg.at[p.bn], xg.at[p.bn], p.core, 23)
    turn(1, NEAR)
    corner(1, OWN)
    for u in (NEAR, FAR, NEARFAR):
        turn(0, u)
    nearfar(1)
    turn(1, FAR)
    for u in range(4):
        corner(0, u)
    w.got(match.at[pl.ds(0, 7)], 92)
    get_match = w.move(match, m_smem)
    w.got(xg.at[p.bnf], 22)
    w.put(xg.at[p.bnf], xg.at[p.bnf], p.core, 23)
    near(2)
    far(2)
    corner(1, NEAR)
    turn(1, NEARFAR)
    complete(0)
    w.got(xg.at[pl.ds(0, 4)], 23)

    lane = lax.broadcasted_iota(jnp.int32, (32, 768), 1)
    mine_lane = ((lane * 2731) >> 16) == lax.broadcasted_iota(jnp.int32, (32, 768), 0)
    lane2 = lax.broadcasted_iota(jnp.int32, (384, 768), 1)
    place = lane2 - 24 * ((lane2 * 2731) >> 16) - lax.broadcasted_iota(jnp.int32, (384, 768), 0)
    flat_vec = wqkv[:, 64:80, :].astype(F32)[:, 8, :].astype(BF16)

    def vector_row(k):
        part = jnp.dot(flat_vec, (place == -24 * k).astype(F32).astype(BF16), preferred_element_type=F32)
        rows[k] = jnp.sum(jnp.where(mine_lane, part, 0.0), axis=0, keepdims=True)

    def up_row(i):
        l3 = lax.broadcasted_iota(jnp.int32, (384, 768), 1) + 768 * i
        d3 = (l3 * 43691) >> 22
        hit = l3 - 96 * d3 - lax.broadcasted_iota(jnp.int32, (384, 768), 0) == -192
        part = jnp.dot(flat_vec, hit.astype(F32).astype(BF16), preferred_element_type=F32)
        owner = ((lax.broadcasted_iota(jnp.int32, (32, 768), 1) + 768 * i) * 43691) >> 22
        here = owner == lax.broadcasted_iota(jnp.int32, (32, 768), 0)
        bup[:, 768 * i : 768 * (i + 1)] = jnp.sum(jnp.where(here, part, 0.0), axis=0, keepdims=True)

    vector_row(0)
    vector_row(1)

    c0 = pl.multiple_of(128 * c, 128)
    b0 = pl.multiple_of(384 * zp + 128 * c, 128)
    b1 = pl.multiple_of(384 * zp + 256, 128)

    columns = sc["cols"]
    for i, v in enumerate((wqkv[:, :, pl.ds(c0, 128)].astype(F32), wqkv[:, :, 256:384].astype(F32))):
        for t in range(3):
            first = 256 * t + 128 * i
            columns[:, first : first + 128] = v[:, 24 * t : 24 * t + 24].reshape(768, 128).astype(BF16)
    for m in range(4):
        r = jnp.dot(xg[2 * m : 2 * m + 2].reshape(256, 768), columns[...], preferred_element_type=F32)
        for t in range(3):
            for tl in range(2):
                part = r[:, 256 * t + 128 * tl : 256 * t + 128 * (tl + 1)]
                if t != 1:
                    part = part + rows[t // 2, :, pl.ds(b1 if tl else b0, 128)]
                qkv[t, tl, 2 * m : 2 * m + 2] = part.astype(BF16).reshape(2, 128, 128)

    get_match.wait()
    att_buf = sc["ab"]

    def mask_head(e, v):
        return jnp.where(left if e == 0 else jnp.logical_not(left), v, zero)

    def weights(e, q, k):
        score = lax.dot_general(mask_head(e, q), k, NT, preferred_element_type=F32) * 0.125
        ex = jnp.exp(score - jnp.max(score, axis=-1, keepdims=True))
        return ex * (1.0 / jnp.sum(ex, axis=-1, keepdims=True))

    def head(tl, e):
        return 6 * zp + (2 * c if tl == 0 else 4) + e

    def attend(tl, blk, i):
        q = qkv[0, tl, blk]
        outs = []
        for e in range(2):
            m = m_smem[blk, g, head(tl, e)]
            pr = weights(e, q, qkv[1, tl, m]).astype(BF16)
            p_buf[tl, e, blk] = pr
            outs.append(jnp.dot(pr, qkv[2, tl, m], preferred_element_type=F32))
        att_buf[i] = jnp.where(left, outs[0], outs[1]).astype(BF16)


    def send_tile(tl, zz, cc, i):
        dst = att.at[g, :, pl.ds(pl.multiple_of(384 * zp + (128 * c if tl == 0 else 256), 128), 128)]
        if i in (0, 8):
            keep.append(w.move(att_buf.at[i], dst))
        else:
            w.put(att_buf.at[i], dst, (s, zz * 2 + cc), 90, lot=90)

    between = (
        lambda: (nearfar(2), corner(2, OWN)), lambda: (turn(2, NEAR), corner(1, FAR)),
        lambda: (corner(1, NEARFAR), turn(2, FAR)), lambda: corner(2, NEAR),
    )
    keep = []
    for j, zz in enumerate((p.zf, p.znf, p.zn, z)):
        trio = [(0, c, 0 if zz is z else 1 + 2 * j), (0, 1 - c, 2 + 2 * j if j < 3 else 7), (1, c, 8 if zz is z else 9 + j)]
        for tl, cc, i in trio:
            attend(tl, zz * 2 + cc, i)
        for tl, cc, i in trio:
            send_tile(tl, zz, cc, i)
        between[j]()
    for k in range(2, 8):
        vector_row(k)
    for i in range(4):
        up_row(i)
    complete(1)

    w.got(att_buf.at[pl.ds(0, 10)], 90)
    for cp in keep + [tok_in, grad_in]:
        cp.wait()

    n1, nlow, act, slope, dh2 = (sc[k] for k in ("n1", "nlow", "act", "slope", "dh2"))
    dtk = sc["dtk"]
    dinner = dtk.reshape(4, 256, 768)

    def whole(ref):
        return ref[...].reshape(256, 768)

    h = whole(tok).astype(F32) + jnp.dot(whole(att), joined(wou[:, :, 0:768]), preferred_element_type=F32) + rows[2]
    h = h - mean(h)
    r1 = lax.rsqrt(mean(h * h) + EPS)
    n1[...] = h * r1
    nlow[...] = (n1[...] * rows[4] + rows[5]).astype(BF16)

    def up(j):
        cols = slice(512 * j, 512 * (j + 1))
        u = jnp.dot(nlow[...], joined(wou[:, :, 768 + 512 * j : 768 + 512 * (j + 1)]), preferred_element_type=F32) + bup[:, cols]
        cdf = 0.5 + 0.5 * lax.erf(u * 0.7071067811865476)
        act[:, cols] = (u * cdf).astype(BF16)
        slope[:, cols] = cdf + u * (jnp.exp(-0.5 * u * u) * 0.3989422804014327)

    up(0)
    up(1)
    up(2)
    turn(2, NEARFAR)
    up(3)
    corner(2, FAR)
    up(4)
    up(5)
    corner(2, NEARFAR)
    complete(2)

    h = jnp.dot(act[...], wd[...], preferred_element_type=F32) + rows[3] + (n1[...] * rows[4] + rows[5])
    h = h - mean(h)
    r2 = lax.rsqrt(mean(h * h) + EPS)
    n2 = h * r2
    result[...] = (n2 * rows[6] + rows[7]).astype(BF16).reshape(2, 128, 768)
    eye = lax.broadcasted_iota(jnp.int32, (128, 128), 0) == lax.broadcasted_iota(jnp.int32, (128, 128), 1)
    keepers = [
        jnp.sum(jnp.where(eye, mask[i : i + 1].astype(F32), 0.0), axis=-1, keepdims=True) for i in range(2)
    ]
    gr = whole(grad).astype(F32) * jnp.concatenate(keepers, axis=0)
    sums = sc["sums"]
    sums[6] = total(gr * n2)
    sums[7] = total(gr)
    e = gr * rows[6]
    d = r2 * (e - mean(e) - n2 * mean(e * n2))
    dh2[...] = d
    dz = sc["dz"]
    dz[...] = d.astype(BF16)
    sums[3] = total(dz[...].astype(F32))

    gd, gu, go, gq, gvec = (sc[k] for k in ("gd", "gu", "go", "gq", "gvec"))

    def down_gradient(ss):
        for i in range(2):
            columns = pl.ds(pl.multiple_of(768 * ss + 384 * i, 128), 384)
            r = lax.dot_general(act[:, columns], dz[...], TN, preferred_element_type=F32)
            gd[ss, 2 * i : 2 * i + 2] = r.astype(BF16).reshape(2, 2, 96, 768)

    chunks = [
        (gd, od, 0, 48, 0, 768),
        (gd, od, 48, 48, 0, 768),
        (gu, ou, 0, 24, 0, 1536),
        (gu, ou, 0, 24, 1536, 1536),
        (go, oo, 0, 24, 0, 768),
        (gvec.reshape(4, 4, 2, 8, 256), ovec, 0, 8, 0, 256),
    ]
    bufs = sc["bufs"]

    def cols(k, half):
        nc = chunks[k][5] // 2
        return pl.ds(half * nc, nc)

    def pair_start(k, which):
        v, out, q0, nr, k0, nc = chunks[k]
        for ss in which:
            src = v.at[ss, :, 1 - c, pl.ds(q0, nr), pl.ds(k0, nc)]
            w.put(src, bufs[k][0].at[ss], p.core, (50 if ss is p.sd else 49, k), lot=50 + k)

    far_column, rest = (p.sd,), (p.sx, p.sy, s)

    def add(k, ss):
        v, out, q0, nr, k0, nc = chunks[k]
        rc = bufs[k][0]

        def one(i):
            rc[ss, i] = rc[ss, i] + v[ss, i, c, q0 : q0 + nr, k0 : k0 + nc]

        loop(4, one)

    def pair_far(k):
        rc, rdx, rdy, rx, ry, rz = bufs[k]
        w.got(rc.at[p.sd], (50, k))
        add(k, p.sd)
        w.put(rc.at[p.sd, :, :, cols(k, 0)], rdx, p.x, (51, k), lot=50 + k)
        w.put(rc.at[p.sd, :, :, cols(k, 1)], rdy, p.y, (52, k), lot=50 + k)

    def pair_rest(k):
        rc, rdx, rdy, rx, ry, rz = bufs[k]
        w.got(rc.at[pl.ds(0, 3)], (49, k))
        add(k, p.sx)
        w.put(rc.at[p.sx, :, :, cols(k, 0)], rx.at[:, :, cols(k, 0)], p.x, (53, k), lot=50 + k)
        add(k, p.sy)
        w.put(rc.at[p.sy, :, :, cols(k, 1)], ry.at[:, :, cols(k, 1)], p.y, (54, k), lot=50 + k)
        add(k, s)

    def diagonal(k):
        rc, rdx, rdy, rx, ry, rz = bufs[k]
        w.got(rdx, (51, k))
        rc[p.sy, :, :, cols(k, 0)] = rc[p.sy, :, :, cols(k, 0)] + rdx[...]
        w.put(rc.at[p.sy, :, :, cols(k, 0)], ry.at[:, :, cols(k, 0)], p.y, (54, k), lot=50 + k)
        w.got(rdy, (52, k))
        rc[p.sx, :, :, cols(k, 1)] = rc[p.sx, :, :, cols(k, 1)] + rdy[...]
        w.put(rc.at[p.sx, :, :, cols(k, 1)], rx.at[:, :, cols(k, 1)], p.x, (53, k), lot=50 + k)

    def plane(k):
        rc, rdx, rdy, rx, ry, rz = bufs[k]
        w.got(rx, (53, k))
        w.got(ry, (54, k))

        def one(i):
            rc[s, i] = (rc[s, i].astype(F32) + rx[i].astype(F32) + ry[i].astype(F32)).astype(rc.dtype)

        loop(4, one)
        w.put(rc.at[s, p.znf], rz.at[0], p.n, (57, k), lot=50 + k)

    def plane_end(k):
        rc, rdx, rdy, rx, ry, rz = bufs[k]
        w.put(rc.at[s, p.zn], rz.at[1], p.n, (58, k), lot=50 + k)

    def last(k):
        rc, rdx, rdy, rx, ry, rz = bufs[k]
        w.got(rz.at[0], (57, k))
        rc[s, p.zf] = rc[s, p.zf] + rz[0]
        w.put(rc.at[s, p.zf], rz.at[2], p.f, (58, k), lot=50 + k)

    def final(k):
        v, out, q0, nr, k0, nc = chunks[k]
        rc, rdx, rdy, rx, ry, rz = bufs[k]
        w.got(rz.at[pl.ds(1, 2)], (58, k))
        out[q0 : q0 + nr, k0 : k0 + nc] = rc[s, z].astype(F32) + rz[1].astype(F32) + rz[2].astype(F32)

    down_gradient(p.sd)
    for k in range(2):
        pair_start(k, far_column)

    def inner_gradient(j):
        cc = slice(768 * j, 768 * (j + 1))
        r = lax.dot_general(dz[...], wd[cc, :], NT, preferred_element_type=F32)
        r = (r * slope[:, cc]).astype(BF16)
        dinner[j] = r
        sc["sup"][:, cc] = total(r.astype(F32))

    for j in range(4):
        inner_gradient(j)
    pair_far(0)
    pair_far(1)
    d = dh2[...]
    for j in range(4):
        wt = joined(wou[:, :, 768 + 768 * j : 768 + 768 * (j + 1)])
        d = d + lax.dot_general(dinner[j], wt, NT, preferred_element_type=F32)
    sums[4] = total(d * n1[...])
    sums[5] = total(d)
    e = d * rows[4]
    d = r1 * (e - mean(e) - n1[...] * mean(e * n1[...]))
    dh1 = dh2
    dh1[...] = d
    dbr = sc["dbr"]
    dbr[...] = d.astype(BF16)
    sums[2] = total(dbr[...].astype(F32))
    datt = sc["datt"]
    r = lax.dot_general(dbr[...], joined(wou[:, :, 0:768]), NT, preferred_element_type=F32)
    datt[...] = r.astype(BF16).reshape(2, 128, 768)

    here = []
    for chip, zz in ((1, p.zn), (2, p.zf), (3, p.znf), (0, z)):
        gg, zq = zz // 2, zz % 2
        for tl, cc in ((0, 1 - c), (0, c), (1, c)):
            src = datt.at[gg, :, pl.ds(pl.multiple_of(384 * zq + (256 if tl else 128 * cc), 128), 128)]
            if zz is z and cc is c:
                here.append(w.move(src, dap.at[tl, b]))
            else:
                w.put(src, dap.at[tl, b], (s, zz * 2 + cc), (91, chip), lot=91)

    def up_gradient(j):
        r = lax.dot_general(nlow[...], dinner[j], TN, preferred_element_type=F32)
        gu[:, :, :, :, 768 * j : 768 * (j + 1)] = r.reshape(4, 4, 2, 24, 768).astype(BF16)

    for ss in rest:
        down_gradient(ss)
    for k in range(2):
        pair_start(k, rest)
    pair_rest(0)
    diagonal(0)
    pair_rest(1)
    diagonal(1)

    def queries(tl, blk):
        da = dap[tl, blk]
        outs = []
        for e in range(2):
            m = m_smem[blk, g, head(tl, e)]
            k, v = qkv[1, tl, m], qkv[2, tl, m]
            pr = p_buf[tl, e, blk].astype(F32)
            dp = lax.dot_general(mask_head(e, da), v, NT, preferred_element_type=F32)
            ds = (pr * (dp - jnp.sum(pr * dp, axis=-1, keepdims=True))).astype(BF16)
            ds_buf[tl, e, blk] = ds
            outs.append(jnp.dot(ds, k, preferred_element_type=F32) * 0.125)
        dqkv[0, tl, blk] = jnp.where(left, outs[0], outs[1]).astype(BF16)

    def keys(tl, n):
        dk, dv = [], []
        for e in range(2):
            cq = 0
            for i in range(8):
                cq = jnp.where(m_smem[i, g, head(tl, e)] == n, i, cq)
            ds, pr = ds_buf[tl, e, cq], p_buf[tl, e, cq]
            dk.append(lax.dot_general(ds, qkv[0, tl, cq], TN, preferred_element_type=F32) * 0.125)
            dv.append(lax.dot_general(pr, dap[tl, cq], TN, preferred_element_type=F32))
        dqkv[1, tl, n] = jnp.where(left, dk[0], dk[1]).astype(BF16)
        dqkv[2, tl, n] = jnp.where(left, dv[0], dv[1]).astype(BF16)

    def both(f, i):
        f(2 * i)
        f(2 * i + 1)

    def queries_from(chip, zz):
        if chip == 0:
            for cp in here:
                cp.wait()
        w.got(att_buf.at[pl.ds(0, 3 if chip else 1)], (91, chip))
        queries(0, zz * 2 + c)
        queries(0, zz * 2 + 1 - c)
        queries(1, zz * 2 + c)

    queries_from(0, z)
    up_gradient(0)
    up_gradient(1)
    pair_start(2, far_column)
    pair_start(2, rest)
    queries_from(1, p.zn)
    pair_far(2)
    pair_rest(2)
    queries_from(2, p.zf)
    queries_from(3, p.znf)
    plane(0)
    plane_end(0)
    loop(4, lambda i: both(lambda n: keys(0, n), i))
    loop(4, lambda i: both(lambda n: keys(1, n), i))

    rtk, rtn, rtf = (sc[k] for k in ("rtk", "rtn", "rtf"))

    def flat(m):
        return jnp.concatenate(
            [dqkv[t, tl, 4 * m : 4 * m + 4].reshape(512, 128) for t in range(3) for tl in range(2)], axis=1
        )

    up_gradient(2)
    up_gradient(3)
    pair_start(3, far_column)
    pair_start(3, rest)
    for m in range(2):
        r = lax.dot_general(flat(m), columns[...], NT, preferred_element_type=F32)
        dtk[2 * m : 2 * m + 2] = r.astype(BF16).reshape(2, 2, 128, 768)
    w.put(dtk.at[:, 1 - c], rtk, p.core, 60)

    rq, accq, rqdx, rqdy, rqx, rqy, rqz = (sc[k] for k in ("rq", "accq", "rqdx", "rqdy", "rqx", "rqy", "rqz"))
    plane(1)
    plane_end(1)
    pair_far(3)
    pair_rest(3)
    w.got(rtk, 60)
    loop(4, lambda i: rtk.__setitem__(i, rtk[i] + dtk[i, c]))
    w.put(rtk.at[p.znf], rtn.at[0], p.n, 62)
    w.put(rtk.at[p.zn], rtn.at[1], p.n, 63)
    r = 0.0
    for m in range(2):
        x = xg[4 * m : 4 * m + 4].reshape(512, 768)
        r = r + lax.dot_general(x, flat(m), TN, preferred_element_type=F32)
    for t in range(3):
        gq[t] = r[:, 256 * t : 256 * (t + 1)].reshape(4, 4, 2, 24, 256).astype(BF16)
    w.put(gq.at[:, :, :, 1 - c], rq, p.core, 61)
    diagonal(2)
    last(0)
    last(1)
    r = lax.dot_general(whole(att), dbr[...], TN, preferred_element_type=F32)
    go[...] = r.reshape(4, 4, 2, 24, 768).astype(BF16)
    pair_start(4, far_column)
    pair_start(4, rest)

    vl = lax.broadcasted_iota(jnp.int32, (128, 768), 1)
    spot = (vl - 24 * ((vl * 2731) >> 16) == lax.broadcasted_iota(jnp.int32, (128, 768), 0)).astype(F32).astype(BF16)

    def fold(part, hit):
        high = part.astype(BF16)
        low = (part - high.astype(F32)).astype(BF16)
        return lax.dot_general(high, hit, NT, preferred_element_type=F32) + lax.dot_general(
            low, hit, NT, preferred_element_type=F32
        )

    def fold_rows(lo, n):
        part = jnp.concatenate([jnp.where(mine_lane, sums[k], 0.0) for k in range(lo, lo + n)], axis=0)
        r = fold(part, spot)
        for k in range(n):
            gvec[:, lo + k, 0:128] = r[32 * k : 32 * (k + 1)]

    gvec[:, :, 128:256] = jnp.zeros((32, 8, 128), F32)
    fold_rows(2, 6)
    r = 0.0
    for i in range(4):
        l3 = lax.broadcasted_iota(jnp.int32, (128, 768), 1) + 768 * i
        hit = (l3 - 96 * ((l3 * 43691) >> 22) == lax.broadcasted_iota(jnp.int32, (128, 768), 0)).astype(F32).astype(BF16)
        owner = ((lax.broadcasted_iota(jnp.int32, (32, 768), 1) + 768 * i) * 43691) >> 22
        at = owner == lax.broadcasted_iota(jnp.int32, (32, 768), 0)
        r = r + fold(jnp.where(at, sc["sup"][:, 768 * i : 768 * (i + 1)], 0.0), hit)
    gvec[:, 0, 128:256] = r

    sums[0] = jnp.zeros((1, 768), F32)
    sums[1] = jnp.zeros((1, 768), F32)
    for r, t in ((0, 0), (1, 2)):
        f = [total(dqkv[t, tl].reshape(1024, 128).astype(F32)) for tl in range(2)]
        sums[r, :, pl.ds(b0, 128)] = f[0]
        sums[r, :, pl.ds(b1, 128)] = f[1]
    fold_rows(0, 2)
    pair_start(5, far_column)
    pair_start(5, rest)

    w.got(rq, 61)
    o0 = pl.multiple_of(128 * (1 - c), 128)

    def pair_q(i):
        for t in range(3):
            for zz in range(4):
                accq[t, i, zz, :, pl.ds(c0, 128)] = gq[t, i, zz, c, :, 0:128]
                accq[t, i, zz, :, pl.ds(o0, 128)] = rq[t, i, zz, :, 0:128]
                accq[t, i, zz, :, 256:384] = gq[t, i, zz, c, :, 128:256] + rq[t, i, zz, :, 128:256]

    pair_q(p.sd)
    w.put(accq.at[:, p.sd, :, :, pl.ds(0, 256)], rqdx, p.x, 64)
    w.put(accq.at[:, p.sd, :, :, pl.ds(256, 128)], rqdy, p.y, 65)
    pair_far(4)
    pair_far(5)
    pair_q(p.sx)
    pair_q(p.sy)
    pair_q(s)
    pair_rest(5)
    pair_rest(4)
    w.got(rtn.at[0], 62)
    rtk[p.zf] = rtk[p.zf] + rtn[0]
    w.put(rtk.at[p.zf], rtf, p.f, 68)
    diagonal(3)
    w.got(rqdx, 64)
    accq[:, p.sy, :, :, 0:256] = accq[:, p.sy, :, :, 0:256] + rqdx[...]
    w.put(accq.at[:, p.sy], rqy, p.y, 66)
    w.got(rqdy, 65)
    accq[:, p.sx, :, :, 256:384] = accq[:, p.sx, :, :, 256:384] + rqdy[...]
    w.put(accq.at[:, p.sx], rqx, p.x, 67)
    plane(2)
    plane_end(2)
    diagonal(4)
    diagonal(5)
    plane(3)
    last(2)
    plane_end(3)
    final(0)
    final(1)
    w.got(rqx, 67)
    w.got(rqy, 66)
    for t in range(3):
        accq[t, s] = (accq[t, s].astype(F32) + rqx[t].astype(F32) + rqy[t].astype(F32)).astype(BF16)
    w.put(accq.at[:, s, p.znf], rqz.at[0], p.f, 80)
    w.put(accq.at[:, s, p.zf], rqz.at[1], p.f, 81)
    plane(4)
    plane_end(4)
    plane(5)
    plane_end(5)
    last(3)
    w.got(rqz.at[0], 80)
    accq[:, s, p.zn] = accq[:, s, p.zn] + rqz[0]
    w.put(accq.at[:, s, p.zn], rqz.at[2], p.n, 82)
    last(4)
    last(5)
    final(2)
    w.got(rtn.at[1], 63)
    w.got(rtf, 68)
    d = dh1[...].reshape(2, 128, 768)
    dtok[...] = d
    dtok[g] = dtok[g] + rtk[z].astype(F32) + rtn[1].astype(F32)
    dtok[1 - g] = dtok[1 - g] + rtf[...].astype(F32)
    w.got(rqz.at[1], 81)
    q0 = pl.multiple_of(384 * zp, 128)
    q1 = pl.multiple_of(384 * (1 - zp), 128)
    for t in range(3):
        oqkv[t, :, pl.ds(q0, 384)] = accq[t, s, z].astype(F32) + rqz[1, t].astype(F32)
    final(3)
    w.got(rqz.at[2], 82)
    for t in range(3):
        oqkv[t, :, pl.ds(q1, 384)] = rqz[2, t].astype(F32)
    final(4)
    final(5)
    w.finish({
        0: wqkv.at[pl.ds(0, 31)], 1: wou.at[pl.ds(0, 31)], 2: wd.at[pl.ds(0, 2976)],
        50: wd.at[pl.ds(0, 1488)], 51: wd.at[pl.ds(0, 1488)],
        52: wou.at[pl.ds(0, 31), :, pl.ds(0, 1536)], 53: wou.at[pl.ds(0, 31), :, pl.ds(0, 1536)],
        54: wou.at[pl.ds(0, 31), :, pl.ds(0, 768)], 55: gvec.at[pl.ds(0, 31)],
        90: att_buf.at[pl.ds(0, 10)], 91: att_buf.at[pl.ds(0, 10)], 92: match.at[pl.ds(0, 7)],
    })


def scratch():
    VM = pltpu.VMEM
    per_chunk = []
    for nr, nc in ((48, 768), (48, 768), (24, 1536), (24, 1536), (24, 768), (8, 256)):
        kind = F32 if nr == 8 else BF16
        shapes = ((4, 4, nr, nc), (4, nr, nc // 2), (4, nr, nc // 2), (4, nr, nc), (4, nr, nc), (3, nr, nc))
        per_chunk.append(tuple(VM(shape, kind) for shape in shapes))
    return dict(
        wou=VM((32, 24, 3840), BF16), wd=VM((3072, 768), BF16), wqkv=VM((32, 80, 384), BF16), raw=VM((3, 24, 768), BF16),
        cols=VM((768, 768), BF16), gvec=VM((32, 8, 256), F32),
        xg=VM((8, 128, 768), BF16), qkv=VM((3, 2, 8, 128, 128), BF16), att=VM((2, 128, 768), BF16),
        match=VM((8, 8, 128), jnp.int32), ms=pltpu.SMEM((8, 8, 128), jnp.int32),
        stage=VM((2, 80, 384), BF16), rows=VM((8, 1, 768), F32), bup=VM((1, 3072), F32),
        tok=VM((2, 128, 768), BF16), grad=VM((2, 128, 768), BF16), vo=VM((8, 384), F32), mo=VM((8, 128), jnp.int32),
        ab=VM((12, 128, 128), BF16), dap=VM((2, 8, 128, 128), BF16), ds=VM((2, 2, 8, 128, 128), BF16),
        p=VM((2, 2, 8, 128, 128), BF16), dqkv=VM((3, 2, 8, 128, 128), BF16),
        n1=VM((256, 768), F32), nlow=VM((256, 768), BF16), act=VM((256, 3072), BF16), slope=VM((256, 3072), F32),
        dh2=VM((256, 768), F32), sums=VM((8, 1, 768), F32), sup=VM((1, 3072), F32),
        dz=VM((256, 768), BF16), dbr=VM((256, 768), BF16), datt=VM((2, 128, 768), BF16),
        gd=VM((4, 4, 2, 96, 768), BF16), gu=VM((4, 4, 2, 24, 3072), BF16), go=VM((4, 4, 2, 24, 768), BF16),
        gq=VM((3, 4, 4, 2, 24, 256), BF16), rq=VM((3, 4, 4, 24, 256), BF16), accq=VM((3, 4, 4, 24, 384), BF16),
        dtk=VM((4, 2, 128, 768), BF16), rtk=VM((4, 128, 768), BF16), rtn=VM((2, 128, 768), BF16), rtf=VM((128, 768), BF16),
        rqdx=VM((3, 4, 24, 256), BF16), rqdy=VM((3, 4, 24, 128), BF16), rqx=VM((3, 4, 24, 384), BF16),
        rqy=VM((3, 4, 24, 384), BF16), rqz=VM((3, 3, 24, 384), BF16), bufs=tuple(per_chunk),
    )


def hand_out(result, od, ou, oo, oqkv, dtok, ovec, *rest):
    outs, sem, lines = rest[:17], rest[17], rest[18:]
    pairs = [(dtok.at[i, pl.ds(64 * j, 64)], outs[1].at[i, pl.ds(64 * j, 64)]) for i in range(2) for j in range(2)]
    pairs += [(result.at[i], outs[0].at[i]) for i in range(2)]
    pairs += [(ou.at[:, pl.ds(1536 * i, 1536)], outs[6].at[:, pl.ds(1536 * i, 1536)]) for i in range(2)]
    pairs += [(od.at[pl.ds(48 * i, 48)], outs[7].at[pl.ds(48 * i, 48)]) for i in range(2)]
    pairs += [(oqkv.at[0], outs[2]), (oqkv.at[1], outs[3]), (oqkv.at[2], outs[4]), (oo, outs[5])]
    copies = [pltpu.make_async_copy(a, o, sem.at[i]) for i, (a, o) in enumerate(pairs)]
    for cp in copies:
        cp.start()
    for i, (row, line) in enumerate(zip((0, 1, 2, None, 3, 4, 5, 6, 7), lines, strict=True)):
        line[...] = ovec[0, 128:224] if row is None else ovec[row, 0:24]
        cp = pltpu.make_async_copy(line, outs[8 + i], sem.at[14 + i])
        cp.start()
        copies.append(cp)
    for cp in copies:
        cp.wait()


def column(
    tokens, grad_out, masked, token_order, cluster_match,
    w_query, w_key, w_value, w_out, w_up, w_down,
    b_query, b_value, b_out, b_up, b_down,
    gain_attn, shift_attn, gain_ffn, shift_ffn,
):
    V = pl.BlockSpec(memory_space=pltpu.VMEM)
    A = pl.BlockSpec(memory_space=pl.ANY)
    S = jax.ShapeDtypeStruct
    vectors = (b_query, b_value, b_out, b_down, gain_attn, shift_attn, gain_ffn, shift_ffn, b_up)
    got = pl.pallas_call(
        layer_kernel,
        out_shape=(
            S((2, 128, 768), BF16), S((96, 768), F32), S((24, 3072), F32), S((24, 768), F32), S((3, 24, 768), F32),
            S((2, 128, 768), F32), S((8, 256), F32),
        ),
        in_specs=[A, A, V, V] + [A] * 6 + [V] * 9,
        out_specs=(V,) * 7,
        scratch_shapes=[scratch(), *(pltpu.SemaphoreType.DMA((n,)) for n in (31, 118, 16))],
        compiler_params=pltpu.CompilerParams(collective_id=0, has_side_effects=True, vmem_limit_bytes=62 << 20),
        name="layer",
    )(tokens, grad_out, masked, cluster_match.reshape(2, 12), w_query, w_key, w_value, w_out, w_up, w_down, *vectors)
    square = S((24, 768), F32)
    outs = (S((2, 128, 768), BF16), S((2, 128, 768), F32)) + (square,) * 4 + (S((24, 3072), F32), S((96, 768), F32))
    outs += tuple(S((n,), F32) for n in (24, 24, 24, 96, 24, 24, 24, 24, 24))
    return pl.pallas_call(
        hand_out,
        out_shape=outs,
        in_specs=[V] * 7,
        out_specs=(A,) * 17,
        scratch_shapes=[pltpu.SemaphoreType.DMA((23,))] + [pltpu.VMEM((96 if i == 3 else 24,), F32) for i in range(9)],
        name="results",
    )(*got)


def solution(mesh):
    fits = mesh.shape[SEQ] == 4 and mesh.shape[BLK] == 8
    return jax.shard_map(
        column if fits else general,
        mesh=mesh,
        in_specs=(
            P(SEQ, BLK, None),
            P(SEQ, BLK, None),
            P(SEQ, BLK),
            P(SEQ, None, BLK),
            P(SEQ, None, BLK),
            P(BOTH, None),
            P(BOTH, None),
            P(BOTH, None),
            P(BOTH, None),
            P(BOTH, None),
            P(BOTH, None),
            P(BOTH),
            P(BOTH),
            P(BOTH),
            P(BOTH),
            P(BOTH),
            P(BOTH),
            P(BOTH),
            P(BOTH),
            P(BOTH),
        ),
        out_specs=(
            P(SEQ, BLK, None),
            P(SEQ, BLK, None),
            P(BOTH, None),
            P(BOTH, None),
            P(BOTH, None),
            P(BOTH, None),
            P(BOTH, None),
            P(BOTH, None),
            P(BOTH),
            P(BOTH),
            P(BOTH),
            P(BOTH),
            P(BOTH),
            P(BOTH),
            P(BOTH),
            P(BOTH),
            P(BOTH),
        ),
        check_vma=False,
    )
```

```python
import functools
import math

import jax
import jax.numpy as jnp
from jax import lax
from jax.experimental import pallas as pl
from jax.experimental.pallas import tpu as pltpu
from jax.sharding import PartitionSpec as P

HEADS = 12
CL = 128
EPS = 1e-05
MESH = pl.DeviceIdType.MESH
SEQ, BLK = BOTH = ("seq", "blk")
F32 = jnp.float32
BF16 = jnp.bfloat16


def norm_rows(hidden, gain_row, shift_row):
    row_mean = jnp.mean(hidden, axis=-1, keepdims=True)
    centered = hidden - row_mean
    variance = jnp.mean(centered * centered, axis=-1, keepdims=True)
    return centered * lax.rsqrt(variance + EPS) * gain_row + shift_row


def gelu_exact(inner_sum):
    return jax.nn.gelu(inner_sum, approximate=False)


def to_heads(flat_rows, groups, local_len):
    return flat_rows.reshape(groups, local_len, HEADS, -1).transpose(0, 2, 1, 3)


def from_heads(head_rows):
    groups, head_count, local_len, head_dim = head_rows.shape
    return head_rows.transpose(0, 2, 1, 3).reshape(groups * local_len, head_count * head_dim)


def reorder(head_rows, positions):
    return jnp.take_along_axis(head_rows, positions[..., None], axis=2)


def general(
    tokens,
    grad_out,
    masked,
    token_order,
    cluster_match,
    w_query,
    w_key,
    w_value,
    w_out,
    w_up,
    w_down,
    b_query,
    b_value,
    b_out,
    b_up,
    b_down,
    gain_attn,
    shift_attn,
    gain_ffn,
    shift_ffn,
):
    groups, local_len, width = tokens.shape
    row_count = groups * local_len
    head_dim = width // HEADS
    clusters = local_len // CL
    score_scale = 1.0 / math.sqrt(head_dim)
    gathered = (
        lax.all_gather(w_query, BOTH, axis=0, tiled=True),
        lax.all_gather(w_key, BOTH, axis=0, tiled=True),
        lax.all_gather(w_value, BOTH, axis=0, tiled=True),
        lax.all_gather(w_out, BOTH, axis=0, tiled=True),
        lax.all_gather(w_up, BOTH, axis=0, tiled=True),
        lax.all_gather(w_down, BOTH, axis=0, tiled=True),
        lax.all_gather(b_query, BOTH, axis=0, tiled=True),
        lax.all_gather(b_value, BOTH, axis=0, tiled=True),
        lax.all_gather(b_out, BOTH, axis=0, tiled=True),
        lax.all_gather(b_up, BOTH, axis=0, tiled=True),
        lax.all_gather(b_down, BOTH, axis=0, tiled=True),
        lax.all_gather(gain_attn, BOTH, axis=0, tiled=True),
        lax.all_gather(shift_attn, BOTH, axis=0, tiled=True),
        lax.all_gather(gain_ffn, BOTH, axis=0, tiled=True),
        lax.all_gather(shift_ffn, BOTH, axis=0, tiled=True),
    )
    (
        full_query,
        full_key,
        full_value,
        full_out,
        full_up,
        full_down,
        bias_query,
        bias_value,
        bias_out,
        bias_up,
        bias_down,
        norm_gain1,
        norm_shift1,
        norm_gain2,
        norm_shift2,
    ) = gathered
    flat_tokens = tokens.reshape(row_count, width)
    inverse = jnp.argsort(token_order, axis=-1)
    cluster_shape = (groups, HEADS, clusters, CL, head_dim)
    query_low = (
        jnp.dot(flat_tokens, full_query, preferred_element_type=jnp.float32)
        + bias_query.astype(jnp.float32)
    ).astype(jnp.bfloat16)
    key_low = jnp.dot(flat_tokens, full_key, preferred_element_type=jnp.float32).astype(
        jnp.bfloat16
    )
    value_low = (
        jnp.dot(flat_tokens, full_value, preferred_element_type=jnp.float32)
        + bias_value.astype(jnp.float32)
    ).astype(jnp.bfloat16)
    query_perm = reorder(to_heads(query_low, groups, local_len), token_order).reshape(cluster_shape)
    key_perm = reorder(to_heads(key_low, groups, local_len), token_order).reshape(cluster_shape)
    value_perm = reorder(to_heads(value_low, groups, local_len), token_order).reshape(cluster_shape)
    empty_sel = jnp.zeros(cluster_shape, jnp.bfloat16)
    key_piece = lax.all_gather(key_perm, BLK, axis=2, tiled=True)
    value_piece = lax.all_gather(value_perm, BLK, axis=2, tiled=True)
    piece_len = key_piece.shape[2]
    offset = cluster_match
    select = (offset[..., None] == jnp.arange(piece_len, dtype=jnp.int32)).astype(jnp.bfloat16)
    inside = ((offset >= 0) & (offset < piece_len))[..., None, None]
    new_keys = jnp.einsum(
        "ghcj,ghjkd->ghckd", select, key_piece, preferred_element_type=jnp.float32
    ).astype(jnp.bfloat16)
    new_values = jnp.einsum(
        "ghcj,ghjkd->ghckd", select, value_piece, preferred_element_type=jnp.float32
    ).astype(jnp.bfloat16)
    key_sel = jnp.where(inside, new_keys, empty_sel)
    value_sel = jnp.where(inside, new_values, empty_sel)
    scores = (
        jnp.einsum("ghcqd,ghckd->ghcqk", query_perm, key_sel, preferred_element_type=jnp.float32)
        * score_scale
    )
    row_max = jnp.max(scores, axis=-1, keepdims=True)
    log_total = row_max + jnp.log(jnp.sum(jnp.exp(scores - row_max), axis=-1, keepdims=True))
    attn_probs = jnp.exp(scores - log_total)
    probs_low = attn_probs.astype(jnp.bfloat16)
    mixed_perm = jnp.einsum(
        "ghcqk,ghckd->ghcqd", probs_low, value_sel, preferred_element_type=jnp.float32
    ).reshape(groups, HEADS, local_len, head_dim)
    attended = from_heads(reorder(mixed_perm, inverse)).astype(jnp.bfloat16)
    branch = jnp.dot(attended, full_out, preferred_element_type=jnp.float32) + bias_out.astype(
        jnp.float32
    )
    resid = flat_tokens.astype(jnp.float32) + branch
    normed, pull_first = jax.vjp(
        norm_rows, resid, norm_gain1.astype(jnp.float32), norm_shift1.astype(jnp.float32)
    )
    normed_low = normed.astype(jnp.bfloat16)
    inner_sum = jnp.dot(normed_low, full_up, preferred_element_type=jnp.float32) + bias_up.astype(
        jnp.float32
    )
    active, pull_gelu = jax.vjp(gelu_exact, inner_sum)
    active_low = active.astype(jnp.bfloat16)
    outer_sum = jnp.dot(
        active_low, full_down, preferred_element_type=jnp.float32
    ) + bias_down.astype(jnp.float32)
    final_rows, pull_second = jax.vjp(
        norm_rows,
        normed + outer_sum,
        norm_gain2.astype(jnp.float32),
        norm_shift2.astype(jnp.float32),
    )
    result = final_rows.astype(jnp.bfloat16).reshape(groups, local_len, width)
    back_weights = (
        lax.all_gather(w_query, BOTH, axis=0, tiled=True),
        lax.all_gather(w_key, BOTH, axis=0, tiled=True),
        lax.all_gather(w_value, BOTH, axis=0, tiled=True),
        lax.all_gather(w_out, BOTH, axis=0, tiled=True),
        lax.all_gather(w_up, BOTH, axis=0, tiled=True),
        lax.all_gather(w_down, BOTH, axis=0, tiled=True),
        lax.all_gather(b_query, BOTH, axis=0, tiled=True),
        lax.all_gather(b_value, BOTH, axis=0, tiled=True),
        lax.all_gather(b_out, BOTH, axis=0, tiled=True),
        lax.all_gather(b_up, BOTH, axis=0, tiled=True),
        lax.all_gather(b_down, BOTH, axis=0, tiled=True),
        lax.all_gather(gain_attn, BOTH, axis=0, tiled=True),
        lax.all_gather(shift_attn, BOTH, axis=0, tiled=True),
        lax.all_gather(gain_ffn, BOTH, axis=0, tiled=True),
        lax.all_gather(shift_ffn, BOTH, axis=0, tiled=True),
    )
    back_query, back_key, back_value, back_out, back_up, back_down = back_weights[:6]
    upstream = grad_out.reshape(row_count, width).astype(jnp.float32) * masked.reshape(
        row_count, 1
    ).astype(jnp.float32)
    d_sum2, d_gain2, d_shift2 = pull_second(upstream)
    d_outer = d_sum2.astype(jnp.bfloat16)
    g_down = jnp.einsum("rf,rd->fd", active_low, d_outer, preferred_element_type=jnp.float32)
    g_bdown = jnp.sum(d_outer.astype(jnp.float32), axis=0)
    d_active = jnp.einsum("rd,fd->rf", d_outer, back_down, preferred_element_type=jnp.float32)
    d_inner = pull_gelu(d_active)[0].astype(jnp.bfloat16)
    g_up = jnp.einsum("rd,rf->df", normed_low, d_inner, preferred_element_type=jnp.float32)
    g_bup = jnp.sum(d_inner.astype(jnp.float32), axis=0)
    d_normed = d_sum2 + jnp.einsum(
        "rf,df->rd", d_inner, back_up, preferred_element_type=jnp.float32
    )
    d_resid, d_gain1, d_shift1 = pull_first(d_normed)
    d_branch = d_resid.astype(jnp.bfloat16)
    g_out = jnp.einsum("ri,rd->id", attended, d_branch, preferred_element_type=jnp.float32)
    g_bout = jnp.sum(d_branch.astype(jnp.float32), axis=0)
    d_attended = jnp.einsum(
        "rd,id->ri", d_branch, back_out, preferred_element_type=jnp.float32
    ).astype(jnp.bfloat16)
    d_mixed = reorder(to_heads(d_attended, groups, local_len), token_order).reshape(cluster_shape)
    scores_again = (
        jnp.einsum("ghcqd,ghckd->ghcqk", query_perm, key_sel, preferred_element_type=jnp.float32)
        * score_scale
    )
    probs_again = jnp.exp(scores_again - log_total)
    probs_again_low = probs_again.astype(jnp.bfloat16)
    d_probs = jnp.einsum(
        "ghcqd,ghckd->ghcqk", d_mixed, value_sel, preferred_element_type=jnp.float32
    )
    d_scores = (
        probs_again * (d_probs - jnp.sum(probs_again * d_probs, axis=-1, keepdims=True))
    ).astype(jnp.bfloat16)
    d_query_perm = (
        jnp.einsum("ghcqk,ghckd->ghcqd", d_scores, key_sel, preferred_element_type=jnp.float32)
        * score_scale
    )
    d_key_sel = (
        jnp.einsum("ghcqk,ghcqd->ghckd", d_scores, query_perm, preferred_element_type=jnp.float32)
        * score_scale
    )
    d_value_sel = jnp.einsum(
        "ghcqk,ghcqd->ghckd", probs_again_low, d_mixed, preferred_element_type=jnp.float32
    )
    sent = jnp.concatenate([d_key_sel, d_value_sel], axis=-1)
    my_start = lax.axis_index(BLK) * clusters
    piece_grads = lax.all_gather(sent.astype(jnp.bfloat16), BLK, axis=2, tiled=True).astype(
        jnp.float32
    )
    piece_match = lax.all_gather(
        cluster_match.astype(jnp.float32).astype(jnp.bfloat16), BLK, axis=2, tiled=True
    ).astype(jnp.float32)
    offset = piece_match.astype(jnp.int32) - my_start
    select = (offset[..., None] == jnp.arange(clusters, dtype=jnp.int32)).astype(jnp.float32)
    owned = jnp.zeros(sent.shape, jnp.float32) + jnp.einsum(
        "ghjc,ghjke->ghcke", select, piece_grads, precision=lax.Precision.HIGHEST
    )
    back_kv = reorder(owned.reshape(groups, HEADS, local_len, 2 * head_dim), inverse)
    d_key = from_heads(back_kv[..., :head_dim]).astype(jnp.bfloat16)
    d_value = from_heads(back_kv[..., head_dim:]).astype(jnp.bfloat16)
    d_query = from_heads(
        reorder(d_query_perm.reshape(groups, HEADS, local_len, head_dim), inverse)
    ).astype(jnp.bfloat16)
    g_query = jnp.einsum("ri,rd->id", flat_tokens, d_query, preferred_element_type=jnp.float32)
    g_key = jnp.einsum("ri,rd->id", flat_tokens, d_key, preferred_element_type=jnp.float32)
    g_value = jnp.einsum("ri,rd->id", flat_tokens, d_value, preferred_element_type=jnp.float32)
    g_bquery = jnp.sum(d_query.astype(jnp.float32), axis=0)
    g_bvalue = jnp.sum(d_value.astype(jnp.float32), axis=0)
    d_tokens_flat = (
        d_resid
        + jnp.einsum("rd,id->ri", d_query, back_query, preferred_element_type=jnp.float32)
        + jnp.einsum("rd,id->ri", d_key, back_key, preferred_element_type=jnp.float32)
        + jnp.einsum("rd,id->ri", d_value, back_value, preferred_element_type=jnp.float32)
    )
    summed = (
        lax.psum_scatter(g_query, BOTH, scatter_dimension=0, tiled=True),
        lax.psum_scatter(g_key, BOTH, scatter_dimension=0, tiled=True),
        lax.psum_scatter(g_value, BOTH, scatter_dimension=0, tiled=True),
        lax.psum_scatter(g_out, BOTH, scatter_dimension=0, tiled=True),
        lax.psum_scatter(g_up, BOTH, scatter_dimension=0, tiled=True),
        lax.psum_scatter(g_down, BOTH, scatter_dimension=0, tiled=True),
        lax.psum_scatter(g_bquery, BOTH, scatter_dimension=0, tiled=True),
        lax.psum_scatter(g_bvalue, BOTH, scatter_dimension=0, tiled=True),
        lax.psum_scatter(g_bout, BOTH, scatter_dimension=0, tiled=True),
        lax.psum_scatter(g_bup, BOTH, scatter_dimension=0, tiled=True),
        lax.psum_scatter(g_bdown, BOTH, scatter_dimension=0, tiled=True),
        lax.psum_scatter(d_gain1, BOTH, scatter_dimension=0, tiled=True),
        lax.psum_scatter(d_shift1, BOTH, scatter_dimension=0, tiled=True),
        lax.psum_scatter(d_gain2, BOTH, scatter_dimension=0, tiled=True),
        lax.psum_scatter(d_shift2, BOTH, scatter_dimension=0, tiled=True),
    )
    return (result, d_tokens_flat.reshape(groups, local_len, width)) + tuple(summed)


OWN, NEAR, FAR, NEARFAR = range(4)
NT = (((1,), (1,)), ((), ()))
TN = (((0,), (0,)), ((), ()))


class Place:
    def __init__(self):
        s, b = lax.axis_index(SEQ), lax.axis_index(BLK)
        self.s, self.b = s, b
        z, c = b // 2, b % 2
        self.z, self.c = z, c
        self.zlo, self.zhi = z % 2, z // 2
        self.sx = s + 1 - 2 * (s % 2)
        self.sy = s + 2 - 4 * (s // 2)
        self.sd = self.sy + 1 - 2 * (s % 2)
        self.zn = z + 1 - 2 * self.zlo
        self.zf = z + 2 - 4 * self.zhi
        self.znf = self.zf + 1 - 2 * self.zlo
        self.bc = b + 1 - 2 * c
        self.bn, self.bf, self.bnf = self.zn * 2 + c, self.zf * 2 + c, self.znf * 2 + c
        self.core = (s, self.bc)
        self.n = (s, self.bn)
        self.f = (s, self.bf)
        self.nf = (s, self.bnf)
        self.x = (self.sx, b)
        self.y = (self.sy, b)


class Wire:
    def __init__(self, send, recv, local):
        self.send, self.recv, self.local = send, recv, local
        self.n_send = self.n_local = self.n_recv = 0
        self.sent, self.slots, self.lots = [], {}, {}

    def slot(self, key):
        if key not in self.slots:
            self.slots[key] = self.n_recv
            self.n_recv += 1
        return self.slots[key]

    def put(self, src, dst, to, key, lot=None):
        at = self.slot(key)
        if lot is None or lot not in self.lots:
            index = self.n_send
            self.n_send += 1
            if lot is not None:
                self.lots[lot] = index
        else:
            index = self.lots[lot]
        cp = pltpu.make_async_remote_copy(
            src, dst, self.send.at[index], self.recv.at[at], device_id=to, device_id_type=MESH
        )
        cp.start()
        if lot is None:
            self.sent.append(cp)

    def got(self, dst, key):
        at = self.slot(key)
        pltpu.make_async_copy(dst, dst, self.recv.at[at]).wait()

    def move(self, src, dst):
        cp = pltpu.make_async_copy(src, dst, self.local.at[self.n_local])
        self.n_local += 1
        cp.start()
        return cp

    def finish(self, sizes):
        for lot, ref in sizes.items():
            pltpu.make_async_copy(ref, ref, self.send.at[self.lots[lot]]).wait()
        for cp in self.sent:
            cp.wait_send()


def greet(peers):
    bar = pltpu.get_barrier_semaphore()
    for to in peers:
        pl.semaphore_signal(bar, inc=1, device_id=to, device_id_type=MESH)
    pl.semaphore_wait(bar, len(peers))


def loop(n, body):
    def run(i, carry):
        body(i)
        return carry

    lax.fori_loop(0, n, run, 0)


def joined(v):
    return v.astype(F32).reshape(768, v.shape[-1]).astype(BF16)


def mean(v):
    return jnp.mean(v, axis=-1, keepdims=True)


def total(v):
    return jnp.sum(v, axis=0, keepdims=True)


def layer_kernel(
    tok_h, go_h, mask, cm, wq, wk, wv, wo_s, wu_s, wd_s,
    *others,
):
    vectors, (result, od, ou, oo, oqkv, dtok, ovec, sc, *sems) = others[:9], others[9:]
    p = Place()
    w = Wire(*sems)
    s, b, z, c = p.s, p.b, p.z, p.c
    zp, g = p.zlo, p.zhi
    zs = (z, p.zn, p.zf, p.znf)
    wou, wd, wqkv, xg, qkv, att = (sc[k] for k in ("wou", "wd", "wqkv", "xg", "qkv", "att"))
    match, m_smem, stage, rows, bup = (sc[k] for k in ("match", "ms", "stage", "rows", "bup"))

    raw = sc["raw"]
    early = [w.move(ref, raw.at[t]) for t, ref in enumerate((wq, wk, wv))]
    tok, grad = sc["tok"], sc["grad"]
    slot = s * 8 + b
    mine = [
        w.move(wo_s, wou.at[slot, :, pl.ds(0, 768)]), w.move(wu_s, wou.at[slot, :, pl.ds(768, 3072)]),
        w.move(wd_s, wd.at[pl.ds(pl.multiple_of(96 * slot, 96), 96)]), w.move(tok_h.at[g], xg.at[b]),
    ]
    tok_in, grad_in = w.move(tok_h, tok), w.move(go_h, grad)
    greet([p.core, p.n, p.f, p.nf, p.x, p.y, (s, p.zn * 2 + 1 - c), (s, p.zf * 2 + 1 - c), (s, p.znf * 2 + 1 - c)])

    def at_rows(n, ss, zz, cc):
        return pl.ds(pl.multiple_of(n * (ss * 8 + zz * 2 + cc), 8), n)

    def reg(k, ss, u, cc, half=None):
        zz = zs[u]
        if k == 0:
            cols = (pl.ds(0, 384), pl.ds(0, 256), pl.ds(256, 128))[0 if half is None else 1 + half]
            return wqkv.at[ss * 8 + zz * 2 + cc, :, cols]
        if k == 1:
            cols = (pl.ds(0, 3840), pl.ds(0, 1792), pl.ds(1792, 2048))[0 if half is None else 1 + half]
            return wou.at[ss * 8 + zz * 2 + cc, :, cols]
        cols = pl.ds(0, 768) if half is None else pl.ds(384 * half, 384)
        return wd.at[at_rows(96, ss, zz, cc), cols]

    def to_plane(k, u, src=None):
        r = reg(k, s, u, c)
        src = r if src is None else src
        w.put(src, r, p.x, (0, k, u), lot=k)
        w.put(src, r, p.y, (1, k, u), lot=k)

    def to_core(k, ss, u):
        r = reg(k, ss, u, c)
        group = [v is ss for v in (s, p.sx, p.sy, p.sd)].index(True) if k == 2 else 0
        w.put(r, r, p.core, (5, k, group), lot=k)

    def z_start(k):
        r = reg(k, s, OWN, c)
        w.put(r, r, p.n, (2, k), lot=k)
        w.put(r, r, p.f, (3, k), lot=k)

    def near(k):
        w.got(reg(k, s, NEAR, c), (2, k))
        to_plane(k, NEAR)
        to_core(k, s, NEAR)

    def far(k):
        r = reg(k, s, FAR, c)
        w.got(r, (3, k))
        w.put(r, r, p.n, (4, k), lot=k)
        to_plane(k, FAR)
        to_core(k, s, FAR)

    def nearfar(k):
        w.got(reg(k, s, NEARFAR, c), (4, k))
        to_plane(k, NEARFAR)
        to_core(k, s, NEARFAR)

    def turn(k, u):
        w.got(reg(k, p.sx, u, c), (0, k, u))
        r = reg(k, p.sx, u, c, 0)
        w.put(r, r, p.y, (6, k, u), lot=k)
        to_core(k, p.sx, u)
        w.got(reg(k, p.sy, u, c), (1, k, u))
        r = reg(k, p.sy, u, c, 1)
        w.put(r, r, p.x, (6, k, u), lot=k)
        to_core(k, p.sy, u)

    def corner(k, u):
        w.got(reg(k, p.sd, u, c), (6, k, u))
        to_core(k, p.sd, u)

    def complete(k):
        w.got((wqkv.at[pl.ds(0, 16)], wou.at[pl.ds(0, 16)])[k], (5, k, 0))

    own = reg(0, s, OWN, c)

    def own_out_up(to, key):
        w.put(wu_s, wou.at[slot, :, pl.ds(768, 3072)], to, key, lot=1)
        w.put(wo_s, wou.at[slot, :, pl.ds(0, 768)], to, key, lot=1)

    own_out_up(p.n, (2, 1))
    own_out_up(p.x, (0, 1, OWN))
    own_out_up(p.y, (1, 1, OWN))
    own_out_up(p.f, (3, 1))
    for cp in early:
        cp.wait()
    vec_own, match_own = sc["vo"], sc["mo"]
    vec_own[...] = jnp.zeros_like(vec_own)
    for k, ref in enumerate(vectors):
        vec_own[0:1, 24 * k : 24 * k + ref.shape[0]] = ref[...].astype(F32).reshape(1, ref.shape[0])
    for h in range(2):
        parts = [raw[t, :, 384 * h : 384 * (h + 1)].astype(F32) for t in range(3)]
        stage[h] = jnp.concatenate(parts + [vec_own[...]], axis=0).astype(BF16)
    w.put(stage.at[1 - zp], own, p.n, (2, 0), lot=0)
    w.put(stage.at[zp], own, p.f, (3, 0), lot=0)
    w.put(stage.at[1 - zp], own, p.nf, (4, 0), lot=0)
    w.put(stage.at[zp], own, p.x, (0, 0, OWN), lot=0)
    w.put(stage.at[zp], own, p.y, (1, 0, OWN), lot=0)
    w.put(tok_h.at[1 - g], xg.at[b], p.f, 21)
    w.put(tok_h.at[g], xg.at[b], p.n, 20)
    to_plane(2, OWN, wd_s)
    match_own[...] = jnp.zeros_like(match_own)
    match_own[0:2, 0:12] = cm[...]
    for zz in zs:
        for cc in (c, 1 - c):
            if not (zz is z and cc is c):
                w.put(match_own, match.at[b], (s, zz * 2 + cc), 92, lot=92)
    w.put(tok_h.at[g], xg.at[b], p.core, 23)
    mine += [w.move(stage.at[zp], own), w.move(match_own, match.at[b])]
    dap, ds_buf, p_buf, dqkv = (sc[k] for k in ("dap", "ds", "p", "dqkv"))
    left = lax.broadcasted_iota(jnp.int32, (128, 128), 1) < 64
    zero = jnp.zeros((128, 128), BF16)
    for i in range(4):
        other = 2 * i + 1 - c
        dap[1, other] = zero
        dqkv[0, 1, other] = zero
        for e in range(2):
            ds_buf[1, e, other] = zero
            p_buf[1, e, other] = zero
    for cp in mine:
        cp.wait()
    for k in range(3):
        to_core(k, s, OWN)
    near(1)
    turn(1, OWN)
    far(1)
    z_start(2)
    for u, name in ((NEAR, 2), (FAR, 3), (NEARFAR, 4)):
        w.got(reg(0, s, u, c), (name, 0))
        to_plane(0, u)
        to_core(0, s, u)
    turn(0, OWN)
    turn(2, OWN)
    w.got(xg.at[p.bf], 21)
    w.put(xg.at[p.bf], xg.at[p.bf], p.n, 22)
    w.put(xg.at[p.bf], xg.at[p.bf], p.core, 23)
    w.got(xg.at[p.bn], 20)
    w.put(xg.at[p.bn], xg.at[p.bn], p.core, 23)
    turn(1, NEAR)
    corner(1, OWN)
    for u in (NEAR, FAR, NEARFAR):
        turn(0, u)
    nearfar(1)
    turn(1, FAR)
    for u in range(4):
        corner(0, u)
    w.got(match.at[pl.ds(0, 7)], 92)
    get_match = w.move(match, m_smem)
    w.got(xg.at[p.bnf], 22)
    w.put(xg.at[p.bnf], xg.at[p.bnf], p.core, 23)
    near(2)
    far(2)
    corner(1, NEAR)
    turn(1, NEARFAR)
    complete(0)
    w.got(xg.at[pl.ds(0, 4)], 23)

    lane = lax.broadcasted_iota(jnp.int32, (32, 768), 1)
    mine_lane = ((lane * 2731) >> 16) == lax.broadcasted_iota(jnp.int32, (32, 768), 0)
    lane2 = lax.broadcasted_iota(jnp.int32, (384, 768), 1)
    place = lane2 - 24 * ((lane2 * 2731) >> 16) - lax.broadcasted_iota(jnp.int32, (384, 768), 0)
    flat_vec = wqkv[:, 64:80, :].astype(F32)[:, 8, :].astype(BF16)

    def vector_row(k):
        part = jnp.dot(flat_vec, (place == -24 * k).astype(F32).astype(BF16), preferred_element_type=F32)
        rows[k] = jnp.sum(jnp.where(mine_lane, part, 0.0), axis=0, keepdims=True)

    def up_row(i):
        l3 = lax.broadcasted_iota(jnp.int32, (384, 768), 1) + 768 * i
        d3 = (l3 * 43691) >> 22
        hit = l3 - 96 * d3 - lax.broadcasted_iota(jnp.int32, (384, 768), 0) == -192
        part = jnp.dot(flat_vec, hit.astype(F32).astype(BF16), preferred_element_type=F32)
        owner = ((lax.broadcasted_iota(jnp.int32, (32, 768), 1) + 768 * i) * 43691) >> 22
        here = owner == lax.broadcasted_iota(jnp.int32, (32, 768), 0)
        bup[:, 768 * i : 768 * (i + 1)] = jnp.sum(jnp.where(here, part, 0.0), axis=0, keepdims=True)

    vector_row(0)
    vector_row(1)

    c0 = pl.multiple_of(128 * c, 128)
    b0 = pl.multiple_of(384 * zp + 128 * c, 128)
    b1 = pl.multiple_of(384 * zp + 256, 128)

    columns = sc["cols"]
    for i, v in enumerate((wqkv[:, :, pl.ds(c0, 128)].astype(F32), wqkv[:, :, 256:384].astype(F32))):
        for t in range(3):
            first = 256 * t + 128 * i
            columns[:, first : first + 128] = v[:, 24 * t : 24 * t + 24].reshape(768, 128).astype(BF16)
    for m in range(4):
        r = jnp.dot(xg[2 * m : 2 * m + 2].reshape(256, 768), columns[...], preferred_element_type=F32)
        for t in range(3):
            for tl in range(2):
                part = r[:, 256 * t + 128 * tl : 256 * t + 128 * (tl + 1)]
                if t != 1:
                    part = part + rows[t // 2, :, pl.ds(b1 if tl else b0, 128)]
                qkv[t, tl, 2 * m : 2 * m + 2] = part.astype(BF16).reshape(2, 128, 128)

    get_match.wait()
    att_buf = sc["ab"]

    def mask_head(e, v):
        return jnp.where(left if e == 0 else jnp.logical_not(left), v, zero)

    def weights(e, q, k):
        score = lax.dot_general(mask_head(e, q), k, NT, preferred_element_type=F32) * 0.125
        ex = jnp.exp(score - jnp.max(score, axis=-1, keepdims=True))
        return ex * (1.0 / jnp.sum(ex, axis=-1, keepdims=True))

    def head(tl, e):
        return 6 * zp + (2 * c if tl == 0 else 4) + e

    def attend(tl, blk, i):
        q = qkv[0, tl, blk]
        outs = []
        for e in range(2):
            m = m_smem[blk, g, head(tl, e)]
            pr = weights(e, q, qkv[1, tl, m]).astype(BF16)
            p_buf[tl, e, blk] = pr
            outs.append(jnp.dot(pr, qkv[2, tl, m], preferred_element_type=F32))
        att_buf[i] = jnp.where(left, outs[0], outs[1]).astype(BF16)


    def send_tile(tl, zz, cc, i):
        dst = att.at[g, :, pl.ds(pl.multiple_of(384 * zp + (128 * c if tl == 0 else 256), 128), 128)]
        if i in (0, 8):
            keep.append(w.move(att_buf.at[i], dst))
        else:
            w.put(att_buf.at[i], dst, (s, zz * 2 + cc), 90, lot=90)

    between = (
        lambda: (nearfar(2), corner(2, OWN)), lambda: (turn(2, NEAR), corner(1, FAR)),
        lambda: (corner(1, NEARFAR), turn(2, FAR)), lambda: corner(2, NEAR),
    )
    keep = []
    for j, zz in enumerate((p.zf, p.znf, p.zn, z)):
        trio = [(0, c, 0 if zz is z else 1 + 2 * j), (0, 1 - c, 2 + 2 * j if j < 3 else 7), (1, c, 8 if zz is z else 9 + j)]
        for tl, cc, i in trio:
            attend(tl, zz * 2 + cc, i)
        for tl, cc, i in trio:
            send_tile(tl, zz, cc, i)
        between[j]()
    for k in range(2, 8):
        vector_row(k)
    for i in range(4):
        up_row(i)
    complete(1)

    w.got(att_buf.at[pl.ds(0, 10)], 90)
    for cp in keep + [tok_in, grad_in]:
        cp.wait()

    n1, nlow, act, slope, dh2 = (sc[k] for k in ("n1", "nlow", "act", "slope", "dh2"))
    dtk = sc["dtk"]
    dinner = dtk.reshape(4, 256, 768)

    def whole(ref):
        return ref[...].reshape(256, 768)

    h = whole(tok).astype(F32) + jnp.dot(whole(att), joined(wou[:, :, 0:768]), preferred_element_type=F32) + rows[2]
    h = h - mean(h)
    r1 = lax.rsqrt(mean(h * h) + EPS)
    n1[...] = h * r1
    nlow[...] = (n1[...] * rows[4] + rows[5]).astype(BF16)

    def up(j):
        cols = slice(512 * j, 512 * (j + 1))
        u = jnp.dot(nlow[...], joined(wou[:, :, 768 + 512 * j : 768 + 512 * (j + 1)]), preferred_element_type=F32) + bup[:, cols]
        cdf = 0.5 + 0.5 * lax.erf(u * 0.7071067811865476)
        act[:, cols] = (u * cdf).astype(BF16)
        slope[:, cols] = cdf + u * (jnp.exp(-0.5 * u * u) * 0.3989422804014327)

    up(0)
    up(1)
    up(2)
    turn(2, NEARFAR)
    up(3)
    corner(2, FAR)
    up(4)
    up(5)

    def down(group, ss):
        w.got(wd.at[pl.ds(0, 384)], (5, 2, group))
        part = pl.ds(pl.multiple_of(768 * ss, 768), 768)
        return jnp.dot(act[:, part], wd[part, :], preferred_element_type=F32)

    dh2[...] = n1[...] * rows[4] + (rows[3] + rows[5])
    for group, ss in enumerate((s, p.sx, p.sy)):
        dh2[...] += down(group, ss)
    corner(2, NEARFAR)
    h = dh2[...] + down(3, p.sd)
    h = h - mean(h)
    r2 = lax.rsqrt(mean(h * h) + EPS)
    n2 = h * r2
    result[...] = (n2 * rows[6] + rows[7]).astype(BF16).reshape(2, 128, 768)
    eye = lax.broadcasted_iota(jnp.int32, (128, 128), 0) == lax.broadcasted_iota(jnp.int32, (128, 128), 1)
    keepers = [
        jnp.sum(jnp.where(eye, mask[i : i + 1].astype(F32), 0.0), axis=-1, keepdims=True) for i in range(2)
    ]
    gr = whole(grad).astype(F32) * jnp.concatenate(keepers, axis=0)
    sums = sc["sums"]
    sums[6] = total(gr * n2)
    sums[7] = total(gr)
    e = gr * rows[6]
    d = r2 * (e - mean(e) - n2 * mean(e * n2))
    dh2[...] = d
    dz = sc["dz"]
    dz[...] = d.astype(BF16)
    sums[3] = total(dz[...].astype(F32))

    gd, gu, go, gq, gvec = (sc[k] for k in ("gd", "gu", "go", "gq", "gvec"))

    def down_gradient(ss):
        for i in range(2):
            columns = pl.ds(pl.multiple_of(768 * ss + 384 * i, 128), 384)
            r = lax.dot_general(act[:, columns], dz[...], TN, preferred_element_type=F32)
            gd[ss, 2 * i : 2 * i + 2] = r.astype(BF16).reshape(2, 2, 96, 768)

    chunks = [
        (gd, od, 0, 48, 0, 768),
        (gd, od, 48, 48, 0, 768),
        (gu, ou, 0, 24, 0, 1536),
        (gu, ou, 0, 24, 1536, 1536),
        (go, oo, 0, 24, 0, 768),
        (gvec.reshape(4, 4, 2, 8, 256), ovec, 0, 8, 0, 256),
    ]
    bufs = sc["bufs"]

    def cols(k, half):
        nc = chunks[k][5] // 2
        return pl.ds(half * nc, nc)

    def pair_start(k, which):
        v, out, q0, nr, k0, nc = chunks[k]
        for ss in which:
            src = v.at[ss, :, 1 - c, pl.ds(q0, nr), pl.ds(k0, nc)]
            w.put(src, bufs[k][0].at[ss], p.core, (50 if ss is p.sd else 49, k), lot=50 + k)

    far_column, rest = (p.sd,), (p.sx, p.sy, s)

    def add(k, ss):
        v, out, q0, nr, k0, nc = chunks[k]
        rc = bufs[k][0]

        def one(i):
            rc[ss, i] = rc[ss, i] + v[ss, i, c, q0 : q0 + nr, k0 : k0 + nc]

        loop(4, one)

    def pair_far(k):
        rc, rdx, rdy, rx, ry, rz = bufs[k]
        w.got(rc.at[p.sd], (50, k))
        add(k, p.sd)
        w.put(rc.at[p.sd, :, :, cols(k, 0)], rdx, p.x, (51, k), lot=50 + k)
        w.put(rc.at[p.sd, :, :, cols(k, 1)], rdy, p.y, (52, k), lot=50 + k)

    def pair_rest(k):
        rc, rdx, rdy, rx, ry, rz = bufs[k]
        w.got(rc.at[pl.ds(0, 3)], (49, k))
        add(k, p.sx)
        w.put(rc.at[p.sx, :, :, cols(k, 0)], rx.at[:, :, cols(k, 0)], p.x, (53, k), lot=50 + k)
        add(k, p.sy)
        w.put(rc.at[p.sy, :, :, cols(k, 1)], ry.at[:, :, cols(k, 1)], p.y, (54, k), lot=50 + k)
        add(k, s)

    def diagonal(k):
        rc, rdx, rdy, rx, ry, rz = bufs[k]
        w.got(rdx, (51, k))
        rc[p.sy, :, :, cols(k, 0)] = rc[p.sy, :, :, cols(k, 0)] + rdx[...]
        w.put(rc.at[p.sy, :, :, cols(k, 0)], ry.at[:, :, cols(k, 0)], p.y, (54, k), lot=50 + k)
        w.got(rdy, (52, k))
        rc[p.sx, :, :, cols(k, 1)] = rc[p.sx, :, :, cols(k, 1)] + rdy[...]
        w.put(rc.at[p.sx, :, :, cols(k, 1)], rx.at[:, :, cols(k, 1)], p.x, (53, k), lot=50 + k)

    def plane(k):
        rc, rdx, rdy, rx, ry, rz = bufs[k]
        w.got(rx, (53, k))
        w.got(ry, (54, k))

        def one(i):
            rc[s, i] = (rc[s, i].astype(F32) + rx[i].astype(F32) + ry[i].astype(F32)).astype(rc.dtype)

        loop(4, one)
        w.put(rc.at[s, p.znf], rz.at[0], p.n, (57, k), lot=50 + k)

    def plane_end(k):
        rc, rdx, rdy, rx, ry, rz = bufs[k]
        w.put(rc.at[s, p.zn], rz.at[1], p.n, (58, k), lot=50 + k)

    def last(k):
        rc, rdx, rdy, rx, ry, rz = bufs[k]
        w.got(rz.at[0], (57, k))
        rc[s, p.zf] = rc[s, p.zf] + rz[0]
        w.put(rc.at[s, p.zf], rz.at[2], p.f, (58, k), lot=50 + k)

    def final(k):
        v, out, q0, nr, k0, nc = chunks[k]
        rc, rdx, rdy, rx, ry, rz = bufs[k]
        w.got(rz.at[pl.ds(1, 2)], (58, k))
        out[q0 : q0 + nr, k0 : k0 + nc] = rc[s, z].astype(F32) + rz[1].astype(F32) + rz[2].astype(F32)

    down_gradient(p.sd)
    for k in range(2):
        pair_start(k, far_column)

    def inner_gradient(j):
        cc = slice(768 * j, 768 * (j + 1))
        r = lax.dot_general(dz[...], wd[cc, :], NT, preferred_element_type=F32)
        r = (r * slope[:, cc]).astype(BF16)
        dinner[j] = r
        sc["sup"][:, cc] = total(r.astype(F32))

    for j in range(4):
        inner_gradient(j)
    pair_far(0)
    pair_far(1)
    d = dh2[...]
    for j in range(4):
        wt = joined(wou[:, :, 768 + 768 * j : 768 + 768 * (j + 1)])
        d = d + lax.dot_general(dinner[j], wt, NT, preferred_element_type=F32)
    sums[4] = total(d * n1[...])
    sums[5] = total(d)
    e = d * rows[4]
    d = r1 * (e - mean(e) - n1[...] * mean(e * n1[...]))
    dh1 = dh2
    dh1[...] = d
    dbr = sc["dbr"]
    dbr[...] = d.astype(BF16)
    sums[2] = total(dbr[...].astype(F32))
    datt = sc["datt"]
    r = lax.dot_general(dbr[...], joined(wou[:, :, 0:768]), NT, preferred_element_type=F32)
    datt[...] = r.astype(BF16).reshape(2, 128, 768)

    here = []
    for chip, zz in ((1, p.zn), (2, p.zf), (3, p.znf), (0, z)):
        gg, zq = zz // 2, zz % 2
        for tl, cc in ((0, 1 - c), (0, c), (1, c)):
            src = datt.at[gg, :, pl.ds(pl.multiple_of(384 * zq + (256 if tl else 128 * cc), 128), 128)]
            if zz is z and cc is c:
                here.append(w.move(src, dap.at[tl, b]))
            else:
                w.put(src, dap.at[tl, b], (s, zz * 2 + cc), (91, chip), lot=91)

    def up_gradient(j):
        r = lax.dot_general(nlow[...], dinner[j], TN, preferred_element_type=F32)
        gu[:, :, :, :, 768 * j : 768 * (j + 1)] = r.reshape(4, 4, 2, 24, 768).astype(BF16)

    for ss in rest:
        down_gradient(ss)
    for k in range(2):
        pair_start(k, rest)

    def queries(tl, blk):
        da = dap[tl, blk]
        outs = []
        for e in range(2):
            m = m_smem[blk, g, head(tl, e)]
            k, v = qkv[1, tl, m], qkv[2, tl, m]
            pr = p_buf[tl, e, blk].astype(F32)
            dp = lax.dot_general(mask_head(e, da), v, NT, preferred_element_type=F32)
            ds = (pr * (dp - jnp.sum(pr * dp, axis=-1, keepdims=True))).astype(BF16)
            ds_buf[tl, e, blk] = ds
            outs.append(jnp.dot(ds, k, preferred_element_type=F32) * 0.125)
        dqkv[0, tl, blk] = jnp.where(left, outs[0], outs[1]).astype(BF16)

    def keys(tl, n):
        dk, dv = [], []
        for e in range(2):
            cq = 0
            for i in range(8):
                cq = jnp.where(m_smem[i, g, head(tl, e)] == n, i, cq)
            ds, pr = ds_buf[tl, e, cq], p_buf[tl, e, cq]
            dk.append(lax.dot_general(ds, qkv[0, tl, cq], TN, preferred_element_type=F32) * 0.125)
            dv.append(lax.dot_general(pr, dap[tl, cq], TN, preferred_element_type=F32))
        dqkv[1, tl, n] = jnp.where(left, dk[0], dk[1]).astype(BF16)
        dqkv[2, tl, n] = jnp.where(left, dv[0], dv[1]).astype(BF16)

    def both(f, i):
        f(2 * i)
        f(2 * i + 1)

    def queries_from(chip, zz):
        if chip == 0:
            for cp in here:
                cp.wait()
        w.got(att_buf.at[pl.ds(0, 3 if chip else 1)], (91, chip))
        queries(0, zz * 2 + c)
        queries(0, zz * 2 + 1 - c)
        queries(1, zz * 2 + c)

    queries_from(0, z)
    pair_rest(0)
    diagonal(0)
    pair_rest(1)
    diagonal(1)
    up_gradient(0)
    up_gradient(1)
    pair_start(2, far_column)
    pair_start(2, rest)
    queries_from(1, p.zn)
    pair_far(2)
    pair_rest(2)
    queries_from(2, p.zf)
    queries_from(3, p.znf)
    plane(0)
    plane_end(0)
    loop(4, lambda i: both(lambda n: keys(0, n), i))
    loop(4, lambda i: both(lambda n: keys(1, n), i))

    rtk, rtn, rtf = (sc[k] for k in ("rtk", "rtn", "rtf"))

    def flat(m):
        return jnp.concatenate(
            [dqkv[t, tl, 4 * m : 4 * m + 4].reshape(512, 128) for t in range(3) for tl in range(2)], axis=1
        )

    up_gradient(2)
    up_gradient(3)
    pair_start(3, far_column)
    pair_start(3, rest)
    for m in range(2):
        r = lax.dot_general(flat(m), columns[...], NT, preferred_element_type=F32)
        dtk[2 * m : 2 * m + 2] = r.astype(BF16).reshape(2, 2, 128, 768)
    w.put(dtk.at[:, 1 - c], rtk, p.core, 60)

    rq, accq, rqdx, rqdy, rqx, rqy, rqz = (sc[k] for k in ("rq", "accq", "rqdx", "rqdy", "rqx", "rqy", "rqz"))
    plane(1)
    plane_end(1)
    pair_far(3)
    pair_rest(3)
    w.got(rtk, 60)
    loop(4, lambda i: rtk.__setitem__(i, rtk[i] + dtk[i, c]))
    w.put(rtk.at[p.znf], rtn.at[0], p.n, 62)
    w.put(rtk.at[p.zn], rtn.at[1], p.n, 63)
    r = 0.0
    for m in range(2):
        x = xg[4 * m : 4 * m + 4].reshape(512, 768)
        r = r + lax.dot_general(x, flat(m), TN, preferred_element_type=F32)
    for t in range(3):
        gq[t] = r[:, 256 * t : 256 * (t + 1)].reshape(4, 4, 2, 24, 256).astype(BF16)
    w.put(gq.at[:, :, :, 1 - c], rq, p.core, 61)
    diagonal(2)
    last(0)
    last(1)
    r = lax.dot_general(whole(att), dbr[...], TN, preferred_element_type=F32)
    go[...] = r.reshape(4, 4, 2, 24, 768).astype(BF16)
    pair_start(4, far_column)
    pair_start(4, rest)

    vl = lax.broadcasted_iota(jnp.int32, (128, 768), 1)
    spot = (vl - 24 * ((vl * 2731) >> 16) == lax.broadcasted_iota(jnp.int32, (128, 768), 0)).astype(F32).astype(BF16)

    def fold(part, hit):
        high = part.astype(BF16)
        low = (part - high.astype(F32)).astype(BF16)
        return lax.dot_general(high, hit, NT, preferred_element_type=F32) + lax.dot_general(
            low, hit, NT, preferred_element_type=F32
        )

    def fold_rows(lo, n):
        part = jnp.concatenate([jnp.where(mine_lane, sums[k], 0.0) for k in range(lo, lo + n)], axis=0)
        r = fold(part, spot)
        for k in range(n):
            gvec[:, lo + k, 0:128] = r[32 * k : 32 * (k + 1)]

    gvec[:, :, 128:256] = jnp.zeros((32, 8, 128), F32)
    fold_rows(2, 6)
    r = 0.0
    for i in range(4):
        l3 = lax.broadcasted_iota(jnp.int32, (128, 768), 1) + 768 * i
        hit = (l3 - 96 * ((l3 * 43691) >> 22) == lax.broadcasted_iota(jnp.int32, (128, 768), 0)).astype(F32).astype(BF16)
        owner = ((lax.broadcasted_iota(jnp.int32, (32, 768), 1) + 768 * i) * 43691) >> 22
        at = owner == lax.broadcasted_iota(jnp.int32, (32, 768), 0)
        r = r + fold(jnp.where(at, sc["sup"][:, 768 * i : 768 * (i + 1)], 0.0), hit)
    gvec[:, 0, 128:256] = r

    sums[0] = jnp.zeros((1, 768), F32)
    sums[1] = jnp.zeros((1, 768), F32)
    for r, t in ((0, 0), (1, 2)):
        f = [total(dqkv[t, tl].reshape(1024, 128).astype(F32)) for tl in range(2)]
        sums[r, :, pl.ds(b0, 128)] = f[0]
        sums[r, :, pl.ds(b1, 128)] = f[1]
    fold_rows(0, 2)
    pair_start(5, far_column)
    pair_start(5, rest)

    w.got(rq, 61)
    o0 = pl.multiple_of(128 * (1 - c), 128)

    def pair_q(i):
        for t in range(3):
            for zz in range(4):
                accq[t, i, zz, :, pl.ds(c0, 128)] = gq[t, i, zz, c, :, 0:128]
                accq[t, i, zz, :, pl.ds(o0, 128)] = rq[t, i, zz, :, 0:128]
                accq[t, i, zz, :, 256:384] = gq[t, i, zz, c, :, 128:256] + rq[t, i, zz, :, 128:256]

    pair_q(p.sd)
    w.put(accq.at[:, p.sd, :, :, pl.ds(0, 256)], rqdx, p.x, 64)
    w.put(accq.at[:, p.sd, :, :, pl.ds(256, 128)], rqdy, p.y, 65)
    pair_far(4)
    pair_far(5)
    pair_q(p.sx)
    pair_q(p.sy)
    pair_q(s)
    pair_rest(5)
    pair_rest(4)
    w.got(rtn.at[0], 62)
    rtk[p.zf] = rtk[p.zf] + rtn[0]
    w.put(rtk.at[p.zf], rtf, p.f, 68)
    diagonal(3)
    w.got(rqdx, 64)
    accq[:, p.sy, :, :, 0:256] = accq[:, p.sy, :, :, 0:256] + rqdx[...]
    w.put(accq.at[:, p.sy], rqy, p.y, 66)
    w.got(rqdy, 65)
    accq[:, p.sx, :, :, 256:384] = accq[:, p.sx, :, :, 256:384] + rqdy[...]
    w.put(accq.at[:, p.sx], rqx, p.x, 67)
    plane(2)
    plane_end(2)
    diagonal(4)
    diagonal(5)
    plane(3)
    last(2)
    plane_end(3)
    final(0)
    final(1)
    w.got(rqx, 67)
    w.got(rqy, 66)
    for t in range(3):
        accq[t, s] = (accq[t, s].astype(F32) + rqx[t].astype(F32) + rqy[t].astype(F32)).astype(BF16)
    w.put(accq.at[:, s, p.znf], rqz.at[0], p.f, 80)
    w.put(accq.at[:, s, p.zf], rqz.at[1], p.f, 81)
    plane(4)
    plane_end(4)
    plane(5)
    plane_end(5)
    last(3)
    w.got(rqz.at[0], 80)
    accq[:, s, p.zn] = accq[:, s, p.zn] + rqz[0]
    w.put(accq.at[:, s, p.zn], rqz.at[2], p.n, 82)
    last(4)
    last(5)
    final(2)
    w.got(rtn.at[1], 63)
    w.got(rtf, 68)
    d = dh1[...].reshape(2, 128, 768)
    dtok[...] = d
    dtok[g] = dtok[g] + rtk[z].astype(F32) + rtn[1].astype(F32)
    dtok[1 - g] = dtok[1 - g] + rtf[...].astype(F32)
    w.got(rqz.at[1], 81)
    q0 = pl.multiple_of(384 * zp, 128)
    q1 = pl.multiple_of(384 * (1 - zp), 128)
    for t in range(3):
        oqkv[t, :, pl.ds(q0, 384)] = accq[t, s, z].astype(F32) + rqz[1, t].astype(F32)
    final(3)
    w.got(rqz.at[2], 82)
    for t in range(3):
        oqkv[t, :, pl.ds(q1, 384)] = rqz[2, t].astype(F32)
    final(4)
    final(5)
    w.finish({
        0: wqkv.at[pl.ds(0, 31)], 1: wou.at[pl.ds(0, 31)], 2: wd.at[pl.ds(0, 2976)],
        50: wd.at[pl.ds(0, 1488)], 51: wd.at[pl.ds(0, 1488)],
        52: wou.at[pl.ds(0, 31), :, pl.ds(0, 1536)], 53: wou.at[pl.ds(0, 31), :, pl.ds(0, 1536)],
        54: wou.at[pl.ds(0, 31), :, pl.ds(0, 768)], 55: gvec.at[pl.ds(0, 31)],
        90: att_buf.at[pl.ds(0, 10)], 91: att_buf.at[pl.ds(0, 10)], 92: match.at[pl.ds(0, 7)],
    })


def scratch():
    VM = pltpu.VMEM
    per_chunk = []
    for nr, nc in ((48, 768), (48, 768), (24, 1536), (24, 1536), (24, 768), (8, 256)):
        kind = F32 if nr == 8 else BF16
        shapes = ((4, 4, nr, nc), (4, nr, nc // 2), (4, nr, nc // 2), (4, nr, nc), (4, nr, nc), (3, nr, nc))
        per_chunk.append(tuple(VM(shape, kind) for shape in shapes))
    return dict(
        wou=VM((32, 24, 3840), BF16), wd=VM((3072, 768), BF16), wqkv=VM((32, 80, 384), BF16), raw=VM((3, 24, 768), BF16),
        cols=VM((768, 768), BF16), gvec=VM((32, 8, 256), F32),
        xg=VM((8, 128, 768), BF16), qkv=VM((3, 2, 8, 128, 128), BF16), att=VM((2, 128, 768), BF16),
        match=VM((8, 8, 128), jnp.int32), ms=pltpu.SMEM((8, 8, 128), jnp.int32),
        stage=VM((2, 80, 384), BF16), rows=VM((8, 1, 768), F32), bup=VM((1, 3072), F32),
        tok=VM((2, 128, 768), BF16), grad=VM((2, 128, 768), BF16), vo=VM((8, 384), F32), mo=VM((8, 128), jnp.int32),
        ab=VM((12, 128, 128), BF16), dap=VM((2, 8, 128, 128), BF16), ds=VM((2, 2, 8, 128, 128), BF16),
        p=VM((2, 2, 8, 128, 128), BF16), dqkv=VM((3, 2, 8, 128, 128), BF16),
        n1=VM((256, 768), F32), nlow=VM((256, 768), BF16), act=VM((256, 3072), BF16), slope=VM((256, 3072), F32),
        dh2=VM((256, 768), F32), sums=VM((8, 1, 768), F32), sup=VM((1, 3072), F32),
        dz=VM((256, 768), BF16), dbr=VM((256, 768), BF16), datt=VM((2, 128, 768), BF16),
        gd=VM((4, 4, 2, 96, 768), BF16), gu=VM((4, 4, 2, 24, 3072), BF16), go=VM((4, 4, 2, 24, 768), BF16),
        gq=VM((3, 4, 4, 2, 24, 256), BF16), rq=VM((3, 4, 4, 24, 256), BF16), accq=VM((3, 4, 4, 24, 384), BF16),
        dtk=VM((4, 2, 128, 768), BF16), rtk=VM((4, 128, 768), BF16), rtn=VM((2, 128, 768), BF16), rtf=VM((128, 768), BF16),
        rqdx=VM((3, 4, 24, 256), BF16), rqdy=VM((3, 4, 24, 128), BF16), rqx=VM((3, 4, 24, 384), BF16),
        rqy=VM((3, 4, 24, 384), BF16), rqz=VM((3, 3, 24, 384), BF16), bufs=tuple(per_chunk),
    )


def hand_out(result, od, ou, oo, oqkv, dtok, ovec, *rest):
    outs, sem, lines = rest[:17], rest[17], rest[18:]
    pairs = [(dtok.at[i, pl.ds(64 * j, 64)], outs[1].at[i, pl.ds(64 * j, 64)]) for i in range(2) for j in range(2)]
    pairs += [(result.at[i], outs[0].at[i]) for i in range(2)]
    pairs += [(ou.at[:, pl.ds(1536 * i, 1536)], outs[6].at[:, pl.ds(1536 * i, 1536)]) for i in range(2)]
    pairs += [(od.at[pl.ds(48 * i, 48)], outs[7].at[pl.ds(48 * i, 48)]) for i in range(2)]
    pairs += [(oqkv.at[0], outs[2]), (oqkv.at[1], outs[3]), (oqkv.at[2], outs[4]), (oo, outs[5])]
    copies = [pltpu.make_async_copy(a, o, sem.at[i]) for i, (a, o) in enumerate(pairs)]
    for cp in copies:
        cp.start()
    for i, (row, line) in enumerate(zip((0, 1, 2, None, 3, 4, 5, 6, 7), lines, strict=True)):
        line[...] = ovec[0, 128:224] if row is None else ovec[row, 0:24]
        cp = pltpu.make_async_copy(line, outs[8 + i], sem.at[14 + i])
        cp.start()
        copies.append(cp)
    for cp in copies:
        cp.wait()


def column(
    tokens, grad_out, masked, token_order, cluster_match,
    w_query, w_key, w_value, w_out, w_up, w_down,
    b_query, b_value, b_out, b_up, b_down,
    gain_attn, shift_attn, gain_ffn, shift_ffn,
):
    V = pl.BlockSpec(memory_space=pltpu.VMEM)
    A = pl.BlockSpec(memory_space=pl.ANY)
    S = jax.ShapeDtypeStruct
    vectors = (b_query, b_value, b_out, b_down, gain_attn, shift_attn, gain_ffn, shift_ffn, b_up)
    got = pl.pallas_call(
        layer_kernel,
        out_shape=(
            S((2, 128, 768), BF16), S((96, 768), F32), S((24, 3072), F32), S((24, 768), F32), S((3, 24, 768), F32),
            S((2, 128, 768), F32), S((8, 256), F32),
        ),
        in_specs=[A, A, V, V] + [A] * 6 + [V] * 9,
        out_specs=(V,) * 7,
        scratch_shapes=[scratch(), *(pltpu.SemaphoreType.DMA((n,)) for n in (31, 121, 16))],
        compiler_params=pltpu.CompilerParams(collective_id=0, has_side_effects=True, vmem_limit_bytes=62 << 20),
        name="layer",
    )(tokens, grad_out, masked, cluster_match.reshape(2, 12), w_query, w_key, w_value, w_out, w_up, w_down, *vectors)
    square = S((24, 768), F32)
    outs = (S((2, 128, 768), BF16), S((2, 128, 768), F32)) + (square,) * 4 + (S((24, 3072), F32), S((96, 768), F32))
    outs += tuple(S((n,), F32) for n in (24, 24, 24, 96, 24, 24, 24, 24, 24))
    return pl.pallas_call(
        hand_out,
        out_shape=outs,
        in_specs=[V] * 7,
        out_specs=(A,) * 17,
        scratch_shapes=[pltpu.SemaphoreType.DMA((23,))] + [pltpu.VMEM((96 if i == 3 else 24,), F32) for i in range(9)],
        name="results",
    )(*got)


def solution(mesh):
    fits = mesh.shape[SEQ] == 4 and mesh.shape[BLK] == 8
    return jax.shard_map(
        column if fits else general,
        mesh=mesh,
        in_specs=(
            P(SEQ, BLK, None),
            P(SEQ, BLK, None),
            P(SEQ, BLK),
            P(SEQ, None, BLK),
            P(SEQ, None, BLK),
            P(BOTH, None),
            P(BOTH, None),
            P(BOTH, None),
            P(BOTH, None),
            P(BOTH, None),
            P(BOTH, None),
            P(BOTH),
            P(BOTH),
            P(BOTH),
            P(BOTH),
            P(BOTH),
            P(BOTH),
            P(BOTH),
            P(BOTH),
            P(BOTH),
        ),
        out_specs=(
            P(SEQ, BLK, None),
            P(SEQ, BLK, None),
            P(BOTH, None),
            P(BOTH, None),
            P(BOTH, None),
            P(BOTH, None),
            P(BOTH, None),
            P(BOTH, None),
            P(BOTH),
            P(BOTH),
            P(BOTH),
            P(BOTH),
            P(BOTH),
            P(BOTH),
            P(BOTH),
            P(BOTH),
            P(BOTH),
        ),
        check_vma=False,
    )
```

```python
import functools
import math

import jax
import jax.numpy as jnp
from jax import lax
from jax.experimental import pallas as pl
from jax.experimental.pallas import tpu as pltpu
from jax.sharding import PartitionSpec as P

HEADS = 12
CL = 128
EPS = 1e-05
MESH = pl.DeviceIdType.MESH
SEQ, BLK = BOTH = ("seq", "blk")
F32 = jnp.float32
BF16 = jnp.bfloat16


def norm_rows(hidden, gain_row, shift_row):
    row_mean = jnp.mean(hidden, axis=-1, keepdims=True)
    centered = hidden - row_mean
    variance = jnp.mean(centered * centered, axis=-1, keepdims=True)
    return centered * lax.rsqrt(variance + EPS) * gain_row + shift_row


def gelu_exact(inner_sum):
    return jax.nn.gelu(inner_sum, approximate=False)


def to_heads(flat_rows, groups, local_len):
    return flat_rows.reshape(groups, local_len, HEADS, -1).transpose(0, 2, 1, 3)


def from_heads(head_rows):
    groups, head_count, local_len, head_dim = head_rows.shape
    return head_rows.transpose(0, 2, 1, 3).reshape(groups * local_len, head_count * head_dim)


def reorder(head_rows, positions):
    return jnp.take_along_axis(head_rows, positions[..., None], axis=2)


def general(
    tokens,
    grad_out,
    masked,
    token_order,
    cluster_match,
    w_query,
    w_key,
    w_value,
    w_out,
    w_up,
    w_down,
    b_query,
    b_value,
    b_out,
    b_up,
    b_down,
    gain_attn,
    shift_attn,
    gain_ffn,
    shift_ffn,
):
    groups, local_len, width = tokens.shape
    row_count = groups * local_len
    head_dim = width // HEADS
    clusters = local_len // CL
    score_scale = 1.0 / math.sqrt(head_dim)
    gathered = (
        lax.all_gather(w_query, BOTH, axis=0, tiled=True),
        lax.all_gather(w_key, BOTH, axis=0, tiled=True),
        lax.all_gather(w_value, BOTH, axis=0, tiled=True),
        lax.all_gather(w_out, BOTH, axis=0, tiled=True),
        lax.all_gather(w_up, BOTH, axis=0, tiled=True),
        lax.all_gather(w_down, BOTH, axis=0, tiled=True),
        lax.all_gather(b_query, BOTH, axis=0, tiled=True),
        lax.all_gather(b_value, BOTH, axis=0, tiled=True),
        lax.all_gather(b_out, BOTH, axis=0, tiled=True),
        lax.all_gather(b_up, BOTH, axis=0, tiled=True),
        lax.all_gather(b_down, BOTH, axis=0, tiled=True),
        lax.all_gather(gain_attn, BOTH, axis=0, tiled=True),
        lax.all_gather(shift_attn, BOTH, axis=0, tiled=True),
        lax.all_gather(gain_ffn, BOTH, axis=0, tiled=True),
        lax.all_gather(shift_ffn, BOTH, axis=0, tiled=True),
    )
    (
        full_query,
        full_key,
        full_value,
        full_out,
        full_up,
        full_down,
        bias_query,
        bias_value,
        bias_out,
        bias_up,
        bias_down,
        norm_gain1,
        norm_shift1,
        norm_gain2,
        norm_shift2,
    ) = gathered
    flat_tokens = tokens.reshape(row_count, width)
    inverse = jnp.argsort(token_order, axis=-1)
    cluster_shape = (groups, HEADS, clusters, CL, head_dim)
    query_low = (
        jnp.dot(flat_tokens, full_query, preferred_element_type=jnp.float32)
        + bias_query.astype(jnp.float32)
    ).astype(jnp.bfloat16)
    key_low = jnp.dot(flat_tokens, full_key, preferred_element_type=jnp.float32).astype(
        jnp.bfloat16
    )
    value_low = (
        jnp.dot(flat_tokens, full_value, preferred_element_type=jnp.float32)
        + bias_value.astype(jnp.float32)
    ).astype(jnp.bfloat16)
    query_perm = reorder(to_heads(query_low, groups, local_len), token_order).reshape(cluster_shape)
    key_perm = reorder(to_heads(key_low, groups, local_len), token_order).reshape(cluster_shape)
    value_perm = reorder(to_heads(value_low, groups, local_len), token_order).reshape(cluster_shape)
    empty_sel = jnp.zeros(cluster_shape, jnp.bfloat16)
    key_piece = lax.all_gather(key_perm, BLK, axis=2, tiled=True)
    value_piece = lax.all_gather(value_perm, BLK, axis=2, tiled=True)
    piece_len = key_piece.shape[2]
    offset = cluster_match
    select = (offset[..., None] == jnp.arange(piece_len, dtype=jnp.int32)).astype(jnp.bfloat16)
    inside = ((offset >= 0) & (offset < piece_len))[..., None, None]
    new_keys = jnp.einsum(
        "ghcj,ghjkd->ghckd", select, key_piece, preferred_element_type=jnp.float32
    ).astype(jnp.bfloat16)
    new_values = jnp.einsum(
        "ghcj,ghjkd->ghckd", select, value_piece, preferred_element_type=jnp.float32
    ).astype(jnp.bfloat16)
    key_sel = jnp.where(inside, new_keys, empty_sel)
    value_sel = jnp.where(inside, new_values, empty_sel)
    scores = (
        jnp.einsum("ghcqd,ghckd->ghcqk", query_perm, key_sel, preferred_element_type=jnp.float32)
        * score_scale
    )
    row_max = jnp.max(scores, axis=-1, keepdims=True)
    log_total = row_max + jnp.log(jnp.sum(jnp.exp(scores - row_max), axis=-1, keepdims=True))
    attn_probs = jnp.exp(scores - log_total)
    probs_low = attn_probs.astype(jnp.bfloat16)
    mixed_perm = jnp.einsum(
        "ghcqk,ghckd->ghcqd", probs_low, value_sel, preferred_element_type=jnp.float32
    ).reshape(groups, HEADS, local_len, head_dim)
    attended = from_heads(reorder(mixed_perm, inverse)).astype(jnp.bfloat16)
    branch = jnp.dot(attended, full_out, preferred_element_type=jnp.float32) + bias_out.astype(
        jnp.float32
    )
    resid = flat_tokens.astype(jnp.float32) + branch
    normed, pull_first = jax.vjp(
        norm_rows, resid, norm_gain1.astype(jnp.float32), norm_shift1.astype(jnp.float32)
    )
    normed_low = normed.astype(jnp.bfloat16)
    inner_sum = jnp.dot(normed_low, full_up, preferred_element_type=jnp.float32) + bias_up.astype(
        jnp.float32
    )
    active, pull_gelu = jax.vjp(gelu_exact, inner_sum)
    active_low = active.astype(jnp.bfloat16)
    outer_sum = jnp.dot(
        active_low, full_down, preferred_element_type=jnp.float32
    ) + bias_down.astype(jnp.float32)
    final_rows, pull_second = jax.vjp(
        norm_rows,
        normed + outer_sum,
        norm_gain2.astype(jnp.float32),
        norm_shift2.astype(jnp.float32),
    )
    result = final_rows.astype(jnp.bfloat16).reshape(groups, local_len, width)
    back_weights = (
        lax.all_gather(w_query, BOTH, axis=0, tiled=True),
        lax.all_gather(w_key, BOTH, axis=0, tiled=True),
        lax.all_gather(w_value, BOTH, axis=0, tiled=True),
        lax.all_gather(w_out, BOTH, axis=0, tiled=True),
        lax.all_gather(w_up, BOTH, axis=0, tiled=True),
        lax.all_gather(w_down, BOTH, axis=0, tiled=True),
        lax.all_gather(b_query, BOTH, axis=0, tiled=True),
        lax.all_gather(b_value, BOTH, axis=0, tiled=True),
        lax.all_gather(b_out, BOTH, axis=0, tiled=True),
        lax.all_gather(b_up, BOTH, axis=0, tiled=True),
        lax.all_gather(b_down, BOTH, axis=0, tiled=True),
        lax.all_gather(gain_attn, BOTH, axis=0, tiled=True),
        lax.all_gather(shift_attn, BOTH, axis=0, tiled=True),
        lax.all_gather(gain_ffn, BOTH, axis=0, tiled=True),
        lax.all_gather(shift_ffn, BOTH, axis=0, tiled=True),
    )
    back_query, back_key, back_value, back_out, back_up, back_down = back_weights[:6]
    upstream = grad_out.reshape(row_count, width).astype(jnp.float32) * masked.reshape(
        row_count, 1
    ).astype(jnp.float32)
    d_sum2, d_gain2, d_shift2 = pull_second(upstream)
    d_outer = d_sum2.astype(jnp.bfloat16)
    g_down = jnp.einsum("rf,rd->fd", active_low, d_outer, preferred_element_type=jnp.float32)
    g_bdown = jnp.sum(d_outer.astype(jnp.float32), axis=0)
    d_active = jnp.einsum("rd,fd->rf", d_outer, back_down, preferred_element_type=jnp.float32)
    d_inner = pull_gelu(d_active)[0].astype(jnp.bfloat16)
    g_up = jnp.einsum("rd,rf->df", normed_low, d_inner, preferred_element_type=jnp.float32)
    g_bup = jnp.sum(d_inner.astype(jnp.float32), axis=0)
    d_normed = d_sum2 + jnp.einsum(
        "rf,df->rd", d_inner, back_up, preferred_element_type=jnp.float32
    )
    d_resid, d_gain1, d_shift1 = pull_first(d_normed)
    d_branch = d_resid.astype(jnp.bfloat16)
    g_out = jnp.einsum("ri,rd->id", attended, d_branch, preferred_element_type=jnp.float32)
    g_bout = jnp.sum(d_branch.astype(jnp.float32), axis=0)
    d_attended = jnp.einsum(
        "rd,id->ri", d_branch, back_out, preferred_element_type=jnp.float32
    ).astype(jnp.bfloat16)
    d_mixed = reorder(to_heads(d_attended, groups, local_len), token_order).reshape(cluster_shape)
    scores_again = (
        jnp.einsum("ghcqd,ghckd->ghcqk", query_perm, key_sel, preferred_element_type=jnp.float32)
        * score_scale
    )
    probs_again = jnp.exp(scores_again - log_total)
    probs_again_low = probs_again.astype(jnp.bfloat16)
    d_probs = jnp.einsum(
        "ghcqd,ghckd->ghcqk", d_mixed, value_sel, preferred_element_type=jnp.float32
    )
    d_scores = (
        probs_again * (d_probs - jnp.sum(probs_again * d_probs, axis=-1, keepdims=True))
    ).astype(jnp.bfloat16)
    d_query_perm = (
        jnp.einsum("ghcqk,ghckd->ghcqd", d_scores, key_sel, preferred_element_type=jnp.float32)
        * score_scale
    )
    d_key_sel = (
        jnp.einsum("ghcqk,ghcqd->ghckd", d_scores, query_perm, preferred_element_type=jnp.float32)
        * score_scale
    )
    d_value_sel = jnp.einsum(
        "ghcqk,ghcqd->ghckd", probs_again_low, d_mixed, preferred_element_type=jnp.float32
    )
    sent = jnp.concatenate([d_key_sel, d_value_sel], axis=-1)
    my_start = lax.axis_index(BLK) * clusters
    piece_grads = lax.all_gather(sent.astype(jnp.bfloat16), BLK, axis=2, tiled=True).astype(
        jnp.float32
    )
    piece_match = lax.all_gather(
        cluster_match.astype(jnp.float32).astype(jnp.bfloat16), BLK, axis=2, tiled=True
    ).astype(jnp.float32)
    offset = piece_match.astype(jnp.int32) - my_start
    select = (offset[..., None] == jnp.arange(clusters, dtype=jnp.int32)).astype(jnp.float32)
    owned = jnp.zeros(sent.shape, jnp.float32) + jnp.einsum(
        "ghjc,ghjke->ghcke", select, piece_grads, precision=lax.Precision.HIGHEST
    )
    back_kv = reorder(owned.reshape(groups, HEADS, local_len, 2 * head_dim), inverse)
    d_key = from_heads(back_kv[..., :head_dim]).astype(jnp.bfloat16)
    d_value = from_heads(back_kv[..., head_dim:]).astype(jnp.bfloat16)
    d_query = from_heads(
        reorder(d_query_perm.reshape(groups, HEADS, local_len, head_dim), inverse)
    ).astype(jnp.bfloat16)
    g_query = jnp.einsum("ri,rd->id", flat_tokens, d_query, preferred_element_type=jnp.float32)
    g_key = jnp.einsum("ri,rd->id", flat_tokens, d_key, preferred_element_type=jnp.float32)
    g_value = jnp.einsum("ri,rd->id", flat_tokens, d_value, preferred_element_type=jnp.float32)
    g_bquery = jnp.sum(d_query.astype(jnp.float32), axis=0)
    g_bvalue = jnp.sum(d_value.astype(jnp.float32), axis=0)
    d_tokens_flat = (
        d_resid
        + jnp.einsum("rd,id->ri", d_query, back_query, preferred_element_type=jnp.float32)
        + jnp.einsum("rd,id->ri", d_key, back_key, preferred_element_type=jnp.float32)
        + jnp.einsum("rd,id->ri", d_value, back_value, preferred_element_type=jnp.float32)
    )
    summed = (
        lax.psum_scatter(g_query, BOTH, scatter_dimension=0, tiled=True),
        lax.psum_scatter(g_key, BOTH, scatter_dimension=0, tiled=True),
        lax.psum_scatter(g_value, BOTH, scatter_dimension=0, tiled=True),
        lax.psum_scatter(g_out, BOTH, scatter_dimension=0, tiled=True),
        lax.psum_scatter(g_up, BOTH, scatter_dimension=0, tiled=True),
        lax.psum_scatter(g_down, BOTH, scatter_dimension=0, tiled=True),
        lax.psum_scatter(g_bquery, BOTH, scatter_dimension=0, tiled=True),
        lax.psum_scatter(g_bvalue, BOTH, scatter_dimension=0, tiled=True),
        lax.psum_scatter(g_bout, BOTH, scatter_dimension=0, tiled=True),
        lax.psum_scatter(g_bup, BOTH, scatter_dimension=0, tiled=True),
        lax.psum_scatter(g_bdown, BOTH, scatter_dimension=0, tiled=True),
        lax.psum_scatter(d_gain1, BOTH, scatter_dimension=0, tiled=True),
        lax.psum_scatter(d_shift1, BOTH, scatter_dimension=0, tiled=True),
        lax.psum_scatter(d_gain2, BOTH, scatter_dimension=0, tiled=True),
        lax.psum_scatter(d_shift2, BOTH, scatter_dimension=0, tiled=True),
    )
    return (result, d_tokens_flat.reshape(groups, local_len, width)) + tuple(summed)


OWN, NEAR, FAR, NEARFAR = range(4)
NT = (((1,), (1,)), ((), ()))
TN = (((0,), (0,)), ((), ()))


class Place:
    def __init__(self):
        s, b = lax.axis_index(SEQ), lax.axis_index(BLK)
        self.s, self.b = s, b
        z, c = b // 2, b % 2
        self.z, self.c = z, c
        self.zlo, self.zhi = z % 2, z // 2
        self.sx = s + 1 - 2 * (s % 2)
        self.sy = s + 2 - 4 * (s // 2)
        self.sd = self.sy + 1 - 2 * (s % 2)
        self.zn = z + 1 - 2 * self.zlo
        self.zf = z + 2 - 4 * self.zhi
        self.znf = self.zf + 1 - 2 * self.zlo
        self.bc = b + 1 - 2 * c
        self.bn, self.bf, self.bnf = self.zn * 2 + c, self.zf * 2 + c, self.znf * 2 + c
        self.core = (s, self.bc)
        self.n = (s, self.bn)
        self.f = (s, self.bf)
        self.nf = (s, self.bnf)
        self.x = (self.sx, b)
        self.y = (self.sy, b)


class Wire:
    def __init__(self, send, recv, local):
        self.send, self.recv, self.local = send, recv, local
        self.n_send = self.n_local = self.n_recv = 0
        self.sent, self.slots, self.lots = [], {}, {}

    def slot(self, key):
        if key not in self.slots:
            self.slots[key] = self.n_recv
            self.n_recv += 1
        return self.slots[key]

    def put(self, src, dst, to, key, lot=None):
        at = self.slot(key)
        if lot is None or lot not in self.lots:
            index = self.n_send
            self.n_send += 1
            if lot is not None:
                self.lots[lot] = index
        else:
            index = self.lots[lot]
        cp = pltpu.make_async_remote_copy(
            src, dst, self.send.at[index], self.recv.at[at], device_id=to, device_id_type=MESH
        )
        cp.start()
        if lot is None:
            self.sent.append(cp)

    def got(self, dst, key):
        at = self.slot(key)
        pltpu.make_async_copy(dst, dst, self.recv.at[at]).wait()

    def move(self, src, dst):
        cp = pltpu.make_async_copy(src, dst, self.local.at[self.n_local])
        self.n_local += 1
        cp.start()
        return cp

    def finish(self, sizes):
        for lot, ref in sizes.items():
            pltpu.make_async_copy(ref, ref, self.send.at[self.lots[lot]]).wait()
        for cp in self.sent:
            cp.wait_send()


def greet(peers):
    bar = pltpu.get_barrier_semaphore()
    for to in peers:
        pl.semaphore_signal(bar, inc=1, device_id=to, device_id_type=MESH)
    pl.semaphore_wait(bar, len(peers))


def loop(n, body):
    def run(i, carry):
        body(i)
        return carry

    lax.fori_loop(0, n, run, 0)


def joined(v):
    return v.astype(F32).reshape(768, v.shape[-1]).astype(BF16)


def mean(v):
    return jnp.mean(v, axis=-1, keepdims=True)


def total(v):
    return jnp.sum(v, axis=0, keepdims=True)


def layer_kernel(
    tok_h, go_h, mask, cm, wq, wk, wv, wo_s, wu_s, wd_s,
    *others,
):
    vectors, (result, od, ou, oo, oqkv, dtok, ovec, sc, *sems) = others[:9], others[9:]
    p = Place()
    w = Wire(*sems)
    s, b, z, c = p.s, p.b, p.z, p.c
    zp, g = p.zlo, p.zhi
    zs = (z, p.zn, p.zf, p.znf)
    wou, wd, wqkv, xg, qkv, att = (sc[k] for k in ("wou", "wd", "wqkv", "xg", "qkv", "att"))
    match, m_smem, stage, rows, bup = (sc[k] for k in ("match", "ms", "stage", "rows", "bup"))

    raw = sc["raw"]
    early = [w.move(ref, raw.at[t]) for t, ref in enumerate((wq, wk, wv))]
    tok, grad = sc["tok"], sc["grad"]
    slot = s * 8 + b
    mine = [
        w.move(wo_s, wou.at[slot, :, pl.ds(0, 768)]), w.move(wu_s, wou.at[slot, :, pl.ds(768, 3072)]),
        w.move(wd_s, wd.at[pl.ds(pl.multiple_of(96 * slot, 96), 96)]), w.move(tok_h.at[g], xg.at[b]),
    ]
    tok_in, grad_in = w.move(tok_h, tok), w.move(go_h, grad)
    greet([p.core, p.n, p.f, p.nf, p.x, p.y, (s, p.zn * 2 + 1 - c), (s, p.zf * 2 + 1 - c), (s, p.znf * 2 + 1 - c)])

    def at_rows(n, ss, zz, cc):
        return pl.ds(pl.multiple_of(n * (ss * 8 + zz * 2 + cc), 8), n)

    def reg(k, ss, u, cc, half=None):
        zz = zs[u]
        if k == 0:
            cols = (pl.ds(0, 384), pl.ds(0, 256), pl.ds(256, 128))[0 if half is None else 1 + half]
            return wqkv.at[ss * 8 + zz * 2 + cc, :, cols]
        if k == 1:
            cols = (pl.ds(0, 3840), pl.ds(0, 1792), pl.ds(1792, 2048))[0 if half is None else 1 + half]
            return wou.at[ss * 8 + zz * 2 + cc, :, cols]
        cols = pl.ds(0, 768) if half is None else pl.ds(384 * half, 384)
        return wd.at[at_rows(96, ss, zz, cc), cols]

    def to_plane(k, u, src=None):
        r = reg(k, s, u, c)
        src = r if src is None else src
        w.put(src, r, p.x, (0, k, u), lot=k)
        w.put(src, r, p.y, (1, k, u), lot=k)

    def to_core(k, ss, u):
        r = reg(k, ss, u, c)
        group = [v is ss for v in (s, p.sx, p.sy, p.sd)].index(True) if k == 2 else 0
        w.put(r, r, p.core, (5, k, group), lot=k)

    def z_start(k):
        r = reg(k, s, OWN, c)
        w.put(r, r, p.n, (2, k), lot=k)
        w.put(r, r, p.f, (3, k), lot=k)

    def near(k):
        w.got(reg(k, s, NEAR, c), (2, k))
        to_plane(k, NEAR)
        to_core(k, s, NEAR)

    def far(k):
        r = reg(k, s, FAR, c)
        w.got(r, (3, k))
        w.put(r, r, p.n, (4, k), lot=k)
        to_plane(k, FAR)
        to_core(k, s, FAR)

    def nearfar(k):
        w.got(reg(k, s, NEARFAR, c), (4, k))
        to_plane(k, NEARFAR)
        to_core(k, s, NEARFAR)

    def turn(k, u):
        w.got(reg(k, p.sx, u, c), (0, k, u))
        r = reg(k, p.sx, u, c, 0)
        w.put(r, r, p.y, (6, k, u), lot=k)
        to_core(k, p.sx, u)
        w.got(reg(k, p.sy, u, c), (1, k, u))
        r = reg(k, p.sy, u, c, 1)
        w.put(r, r, p.x, (6, k, u), lot=k)
        to_core(k, p.sy, u)

    def corner(k, u):
        w.got(reg(k, p.sd, u, c), (6, k, u))
        to_core(k, p.sd, u)

    def complete(k):
        w.got((wqkv.at[pl.ds(0, 16)], wou.at[pl.ds(0, 16)])[k], (5, k, 0))

    own = reg(0, s, OWN, c)

    def own_out_up(to, key):
        w.put(wu_s, wou.at[slot, :, pl.ds(768, 3072)], to, key, lot=1)
        w.put(wo_s, wou.at[slot, :, pl.ds(0, 768)], to, key, lot=1)

    own_out_up(p.n, (2, 1))
    own_out_up(p.x, (0, 1, OWN))
    own_out_up(p.y, (1, 1, OWN))
    own_out_up(p.f, (3, 1))
    for cp in early:
        cp.wait()
    vec_own, match_own = sc["vo"], sc["mo"]
    vec_own[...] = jnp.zeros_like(vec_own)
    for k, ref in enumerate(vectors):
        vec_own[0:1, 24 * k : 24 * k + ref.shape[0]] = ref[...].astype(F32).reshape(1, ref.shape[0])
    for h in range(2):
        parts = [raw[t, :, 384 * h : 384 * (h + 1)].astype(F32) for t in range(3)]
        stage[h] = jnp.concatenate(parts + [vec_own[...]], axis=0).astype(BF16)
    w.put(stage.at[1 - zp], own, p.n, (2, 0), lot=0)
    w.put(stage.at[zp], own, p.f, (3, 0), lot=0)
    w.put(stage.at[1 - zp], own, p.nf, (4, 0), lot=0)
    w.put(stage.at[zp], own, p.x, (0, 0, OWN), lot=0)
    w.put(stage.at[zp], own, p.y, (1, 0, OWN), lot=0)
    w.put(tok_h.at[1 - g], xg.at[b], p.f, 21)
    w.put(tok_h.at[g], xg.at[b], p.n, 20)
    to_plane(2, OWN, wd_s)
    match_own[...] = jnp.zeros_like(match_own)
    match_own[0:2, 0:12] = cm[...]
    for zz in zs:
        for cc in (c, 1 - c):
            if not (zz is z and cc is c):
                w.put(match_own, match.at[b], (s, zz * 2 + cc), 92, lot=92)
    w.put(tok_h.at[g], xg.at[b], p.core, 23)
    mine += [w.move(stage.at[zp], own), w.move(match_own, match.at[b])]
    dap, ds_buf, p_buf, dqkv = (sc[k] for k in ("dap", "ds", "p", "dqkv"))
    left = lax.broadcasted_iota(jnp.int32, (128, 128), 1) < 64
    zero = jnp.zeros((128, 128), BF16)
    for i in range(4):
        other = 2 * i + 1 - c
        dap[1, other] = zero
        dqkv[0, 1, other] = zero
        for e in range(2):
            ds_buf[1, e, other] = zero
            p_buf[1, e, other] = zero
    for cp in mine:
        cp.wait()
    for k in range(3):
        to_core(k, s, OWN)
    near(1)
    turn(1, OWN)
    far(1)
    z_start(2)
    for u, name in ((NEAR, 2), (FAR, 3), (NEARFAR, 4)):
        w.got(reg(0, s, u, c), (name, 0))
        to_plane(0, u)
        to_core(0, s, u)
    turn(0, OWN)
    turn(2, OWN)
    w.got(xg.at[p.bf], 21)
    w.put(xg.at[p.bf], xg.at[p.bf], p.n, 22)
    w.put(xg.at[p.bf], xg.at[p.bf], p.core, 23)
    w.got(xg.at[p.bn], 20)
    w.put(xg.at[p.bn], xg.at[p.bn], p.core, 23)
    turn(1, NEAR)
    corner(1, OWN)
    for u in (NEAR, FAR, NEARFAR):
        turn(0, u)
    nearfar(1)
    turn(1, FAR)
    for u in range(4):
        corner(0, u)
    w.got(match.at[pl.ds(0, 7)], 92)
    get_match = w.move(match, m_smem)
    w.got(xg.at[p.bnf], 22)
    w.put(xg.at[p.bnf], xg.at[p.bnf], p.core, 23)
    near(2)
    far(2)
    corner(1, NEAR)
    turn(1, NEARFAR)
    complete(0)
    w.got(xg.at[pl.ds(0, 4)], 23)

    lane = lax.broadcasted_iota(jnp.int32, (32, 768), 1)
    mine_lane = ((lane * 2731) >> 16) == lax.broadcasted_iota(jnp.int32, (32, 768), 0)
    lane2 = lax.broadcasted_iota(jnp.int32, (384, 768), 1)
    place = lane2 - 24 * ((lane2 * 2731) >> 16) - lax.broadcasted_iota(jnp.int32, (384, 768), 0)
    flat_vec = wqkv[:, 64:80, :].astype(F32)[:, 8, :].astype(BF16)

    def vector_row(k):
        part = jnp.dot(flat_vec, (place == -24 * k).astype(F32).astype(BF16), preferred_element_type=F32)
        rows[k] = jnp.sum(jnp.where(mine_lane, part, 0.0), axis=0, keepdims=True)

    def up_row(i):
        l3 = lax.broadcasted_iota(jnp.int32, (384, 768), 1) + 768 * i
        d3 = (l3 * 43691) >> 22
        hit = l3 - 96 * d3 - lax.broadcasted_iota(jnp.int32, (384, 768), 0) == -192
        part = jnp.dot(flat_vec, hit.astype(F32).astype(BF16), preferred_element_type=F32)
        owner = ((lax.broadcasted_iota(jnp.int32, (32, 768), 1) + 768 * i) * 43691) >> 22
        here = owner == lax.broadcasted_iota(jnp.int32, (32, 768), 0)
        bup[:, 768 * i : 768 * (i + 1)] = jnp.sum(jnp.where(here, part, 0.0), axis=0, keepdims=True)

    vector_row(0)
    vector_row(1)

    c0 = pl.multiple_of(128 * c, 128)
    b0 = pl.multiple_of(384 * zp + 128 * c, 128)
    b1 = pl.multiple_of(384 * zp + 256, 128)

    columns = sc["cols"]
    for i, v in enumerate((wqkv[:, :, pl.ds(c0, 128)].astype(F32), wqkv[:, :, 256:384].astype(F32))):
        for t in range(3):
            first = 256 * t + 128 * i
            columns[:, first : first + 128] = v[:, 24 * t : 24 * t + 24].reshape(768, 128).astype(BF16)
    for m in range(4):
        r = jnp.dot(xg[2 * m : 2 * m + 2].reshape(256, 768), columns[...], preferred_element_type=F32)
        for t in range(3):
            for tl in range(2):
                part = r[:, 256 * t + 128 * tl : 256 * t + 128 * (tl + 1)]
                if t != 1:
                    part = part + rows[t // 2, :, pl.ds(b1 if tl else b0, 128)]
                qkv[t, tl, 2 * m : 2 * m + 2] = part.astype(BF16).reshape(2, 128, 128)

    get_match.wait()
    att_buf = sc["ab"]

    def mask_head(e, v):
        return jnp.where(left if e == 0 else jnp.logical_not(left), v, zero)

    def weights(e, q, k):
        score = lax.dot_general(mask_head(e, q), k, NT, preferred_element_type=F32) * 0.125
        ex = jnp.exp(score - jnp.max(score, axis=-1, keepdims=True))
        return ex * (1.0 / jnp.sum(ex, axis=-1, keepdims=True))

    def head(tl, e):
        return 6 * zp + (2 * c if tl == 0 else 4) + e

    def attend(tl, blk, i):
        q = qkv[0, tl, blk]
        outs = []
        for e in range(2):
            m = m_smem[blk, g, head(tl, e)]
            pr = weights(e, q, qkv[1, tl, m]).astype(BF16)
            p_buf[tl, e, blk] = pr
            outs.append(jnp.dot(pr, qkv[2, tl, m], preferred_element_type=F32))
        att_buf[i] = jnp.where(left, outs[0], outs[1]).astype(BF16)


    def send_tile(tl, zz, cc, i):
        dst = att.at[g, :, pl.ds(pl.multiple_of(384 * zp + (128 * c if tl == 0 else 256), 128), 128)]
        if i in (0, 8):
            keep.append(w.move(att_buf.at[i], dst))
        else:
            w.put(att_buf.at[i], dst, (s, zz * 2 + cc), 90, lot=90)

    between = (
        lambda: (nearfar(2), corner(2, OWN)), lambda: (turn(2, NEAR), corner(1, FAR)),
        lambda: (corner(1, NEARFAR), turn(2, FAR)), lambda: corner(2, NEAR),
    )
    keep = []
    for j, zz in enumerate((p.zf, p.znf, p.zn, z)):
        trio = [(0, c, 0 if zz is z else 1 + 2 * j), (0, 1 - c, 2 + 2 * j if j < 3 else 7), (1, c, 8 if zz is z else 9 + j)]
        for tl, cc, i in trio:
            attend(tl, zz * 2 + cc, i)
        for tl, cc, i in trio:
            send_tile(tl, zz, cc, i)
        between[j]()
    for k in range(2, 8):
        vector_row(k)
    for i in range(4):
        up_row(i)
    complete(1)

    w.got(att_buf.at[pl.ds(0, 10)], 90)
    for cp in keep + [tok_in, grad_in]:
        cp.wait()

    n1, nlow, act, slope, dh2 = (sc[k] for k in ("n1", "nlow", "act", "slope", "dh2"))
    dtk = sc["dtk"]
    dinner = dtk.reshape(4, 256, 768)

    def whole(ref):
        return ref[...].reshape(256, 768)

    h = whole(tok).astype(F32) + jnp.dot(whole(att), joined(wou[:, :, 0:768]), preferred_element_type=F32) + rows[2]
    h = h - mean(h)
    r1 = lax.rsqrt(mean(h * h) + EPS)
    n1[...] = h * r1
    nlow[...] = (n1[...] * rows[4] + rows[5]).astype(BF16)

    def up(j):
        cols = slice(512 * j, 512 * (j + 1))
        u = jnp.dot(nlow[...], joined(wou[:, :, 768 + 512 * j : 768 + 512 * (j + 1)]), preferred_element_type=F32) + bup[:, cols]
        cdf = 0.5 + 0.5 * lax.erf(u * 0.7071067811865476)
        act[:, cols] = (u * cdf).astype(BF16)
        slope[:, cols] = cdf + u * (jnp.exp(-0.5 * u * u) * 0.3989422804014327)

    up(0)
    up(1)
    up(2)
    turn(2, NEARFAR)
    up(3)
    corner(2, FAR)
    up(4)
    up(5)

    def down(group, ss):
        w.got(wd.at[pl.ds(0, 384)], (5, 2, group))
        part = pl.ds(pl.multiple_of(768 * ss, 768), 768)
        return jnp.dot(act[:, part], wd[part, :], preferred_element_type=F32)

    dh2[...] = n1[...] * rows[4] + (rows[3] + rows[5])
    for group, ss in enumerate((s, p.sx, p.sy)):
        dh2[...] += down(group, ss)
    corner(2, NEARFAR)
    h = dh2[...] + down(3, p.sd)
    h = h - mean(h)
    r2 = lax.rsqrt(mean(h * h) + EPS)
    n2 = h * r2
    eye = lax.broadcasted_iota(jnp.int32, (128, 128), 0) == lax.broadcasted_iota(jnp.int32, (128, 128), 1)
    keepers = [
        jnp.sum(jnp.where(eye, mask[i : i + 1].astype(F32), 0.0), axis=-1, keepdims=True) for i in range(2)
    ]
    gr = whole(grad).astype(F32) * jnp.concatenate(keepers, axis=0)
    sums = sc["sums"]
    e = gr * rows[6]
    d = r2 * (e - mean(e) - n2 * mean(e * n2))
    dh2[...] = d
    dz = sc["dz"]
    dz[...] = d.astype(BF16)

    gd, gu, go, gq, gvec = (sc[k] for k in ("gd", "gu", "go", "gq", "gvec"))

    def down_gradient(ss):
        for i in range(2):
            columns = pl.ds(pl.multiple_of(768 * ss + 384 * i, 128), 384)
            r = lax.dot_general(act[:, columns], dz[...], TN, preferred_element_type=F32)
            gd[ss, 2 * i : 2 * i + 2] = r.astype(BF16).reshape(2, 2, 96, 768)

    chunks = [
        (gd, od, 0, 48, 0, 768),
        (gd, od, 48, 48, 0, 768),
        (gu, ou, 0, 24, 0, 1536),
        (gu, ou, 0, 24, 1536, 1536),
        (go, oo, 0, 24, 0, 768),
        (gvec.reshape(4, 4, 2, 8, 256), ovec, 0, 8, 0, 256),
    ]
    bufs = sc["bufs"]

    def cols(k, half):
        nc = chunks[k][5]
        first = 640 if k == 3 else nc // 2
        return pl.ds(first * half, nc - first if half else first)

    def pair_start(k, which):
        v, out, q0, nr, k0, nc = chunks[k]
        for ss in which:
            src = v.at[ss, :, 1 - c, pl.ds(q0, nr), pl.ds(k0, nc)]
            w.put(src, bufs[k][0].at[ss], p.core, (50 if ss is p.sd else 49, k), lot=50 + k)

    far_column, rest = (p.sd,), (p.sx, p.sy, s)

    def add(k, ss):
        v, out, q0, nr, k0, nc = chunks[k]
        rc = bufs[k][0]

        def one(i):
            rc[ss, i] = rc[ss, i] + v[ss, i, c, q0 : q0 + nr, k0 : k0 + nc]

        loop(4, one)

    def pair_far(k):
        rc, rdx, rdy, rx, ry, rz = bufs[k]
        w.got(rc.at[p.sd], (50, k))
        add(k, p.sd)
        w.put(rc.at[p.sd, :, :, cols(k, 0)], rdx, p.x, (51, k), lot=50 + k)
        w.put(rc.at[p.sd, :, :, cols(k, 1)], rdy, p.y, (52, k), lot=50 + k)

    def pair_rest(k):
        rc, rdx, rdy, rx, ry, rz = bufs[k]
        w.got(rc.at[pl.ds(0, 3)], (49, k))
        add(k, p.sx)
        w.put(rc.at[p.sx, :, :, cols(k, 0)], rx.at[:, :, cols(k, 0)], p.x, (53, k), lot=50 + k)
        add(k, p.sy)
        w.put(rc.at[p.sy, :, :, cols(k, 1)], ry.at[:, :, cols(k, 1)], p.y, (54, k), lot=50 + k)
        add(k, s)

    def diagonal(k):
        rc, rdx, rdy, rx, ry, rz = bufs[k]
        w.got(rdx, (51, k))
        rc[p.sy, :, :, cols(k, 0)] = rc[p.sy, :, :, cols(k, 0)] + rdx[...]
        w.put(rc.at[p.sy, :, :, cols(k, 0)], ry.at[:, :, cols(k, 0)], p.y, (54, k), lot=50 + k)
        w.got(rdy, (52, k))
        rc[p.sx, :, :, cols(k, 1)] = rc[p.sx, :, :, cols(k, 1)] + rdy[...]
        w.put(rc.at[p.sx, :, :, cols(k, 1)], rx.at[:, :, cols(k, 1)], p.x, (53, k), lot=50 + k)

    def plane(k):
        rc, rdx, rdy, rx, ry, rz = bufs[k]
        w.got(rx, (53, k))
        w.got(ry, (54, k))

        def one(i):
            rc[s, i] = (rc[s, i].astype(F32) + rx[i].astype(F32) + ry[i].astype(F32)).astype(rc.dtype)

        loop(4, one)
        w.put(rc.at[s, p.znf], rz.at[0], p.n, (57, k), lot=50 + k)

    def plane_end(k):
        rc, rdx, rdy, rx, ry, rz = bufs[k]
        w.put(rc.at[s, p.zn], rz.at[1], p.n, (58, k), lot=50 + k)

    def last(k):
        rc, rdx, rdy, rx, ry, rz = bufs[k]
        w.got(rz.at[0], (57, k))
        rc[s, p.zf] = rc[s, p.zf] + rz[0]
        w.put(rc.at[s, p.zf], rz.at[2], p.f, (58, k), lot=50 + k)

    def final(k):
        v, out, q0, nr, k0, nc = chunks[k]
        rc, rdx, rdy, rx, ry, rz = bufs[k]
        w.got(rz.at[pl.ds(1, 2)], (58, k))
        out[q0 : q0 + nr, k0 : k0 + nc] = rc[s, z].astype(F32) + rz[1].astype(F32) + rz[2].astype(F32)

    down_gradient(p.sd)
    for k in range(2):
        pair_start(k, far_column)

    def inner_gradient(j):
        cc = slice(768 * j, 768 * (j + 1))
        r = lax.dot_general(dz[...], wd[cc, :], NT, preferred_element_type=F32)
        r = (r * slope[:, cc]).astype(BF16)
        dinner[j] = r

    for j in range(4):
        inner_gradient(j)
    pair_far(0)
    pair_far(1)
    d = dh2[...]
    for j in range(4):
        wt = joined(wou[:, :, 768 + 768 * j : 768 + 768 * (j + 1)])
        d = d + lax.dot_general(dinner[j], wt, NT, preferred_element_type=F32)
    d_normed = d
    e = d * rows[4]
    d = r1 * (e - mean(e) - n1[...] * mean(e * n1[...]))
    dh1 = dh2
    dh1[...] = d
    dbr = sc["dbr"]
    dbr[...] = d.astype(BF16)
    datt = sc["datt"]
    r = lax.dot_general(dbr[...], joined(wou[:, :, 0:768]), NT, preferred_element_type=F32)
    datt[...] = r.astype(BF16).reshape(2, 128, 768)

    here = []
    for chip, zz in ((1, p.zn), (2, p.zf), (3, p.znf), (0, z)):
        gg, zq = zz // 2, zz % 2
        for tl, cc in ((0, 1 - c), (0, c), (1, c)):
            src = datt.at[gg, :, pl.ds(pl.multiple_of(384 * zq + (256 if tl else 128 * cc), 128), 128)]
            if zz is z and cc is c:
                here.append(w.move(src, dap.at[tl, b]))
            else:
                w.put(src, dap.at[tl, b], (s, zz * 2 + cc), (91, chip), lot=91)

    def up_gradient(j):
        r = lax.dot_general(nlow[...], dinner[j], TN, preferred_element_type=F32)
        gu[:, :, :, :, 768 * j : 768 * (j + 1)] = r.reshape(4, 4, 2, 24, 768).astype(BF16)

    for ss in rest:
        down_gradient(ss)
    for k in range(2):
        pair_start(k, rest)

    def queries(tl, blk):
        da = dap[tl, blk]
        outs = []
        for e in range(2):
            m = m_smem[blk, g, head(tl, e)]
            k, v = qkv[1, tl, m], qkv[2, tl, m]
            pr = p_buf[tl, e, blk].astype(F32)
            dp = lax.dot_general(mask_head(e, da), v, NT, preferred_element_type=F32)
            ds = (pr * (dp - jnp.sum(pr * dp, axis=-1, keepdims=True))).astype(BF16)
            ds_buf[tl, e, blk] = ds
            outs.append(jnp.dot(ds, k, preferred_element_type=F32) * 0.125)
        dqkv[0, tl, blk] = jnp.where(left, outs[0], outs[1]).astype(BF16)

    def keys(tl, n):
        dk, dv = [], []
        for e in range(2):
            cq = 0
            for i in range(8):
                cq = jnp.where(m_smem[i, g, head(tl, e)] == n, i, cq)
            ds, pr = ds_buf[tl, e, cq], p_buf[tl, e, cq]
            dk.append(lax.dot_general(ds, qkv[0, tl, cq], TN, preferred_element_type=F32) * 0.125)
            dv.append(lax.dot_general(pr, dap[tl, cq], TN, preferred_element_type=F32))
        dqkv[1, tl, n] = jnp.where(left, dk[0], dk[1]).astype(BF16)
        dqkv[2, tl, n] = jnp.where(left, dv[0], dv[1]).astype(BF16)

    def both(f, i):
        f(2 * i)
        f(2 * i + 1)

    def queries_from(chip, zz):
        if chip == 0:
            for cp in here:
                cp.wait()
        w.got(att_buf.at[pl.ds(0, 3 if chip else 1)], (91, chip))
        queries(0, zz * 2 + c)
        queries(0, zz * 2 + 1 - c)
        queries(1, zz * 2 + c)

    queries_from(0, z)
    pair_rest(0)
    diagonal(0)
    pair_rest(1)
    diagonal(1)
    up_gradient(0)
    up_gradient(1)
    pair_start(2, far_column)
    pair_start(2, rest)
    queries_from(1, p.zn)
    pair_far(2)
    pair_rest(2)
    for j in range(4):
        sc["sup"][:, 768 * j : 768 * (j + 1)] = total(dinner[j].astype(F32))
    result[...] = (n2 * rows[6] + rows[7]).astype(BF16).reshape(2, 128, 768)
    sums[2] = total(dbr[...].astype(F32))
    sums[3] = total(dz[...].astype(F32))
    sums[4] = total(d_normed * n1[...])
    sums[5] = total(d_normed)
    sums[6] = total(gr * n2)
    sums[7] = total(gr)
    queries_from(2, p.zf)
    queries_from(3, p.znf)
    plane(0)
    plane_end(0)
    loop(4, lambda i: both(lambda n: keys(0, n), i))
    loop(4, lambda i: both(lambda n: keys(1, n), i))

    rtk, rtn, rtf = (sc[k] for k in ("rtk", "rtn", "rtf"))

    def flat(m):
        return jnp.concatenate(
            [dqkv[t, tl, 4 * m : 4 * m + 4].reshape(512, 128) for t in range(3) for tl in range(2)], axis=1
        )

    up_gradient(2)
    up_gradient(3)
    pair_start(3, far_column)
    pair_start(3, rest)
    for m in range(2):
        r = lax.dot_general(flat(m), columns[...], NT, preferred_element_type=F32)
        dtk[2 * m : 2 * m + 2] = r.astype(BF16).reshape(2, 2, 128, 768)
    w.put(dtk.at[:, 1 - c], rtk, p.core, 60)

    rq, accq, rqdx, rqdy, rqx, rqy, rqz = (sc[k] for k in ("rq", "accq", "rqdx", "rqdy", "rqx", "rqy", "rqz"))
    plane(1)
    plane_end(1)
    pair_far(3)
    pair_rest(3)
    w.got(rtk, 60)
    loop(4, lambda i: rtk.__setitem__(i, rtk[i] + dtk[i, c]))
    w.put(rtk.at[p.znf], rtn.at[0], p.n, 62)
    w.put(rtk.at[p.zn], rtn.at[1], p.n, 63)
    r = 0.0
    for m in range(2):
        x = xg[4 * m : 4 * m + 4].reshape(512, 768)
        r = r + lax.dot_general(x, flat(m), TN, preferred_element_type=F32)
    for t in range(3):
        gq[t] = r[:, 256 * t : 256 * (t + 1)].reshape(4, 4, 2, 24, 256).astype(BF16)
    w.put(gq.at[:, :, :, 1 - c], rq, p.core, 61)
    diagonal(2)
    last(0)
    last(1)
    r = lax.dot_general(whole(att), dbr[...], TN, preferred_element_type=F32)
    go[...] = r.reshape(4, 4, 2, 24, 768).astype(BF16)
    pair_start(4, far_column)
    pair_start(4, rest)

    vl = lax.broadcasted_iota(jnp.int32, (128, 768), 1)
    spot = (vl - 24 * ((vl * 2731) >> 16) == lax.broadcasted_iota(jnp.int32, (128, 768), 0)).astype(F32).astype(BF16)

    def fold(part, hit):
        high = part.astype(BF16)
        low = (part - high.astype(F32)).astype(BF16)
        return lax.dot_general(high, hit, NT, preferred_element_type=F32) + lax.dot_general(
            low, hit, NT, preferred_element_type=F32
        )

    def fold_rows(lo, n):
        part = jnp.concatenate([jnp.where(mine_lane, sums[k], 0.0) for k in range(lo, lo + n)], axis=0)
        r = fold(part, spot)
        for k in range(n):
            gvec[:, lo + k, 0:128] = r[32 * k : 32 * (k + 1)]

    gvec[:, :, 128:256] = jnp.zeros((32, 8, 128), F32)
    fold_rows(2, 6)
    r = 0.0
    for i in range(4):
        l3 = lax.broadcasted_iota(jnp.int32, (128, 768), 1) + 768 * i
        hit = (l3 - 96 * ((l3 * 43691) >> 22) == lax.broadcasted_iota(jnp.int32, (128, 768), 0)).astype(F32).astype(BF16)
        owner = ((lax.broadcasted_iota(jnp.int32, (32, 768), 1) + 768 * i) * 43691) >> 22
        at = owner == lax.broadcasted_iota(jnp.int32, (32, 768), 0)
        r = r + fold(jnp.where(at, sc["sup"][:, 768 * i : 768 * (i + 1)], 0.0), hit)
    gvec[:, 0, 128:256] = r

    sums[0] = jnp.zeros((1, 768), F32)
    sums[1] = jnp.zeros((1, 768), F32)
    for r, t in ((0, 0), (1, 2)):
        f = [total(dqkv[t, tl].reshape(1024, 128).astype(F32)) for tl in range(2)]
        sums[r, :, pl.ds(b0, 128)] = f[0]
        sums[r, :, pl.ds(b1, 128)] = f[1]
    fold_rows(0, 2)
    pair_start(5, far_column)
    pair_start(5, rest)

    w.got(rq, 61)
    o0 = pl.multiple_of(128 * (1 - c), 128)

    def pair_q(i):
        for t in range(3):
            for zz in range(4):
                accq[t, i, zz, :, pl.ds(c0, 128)] = gq[t, i, zz, c, :, 0:128]
                accq[t, i, zz, :, pl.ds(o0, 128)] = rq[t, i, zz, :, 0:128]
                accq[t, i, zz, :, 256:384] = gq[t, i, zz, c, :, 128:256] + rq[t, i, zz, :, 128:256]

    pair_q(p.sd)
    w.put(accq.at[:, p.sd, :, :, pl.ds(0, 256)], rqdx, p.x, 64)
    w.put(accq.at[:, p.sd, :, :, pl.ds(256, 128)], rqdy, p.y, 65)
    pair_far(4)
    pair_far(5)
    pair_q(p.sx)
    pair_q(p.sy)
    pair_q(s)
    pair_rest(5)
    pair_rest(4)
    w.got(rtn.at[0], 62)
    rtk[p.zf] = rtk[p.zf] + rtn[0]
    w.put(rtk.at[p.zf], rtf, p.f, 68)
    diagonal(3)
    w.got(rqdx, 64)
    accq[:, p.sy, :, :, 0:256] = accq[:, p.sy, :, :, 0:256] + rqdx[...]
    w.put(accq.at[:, p.sy], rqy, p.y, 66)
    w.got(rqdy, 65)
    accq[:, p.sx, :, :, 256:384] = accq[:, p.sx, :, :, 256:384] + rqdy[...]
    w.put(accq.at[:, p.sx], rqx, p.x, 67)
    plane(2)
    plane_end(2)
    diagonal(4)
    diagonal(5)
    plane(3)
    last(2)
    plane_end(3)
    final(0)
    final(1)
    w.got(rqx, 67)
    w.got(rqy, 66)
    for t in range(3):
        accq[t, s] = (accq[t, s].astype(F32) + rqx[t].astype(F32) + rqy[t].astype(F32)).astype(BF16)
    w.put(accq.at[:, s, p.znf], rqz.at[0], p.f, 80)
    w.put(accq.at[:, s, p.zf], rqz.at[1], p.f, 81)
    plane(4)
    plane_end(4)
    plane(5)
    plane_end(5)
    last(3)
    w.got(rqz.at[0], 80)
    accq[:, s, p.zn] = accq[:, s, p.zn] + rqz[0]
    w.put(accq.at[:, s, p.zn], rqz.at[2], p.n, 82)
    last(4)
    last(5)
    final(2)
    w.got(rtn.at[1], 63)
    w.got(rtf, 68)
    d = dh1[...].reshape(2, 128, 768)
    dtok[...] = d
    dtok[g] = dtok[g] + rtk[z].astype(F32) + rtn[1].astype(F32)
    dtok[1 - g] = dtok[1 - g] + rtf[...].astype(F32)
    w.got(rqz.at[1], 81)
    q0 = pl.multiple_of(384 * zp, 128)
    q1 = pl.multiple_of(384 * (1 - zp), 128)
    for t in range(3):
        oqkv[t, :, pl.ds(q0, 384)] = accq[t, s, z].astype(F32) + rqz[1, t].astype(F32)
    final(3)
    w.got(rqz.at[2], 82)
    for t in range(3):
        oqkv[t, :, pl.ds(q1, 384)] = rqz[2, t].astype(F32)
    final(4)
    final(5)
    w.finish({
        0: wqkv.at[pl.ds(0, 31)], 1: wou.at[pl.ds(0, 31)], 2: wd.at[pl.ds(0, 2976)],
        50: wd.at[pl.ds(0, 1488)], 51: wd.at[pl.ds(0, 1488)],
        52: wou.at[pl.ds(0, 31), :, pl.ds(0, 1536)], 53: wou.at[pl.ds(0, 31), :, pl.ds(0, 1536)],
        54: wou.at[pl.ds(0, 31), :, pl.ds(0, 768)], 55: gvec.at[pl.ds(0, 31)],
        90: att_buf.at[pl.ds(0, 10)], 91: att_buf.at[pl.ds(0, 10)], 92: match.at[pl.ds(0, 7)],
    })


def scratch():
    VM = pltpu.VMEM
    per_chunk = []
    for nr, nc in ((48, 768), (48, 768), (24, 1536), (24, 1536), (24, 768), (8, 256)):
        kind = F32 if nr == 8 else BF16
        first = 640 if len(per_chunk) == 3 else nc // 2
        shapes = ((4, 4, nr, nc), (4, nr, first), (4, nr, nc - first), (4, nr, nc), (4, nr, nc), (3, nr, nc))
        per_chunk.append(tuple(VM(shape, kind) for shape in shapes))
    return dict(
        wou=VM((32, 24, 3840), BF16), wd=VM((3072, 768), BF16), wqkv=VM((32, 80, 384), BF16), raw=VM((3, 24, 768), BF16),
        cols=VM((768, 768), BF16), gvec=VM((32, 8, 256), F32),
        xg=VM((8, 128, 768), BF16), qkv=VM((3, 2, 8, 128, 128), BF16), att=VM((2, 128, 768), BF16),
        match=VM((8, 8, 128), jnp.int32), ms=pltpu.SMEM((8, 8, 128), jnp.int32),
        stage=VM((2, 80, 384), BF16), rows=VM((8, 1, 768), F32), bup=VM((1, 3072), F32),
        tok=VM((2, 128, 768), BF16), grad=VM((2, 128, 768), BF16), vo=VM((8, 384), F32), mo=VM((8, 128), jnp.int32),
        ab=VM((12, 128, 128), BF16), dap=VM((2, 8, 128, 128), BF16), ds=VM((2, 2, 8, 128, 128), BF16),
        p=VM((2, 2, 8, 128, 128), BF16), dqkv=VM((3, 2, 8, 128, 128), BF16),
        n1=VM((256, 768), F32), nlow=VM((256, 768), BF16), act=VM((256, 3072), BF16), slope=VM((256, 3072), F32),
        dh2=VM((256, 768), F32), sums=VM((8, 1, 768), F32), sup=VM((1, 3072), F32),
        dz=VM((256, 768), BF16), dbr=VM((256, 768), BF16), datt=VM((2, 128, 768), BF16),
        gd=VM((4, 4, 2, 96, 768), BF16), gu=VM((4, 4, 2, 24, 3072), BF16), go=VM((4, 4, 2, 24, 768), BF16),
        gq=VM((3, 4, 4, 2, 24, 256), BF16), rq=VM((3, 4, 4, 24, 256), BF16), accq=VM((3, 4, 4, 24, 384), BF16),
        dtk=VM((4, 2, 128, 768), BF16), rtk=VM((4, 128, 768), BF16), rtn=VM((2, 128, 768), BF16), rtf=VM((128, 768), BF16),
        rqdx=VM((3, 4, 24, 256), BF16), rqdy=VM((3, 4, 24, 128), BF16), rqx=VM((3, 4, 24, 384), BF16),
        rqy=VM((3, 4, 24, 384), BF16), rqz=VM((3, 3, 24, 384), BF16), bufs=tuple(per_chunk),
    )


def hand_out(result, od, ou, oo, oqkv, dtok, ovec, *rest):
    outs, sem, lines = rest[:17], rest[17], rest[18:]
    pairs = [(dtok.at[i, pl.ds(64 * j, 64)], outs[1].at[i, pl.ds(64 * j, 64)]) for i in range(2) for j in range(2)]
    pairs += [(result.at[i], outs[0].at[i]) for i in range(2)]
    pairs += [(ou.at[:, pl.ds(1536 * i, 1536)], outs[6].at[:, pl.ds(1536 * i, 1536)]) for i in range(2)]
    pairs += [(od.at[pl.ds(48 * i, 48)], outs[7].at[pl.ds(48 * i, 48)]) for i in range(2)]
    pairs += [(oqkv.at[0], outs[2]), (oqkv.at[1], outs[3]), (oqkv.at[2], outs[4]), (oo, outs[5])]
    copies = [pltpu.make_async_copy(a, o, sem.at[i]) for i, (a, o) in enumerate(pairs)]
    for cp in copies:
        cp.start()
    for i, (row, line) in enumerate(zip((0, 1, 2, None, 3, 4, 5, 6, 7), lines, strict=True)):
        line[...] = ovec[0, 128:224] if row is None else ovec[row, 0:24]
        cp = pltpu.make_async_copy(line, outs[8 + i], sem.at[14 + i])
        cp.start()
        copies.append(cp)
    for cp in copies:
        cp.wait()


def column(
    tokens, grad_out, masked, token_order, cluster_match,
    w_query, w_key, w_value, w_out, w_up, w_down,
    b_query, b_value, b_out, b_up, b_down,
    gain_attn, shift_attn, gain_ffn, shift_ffn,
):
    V = pl.BlockSpec(memory_space=pltpu.VMEM)
    A = pl.BlockSpec(memory_space=pl.ANY)
    S = jax.ShapeDtypeStruct
    vectors = (b_query, b_value, b_out, b_down, gain_attn, shift_attn, gain_ffn, shift_ffn, b_up)
    got = pl.pallas_call(
        layer_kernel,
        out_shape=(
            S((2, 128, 768), BF16), S((96, 768), F32), S((24, 3072), F32), S((24, 768), F32), S((3, 24, 768), F32),
            S((2, 128, 768), F32), S((8, 256), F32),
        ),
        in_specs=[A, A, V, V] + [A] * 6 + [V] * 9,
        out_specs=(V,) * 7,
        scratch_shapes=[scratch(), *(pltpu.SemaphoreType.DMA((n,)) for n in (31, 121, 16))],
        compiler_params=pltpu.CompilerParams(collective_id=0, has_side_effects=True, vmem_limit_bytes=62 << 20),
        name="layer",
    )(tokens, grad_out, masked, cluster_match.reshape(2, 12), w_query, w_key, w_value, w_out, w_up, w_down, *vectors)
    square = S((24, 768), F32)
    outs = (S((2, 128, 768), BF16), S((2, 128, 768), F32)) + (square,) * 4 + (S((24, 3072), F32), S((96, 768), F32))
    outs += tuple(S((n,), F32) for n in (24, 24, 24, 96, 24, 24, 24, 24, 24))
    return pl.pallas_call(
        hand_out,
        out_shape=outs,
        in_specs=[V] * 7,
        out_specs=(A,) * 17,
        scratch_shapes=[pltpu.SemaphoreType.DMA((23,))] + [pltpu.VMEM((96 if i == 3 else 24,), F32) for i in range(9)],
        name="results",
    )(*got)


def solution(mesh):
    fits = mesh.shape[SEQ] == 4 and mesh.shape[BLK] == 8
    return jax.shard_map(
        column if fits else general,
        mesh=mesh,
        in_specs=(
            P(SEQ, BLK, None),
            P(SEQ, BLK, None),
            P(SEQ, BLK),
            P(SEQ, None, BLK),
            P(SEQ, None, BLK),
            P(BOTH, None),
            P(BOTH, None),
            P(BOTH, None),
            P(BOTH, None),
            P(BOTH, None),
            P(BOTH, None),
            P(BOTH),
            P(BOTH),
            P(BOTH),
            P(BOTH),
            P(BOTH),
            P(BOTH),
            P(BOTH),
            P(BOTH),
            P(BOTH),
        ),
        out_specs=(
            P(SEQ, BLK, None),
            P(SEQ, BLK, None),
            P(BOTH, None),
            P(BOTH, None),
            P(BOTH, None),
            P(BOTH, None),
            P(BOTH, None),
            P(BOTH, None),
            P(BOTH),
            P(BOTH),
            P(BOTH),
            P(BOTH),
            P(BOTH),
            P(BOTH),
            P(BOTH),
            P(BOTH),
            P(BOTH),
        ),
        check_vma=False,
    )
```
